32 devices in a mesh: dp: 2 (over y), ctx: 4 (over x, core), exp: 4 (over z).
Axes of the slice: x: 2, y: 2, z: 4, core: 2. Of those that a mesh axis runs over, the one named last changes fastest.
Arguments:
- tokens: bfloat16 [2, 4, 512, 2048], P('dp', 'exp', 'ctx'), may hold values from -6 to 6
- cotangent: bfloat16 [2, 4, 512, 2048], P('dp', 'exp', 'ctx'), may hold values from -6 to 6
- positions: int32 [2, 4, 512], P('dp', 'exp', 'ctx'), may hold values from 0 to 511, each once within a row
- lengths: int32 [2, 4, 3], P('dp', 'exp'), may hold values from 1 to 384, 512 in all within a row
- routes: int32 [2, 4, 512, 4], P('dp', 'exp', 'ctx'), may hold values from 0 to 7, all different within a row; in each aligned block of 128 rows (0 to 127, 128 to 255, ..., all dimensions but the last counted through in order) at most 128 rows name the same one
- norm_attn: bfloat16 [2048], P(('dp', 'ctx', 'exp')), may hold values from 0.5 to 1.5
- w_query: bfloat16 [2048, 2048], P(('dp', 'ctx', 'exp')), may hold values from -0.125 to 0.125
- bias_query: bfloat16 [2048], P(('dp', 'ctx', 'exp')), may hold values from -0.59765625 to 0.59765625
- w_key: bfloat16 [2048, 2048], P(('dp', 'ctx', 'exp')), may hold values from -0.125 to 0.125
- bias_key: bfloat16 [2048], P(('dp', 'ctx', 'exp')), may hold values from -0.59765625 to 0.59765625
- w_value: bfloat16 [2048, 2048], P(('dp', 'ctx', 'exp')), may hold values from -0.125 to 0.125
- bias_value: bfloat16 [2048], P(('dp', 'ctx', 'exp')), may hold values from -0.59765625 to 0.59765625
- w_output: bfloat16 [2048, 2048], P(('dp', 'ctx', 'exp')), may hold values from -1 to 1
- norm_moe: bfloat16 [2048], P(('dp', 'ctx', 'exp')), may hold values from 0.5 to 1.5
- w_router: bfloat16 [2048, 8], P(('dp', 'ctx', 'exp')), may hold values from -0.0625 to 0.0625
- w_shared_gate: bfloat16 [2048, 5632], P(('dp', 'ctx', 'exp')), may hold values from -0.125 to 0.125
- w_shared_up: bfloat16 [2048, 5632], P(('dp', 'ctx', 'exp')), may hold values from -0.125 to 0.125
- w_shared_down: bfloat16 [5632, 2048], P(('dp', 'ctx', 'exp')), may hold values from -0.21875 to 0.21875
- w_shared_score: bfloat16 [2048], P(('dp', 'ctx', 'exp')), may hold values from -0.125 to 0.125
- w_expert_gate: bfloat16 [8, 2048, 1408], P('exp', ('dp', 'ctx')), may hold values from -0.125 to 0.125
- w_expert_up: bfloat16 [8, 2048, 1408], P('exp', ('dp', 'ctx')), may hold values from -0.125 to 0.125
- w_expert_down: bfloat16 [8, 1408, 2048], P('exp', ('dp', 'ctx')), may hold values from -1.75 to 1.75
Outputs:
- mixed: bfloat16 [2, 4, 512, 2048], P('dp', 'exp', 'ctx')
- grad_tokens: bfloat16 [2, 4, 512, 2048], P('dp', 'exp', 'ctx')
- grad_norm_attn: float32 [2048], P(('dp', 'ctx', 'exp'))
- grad_w_query: float32 [2048, 2048], P(('dp', 'ctx', 'exp'))
- grad_bias_query: float32 [2048], P(('dp', 'ctx', 'exp'))
- grad_w_key: float32 [2048, 2048], P(('dp', 'ctx', 'exp'))
- grad_bias_key: float32 [2048], P(('dp', 'ctx', 'exp'))
- grad_w_value: float32 [2048, 2048], P(('dp', 'ctx', 'exp'))
- grad_bias_value: float32 [2048], P(('dp', 'ctx', 'exp'))
- grad_w_output: float32 [2048, 2048], P(('dp', 'ctx', 'exp'))
- grad_norm_moe: float32 [2048], P(('dp', 'ctx', 'exp'))
- grad_w_router: float32 [2048, 8], P(('dp', 'ctx', 'exp'))
- grad_w_shared_gate: float32 [2048, 5632], P(('dp', 'ctx', 'exp'))
- grad_w_shared_up: float32 [2048, 5632], P(('dp', 'ctx', 'exp'))
- grad_w_shared_down: float32 [5632, 2048], P(('dp', 'ctx', 'exp'))
- grad_w_shared_score: float32 [2048], P(('dp', 'ctx', 'exp'))
- grad_w_expert_gate: float32 [8, 2048, 1408], P('exp', ('dp', 'ctx'))
- grad_w_expert_up: float32 [8, 2048, 1408], P('exp', ('dp', 'ctx'))
- grad_w_expert_down: float32 [8, 1408, 2048], P('exp', ('dp', 'ctx'))
The draws below stay inside these ranges and needn't reach their ends.
Inputs may be any that keep to these rules, and one draw needn't show every extreme that they name: `positions`: within each group of 512 tokens every position appears once. The 3 lengths of a group sum to 512, and the longest is 384. `routes`: each token names 4 different experts; among the 128 tokens of one device no expert is named more than 128 times, a bound that some block reaches.
All inputs are finite; a program needn't handle non-finite values.
Results may differ from the reference program's by a relative error of at most 0.039.
Values may be sent and summed in bfloat16 or wider, within the bound.
A program may use at most 384 MiB of HBM per device.

```python
import math
import jax
import jax.numpy as jnp
import numpy as np
from jax import lax

D = 2048
HEADS = 16
HD = 128
FFE = 1408
FF_S = 5632
TOP = 4
NSEQ = 3
TOK_DEV = 128
EXPERTS = 8
GROUP = 512
MAXLEN = 384
CAP = 128
N_DP = 2
N_EXP = 4


def shard_levels(stream_key, dims, shards, low, high):
    level = 1.0
    for position, blocks in shards:
        draws = jax.random.uniform(jax.random.fold_in(jax.random.fold_in(stream_key, 6), position), (blocks,), jnp.float32, low / len(shards), high / len(shards))
        level = level * jnp.repeat(jnp.exp(draws), dims[position] // blocks).reshape((-1,) + (1,) * (len(dims) - 1 - position))
    return level


def split_up(amount, total, reach, slope):
    portions = [(1 << 20) // math.isqrt(rank ** slope) + 1 for rank in range(2, amount + 1)]
    rest, holding = total - reach - (amount - 1), [1] * (amount - 1)
    while rest > 0:
        candidates = [i for i in range(amount - 1) if holding[i] < reach]
        whole, budget = sum([portions[i] for i in candidates]), rest
        for i in candidates:
            addition = min(reach - holding[i], max(1, budget * portions[i] // whole), rest)
            holding[i] = holding[i] + addition
            rest = rest - addition
    return np.array([reach] + holding)


def ragged_sizes(rng, amount, total, limit, skew):
    if amount == 2:
        one = jax.random.randint(rng, (), max(1, total - limit), min(limit, total - 1) + 1)
        return jnp.stack([one, total - one])
    sizes = jnp.asarray(split_up(amount, total, limit, skew), jnp.int32)
    twos = (amount - 1) // 2
    giver, receiver = sizes[1:1 + 2 * twos:2], sizes[2:2 + 2 * twos:2]
    room = jnp.minimum(giver - 1, limit - receiver)
    moved = jax.random.randint(jax.random.fold_in(rng, 1), (twos,), 0, 1 << 20) % (room + 1)
    sizes = sizes.at[1:1 + 2 * twos:2].set(giver - moved).at[2:2 + 2 * twos:2].set(receiver + moved)
    return sizes[jax.random.permutation(jax.random.fold_in(rng, 2), amount)]


def routed_block(rng, own, number, rows, number_of, top, limit, slope):
    ranking = jax.random.permutation(rng, number_of)
    crowded, ordinary = portions_of(number_of, rows * top, limit, slope, True), portions_of(number_of, rows * top, limit, slope, False)
    places = jnp.arange(number_of)

    def named(sizes, offset_by):
        used = int((sizes > 0).sum())
        fixed = max(1, used // 4)
        moved = fixed + (places - fixed + offset_by * (used - fixed)) % max(1, number_of - fixed)
        return jnp.zeros((number_of,), jnp.int32).at[ranking[jnp.where(places < fixed, places, moved)]].set(jnp.asarray(sizes, jnp.int32))

    sizes = jnp.where(number % 4 == 0, named(crowded, number // 4), named(ordinary, number - number // 4 - 1))
    mixed = jax.random.permutation(jax.random.fold_in(own, 3), number_of)
    giver, receiver = mixed[0:number_of // 2 * 2:2], mixed[1:number_of // 2 * 2:2]
    slack = jnp.minimum(sizes[giver] - 1, limit - sizes[receiver]) // 2
    slack = jnp.where((giver == ranking[0]) | (receiver == ranking[0]) | (sizes[receiver] == 0), 0, jnp.maximum(slack, 0))
    moved = jax.random.randint(jax.random.fold_in(own, 4), (number_of // 2,), 0, 1 << 20) % (slack + 1)
    sizes = sizes.at[giver].add(-moved).at[receiver].add(moved)
    labels = jnp.searchsorted(jnp.cumsum(sizes), jnp.arange(rows * top), side="right").astype(jnp.int32)
    listing = labels.reshape(top, rows).T
    listing = listing[jax.random.permutation(jax.random.fold_in(own, 1), rows)]
    offset_by = jax.random.randint(jax.random.fold_in(own, 2), (rows, 1), 0, top)
    return jnp.take_along_axis(listing, (jnp.arange(top)[None, :] + offset_by) % top, axis=1)


def portions_of(number_of, total, limit, slope, full):
    portions = [(1 << 20) // math.isqrt(grade ** slope) + 1 for grade in range(1, number_of + 1)]
    largest = limit if full else min(limit, max(-(-total // number_of), total * portions[0] // sum(portions)))
    least = 1 if total - largest >= number_of - 1 else 0
    given, spare = [largest] + [least] * (number_of - 1), total - largest - least * (number_of - 1)
    while spare > 0:
        movable = [i for i in range(1, number_of) if given[i] < largest] or [i for i in range(1, number_of) if given[i] < limit]
        whole, left = sum([portions[i] for i in movable]), spare
        for i in movable:
            more = min(limit - given[i], max(1, left * portions[i] // whole), spare)
            given[i] = given[i] + more
            spare = spare - more
    return np.array(given)


def noise(rng, extent, width, bound, shards=(), held_as=jnp.bfloat16):
    values = width * jax.random.normal(rng, extent, jnp.float32)
    if shards:
        values = values * shard_levels(rng, extent, shards, -0.22, 0.18)
    return jnp.clip(values, -bound, bound).astype(held_as)


def setup_inputs(seed: int = 0) -> dict:
    streams_of = jax.random.split(jax.random.key(seed), 23)
    tokens = noise(streams_of[0], (N_DP, N_EXP, GROUP, D), 1.0, 6.0, ((0, 2), (1, 4), (2, 4)))
    cotangent = noise(streams_of[1], (N_DP, N_EXP, GROUP, D), 1.0, 6.0, ((0, 2), (1, 4), (2, 4)))
    positions = jax.vmap(lambda own: jax.random.permutation(own, GROUP))(jax.random.split(streams_of[2], N_DP * N_EXP)).reshape((N_DP, N_EXP, GROUP)).astype(jnp.int32)
    lengths = jax.vmap(lambda own: ragged_sizes(own, NSEQ, GROUP, MAXLEN, 1))(jax.random.split(streams_of[3], N_DP * N_EXP)).reshape((N_DP, N_EXP, NSEQ)).astype(jnp.int32)
    routes_keys = jax.random.split(jax.random.fold_in(streams_of[4], 1), N_DP * N_EXP * GROUP // TOK_DEV)
    routes_turns = jax.random.permutation(jax.random.fold_in(streams_of[4], 3), N_DP * N_EXP * GROUP // TOK_DEV)
    routes = jax.vmap(lambda own, number: routed_block(jax.random.fold_in(streams_of[4], 2), own, number, TOK_DEV, EXPERTS, TOP, CAP, 1))(routes_keys, routes_turns).reshape((N_DP, N_EXP, GROUP, TOP))
    norm_attn = jnp.clip(1.0 + 0.1 * jax.random.normal(streams_of[5], (D,), jnp.float32), 0.5, 1.5).astype(jnp.bfloat16)
    w_query = noise(streams_of[6], (D, D), D ** -0.5, 0.125, ((0, 32),))
    bias_query = noise(streams_of[7], (D,), 0.1, 0.59765625, ((0, 32),))
    w_key = noise(streams_of[8], (D, D), D ** -0.5, 0.125, ((0, 32),))
    bias_key = noise(streams_of[9], (D,), 0.1, 0.59765625, ((0, 32),))
    w_value = noise(streams_of[10], (D, D), D ** -0.5, 0.125, ((0, 32),))
    bias_value = noise(streams_of[11], (D,), 0.1, 0.59765625, ((0, 32),))
    w_output = noise(streams_of[12], (D, D), (D // 64) ** -0.5, 1.0, ((0, 32),))
    norm_moe = jnp.clip(1.0 + 0.1 * jax.random.normal(streams_of[13], (D,), jnp.float32), 0.5, 1.5).astype(jnp.bfloat16)
    w_router = noise(streams_of[14], (D, EXPERTS), (4 * D) ** -0.5, 0.0625, ((0, 32),))
    w_shared_gate = noise(streams_of[15], (D, FF_S), D ** -0.5, 0.125, ((0, 32),))
    w_shared_up = noise(streams_of[16], (D, FF_S), D ** -0.5, 0.125, ((0, 32),))
    w_shared_down = noise(streams_of[17], (FF_S, D), (FF_S // 8) ** -0.5, 0.21875, ((0, 32),))
    w_shared_score = noise(streams_of[18], (D,), D ** -0.5, 0.125, ((0, 32),))
    w_expert_gate = noise(streams_of[19], (EXPERTS, D, FFE), D ** -0.5, 0.125, ((0, 4), (1, 8)))
    w_expert_up = noise(streams_of[20], (EXPERTS, D, FFE), D ** -0.5, 0.125, ((0, 4), (1, 8)))
    w_expert_down = noise(streams_of[21], (EXPERTS, FFE, D), (max(FFE // 128, 1)) ** -0.5, 1.75, ((0, 4), (1, 8)))
    return dict(tokens=tokens, cotangent=cotangent, positions=positions, lengths=lengths, routes=routes, norm_attn=norm_attn, w_query=w_query, bias_query=bias_query, w_key=w_key, bias_key=bias_key, w_value=w_value, bias_value=bias_value, w_output=w_output, norm_moe=norm_moe, w_router=w_router, w_shared_gate=w_shared_gate, w_shared_up=w_shared_up, w_shared_down=w_shared_down, w_shared_score=w_shared_score, w_expert_gate=w_expert_gate, w_expert_up=w_expert_up, w_expert_down=w_expert_down)


EPSILON = 1e-06
ROTARY_BASE = 1000000.0
NEGATIVE = -1e+30
PRECISE = lax.Precision.HIGHEST

@jax.custom_vjp
def low(v):
    return lax.optimization_barrier(v.astype(jnp.bfloat16)).astype(jnp.float32)

@jax.custom_vjp
def low_back(v):
    return v

def low_keep(v):
    return (low(v), None)

def low_pass(kept, grad):
    return (grad,)

def back_keep(v):
    return (v, None)

def back_low(kept, grad):
    return (low(grad),)
low.defvjp(low_keep, low_pass)
low_back.defvjp(back_keep, back_low)

def matmul(left, right):
    return jnp.dot(left, right, precision=PRECISE)

def rms_norm(value, gain):
    return value * lax.rsqrt(lax.optimization_barrier(jnp.mean(value * value, axis=-1, keepdims=True)) + EPSILON) * gain

def rotate(value, cos_table, sin_table):
    half_dim = value.shape[-1] // 2
    first = value[..., :half_dim]
    second = value[..., half_dim:]
    return jnp.concatenate([first * cos_table - second * sin_table, second * cos_table + first * sin_table], -1)

def attend(piece):
    query, keys, values, pos_row, seg_row = piece
    scores = low_back(jnp.einsum('qhd,khd->hqk', query, keys, precision=PRECISE) * HD ** (-0.5))
    allowed = (seg_row[None, :] == seg_row[:, None]) & (pos_row[None, :] <= pos_row[:, None])
    scores = jnp.where(allowed[None], scores, NEGATIVE)
    weights_low = low(jax.nn.softmax(scores, axis=-1))
    return jnp.einsum('hqk,khd->qhd', weights_low, values, precision=PRECISE)

def reference(tokens, cotangent, positions, lengths, routes, norm_attn, w_query, bias_query, w_key, bias_key, w_value, bias_value, w_output, norm_moe, w_router, w_shared_gate, w_shared_up, w_shared_down, w_shared_score, w_expert_gate, w_expert_up, w_expert_down):
    groups = tokens.shape[0] * tokens.shape[1]
    group_len = tokens.shape[2]
    model_width = tokens.shape[3]
    total = groups * group_len
    n_experts = w_router.shape[1]
    blocks = total // TOK_DEV
    pos_all = positions.reshape(groups, group_len)
    seq_lens = lengths.reshape(groups, -1)
    seq_ends = jnp.cumsum(seq_lens, 1)
    after_end = (pos_all[:, :, None] >= seq_ends[:, None, :]).astype(jnp.int32)
    seg_all = lax.optimization_barrier(jnp.sum(after_end, 2))
    rel_all = pos_all - lax.optimization_barrier(jnp.sum(after_end * seq_lens[:, None, :], 2))
    half_dim = HD // 2
    freq = ROTARY_BASE ** (-(jnp.arange(half_dim, dtype=jnp.float32) * 2.0 / HD))
    angle = rel_all.astype(jnp.float32)[:, :, None] * freq
    cos_table = jnp.cos(angle)[:, :, None, :]
    sin_table = jnp.sin(angle)[:, :, None, :]
    route_rows = routes.reshape(blocks, TOK_DEV * TOP)
    onehot = (route_rows[:, :, None] == jnp.arange(n_experts, dtype=jnp.int32)[None, None, :]).astype(jnp.int32)
    before = jnp.cumsum(onehot, 1) - onehot
    slots = lax.optimization_barrier(jnp.sum(before * onehot, 2))
    dest = (route_rows * (blocks * CAP) + jnp.arange(blocks, dtype=jnp.int32)[:, None] * CAP + slots).reshape(-1).astype(jnp.int32)
    source_index = jnp.full((n_experts * blocks * CAP,), total, jnp.int32)
    source_index = source_index.at[dest].set((jnp.arange(total * TOP, dtype=jnp.int32) // TOP).astype(jnp.int32))
    source_index = source_index.reshape(n_experts, blocks * CAP)
    chosen_ids = routes.reshape(total, TOP)

    def forward_step(input_tokens, attention_gain, query_matrix, query_offset_bias, key_matrix, key_offset_bias, value_matrix, value_offset_bias, output_matrix, mixture_gain, router_matrix, shared_gate_matrix, shared_up_matrix, shared_down_matrix, shared_score_matrix, expert_gate_matrix, expert_up_matrix, expert_down_matrix):
        normed_one = low(rms_norm(input_tokens, attention_gain))
        query_lin = low_back(matmul(normed_one, query_matrix) + query_offset_bias)
        key_lin = low_back(matmul(normed_one, key_matrix) + key_offset_bias)
        value_lin = low_back(matmul(normed_one, value_matrix) + value_offset_bias)
        query = low(rotate(query_lin.reshape(groups, group_len, HEADS, HD), cos_table, sin_table))
        keys = low(rotate(key_lin.reshape(groups, group_len, HEADS, HD), cos_table, sin_table))
        values = low(value_lin).reshape(groups, group_len, HEADS, HD)
        attn = lax.map(jax.checkpoint(attend), (query, keys, values, pos_all, seg_all))
        attn_low = low(low_back(attn.reshape(total, model_width)))
        resid = input_tokens + low_back(matmul(attn_low, output_matrix))
        normed_two = low(rms_norm(resid, mixture_gain))
        logits = low_back(matmul(normed_two, router_matrix))
        router = jax.nn.softmax(logits, axis=-1)
        gates = jnp.take_along_axis(router, chosen_ids, axis=1)
        padded_rows = jnp.concatenate([normed_two, jnp.zeros((1, model_width), jnp.float32)], 0)

        def expert_slot(piece):
            index_row, gate_w, up_w, down_w = piece
            rows = low_back(padded_rows[index_row])
            gate_pre = low_back(matmul(rows, gate_w))
            up_pre = low_back(matmul(rows, up_w))
            hidden = low(jax.nn.silu(gate_pre) * up_pre)
            return low(low_back(matmul(hidden, down_w)))
        output_tokens = lax.map(jax.checkpoint(expert_slot), (source_index, expert_gate_matrix, expert_up_matrix, expert_down_matrix))
        picked = output_tokens.reshape(-1, model_width)[dest].reshape(total, TOP, model_width)
        moe = lax.optimization_barrier(jnp.sum(gates[:, :, None] * picked, 1))
        shared_gate = low_back(matmul(normed_two, shared_gate_matrix))
        shared_up = low_back(matmul(normed_two, shared_up_matrix))
        shared_hidden = low(jax.nn.silu(shared_gate) * shared_up)
        shared = low_back(matmul(shared_hidden, shared_down_matrix))
        score = jax.nn.sigmoid(matmul(normed_two, shared_score_matrix))
        return resid + moe + score[:, None] * shared
    arrays = [tokens.reshape(total, model_width), norm_attn, w_query, bias_query, w_key, bias_key, w_value, bias_value, w_output, norm_moe, w_router, w_shared_gate, w_shared_up, w_shared_down, w_shared_score, w_expert_gate, w_expert_up, w_expert_down]
    floats = [array.astype(jnp.float32) for array in arrays]
    mixed, pullback = jax.vjp(forward_step, *floats)
    grads = pullback(cotangent.reshape(total, model_width).astype(jnp.float32))
    return (mixed.astype(jnp.bfloat16).reshape(tokens.shape), grads[0].astype(jnp.bfloat16).reshape(tokens.shape), grads[1], grads[2], grads[3], grads[4], grads[5], grads[6], grads[7], grads[8], grads[9], grads[10], grads[11], grads[12], grads[13], grads[14], grads[15], grads[16], grads[17])
```

```python
import jax
import jax.numpy as jnp
from jax import lax
from jax.sharding import Mesh
from jax.sharding import PartitionSpec as P

HD = 128
CORES = 2
EPSILON = 1e-06
ROTARY_BASE = 1000000.0
NEGATIVE = -1e30
BF = jnp.bfloat16
F32 = jnp.float32


def project(left, right):
    return jnp.dot(left, right, preferred_element_type=F32)


def project_t(left, right):
    return lax.dot_general(left, right, (((1,), (1,)), ((), ())), preferred_element_type=F32)


def weight_grad(left, right):
    return lax.dot_general(left, right, (((0,), (0,)), ((), ())), preferred_element_type=F32)


def rms_parts(value):
    inverse = lax.rsqrt(jnp.mean(value * value, axis=-1, keepdims=True) + EPSILON)
    return (value * inverse, inverse)


def rotate(value, cos_table, sin_table, direction):
    half_dim = value.shape[-1] // 2
    first = value[..., :half_dim]
    second = value[..., half_dim:]
    return jnp.concatenate(
        [
            first * cos_table - direction * second * sin_table,
            second * cos_table + direction * first * sin_table,
        ],
        -1,
    )


def silu_parts(value):
    sigmoid = jax.nn.sigmoid(value)
    return (value * sigmoid, sigmoid * (1.0 + value * (1.0 - sigmoid)))


def fetch(value, axis, step):
    size = lax.axis_size(axis)
    if step % size == 0:
        return value
    return lax.ppermute(value, axis, [((i + step) % size, i) for i in range(size)])


def push(value, axis, step):
    size = lax.axis_size(axis)
    return lax.ppermute(value, axis, [(i, (i + step) % size) for i in range(size)])


def roll_to_relative(value, axis, dim):
    size = lax.axis_size(axis)
    both = lax.concatenate([value, value], dim)
    return lax.dynamic_slice_in_dim(both, lax.axis_index(axis), size, dim)


def roll_to_absolute(value, axis, dim):
    size = lax.axis_size(axis)
    both = lax.concatenate([value, value], dim)
    start = lax.rem(size - lax.axis_index(axis), size)
    return lax.dynamic_slice_in_dim(both, start, size, dim)


def spread(value):
    line = [fetch(value, "exp", k) for k in range(lax.axis_size("exp"))]
    other = [fetch(piece, "core", 1) for piece in line]
    return jnp.stack(line + other).reshape((CORES, len(line)) + value.shape)


def collect(partial):
    line = lax.axis_size("exp")
    halves = [
        partial[0, k].astype(F32) + push(partial[1, k], "core", 1).astype(F32) for k in range(line)
    ]
    total = halves[0]
    for k in range(1, line):
        total = total + push(halves[k].astype(BF), "exp", k).astype(F32)
    return total


def ring(value, first):
    n_dp = lax.axis_size("dp")
    n_cx = lax.axis_size("cx")
    if first == "cx":
        near = [fetch(value, "cx", k) for k in range(n_cx)]
        return [[fetch(near[k], "dp", j) for k in range(n_cx)] for j in range(n_dp)]
    near = [fetch(value, "dp", j) for j in range(n_dp)]
    return [[fetch(near[j], "cx", k) for k in range(n_cx)] for j in range(n_dp)]


def join(pieces):
    return jnp.concatenate([piece for line in pieces for piece in line], 0)


def place(pieces):
    n_dp = len(pieces)
    n_cx = len(pieces[0])
    rows, width = pieces[0][0].shape
    whole = jnp.zeros((n_dp * n_cx * rows, width), pieces[0][0].dtype)
    for j in range(n_dp):
        for k in range(n_cx):
            dp = lax.rem(lax.axis_index("dp") + j, n_dp)
            cx = lax.rem(lax.axis_index("cx") + k, n_cx)
            whole = lax.dynamic_update_slice_in_dim(
                whole, pieces[j][k], (dp * n_cx + cx) * rows, 0
            )
    return whole


def sum_scatter(make, first):
    n_dp = lax.axis_size("dp")
    n_cx = lax.axis_size("cx")
    if first == "cx":
        outer, inner, n_outer, n_inner = "dp", "cx", n_dp, n_cx
        term = make
    else:
        outer, inner, n_outer, n_inner = "cx", "dp", n_cx, n_dp

        def term(a, b):
            return make(b, a)

    sums = []
    for a in list(range(1, n_outer)) + [0]:
        sent = [push(term(a, b).astype(BF), inner, b) for b in range(1, n_inner)]
        total = term(a, 0).astype(F32)
        for piece in sent:
            total = total + piece.astype(F32)
        sums.append((a, total))
    result = sums[-1][1]
    for a, total in sums[:-1]:
        result = result + push(total.astype(BF), outer, a).astype(F32)
    return result


def row_blocks(value):
    n_dp = lax.axis_size("dp")
    n_cx = lax.axis_size("cx")
    rows = value.shape[0] // (n_dp * n_cx)

    def make(j, k):
        dp = lax.rem(lax.axis_index("dp") + j, n_dp)
        cx = lax.rem(lax.axis_index("cx") + k, n_cx)
        return lax.dynamic_slice_in_dim(value, (dp * n_cx + cx) * rows, rows, 0)

    return make


def sum_small(value):
    for axis in ("dp", "cx", "core", "exp"):
        own = roll_to_relative(value, axis, 1)
        total = own[:, 0]
        for k in range(1, lax.axis_size(axis)):
            total = total + push(own[:, k], axis, k)
        value = total
    return value


def gather_small(value):
    for axis in ("exp", "core", "cx", "dp"):
        line = jnp.stack([fetch(value, axis, k) for k in range(lax.axis_size(axis))], 1)
        value = roll_to_absolute(line, axis, 1)
    return value.reshape(value.shape[0], -1)


def on_device(
    tokens,
    cotangent,
    positions,
    lengths,
    routes,
    norm_attn,
    w_query,
    bias_query,
    w_key,
    bias_key,
    w_value,
    bias_value,
    w_output,
    norm_moe,
    w_router,
    w_shared_gate,
    w_shared_up,
    w_shared_down,
    w_shared_score,
    w_expert_gate,
    w_expert_up,
    w_expert_down,
):
    n_dp = lax.axis_size("dp")
    n_cx = lax.axis_size("cx")
    n_exp = lax.axis_size("exp")
    exp_at = lax.axis_index("exp")
    core_at = lax.axis_index("core")
    n_tp = CORES * n_exp
    n_data = n_dp * n_cx
    tok, width = tokens.shape[2:]
    shard = w_query.shape[0]
    block = CORES * n_exp * shard
    col = width // n_tp
    heads = col // HD
    n_experts = w_router.shape[1]
    sub = w_shared_down.shape[0]
    sub_width = n_data * sub
    every = tok * n_tp
    scale = HD ** (-0.5)
    top = routes.shape[3]

    def to_relative(value):
        parts = value.reshape(value.shape[:-1] + (n_dp, n_cx, block))
        dim = value.ndim - 1
        parts = roll_to_relative(parts, "dp", dim)
        parts = roll_to_relative(parts, "cx", dim + 1)
        return parts.reshape(value.shape)

    def to_absolute(value):
        parts = value.reshape(value.shape[:-1] + (n_dp, n_cx, block))
        dim = value.ndim - 1
        parts = roll_to_absolute(parts, "dp", dim)
        parts = roll_to_absolute(parts, "cx", dim + 1)
        return parts.reshape(value.shape)

    def by_core(first, second):
        return jnp.where(core_at == 0, first, second)

    x_own = tokens.reshape(tok, width)
    cot_own = cotangent.reshape(tok, width)

    small = jnp.concatenate(
        [
            norm_attn[None],
            norm_moe[None],
            w_shared_score[None],
            bias_query[None],
            bias_key[None],
            bias_value[None],
            w_router.T,
        ]
    )
    small = gather_small(small.astype(F32))
    gain_attn = to_relative(small[0])
    gain_moe = small[1]
    score_vec = small[2]
    router_full = small[6:].T.astype(BF)
    rank = exp_at * CORES + core_at
    biases = lax.dynamic_slice_in_dim(small[3:6], rank * col, col, 1).reshape(3 * col)

    ints = jnp.concatenate(
        [
            positions.reshape(1, tok),
            routes.reshape(tok, top).T,
            jnp.pad(lengths.reshape(1, -1), ((0, 0), (0, tok - lengths.shape[2]))),
        ]
    )
    ints = spread(ints)
    pos_tok = ints[:, :, 0]
    route_tok = jnp.swapaxes(ints[:, :, 1 : 1 + top], 2, 3).reshape(every, top)
    seq_lens = ints[0, :, 1 + top, : lengths.shape[2]]
    seq_ends = jnp.cumsum(seq_lens, 1)
    pos_group = jnp.swapaxes(pos_tok, 0, 1).reshape(n_exp, CORES * tok)
    after_end = (pos_group[:, :, None] >= seq_ends[:, None, :]).astype(jnp.int32)
    seg_group = jnp.sum(after_end, 2)
    rel_group = pos_group - jnp.sum(after_end * seq_lens[:, None, :], 2)
    code = jnp.stack([pos_group, seg_group])
    code_keys = jnp.concatenate([fetch(code, "cx", k) for k in range(n_cx)], 2)
    allowed = (code_keys[1][:, None, :] == seg_group[:, :, None]) & (
        code_keys[0][:, None, :] <= pos_group[:, :, None]
    )
    freq = ROTARY_BASE ** (-(jnp.arange(HD // 2, dtype=F32) * 2.0 / HD))
    angle = rel_group.astype(F32)[:, :, None] * freq
    cos_table = jnp.cos(angle)[:, :, None, :]
    sin_table = jnp.sin(angle)[:, :, None, :]

    x_rel = spread(to_relative(x_own))

    def exchange(value):
        return lax.all_to_all(value, ("core", "exp"), split_axis=0, concat_axis=0, tiled=True)

    def head_columns(value):
        parts = value.reshape(shard, n_exp, CORES, col)
        return jnp.transpose(parts, (2, 1, 0, 3)).reshape(n_tp, shard, col)

    def hidden_columns(value):
        parts = value.reshape(shard, n_data, CORES, n_exp, sub)
        return jnp.transpose(parts, (2, 3, 0, 1, 4)).reshape(n_tp, shard, sub_width)

    qkv_block = exchange(
        jnp.concatenate([head_columns(w_query), head_columns(w_key), head_columns(w_value)], 2)
    ).reshape(block, 3 * col)
    half = block // 2
    qkv_a = ring(qkv_block[:half], "cx")
    qkv_b = ring(qkv_block[half:], "dp")
    w_qkv = jnp.concatenate(
        [
            piece
            for line_a, line_b in zip(qkv_a, qkv_b)
            for pair in zip(line_a, line_b)
            for piece in pair
        ],
        0,
    )
    out_rows = place(ring(w_output, "dp"))
    w_out = lax.all_to_all(
        out_rows.reshape(n_data, shard, width), "exp", split_axis=0, concat_axis=0, tiled=True
    ).reshape(col, width)
    cot_tok = spread(cot_own)
    gu_block = exchange(
        jnp.concatenate([hidden_columns(w_shared_gate), hidden_columns(w_shared_up)], 2)
    ).reshape(block, 2 * sub_width)
    w_sgu = join(ring(gu_block, "cx"))
    w_sdown = place(ring(w_shared_down, "dp"))

    def own_expert(value):
        mine = by_core(value[0], value[1])
        theirs = push(by_core(value[1], value[0]), "core", 1)
        return jnp.concatenate([by_core(mine, theirs), by_core(theirs, mine)], 0)

    w_egate = join(ring(own_expert(w_expert_gate), "cx"))
    w_eup = join(ring(own_expert(w_expert_up), "dp"))
    w_edown = place(ring(own_expert(w_expert_down), "dp"))

    x_all = x_rel.reshape(every, width).astype(F32)
    normal_one, inverse_one = rms_parts(x_all)
    normed_one = (normal_one * gain_attn).astype(BF)
    qkv = project(normed_one, w_qkv) + biases

    def by_group(value):
        parts = value.reshape(CORES, n_exp, tok, -1)
        return jnp.swapaxes(parts, 0, 1).reshape(n_exp, CORES * tok, heads, HD)

    def by_token(value):
        parts = value.reshape(n_exp, CORES, tok, heads * HD)
        return jnp.swapaxes(parts, 0, 1).reshape(every, heads * HD)

    query = rotate(by_group(qkv[:, :col]), cos_table, sin_table, 1.0).astype(BF)
    key = rotate(by_group(qkv[:, col : 2 * col]), cos_table, sin_table, 1.0).astype(BF)
    value = by_group(qkv[:, 2 * col :]).astype(BF)
    key_value = jnp.stack([key, value])
    key_value = jnp.concatenate([fetch(key_value, "cx", k) for k in range(n_cx)], 2)
    keys, values = key_value[0], key_value[1]
    scores = jnp.einsum("gqhd,gkhd->ghqk", query, keys, preferred_element_type=F32) * scale
    scores = jnp.where(allowed[:, None], scores, NEGATIVE)
    weights = jnp.exp(scores - jnp.max(scores, -1, keepdims=True))
    weights = weights / jnp.sum(weights, -1, keepdims=True)
    probs = weights.astype(BF)
    attn = jnp.einsum("ghqk,gkhd->gqhd", probs, values, preferred_element_type=F32)
    attn_low = by_token(attn.astype(BF))
    partial = project(attn_low, w_out).astype(BF)
    resid = x_own.astype(F32) + collect(partial.reshape(CORES, n_exp, tok, width))

    normal_two, inverse_two = rms_parts(resid)
    normed_two_own = (normal_two * gain_moe).astype(BF)
    normed_two = spread(to_relative(normed_two_own)).reshape(every, width)
    small_cols = jnp.concatenate([router_full, score_vec.astype(BF)[:, None]], 1)
    small_out = project(normed_two, to_relative(small_cols.T).T)
    router_all = jax.nn.softmax(small_out[:, :n_experts], axis=-1)
    score_all = jax.nn.sigmoid(small_out[:, n_experts])
    chosen = jnp.any(route_tok == rank, axis=1)
    at_rank = (jnp.arange(n_experts) == rank).astype(F32)
    gate = jnp.where(chosen, jnp.sum(router_all * at_rank[None, :], 1), 0.0)
    cot_all = cot_tok.reshape(every, width).astype(F32)

    shared_pre = project(normed_two, w_sgu)
    s_gate = shared_pre[:, :sub_width]
    s_up = shared_pre[:, sub_width:]
    s_act, s_slope = silu_parts(s_gate)
    s_hidden = (s_act * s_up).astype(BF)
    shared = project(s_hidden, w_sdown)
    e_gate = project(normed_two, w_egate)
    e_up = project(normed_two, w_eup)
    e_act, e_slope = silu_parts(e_gate)
    e_hidden = (e_act * e_up).astype(BF)
    e_out = project(e_hidden, w_edown).astype(BF).astype(F32)
    mix = (score_all[:, None] * shared + gate[:, None] * e_out).astype(BF)
    dots = jnp.stack(
        [
            jnp.where(chosen, jnp.sum(cot_all * e_out, 1), 0.0),
            jnp.sum(cot_all * shared, 1),
        ]
    )

    d_shared = (score_all[:, None] * cot_all).astype(BF)
    d_sh = project_t(d_shared, w_sdown)
    d_sgu = jnp.concatenate(
        [(d_sh * s_up * s_slope).astype(BF), (d_sh * s_act).astype(BF)], 1
    )
    d_eout = (gate[:, None] * cot_all).astype(BF)
    d_eh = project_t(d_eout, w_edown)
    d_eg = (d_eh * e_up * e_slope).astype(BF)
    d_eu = (d_eh * e_act).astype(BF)
    partial_two = (
        project_t(d_sgu, w_sgu) + project_t(d_eg, w_egate) + project_t(d_eu, w_eup)
    ).astype(BF)
    summed_two = to_absolute(collect(partial_two.reshape(CORES, n_exp, tok, width)))
    mixed = (resid + collect(mix.reshape(CORES, n_exp, tok, width))).astype(BF)

    dots = dots.reshape(2, CORES, n_exp, tok)
    pair = jnp.stack([dots[:, 0], push(dots[:, 1], "core", 1)])
    d_router = jnp.zeros((tok, n_experts), F32)
    d_score = jnp.zeros((tok,), F32)
    for k in range(n_exp):
        came = pair[:, :, k] if k == 0 else push(pair[:, :, k], "exp", k)
        for c in range(CORES):
            source = lax.rem(exp_at - k + n_exp, n_exp) * CORES + lax.rem(core_at + c, CORES)
            spot = (jnp.arange(n_experts) == source).astype(F32)
            d_router = d_router + came[c, 0][:, None] * spot[None, :]
            d_score = d_score + came[c, 1]
    router_own = router_all[:tok]
    score_own = score_all[:tok]
    d_score = d_score * score_own * (1.0 - score_own)
    d_logits = (
        router_own * (d_router - jnp.sum(router_own * d_router, 1, keepdims=True))
    ).astype(BF)
    d_normed_two = (
        summed_two + project_t(d_logits, router_full) + d_score[:, None] * score_vec[None, :]
    )
    grad_router = weight_grad(d_logits, normed_two_own)
    grad_score = jnp.sum(d_score[:, None] * normed_two_own.astype(F32), 0)
    grad_gain_moe = jnp.sum(d_normed_two * normal_two, 0)
    d_hat_two = d_normed_two * gain_moe
    d_resid = cot_own.astype(F32) + inverse_two * (
        d_hat_two - normal_two * jnp.mean(d_hat_two * normal_two, 1, keepdims=True)
    )

    def feature_terms(rows, right):
        def make(j, k):
            start = (j * n_cx + k) * block
            return weight_grad(rows[:, start : start + block], right)

        return make

    def to_both(value):
        rows = value.shape[0] // 2
        low = value[:rows]
        high = value[rows:]
        mine = by_core(low, high)
        theirs = push(by_core(high, low).astype(BF), "core", 1).astype(F32)
        return jnp.stack([by_core(mine, theirs), by_core(theirs, mine)])

    grad_edown = to_both(sum_scatter(row_blocks(weight_grad(e_hidden, d_eout)), "cx"))
    grad_egate = to_both(sum_scatter(feature_terms(normed_two, d_eg), "dp"))
    grad_eup = to_both(sum_scatter(feature_terms(normed_two, d_eu), "cx"))
    grad_sdown = sum_scatter(row_blocks(weight_grad(s_hidden, d_shared)), "cx")
    grad_sgu = sum_scatter(feature_terms(normed_two, d_sgu), "dp")
    grad_sgu = exchange(grad_sgu.astype(BF).reshape(n_tp, shard, 2 * sub_width))

    def from_hidden(value):
        parts = value.reshape(CORES, n_exp, shard, n_data, sub)
        return jnp.transpose(parts, (2, 3, 0, 1, 4)).reshape(shard, -1).astype(F32)

    d_proj_own = d_resid.astype(BF)
    d_proj = spread(d_proj_own).reshape(every, width)
    d_attn = by_group(project_t(d_proj, w_out).astype(BF))
    delta = jnp.sum(d_attn.astype(F32) * attn, -1)
    d_probs = jnp.einsum("gqhd,gkhd->ghqk", d_attn, values, preferred_element_type=F32)
    d_scores = (weights * (d_probs - jnp.swapaxes(delta, 1, 2)[..., None])).astype(BF)
    d_query = jnp.einsum("ghqk,gkhd->gqhd", d_scores, keys, preferred_element_type=F32) * scale
    d_key = jnp.einsum("ghqk,gqhd->gkhd", d_scores, query, preferred_element_type=F32) * scale
    d_value = jnp.einsum("ghqk,gqhd->gkhd", probs, d_attn, preferred_element_type=F32)
    d_kv = jnp.stack([d_key, d_value]).reshape(2, n_exp, n_cx, CORES * tok, heads, HD)
    d_kv_own = d_kv[:, :, 0]
    for k in range(1, n_cx):
        d_kv_own = d_kv_own + push(d_kv[:, :, k].astype(BF), "cx", k).astype(F32)
    d_qkv = jnp.concatenate(
        [
            by_token(rotate(d_query, cos_table, sin_table, -1.0).astype(BF)),
            by_token(rotate(d_kv_own[0], cos_table, sin_table, -1.0).astype(BF)),
            by_token(d_kv_own[1].astype(BF)),
        ],
        1,
    )
    partial_one = project_t(d_qkv, w_qkv)
    d_normed_one = collect(partial_one.astype(BF).reshape(CORES, n_exp, tok, width))
    grad_gain_attn = to_absolute(jnp.sum(partial_one * normal_one, 0))
    d_hat_one = d_normed_one * gain_attn
    normal_own = normal_one[:tok]
    from_attn = inverse_one[:tok] * (
        d_hat_one - normal_own * jnp.mean(d_hat_one * normal_own, 1, keepdims=True)
    )
    grad_tokens = (d_resid + to_absolute(from_attn)).astype(BF)
    grad_qkv = sum_scatter(feature_terms(normed_one, d_qkv), "cx")
    grad_qkv = exchange(grad_qkv.astype(BF).reshape(n_tp, shard, 3 * col))

    def from_heads(value):
        parts = value.reshape(CORES, n_exp, shard, col)
        return jnp.transpose(parts, (2, 1, 0, 3)).reshape(shard, width).astype(F32)

    grad_out = lax.all_to_all(
        weight_grad(attn_low, d_proj).astype(BF).reshape(n_exp, shard, width),
        "exp",
        split_axis=0,
        concat_axis=0,
        tiled=True,
    ).reshape(n_data * shard, width)
    grad_out = sum_scatter(row_blocks(grad_out), "dp")

    grad_bias = jnp.sum(d_qkv.astype(F32), 0).reshape(3, col)
    grad_bias = lax.dynamic_update_slice_in_dim(
        jnp.zeros((3, width), F32), grad_bias, rank * col, 1
    )
    totals = jnp.concatenate(
        [
            grad_gain_attn[None],
            grad_gain_moe[None],
            grad_score[None],
            grad_bias,
            grad_router,
        ]
    )
    totals = sum_small(totals.reshape(-1, n_dp, n_cx, CORES, n_exp, shard))
    return (
        mixed.reshape(tokens.shape),
        grad_tokens.reshape(tokens.shape),
        totals[0],
        from_heads(grad_qkv[:, :, :col]),
        totals[3],
        from_heads(grad_qkv[:, :, col : 2 * col]),
        totals[4],
        from_heads(grad_qkv[:, :, 2 * col :]),
        totals[5],
        grad_out,
        totals[1],
        totals[6:].T,
        from_hidden(grad_sgu[:, :, :sub_width]),
        from_hidden(grad_sgu[:, :, sub_width:]),
        grad_sdown,
        totals[2],
        grad_egate,
        grad_eup,
        grad_edown,
    )


def solution(mesh):
    sizes = dict(mesh.shape)
    fine = Mesh(
        mesh.devices.reshape(sizes["dp"], sizes["ctx"] // CORES, CORES, sizes["exp"]),
        ("dp", "cx", "core", "exp"),
    )
    own = P("dp", "exp", ("cx", "core"), None)
    flat = P(("dp", "cx", "core", "exp"))
    rows = P(("dp", "cx", "core", "exp"), None)
    expert = P("exp", ("dp", "cx", "core"), None)
    placed = (
        own,
        own,
        P("dp", "exp", ("cx", "core")),
        P("dp", "exp", None),
        own,
        flat,
        rows,
        flat,
        rows,
        flat,
        rows,
        flat,
        rows,
        flat,
        rows,
        rows,
        rows,
        rows,
        flat,
        expert,
        expert,
        expert,
    )
    return jax.shard_map(
        on_device,
        mesh=fine,
        in_specs=placed,
        out_specs=(
            own,
            own,
            flat,
            rows,
            flat,
            rows,
            flat,
            rows,
            flat,
            rows,
            flat,
            rows,
            rows,
            rows,
            rows,
            flat,
            expert,
            expert,
            expert,
        ),
        check_vma=False,
    )
```

```python
import functools

import jax
import jax.numpy as jnp
from jax import lax
from jax.experimental import pallas as pl
from jax.experimental.pallas import tpu as pltpu
from jax.sharding import Mesh
from jax.sharding import PartitionSpec as P

HD = 128
CORES = 2
EPSILON = 1e-06
ROTARY_BASE = 1000000.0
NEGATIVE = -1e30
BF = jnp.bfloat16
F32 = jnp.float32


def project(left, right):
    return jnp.dot(left, right, preferred_element_type=F32)


def project_t(left, right):
    return lax.dot_general(left, right, (((1,), (1,)), ((), ())), preferred_element_type=F32)


def weight_grad(left, right):
    return lax.dot_general(left, right, (((0,), (0,)), ((), ())), preferred_element_type=F32)


def rms_parts(value):
    inverse = lax.rsqrt(jnp.mean(value * value, axis=-1, keepdims=True) + EPSILON)
    return (value * inverse, inverse)


def rotate(value, cos_table, sin_table, direction):
    half_dim = value.shape[-1] // 2
    first = value[..., :half_dim]
    second = value[..., half_dim:]
    return jnp.concatenate(
        [
            first * cos_table - direction * second * sin_table,
            second * cos_table + direction * first * sin_table,
        ],
        -1,
    )


def silu_parts(value):
    sigmoid = jax.nn.sigmoid(value)
    return (value * sigmoid, sigmoid * (1.0 + value * (1.0 - sigmoid)))


def fetch(value, axis, step):
    size = lax.axis_size(axis)
    if step % size == 0:
        return value
    return lax.ppermute(value, axis, [((i + step) % size, i) for i in range(size)])


def push(value, axis, step):
    size = lax.axis_size(axis)
    return lax.ppermute(value, axis, [(i, (i + step) % size) for i in range(size)])


def roll_to_relative(value, axis, dim):
    size = lax.axis_size(axis)
    both = lax.concatenate([value, value], dim)
    return lax.dynamic_slice_in_dim(both, lax.axis_index(axis), size, dim)


def roll_to_absolute(value, axis, dim):
    size = lax.axis_size(axis)
    both = lax.concatenate([value, value], dim)
    start = lax.rem(size - lax.axis_index(axis), size)
    return lax.dynamic_slice_in_dim(both, start, size, dim)


def spread(value):
    line = [fetch(value, "exp", k) for k in range(lax.axis_size("exp"))]
    other = [fetch(piece, "core", 1) for piece in line]
    return jnp.stack(line + other).reshape((CORES, len(line)) + value.shape)


def collect(partial):
    line = lax.axis_size("exp")
    halves = [
        partial[0, k].astype(F32) + push(partial[1, k], "core", 1).astype(F32) for k in range(line)
    ]
    total = halves[0]
    for k in range(1, line):
        total = total + push(halves[k].astype(BF), "exp", k).astype(F32)
    return total


def sum_scatter(make, first):
    n_dp = lax.axis_size("dp")
    n_cx = lax.axis_size("cx")
    if first == "cx":
        outer, inner, n_outer, n_inner = "dp", "cx", n_dp, n_cx
        term = make
    else:
        outer, inner, n_outer, n_inner = "cx", "dp", n_cx, n_dp

        def term(a, b):
            return make(b, a)

    sums = []
    for a in list(range(1, n_outer)) + [0]:
        sent = [push(term(a, b).astype(BF), inner, b) for b in range(1, n_inner)]
        total = term(a, 0).astype(F32)
        for piece in sent:
            total = total + piece.astype(F32)
        sums.append((a, total))
    result = sums[-1][1]
    for a, total in sums[:-1]:
        result = result + push(total.astype(BF), outer, a).astype(F32)
    return result


def row_blocks(value):
    n_dp = lax.axis_size("dp")
    n_cx = lax.axis_size("cx")
    rows = value.shape[0] // (n_dp * n_cx)

    def make(j, k):
        dp = lax.rem(lax.axis_index("dp") + j, n_dp)
        cx = lax.rem(lax.axis_index("cx") + k, n_cx)
        return lax.dynamic_slice_in_dim(value, (dp * n_cx + cx) * rows, rows, 0)

    return make


def sum_small(value):
    for axis in ("dp", "cx", "core", "exp"):
        own = roll_to_relative(value, axis, 1)
        total = own[:, 0]
        for k in range(1, lax.axis_size(axis)):
            total = total + push(own[:, k], axis, k)
        value = total
    return value


def gather_small(value):
    for axis in ("exp", "core", "cx", "dp"):
        line = jnp.stack([fetch(value, axis, k) for k in range(lax.axis_size(axis))], 1)
        value = roll_to_absolute(line, axis, 1)
    return value.reshape(value.shape[0], -1)


MESH = pl.DeviceIdType.MESH
ANY = pl.BlockSpec(memory_space=pl.ANY)
VMEM = pl.BlockSpec(memory_space=pltpu.VMEM)


def places():
    return tuple(lax.axis_index(axis) for axis in ("dp", "cx", "core", "exp"))


def moved(dp=0, cx=0, core=0, exp=0):
    steps = (dp, cx, core, exp)
    return tuple(
        at if step == 0 else lax.rem(at + step, lax.axis_size(axis))
        for at, step, axis in zip(places(), steps, ("dp", "cx", "core", "exp"))
    )


def copy_to(source, target, send_sem, recv_sem, device):
    copy = pltpu.make_async_remote_copy(
        src_ref=source,
        dst_ref=target,
        send_sem=send_sem,
        recv_sem=recv_sem,
        device_id=device,
        device_id_type=MESH,
    )
    copy.start()
    return copy


def greet(devices):
    barrier = pltpu.get_barrier_semaphore()
    for device in devices:
        pl.semaphore_signal(barrier, inc=1, device_id=device, device_id_type=MESH)
    pl.semaphore_wait(barrier, len(devices))


def line_peers():
    return [moved(exp=k) for k in range(1, lax.axis_size("exp"))]


def plane_peers():
    steps = [(j, k) for j in range(lax.axis_size("dp")) for k in range(lax.axis_size("cx"))]
    return [moved(dp=j, cx=k) for j, k in steps[1:]]


class Spread:
    def __init__(self, source, out, sems):
        self.source, self.out, self.sems = source, out, sems
        self.line = lax.axis_size("exp")

    def start(self):
        send, recv, local = self.sems
        self.local = pltpu.make_async_copy(self.source, self.out.at[0, 0], local)
        self.local.start()
        self.near = [
            copy_to(
                self.source,
                self.out.at[0, self.line - k],
                send.at[0, k],
                recv.at[0, k],
                moved(exp=k),
            )
            for k in range(1, self.line)
        ]
        self.far = [
            copy_to(self.source, self.out.at[1, 0], send.at[1, 0], recv.at[1, 0], moved(core=1))
        ]

    def forward(self):
        send, recv, _ = self.sems
        for k in sorted(range(1, self.line), key=lambda k: min(k, self.line - k)):
            self.near[k - 1].wait_recv()
            slot = self.line - k
            self.far.append(
                copy_to(
                    self.out.at[0, slot],
                    self.out.at[1, slot],
                    send.at[1, k],
                    recv.at[1, k],
                    moved(core=1),
                )
            )

    def finish(self):
        self.local.wait()
        for copy in self.near:
            copy.wait_send()
        for copy in self.far:
            copy.wait()

    @staticmethod
    def scratch(line):
        return [
            pltpu.SemaphoreType.DMA((CORES, line)),
            pltpu.SemaphoreType.DMA((CORES, line)),
            pltpu.SemaphoreType.DMA,
        ]


class Columns:
    def __init__(self, cols, out, sems):
        self.cols, self.out, self.sems = cols, out, sems

    def start(self):
        send, recv, local = self.sems
        line = lax.axis_size("exp")
        _, _, core, exp = places()
        self.local = pltpu.make_async_copy(
            self.cols.at[core, exp], self.out.at[core, exp], local
        )
        self.local.start()
        self.copies = []
        for c in range(CORES):
            for k in range(line):
                if c or k:
                    target = moved(core=c, exp=k)
                    self.copies.append(
                        copy_to(
                            self.cols.at[target[2], target[3]],
                            self.out.at[core, exp],
                            send.at[c, k],
                            recv.at[c, k],
                            target,
                        )
                    )

    def arrive(self):
        self.local.wait()
        for copy in self.copies:
            copy.wait_recv()

    def finish(self):
        for copy in self.copies:
            copy.wait_send()

    scratch = Spread.scratch


class Plane:
    def __init__(self, out, sems):
        self.out, self.sems = out, sems
        self.n = (lax.axis_size("dp"), lax.axis_size("cx"))

    def send(self, half, j, k, dp, cx):
        send, recv = self.sems
        at = places()
        n_dp, n_cx = self.n
        from_dp = lax.rem(at[0] + n_dp - j, n_dp)
        from_cx = lax.rem(at[1] + n_cx - k, n_cx)
        block = self.out.at[from_dp, from_cx, half]
        a, b = j + dp, k + cx
        return copy_to(
            block, block, send.at[half, a, b], recv.at[half, a, b], moved(dp=dp, cx=cx)
        )

    def start(self):
        n_dp, n_cx = self.n
        self.along_cx = [[self.send(h, 0, 0, 0, k) for k in range(1, n_cx)] for h in range(2)]
        self.along_dp = [[self.send(h, 0, 0, j, 0) for j in range(1, n_dp)] for h in range(2)]

    def forward(self):
        n_dp, n_cx = self.n
        self.rest = []
        for k in range(1, n_cx):
            self.along_cx[0][k - 1].wait_recv()
            for j in range(1, n_dp):
                self.rest.append(self.send(0, 0, k, j, 0))
        for j in range(1, n_dp):
            self.along_dp[1][j - 1].wait_recv()
            for k in range(1, n_cx):
                self.rest.append(self.send(1, j, 0, 0, k))

    def finish(self):
        for copy in self.along_cx[1] + self.along_dp[0] + self.rest:
            copy.wait()
        for copy in self.along_cx[0] + self.along_dp[1]:
            copy.wait_send()

    @staticmethod
    def scratch(n_dp, n_cx):
        return [
            pltpu.SemaphoreType.DMA((2, n_dp, n_cx)),
            pltpu.SemaphoreType.DMA((2, n_dp, n_cx)),
        ]


def params(number):
    return pltpu.CompilerParams(
        collective_id=number, has_side_effects=True, vmem_limit_bytes=40 * 2**20
    )


def cost(micros, moved_bytes):
    return pl.CostEstimate(
        flops=int(micros * 9e8), bytes_accessed=moved_bytes, transcendentals=0
    )


def tp_peers():
    line = lax.axis_size("exp")
    steps = [(c, k) for c in range(CORES) for k in range(line)]
    return [moved(core=c, exp=k) for c, k in steps[1:]]


def load_body(x_ref, cols_ref, wo_ref, xall_ref, wqkv_ref, woall_ref, *sems):
    dp, cx, _, _ = places()
    greet(tp_peers() + plane_peers())
    tokens = Spread(x_ref, xall_ref, sems[0:3])
    block = wqkv_ref.at[dp, cx]
    columns = Columns(cols_ref, block, sems[3:6])
    plane = Plane(wqkv_ref, sems[6:8])
    send, recv, local = sems[8:11]
    columns.start()
    tokens.start()
    own = pltpu.make_async_copy(wo_ref, woall_ref.at[dp, cx], local)
    own.start()
    columns.arrive()
    plane.start()
    tokens.forward()
    plane.forward()
    outs = []
    for j in range(lax.axis_size("dp")):
        for k in range(lax.axis_size("cx")):
            if j or k:
                outs.append(
                    copy_to(
                        wo_ref,
                        woall_ref.at[dp, cx],
                        send.at[j, k],
                        recv.at[j, k],
                        moved(dp=j, cx=k),
                    )
                )
    columns.finish()
    tokens.finish()
    plane.finish()
    own.wait()
    for copy in outs:
        copy.wait()


def load(x_own, cols, w_output):
    n_dp, n_cx, line = (lax.axis_size(axis) for axis in ("dp", "cx", "exp"))
    return pl.pallas_call(
        load_body,
        out_shape=(
            jax.ShapeDtypeStruct((CORES, line) + x_own.shape, BF),
            jax.ShapeDtypeStruct((n_dp, n_cx) + cols.shape, BF),
            jax.ShapeDtypeStruct((n_dp, n_cx) + w_output.shape, BF),
        ),
        in_specs=[ANY] * 3,
        out_specs=(ANY,) * 3,
        scratch_shapes=Spread.scratch(line)
        + Columns.scratch(line)
        + Plane.scratch(n_dp, n_cx)
        + [
            pltpu.SemaphoreType.DMA((n_dp, n_cx)),
            pltpu.SemaphoreType.DMA((n_dp, n_cx)),
            pltpu.SemaphoreType.DMA,
        ],
        compiler_params=params(0),
        cost_estimate=cost(60, 2**22),
    )(x_own, cols, w_output)


def keys_body(kv_ref, cols_ref, wo_ref, kvall_ref, gu_ref, wout_ref, *sems):
    _, _, _, exp = places()
    n_cx = lax.axis_size("cx")
    line = lax.axis_size("exp")
    greet(tp_peers() + [moved(cx=k) for k in range(1, n_cx)])
    send, recv, local = sems[3:6]
    own = pltpu.make_async_copy(kv_ref, kvall_ref.at[0], local)
    own.start()
    keys = [
        copy_to(kv_ref, kvall_ref.at[n_cx - k], send.at[k], recv.at[k], moved(cx=k))
        for k in range(1, n_cx)
    ]
    columns = Columns(cols_ref, gu_ref, sems[0:3])
    columns.start()
    send, recv, local = sems[6:9]
    keep = pltpu.make_async_copy(wo_ref.at[exp // n_cx, exp % n_cx], wout_ref.at[exp], local)
    keep.start()
    outs = []
    for k in range(1, line):
        target = moved(exp=k)
        at = target[3]
        outs.append(
            copy_to(
                wo_ref.at[at // n_cx, at % n_cx],
                wout_ref.at[exp],
                send.at[k],
                recv.at[k],
                target,
            )
        )
    own.wait()
    keep.wait()
    columns.arrive()
    columns.finish()
    for copy in keys + outs:
        copy.wait()


def keys_call(kv, cols, wo_all):
    n_cx, line = lax.axis_size("cx"), lax.axis_size("exp")
    return pl.pallas_call(
        keys_body,
        out_shape=(
            jax.ShapeDtypeStruct((n_cx,) + kv.shape, BF),
            jax.ShapeDtypeStruct(cols.shape, BF),
            jax.ShapeDtypeStruct((line,) + wo_all.shape[2:], BF),
        ),
        in_specs=[ANY] * 3,
        out_specs=(ANY,) * 3,
        scratch_shapes=Columns.scratch(line)
        + [
            pltpu.SemaphoreType.DMA((n_cx,)),
            pltpu.SemaphoreType.DMA((n_cx,)),
            pltpu.SemaphoreType.DMA,
            pltpu.SemaphoreType.DMA((line,)),
            pltpu.SemaphoreType.DMA((line,)),
            pltpu.SemaphoreType.DMA,
        ],
        compiler_params=params(1),
        cost_estimate=cost(40, 2**22),
    )(kv, cols, wo_all)


class Collect:
    def __init__(self, partial, kept, near, half, far, sems):
        self.partial, self.kept, self.near, self.half, self.far = partial, kept, near, half, far
        self.sems = sems
        self.line = lax.axis_size("exp")
        self.order = list(range(1, self.line)) + [0]

    def start(self):
        core_send, core_recv, _, _, local = self.sems
        self.swaps, self.loads = {}, {}
        for k in self.order:
            self.swaps[k] = copy_to(
                self.partial.at[1, k],
                self.near.at[k],
                core_send.at[k],
                core_recv.at[k],
                moved(core=1),
            )
            self.loads[k] = pltpu.make_async_copy(
                self.partial.at[0, k], self.kept.at[k], local.at[k]
            )
            self.loads[k].start()

    def pair(self, k):
        self.loads[k].wait()
        self.swaps[k].wait_recv()
        return self.kept[k].astype(F32) + self.near[k].astype(F32)

    def reduce(self):
        _, _, send, recv, _ = self.sems
        copies = []
        for k in self.order[:-1]:
            self.half[k] = self.pair(k).astype(BF)
            copies.append(
                copy_to(
                    self.half.at[k], self.far.at[k], send.at[k], recv.at[k], moved(exp=k)
                )
            )
        total = self.pair(0)
        self.copies = copies
        for k, copy in sorted(zip(self.order, copies), key=lambda p: min(p[0], self.line - p[0])):
            copy.wait_recv()
            total = total + self.far[k].astype(F32)
        return total

    def finish(self):
        for k in self.order:
            self.swaps[k].wait_send()
        for copy in self.copies:
            copy.wait_send()

    @staticmethod
    def scratch(line, tok, width):
        buffer = pltpu.VMEM((line, tok, width), BF)
        return [buffer] * 4 + [pltpu.SemaphoreType.DMA((line,))] * 5


def ahead_body(
    partial_ref, x_ref, gain_ref, gu_ref, sd_ref, resid_ref, all_ref, wgu_ref, wsd_ref, *rest
):
    dp, cx, _, _ = places()
    greet(line_peers() + [moved(core=1)] + plane_peers())
    bufs, sems = rest[:4], rest[4:]
    normed_ref = sems[-1]
    collect = Collect(partial_ref, *bufs, sems[0:5])
    collect.start()
    local = sems[5]
    keep = [
        pltpu.make_async_copy(gu_ref, wgu_ref.at[dp, cx], local.at[0]),
        pltpu.make_async_copy(sd_ref, wsd_ref.at[dp, cx], local.at[1]),
    ]
    for copy in keep:
        copy.start()
    for copy in keep:
        copy.wait()
    gu = Plane(wgu_ref, sems[6:8])
    sd = Plane(wsd_ref, sems[8:10])
    gu.start()
    sd.start()
    total = collect.reduce()
    resid = x_ref[...].astype(F32) + total
    resid_ref[...] = resid
    normal, _ = rms_parts(resid)
    normed_ref[...] = (normal * gain_ref[...]).astype(BF)
    spread = Spread(normed_ref, all_ref, sems[10:13])
    spread.start()
    gu.forward()
    sd.forward()
    spread.forward()
    collect.finish()
    spread.finish()
    gu.finish()
    sd.finish()


def ahead(partial, x_own, gain, gu, sd):
    n_dp, n_cx, line = (lax.axis_size(axis) for axis in ("dp", "cx", "exp"))
    tok, width = x_own.shape
    return pl.pallas_call(
        ahead_body,
        out_shape=(
            jax.ShapeDtypeStruct((tok, width), F32),
            jax.ShapeDtypeStruct((CORES, line, tok, width), BF),
            jax.ShapeDtypeStruct((n_dp, n_cx) + gu.shape, BF),
            jax.ShapeDtypeStruct((n_dp, n_cx) + sd.shape, BF),
        ),
        in_specs=[ANY, VMEM, VMEM, ANY, ANY],
        out_specs=(VMEM, ANY, ANY, ANY),
        scratch_shapes=Collect.scratch(line, tok, width)
        + [pltpu.SemaphoreType.DMA((2,))]
        + Plane.scratch(n_dp, n_cx)
        + Plane.scratch(n_dp, n_cx)
        + Spread.scratch(line)
        + [pltpu.VMEM((tok, width), BF)],
        compiler_params=params(2),
        cost_estimate=cost(110, 2**22),
    )(partial, x_own, gain, gu, sd)


def back_body(
    partial_ref, extra_ref, resid_ref, gain_ref, cot_ref, dn_ref, dr_ref, all_ref, *rest
):
    greet(line_peers() + [moved(core=1)])
    bufs, sems = rest[:4], rest[4:]
    proj_ref = sems[-1]
    collect = Collect(partial_ref, *bufs, sems[0:5])
    collect.start()
    normal, inverse = rms_parts(resid_ref[...])
    d_normed = collect.reduce() + extra_ref[...]
    dn_ref[...] = d_normed
    d_hat = d_normed * gain_ref[...]
    d_resid = cot_ref[...].astype(F32) + inverse * (
        d_hat - normal * jnp.mean(d_hat * normal, 1, keepdims=True)
    )
    dr_ref[...] = d_resid
    proj_ref[...] = d_resid.astype(BF)
    spread = Spread(proj_ref, all_ref, sems[5:8])
    spread.start()
    spread.forward()
    collect.finish()
    spread.finish()


def back(partial, extra, resid, gain, cot):
    line = lax.axis_size("exp")
    tok, width = resid.shape
    return pl.pallas_call(
        back_body,
        out_shape=(
            jax.ShapeDtypeStruct((tok, width), F32),
            jax.ShapeDtypeStruct((tok, width), F32),
            jax.ShapeDtypeStruct((CORES, line, tok, width), BF),
        ),
        in_specs=[ANY, VMEM, VMEM, VMEM, VMEM],
        out_specs=(VMEM, VMEM, ANY),
        scratch_shapes=Collect.scratch(line, tok, width)
        + Spread.scratch(line)
        + [pltpu.VMEM((tok, width), BF)],
        compiler_params=params(3),
        cost_estimate=cost(110, 2**22),
    )(partial, extra, resid, gain, cot)


def last_body(partial_ref, out_ref, *rest):
    greet(line_peers() + [moved(core=1)])
    collect = Collect(partial_ref, *rest[:4], rest[4:])
    collect.start()
    out_ref[...] = collect.reduce()
    collect.finish()


def last(partial):
    line = lax.axis_size("exp")
    tok, width = partial.shape[2:]
    return pl.pallas_call(
        last_body,
        out_shape=jax.ShapeDtypeStruct((tok, width), F32),
        in_specs=[ANY],
        out_specs=VMEM,
        scratch_shapes=Collect.scratch(line, tok, width),
        compiler_params=params(4),
        cost_estimate=cost(60, 2**22),
    )(partial)


def on_device(
    tokens,
    cotangent,
    positions,
    lengths,
    routes,
    norm_attn,
    w_query,
    bias_query,
    w_key,
    bias_key,
    w_value,
    bias_value,
    w_output,
    norm_moe,
    w_router,
    w_shared_gate,
    w_shared_up,
    w_shared_down,
    w_shared_score,
    w_expert_gate,
    w_expert_up,
    w_expert_down,
):
    n_dp = lax.axis_size("dp")
    n_cx = lax.axis_size("cx")
    n_exp = lax.axis_size("exp")
    exp_at = lax.axis_index("exp")
    core_at = lax.axis_index("core")
    n_tp = CORES * n_exp
    n_data = n_dp * n_cx
    tok, width = tokens.shape[2:]
    shard = w_query.shape[0]
    block = CORES * n_exp * shard
    col = width // n_tp
    heads = col // HD
    n_experts = w_router.shape[1]
    sub = w_shared_down.shape[0]
    sub_width = n_data * sub
    every = tok * n_tp
    scale = HD ** (-0.5)
    top = routes.shape[3]
    ffe = w_expert_gate.shape[2]

    def by_core(first, second):
        return jnp.where(core_at == 0, first, second)

    x_own = tokens.reshape(tok, width)
    cot_own = cotangent.reshape(tok, width)

    small = jnp.concatenate(
        [
            norm_attn[None],
            norm_moe[None],
            w_shared_score[None],
            bias_query[None],
            bias_key[None],
            bias_value[None],
            w_router.T,
        ]
    )
    small = gather_small(small.astype(F32))
    gain_attn = small[0]
    gain_moe = small[1]
    score_vec = small[2]
    router_full = small[6:].T.astype(BF)
    rank = exp_at * CORES + core_at
    biases = lax.dynamic_slice_in_dim(small[3:6], rank * col, col, 1).reshape(3 * col)

    ints = jnp.concatenate(
        [
            positions.reshape(1, tok),
            routes.reshape(tok, top).T,
            jnp.pad(lengths.reshape(1, -1), ((0, 0), (0, tok - lengths.shape[2]))),
        ]
    )
    ints = spread(ints)
    pos_tok = ints[:, :, 0]
    route_tok = jnp.swapaxes(ints[:, :, 1 : 1 + top], 2, 3).reshape(every, top)
    seq_lens = ints[0, :, 1 + top, : lengths.shape[2]]
    seq_ends = jnp.cumsum(seq_lens, 1)
    pos_group = jnp.swapaxes(pos_tok, 0, 1).reshape(n_exp, CORES * tok)
    after_end = (pos_group[:, :, None] >= seq_ends[:, None, :]).astype(jnp.int32)
    seg_group = jnp.sum(after_end, 2)
    rel_group = pos_group - jnp.sum(after_end * seq_lens[:, None, :], 2)
    code = jnp.stack([pos_group, seg_group])
    code_keys = jnp.concatenate([fetch(code, "cx", k) for k in range(n_cx)], 2)
    allowed = (code_keys[1][:, None, :] == seg_group[:, :, None]) & (
        code_keys[0][:, None, :] <= pos_group[:, :, None]
    )
    freq = ROTARY_BASE ** (-(jnp.arange(HD // 2, dtype=F32) * 2.0 / HD))
    angle = rel_group.astype(F32)[:, :, None] * freq
    cos_table = jnp.cos(angle)[:, :, None, :]
    sin_table = jnp.sin(angle)[:, :, None, :]

    def exchange(value):
        return lax.all_to_all(value, ("core", "exp"), split_axis=0, concat_axis=0, tiled=True)

    def head_columns(value):
        parts = value.reshape(shard, n_exp, CORES, col)
        return jnp.transpose(parts, (2, 1, 0, 3))

    def hidden_columns(value):
        parts = value.reshape(shard, n_data, CORES, n_exp, sub)
        return jnp.transpose(parts, (2, 3, 0, 1, 4)).reshape(CORES, n_exp, shard, sub_width)

    def own_expert(value):
        mine = by_core(value[0], value[1])
        theirs = push(by_core(value[1], value[0]), "core", 1)
        return jnp.concatenate([by_core(mine, theirs), by_core(theirs, mine)], 0)

    e_gu_part = own_expert(jnp.concatenate([w_expert_gate, w_expert_up], 2))
    e_down_part = own_expert(w_expert_down)
    qkv_cols = jnp.concatenate(
        [head_columns(w_query), head_columns(w_key), head_columns(w_value)], 3
    )
    x_own, e_gu_part, e_down_part = lax.optimization_barrier((x_own, e_gu_part, e_down_part))
    w_egu = lax.all_gather(e_gu_part, ("dp", "cx"), axis=0, tiled=True)
    w_edown = lax.all_gather(e_down_part, ("dp", "cx"), axis=0, tiled=True)
    x_all, w_qkv, wo_all = load(x_own, qkv_cols, w_output)
    w_qkv = w_qkv.reshape(width, 3 * col)
    gu_cols = jnp.concatenate(
        [hidden_columns(w_shared_gate), hidden_columns(w_shared_up)], 3
    )

    x_all = x_all.reshape(every, width).astype(F32)
    normal_one, inverse_one = rms_parts(x_all)
    normed_one = (normal_one * gain_attn).astype(BF)
    qkv = project(normed_one, w_qkv) + biases

    def by_group(value):
        parts = value.reshape(CORES, n_exp, tok, -1)
        return jnp.swapaxes(parts, 0, 1).reshape(n_exp, CORES * tok, heads, HD)

    def by_token(value):
        parts = value.reshape(n_exp, CORES, tok, heads * HD)
        return jnp.swapaxes(parts, 0, 1).reshape(every, heads * HD)

    query = rotate(by_group(qkv[:, :col]), cos_table, sin_table, 1.0).astype(BF)
    key = rotate(by_group(qkv[:, col : 2 * col]), cos_table, sin_table, 1.0).astype(BF)
    value = by_group(qkv[:, 2 * col :]).astype(BF)
    key_value = jnp.stack([key, value]).reshape(2, n_exp, CORES * tok, col)
    key_value, gu_block, w_out = keys_call(key_value, gu_cols, wo_all)
    w_out = w_out.reshape(col, width)
    cot_own, key_value = lax.optimization_barrier((cot_own, key_value))
    cot_tok = spread(cot_own)
    key_value = jnp.moveaxis(key_value, 0, 2).reshape(
        2, n_exp, n_cx * CORES * tok, heads, HD
    )
    keys, values = key_value[0], key_value[1]
    scores = jnp.einsum("gqhd,gkhd->ghqk", query, keys, preferred_element_type=F32) * scale
    scores = jnp.where(allowed[:, None], scores, NEGATIVE)
    weights = jnp.exp(scores - jnp.max(scores, -1, keepdims=True))
    weights = weights / jnp.sum(weights, -1, keepdims=True)
    probs = weights.astype(BF)
    attn = jnp.einsum("ghqk,gkhd->gqhd", probs, values, preferred_element_type=F32)
    attn_low = by_token(attn.astype(BF))
    partial = project(attn_low, w_out).astype(BF)
    resid, normed_two, w_sgu, w_sdown = ahead(
        partial.reshape(CORES, n_exp, tok, width),
        x_own,
        gain_moe[None],
        gu_block,
        w_shared_down.reshape(2, sub // 2, width),
    )
    normed_two = normed_two.reshape(every, width)
    normed_two_own = normed_two[:tok]
    w_sgu = w_sgu.reshape(width, 2 * sub_width)
    w_sdown = w_sdown.reshape(sub_width, width)

    small_cols = jnp.concatenate([router_full, score_vec.astype(BF)[:, None]], 1)
    small_out = project(normed_two, small_cols)
    router_all = jax.nn.softmax(small_out[:, :n_experts], axis=-1)
    score_all = jax.nn.sigmoid(small_out[:, n_experts])
    chosen = jnp.any(route_tok == rank, axis=1)
    at_rank = (jnp.arange(n_experts) == rank).astype(F32)
    gate = jnp.where(chosen, jnp.sum(router_all * at_rank[None, :], 1), 0.0)
    cot_all = cot_tok.reshape(every, width).astype(F32)

    shared_pre = project(normed_two, w_sgu)
    s_gate = shared_pre[:, :sub_width]
    s_up = shared_pre[:, sub_width:]
    s_act, s_slope = silu_parts(s_gate)
    s_hidden = (s_act * s_up).astype(BF)
    shared = project(s_hidden, w_sdown)
    expert_pre = project(normed_two, w_egu)
    e_gate = expert_pre[:, :ffe]
    e_up = expert_pre[:, ffe:]
    e_act, e_slope = silu_parts(e_gate)
    e_hidden = (e_act * e_up).astype(BF)
    e_out = project(e_hidden, w_edown).astype(BF).astype(F32)
    mix = (score_all[:, None] * shared + gate[:, None] * e_out).astype(BF)
    dots = jnp.stack(
        [
            jnp.where(chosen, jnp.sum(cot_all * e_out, 1), 0.0),
            jnp.sum(cot_all * shared, 1),
        ]
    )

    d_shared = (score_all[:, None] * cot_all).astype(BF)
    d_sh = project_t(d_shared, w_sdown)
    d_sgu = jnp.concatenate(
        [(d_sh * s_up * s_slope).astype(BF), (d_sh * s_act).astype(BF)], 1
    )
    d_eout = (gate[:, None] * cot_all).astype(BF)
    d_eh = project_t(d_eout, w_edown)
    d_egu = jnp.concatenate(
        [(d_eh * e_up * e_slope).astype(BF), (d_eh * e_act).astype(BF)], 1
    )
    grad_egu = weight_grad(normed_two, d_egu).astype(BF)
    grad_edown = weight_grad(e_hidden, d_eout).astype(BF)
    partial_two = (project_t(d_sgu, w_sgu) + project_t(d_egu, w_egu)).astype(BF)
    grad_egu, grad_edown, partial_two = lax.optimization_barrier(
        (grad_egu, grad_edown, partial_two)
    )
    grad_egu = lax.psum_scatter(grad_egu, ("dp", "cx"), scatter_dimension=0, tiled=True)
    grad_edown = lax.psum_scatter(grad_edown, ("dp", "cx"), scatter_dimension=0, tiled=True)

    dots = dots.reshape(2, CORES, n_exp, tok)
    pair = jnp.stack([dots[:, 0], push(dots[:, 1], "core", 1)])
    d_router = jnp.zeros((tok, n_experts), F32)
    d_score = jnp.zeros((tok,), F32)
    for k in range(n_exp):
        came = pair[:, :, k] if k == 0 else push(pair[:, :, k], "exp", k)
        for c in range(CORES):
            source = lax.rem(exp_at - k + n_exp, n_exp) * CORES + lax.rem(core_at + c, CORES)
            spot = (jnp.arange(n_experts) == source).astype(F32)
            d_router = d_router + came[c, 0][:, None] * spot[None, :]
            d_score = d_score + came[c, 1]
    router_own = router_all[:tok]
    score_own = score_all[:tok]
    d_score = d_score * score_own * (1.0 - score_own)
    d_logits = (
        router_own * (d_router - jnp.sum(router_own * d_router, 1, keepdims=True))
    ).astype(BF)
    extra = project_t(d_logits, router_full) + d_score[:, None] * score_vec[None, :]
    d_normed_two, d_resid, d_proj = back(
        partial_two.reshape(CORES, n_exp, tok, width), extra, resid, gain_moe[None], cot_own
    )
    d_proj = d_proj.reshape(every, width)
    mix, d_proj = lax.optimization_barrier((mix, d_proj))
    mixed = (resid + collect(mix.reshape(CORES, n_exp, tok, width))).astype(BF)
    grad_router = weight_grad(d_logits, normed_two_own)
    grad_score = jnp.sum(d_score[:, None] * normed_two_own.astype(F32), 0)
    grad_gain_moe = jnp.sum(d_normed_two * rms_parts(resid)[0], 0)

    def to_both(value):
        rows = value.shape[0] // 2
        low = value[:rows].astype(F32)
        high = value[rows:].astype(F32)
        mine = by_core(low, high)
        theirs = push(by_core(high, low).astype(BF), "core", 1).astype(F32)
        return jnp.stack([by_core(mine, theirs), by_core(theirs, mine)])

    grad_egu = to_both(grad_egu)
    grad_edown = to_both(grad_edown)
    grad_sdown = sum_scatter(row_blocks(weight_grad(s_hidden, d_shared).astype(BF)), "cx")
    grad_sgu = sum_scatter(row_blocks(weight_grad(normed_two, d_sgu).astype(BF)), "dp")
    grad_sgu = exchange(grad_sgu.astype(BF).reshape(n_tp, shard, 2 * sub_width))

    def from_hidden(value):
        parts = value.reshape(CORES, n_exp, shard, n_data, sub)
        return jnp.transpose(parts, (2, 3, 0, 1, 4)).reshape(shard, -1).astype(F32)

    d_attn = by_group(project_t(d_proj, w_out).astype(BF))
    delta = jnp.sum(d_attn.astype(F32) * attn, -1)
    d_probs = jnp.einsum("gqhd,gkhd->ghqk", d_attn, values, preferred_element_type=F32)
    d_scores = (weights * (d_probs - jnp.swapaxes(delta, 1, 2)[..., None])).astype(BF)
    d_query = jnp.einsum("ghqk,gkhd->gqhd", d_scores, keys, preferred_element_type=F32) * scale
    d_key = jnp.einsum("ghqk,gqhd->gkhd", d_scores, query, preferred_element_type=F32) * scale
    d_value = jnp.einsum("ghqk,gqhd->gkhd", probs, d_attn, preferred_element_type=F32)
    d_kv = jnp.stack([d_key, d_value]).reshape(2, n_exp, n_cx, CORES * tok, heads, HD)
    d_kv_own = d_kv[:, :, 0]
    for k in range(1, n_cx):
        d_kv_own = d_kv_own + push(d_kv[:, :, k].astype(BF), "cx", k).astype(F32)
    d_qkv = jnp.concatenate(
        [
            by_token(rotate(d_query, cos_table, sin_table, -1.0).astype(BF)),
            by_token(rotate(d_kv_own[0], cos_table, sin_table, -1.0).astype(BF)),
            by_token(d_kv_own[1].astype(BF)),
        ],
        1,
    )
    partial_one = project_t(d_qkv, w_qkv)
    d_normed_one = last(partial_one.astype(BF).reshape(CORES, n_exp, tok, width))
    grad_gain_attn = jnp.sum(partial_one * normal_one, 0)
    d_hat_one = d_normed_one * gain_attn
    normal_own = normal_one[:tok]
    from_attn = inverse_one[:tok] * (
        d_hat_one - normal_own * jnp.mean(d_hat_one * normal_own, 1, keepdims=True)
    )
    grad_tokens = (d_resid + from_attn).astype(BF)
    grad_qkv = sum_scatter(row_blocks(weight_grad(normed_one, d_qkv).astype(BF)), "cx")
    grad_qkv = exchange(grad_qkv.astype(BF).reshape(n_tp, shard, 3 * col))

    def from_heads(value):
        parts = value.reshape(CORES, n_exp, shard, col)
        return jnp.transpose(parts, (2, 1, 0, 3)).reshape(shard, width).astype(F32)

    grad_out = lax.all_to_all(
        weight_grad(attn_low, d_proj).astype(BF).reshape(n_exp, shard, width),
        "exp",
        split_axis=0,
        concat_axis=0,
        tiled=True,
    ).reshape(n_data * shard, width)
    grad_out = sum_scatter(row_blocks(grad_out), "dp")

    grad_bias = jnp.sum(d_qkv.astype(F32), 0).reshape(3, col)
    grad_bias = lax.dynamic_update_slice_in_dim(
        jnp.zeros((3, width), F32), grad_bias, rank * col, 1
    )
    totals = jnp.concatenate(
        [
            grad_gain_attn[None],
            grad_gain_moe[None],
            grad_score[None],
            grad_bias,
            grad_router,
        ]
    )
    totals = sum_small(totals.reshape(-1, n_dp, n_cx, CORES, n_exp, shard))
    return (
        mixed.reshape(tokens.shape),
        grad_tokens.reshape(tokens.shape),
        totals[0],
        from_heads(grad_qkv[:, :, :col]),
        totals[3],
        from_heads(grad_qkv[:, :, col : 2 * col]),
        totals[4],
        from_heads(grad_qkv[:, :, 2 * col :]),
        totals[5],
        grad_out,
        totals[1],
        totals[6:].T,
        from_hidden(grad_sgu[:, :, :sub_width]),
        from_hidden(grad_sgu[:, :, sub_width:]),
        grad_sdown,
        totals[2],
        grad_egu[:, :, :ffe],
        grad_egu[:, :, ffe:],
        grad_edown,
    )


def solution(mesh):
    sizes = dict(mesh.shape)
    fine = Mesh(
        mesh.devices.reshape(sizes["dp"], sizes["ctx"] // CORES, CORES, sizes["exp"]),
        ("dp", "cx", "core", "exp"),
    )
    own = P("dp", "exp", ("cx", "core"), None)
    flat = P(("dp", "cx", "core", "exp"))
    rows = P(("dp", "cx", "core", "exp"), None)
    expert = P("exp", ("dp", "cx", "core"), None)
    placed = (
        own,
        own,
        P("dp", "exp", ("cx", "core")),
        P("dp", "exp", None),
        own,
        flat,
        rows,
        flat,
        rows,
        flat,
        rows,
        flat,
        rows,
        flat,
        rows,
        rows,
        rows,
        rows,
        flat,
        expert,
        expert,
        expert,
    )
    return jax.shard_map(
        on_device,
        mesh=fine,
        in_specs=placed,
        out_specs=(
            own,
            own,
            flat,
            rows,
            flat,
            rows,
            flat,
            rows,
            flat,
            rows,
            flat,
            rows,
            rows,
            rows,
            rows,
            flat,
            expert,
            expert,
            expert,
        ),
        check_vma=False,
    )
```

```python
import itertools

import jax
import jax.numpy as jnp
from jax import lax
from jax.experimental import pallas as pl
from jax.experimental.pallas import tpu as pltpu
from jax.sharding import Mesh
from jax.sharding import PartitionSpec as P

HD = 128
CORES = 2
EPSILON = 1e-06
ROTARY_BASE = 1000000.0
NEGATIVE = -1e30
BF = jnp.bfloat16
F32 = jnp.float32


def project(left, right):
    return jnp.dot(left, right, preferred_element_type=F32)


def project_t(left, right):
    return lax.dot_general(left, right, (((1,), (1,)), ((), ())), preferred_element_type=F32)


def weight_grad(left, right):
    return lax.dot_general(left, right, (((0,), (0,)), ((), ())), preferred_element_type=F32)


def rms_parts(value):
    inverse = lax.rsqrt(jnp.mean(value * value, axis=-1, keepdims=True) + EPSILON)
    return (value * inverse, inverse)


def rotate(value, cos_table, sin_table, direction):
    half_dim = value.shape[-1] // 2
    first = value[..., :half_dim]
    second = value[..., half_dim:]
    return jnp.concatenate(
        [
            first * cos_table - direction * second * sin_table,
            second * cos_table + direction * first * sin_table,
        ],
        -1,
    )


def silu_parts(value):
    sigmoid = jax.nn.sigmoid(value)
    return (value * sigmoid, sigmoid * (1.0 + value * (1.0 - sigmoid)))


def fetch(value, axis, step):
    size = lax.axis_size(axis)
    if step % size == 0:
        return value
    return lax.ppermute(value, axis, [((i + step) % size, i) for i in range(size)])


def push(value, axis, step):
    size = lax.axis_size(axis)
    return lax.ppermute(value, axis, [(i, (i + step) % size) for i in range(size)])


def roll_to_relative(value, axis, dim):
    size = lax.axis_size(axis)
    both = lax.concatenate([value, value], dim)
    return lax.dynamic_slice_in_dim(both, lax.axis_index(axis), size, dim)


def roll_to_absolute(value, axis, dim):
    size = lax.axis_size(axis)
    both = lax.concatenate([value, value], dim)
    start = lax.rem(size - lax.axis_index(axis), size)
    return lax.dynamic_slice_in_dim(both, start, size, dim)


def spread(value):
    line = [fetch(value, "exp", k) for k in range(lax.axis_size("exp"))]
    other = [fetch(piece, "core", 1) for piece in line]
    return jnp.stack(line + other).reshape((CORES, len(line)) + value.shape)


def collect(partial):
    line = lax.axis_size("exp")
    halves = [
        partial[0, k].astype(F32) + push(partial[1, k], "core", 1).astype(F32) for k in range(line)
    ]
    total = halves[0]
    for k in range(1, line):
        total = total + push(halves[k].astype(BF), "exp", k).astype(F32)
    return total


def sum_scatter(make, first):
    n_dp = lax.axis_size("dp")
    n_cx = lax.axis_size("cx")
    if first == "cx":
        outer, inner, n_outer, n_inner = "dp", "cx", n_dp, n_cx
        term = make
    else:
        outer, inner, n_outer, n_inner = "cx", "dp", n_cx, n_dp

        def term(a, b):
            return make(b, a)

    sums = []
    for a in list(range(1, n_outer)) + [0]:
        sent = [push(term(a, b).astype(BF), inner, b) for b in range(1, n_inner)]
        total = term(a, 0).astype(F32)
        for piece in sent:
            total = total + piece.astype(F32)
        sums.append((a, total))
    result = sums[-1][1]
    for a, total in sums[:-1]:
        result = result + push(total.astype(BF), outer, a).astype(F32)
    return result


def row_blocks(value):
    n_dp = lax.axis_size("dp")
    n_cx = lax.axis_size("cx")
    rows = value.shape[0] // (n_dp * n_cx)

    def make(j, k):
        dp = lax.rem(lax.axis_index("dp") + j, n_dp)
        cx = lax.rem(lax.axis_index("cx") + k, n_cx)
        return lax.dynamic_slice_in_dim(value, (dp * n_cx + cx) * rows, rows, 0)

    return make


def sum_small(value):
    for axis in ("dp", "cx", "core", "exp"):
        own = roll_to_relative(value, axis, 1)
        total = own[:, 0]
        for k in range(1, lax.axis_size(axis)):
            total = total + push(own[:, k], axis, k)
        value = total
    return value


MESH = pl.DeviceIdType.MESH
ANY = pl.BlockSpec(memory_space=pl.ANY)
VMEM = pl.BlockSpec(memory_space=pltpu.VMEM)


def places():
    return tuple(lax.axis_index(axis) for axis in ("dp", "cx", "core", "exp"))


def moved(dp=0, cx=0, core=0, exp=0):
    steps = (dp, cx, core, exp)
    return tuple(
        at if step == 0 else lax.rem(at + step, lax.axis_size(axis))
        for at, step, axis in zip(places(), steps, ("dp", "cx", "core", "exp"))
    )


def copy_to(source, target, send_sem, recv_sem, device):
    copy = pltpu.make_async_remote_copy(
        src_ref=source,
        dst_ref=target,
        send_sem=send_sem,
        recv_sem=recv_sem,
        device_id=device,
        device_id_type=MESH,
    )
    copy.start()
    return copy


def greet(devices):
    barrier = pltpu.get_barrier_semaphore()
    for device in devices:
        pl.semaphore_signal(barrier, inc=1, device_id=device, device_id_type=MESH)
    pl.semaphore_wait(barrier, len(devices))


def line_peers():
    return [moved(exp=k) for k in range(1, lax.axis_size("exp"))]


def plane_peers():
    steps = [(j, k) for j in range(lax.axis_size("dp")) for k in range(lax.axis_size("cx"))]
    return [moved(dp=j, cx=k) for j, k in steps[1:]]


class Spread:
    def __init__(self, source, out, sems):
        self.source, self.out = source, out
        self.up, self.down, self.over, self.local = sems
        self.line = lax.axis_size("exp")
        self.at = lax.axis_index("exp")

    def hop(self, step, way):
        slot = (self.line - step) % self.line if way > 0 else step
        landing = self.line - step - 1 if way > 0 else step + 1
        sems = self.up if way > 0 else self.down
        return pltpu.make_async_remote_copy(
            src_ref=self.source if step == 0 else self.out.at[0, slot],
            dst_ref=self.out.at[0, landing],
            send_sem=sems.at[0, step],
            recv_sem=sems.at[1, step + 1],
            device_id=moved(exp=1 if way > 0 else self.line - 1),
            device_id_type=MESH,
        )

    def sends(self, step, way):
        if way > 0:
            return jnp.logical_and(self.at >= step, self.at < self.line - 1)
        return jnp.logical_and(self.at + step <= self.line - 1, self.at > 0)

    def gets(self, step, way):
        return self.at >= step if way > 0 else self.at + step <= self.line - 1

    def across(self, slot):
        return pltpu.make_async_remote_copy(
            src_ref=self.source if slot == 0 else self.out.at[0, slot],
            dst_ref=self.out.at[1, slot],
            send_sem=self.over.at[0, slot],
            recv_sem=self.over.at[1, slot],
            device_id=moved(core=1),
            device_id_type=MESH,
        )

    def start(self):
        self.keep = pltpu.make_async_copy(self.source, self.out.at[0, 0], self.local)
        self.keep.start()
        for way in (1, -1):
            pl.when(self.sends(0, way))(self.hop(0, way).start)
        self.across(0).start()

    def forward(self):
        for step in range(1, self.line):
            for way in (1, -1):
                slot = self.line - step if way > 0 else step

                @pl.when(self.gets(step, way))
                def _():
                    self.hop(step - 1, way).wait_recv()
                    self.across(slot).start()

                if step < self.line - 1:
                    pl.when(self.sends(step, way))(self.hop(step, way).start)

    def finish(self):
        self.keep.wait()
        for step in range(self.line - 1):
            for way in (1, -1):
                pl.when(self.sends(step, way))(self.hop(step, way).wait_send)
        for slot in range(self.line):
            self.across(slot).wait()

    @staticmethod
    def scratch(line):
        return [
            pltpu.SemaphoreType.DMA((2, line)),
            pltpu.SemaphoreType.DMA((2, line)),
            pltpu.SemaphoreType.DMA((2, line)),
            pltpu.SemaphoreType.DMA,
        ]


class Columns:
    def __init__(self, cols, out, sems):
        self.cols, self.out, self.sems = cols, out, sems

    def start(self):
        send, recv, local = self.sems
        line = lax.axis_size("exp")
        _, _, core, exp = places()
        self.local = pltpu.make_async_copy(
            self.cols.at[core, exp], self.out.at[core, exp], local
        )
        self.local.start()
        self.copies = []
        for c in range(CORES):
            for k in range(line):
                if c or k:
                    target = moved(core=c, exp=k)
                    self.copies.append(
                        copy_to(
                            self.cols.at[target[2], target[3]],
                            self.out.at[core, exp],
                            send.at[c, k],
                            recv.at[c, k],
                            target,
                        )
                    )

    def arrive(self):
        self.local.wait()
        for copy in self.copies:
            copy.wait_recv()

    def finish(self):
        for copy in self.copies:
            copy.wait_send()

    @staticmethod
    def scratch(line):
        return [
            pltpu.SemaphoreType.DMA((CORES, line)),
            pltpu.SemaphoreType.DMA((CORES, line)),
            pltpu.SemaphoreType.DMA,
        ]


class Plane:
    def __init__(self, out, sems):
        self.out, self.sems = out, sems
        self.n = (lax.axis_size("dp"), lax.axis_size("cx"))

    def send(self, half, j, k, dp, cx):
        send, recv = self.sems
        at = places()
        n_dp, n_cx = self.n
        from_dp = lax.rem(at[0] + n_dp - j, n_dp)
        from_cx = lax.rem(at[1] + n_cx - k, n_cx)
        block = self.out.at[from_dp, from_cx, half]
        a, b = j + dp, k + cx
        return copy_to(
            block, block, send.at[half, a, b], recv.at[half, a, b], moved(dp=dp, cx=cx)
        )

    def start(self):
        n_dp, n_cx = self.n
        self.along_cx = [[self.send(h, 0, 0, 0, k) for k in range(1, n_cx)] for h in range(2)]
        self.along_dp = [[self.send(h, 0, 0, j, 0) for j in range(1, n_dp)] for h in range(2)]

    def forward(self):
        n_dp, n_cx = self.n
        self.rest = []
        for k in range(1, n_cx):
            self.along_cx[0][k - 1].wait_recv()
            for j in range(1, n_dp):
                self.rest.append(self.send(0, 0, k, j, 0))
        for j in range(1, n_dp):
            self.along_dp[1][j - 1].wait_recv()
            for k in range(1, n_cx):
                self.rest.append(self.send(1, j, 0, 0, k))

    def finish(self):
        for copy in self.along_cx[1] + self.along_dp[0] + self.rest:
            copy.wait()
        for copy in self.along_cx[0] + self.along_dp[1]:
            copy.wait_send()

    @staticmethod
    def scratch(n_dp, n_cx):
        return [
            pltpu.SemaphoreType.DMA((2, n_dp, n_cx)),
            pltpu.SemaphoreType.DMA((2, n_dp, n_cx)),
        ]


def params(number):
    return pltpu.CompilerParams(
        collective_id=number, has_side_effects=True, vmem_limit_bytes=40 * 2**20
    )


def cost():
    return pl.CostEstimate(flops=1, bytes_accessed=1, transcendentals=0)


def tp_peers():
    line = lax.axis_size("exp")
    steps = [(c, k) for c in range(CORES) for k in range(line)]
    return [moved(core=c, exp=k) for c, k in steps[1:]]


def all_peers():
    sizes = [range(lax.axis_size(axis)) for axis in ("dp", "cx", "core", "exp")]
    return [moved(*steps) for steps in itertools.product(*sizes) if any(steps)]


def load_body(x_ref, cols_ref, wo_ref, pack_ref, xall_ref, wqkv_ref, woall_ref, packs_ref, *sems):
    dp, cx, core, exp = places()
    greet(all_peers())
    tokens = Spread(x_ref, xall_ref, sems[0:4])
    block = wqkv_ref.at[dp, cx]
    columns = Columns(cols_ref, block, sems[4:7])
    plane = Plane(wqkv_ref, sems[7:9])
    send, recv, local = sems[9:12]
    columns.start()
    tokens.start()
    own = [
        pltpu.make_async_copy(wo_ref, woall_ref.at[dp, cx], local.at[0]),
        pltpu.make_async_copy(pack_ref, packs_ref.at[dp, cx, core, exp], local.at[1]),
    ]
    for copy in own:
        copy.start()
    pack_send, pack_recv = sems[12:14]
    sizes = [range(lax.axis_size(axis)) for axis in ("dp", "cx", "core", "exp")]
    outs = [
        copy_to(
            pack_ref,
            packs_ref.at[dp, cx, core, exp],
            pack_send.at[steps],
            pack_recv.at[steps],
            moved(*steps),
        )
        for steps in itertools.product(*sizes)
        if any(steps)
    ]
    columns.arrive()
    plane.start()
    tokens.forward()
    plane.forward()
    for j in range(lax.axis_size("dp")):
        for k in range(lax.axis_size("cx")):
            if j or k:
                outs.append(
                    copy_to(
                        wo_ref,
                        woall_ref.at[dp, cx],
                        send.at[j, k],
                        recv.at[j, k],
                        moved(dp=j, cx=k),
                    )
                )
    columns.finish()
    tokens.finish()
    plane.finish()
    for copy in own + outs:
        copy.wait()


def load(x_own, cols, w_output, pack):
    n_dp, n_cx, line = (lax.axis_size(axis) for axis in ("dp", "cx", "exp"))
    return pl.pallas_call(
        load_body,
        out_shape=(
            jax.ShapeDtypeStruct((CORES, line) + x_own.shape, BF),
            jax.ShapeDtypeStruct((n_dp, n_cx) + cols.shape, BF),
            jax.ShapeDtypeStruct((n_dp, n_cx) + w_output.shape, BF),
            jax.ShapeDtypeStruct((n_dp, n_cx, CORES, line) + pack.shape, F32),
        ),
        in_specs=[ANY] * 4,
        out_specs=(ANY,) * 4,
        scratch_shapes=Spread.scratch(line)
        + Columns.scratch(line)
        + Plane.scratch(n_dp, n_cx)
        + [
            pltpu.SemaphoreType.DMA((n_dp, n_cx)),
            pltpu.SemaphoreType.DMA((n_dp, n_cx)),
            pltpu.SemaphoreType.DMA((2,)),
            pltpu.SemaphoreType.DMA((n_dp, n_cx, CORES, line)),
            pltpu.SemaphoreType.DMA((n_dp, n_cx, CORES, line)),
        ],
        compiler_params=params(0),
        cost_estimate=cost(),
    )(x_own, cols, w_output, pack)


def keys_body(kv_ref, cols_ref, wo_ref, kvall_ref, gu_ref, wout_ref, *sems):
    _, _, _, exp = places()
    n_cx = lax.axis_size("cx")
    line = lax.axis_size("exp")
    greet(tp_peers() + [moved(cx=k) for k in range(1, n_cx)])
    send, recv, local = sems[3:6]
    own = pltpu.make_async_copy(kv_ref, kvall_ref.at[0], local)
    own.start()
    keys = [
        copy_to(kv_ref, kvall_ref.at[n_cx - k], send.at[k], recv.at[k], moved(cx=k))
        for k in range(1, n_cx)
    ]
    columns = Columns(cols_ref, gu_ref, sems[0:3])
    columns.start()
    send, recv, local = sems[6:9]
    keep = pltpu.make_async_copy(wo_ref.at[exp // n_cx, exp % n_cx], wout_ref.at[exp], local)
    keep.start()
    outs = []
    for k in range(1, line):
        target = moved(exp=k)
        at = target[3]
        outs.append(
            copy_to(
                wo_ref.at[at // n_cx, at % n_cx],
                wout_ref.at[exp],
                send.at[k],
                recv.at[k],
                target,
            )
        )
    own.wait()
    keep.wait()
    columns.arrive()
    columns.finish()
    for copy in keys + outs:
        copy.wait()


def keys_call(kv, cols, wo_all):
    n_cx, line = lax.axis_size("cx"), lax.axis_size("exp")
    return pl.pallas_call(
        keys_body,
        out_shape=(
            jax.ShapeDtypeStruct((n_cx,) + kv.shape, BF),
            jax.ShapeDtypeStruct(cols.shape, BF),
            jax.ShapeDtypeStruct((line,) + wo_all.shape[2:], BF),
        ),
        in_specs=[ANY] * 3,
        out_specs=(ANY,) * 3,
        scratch_shapes=Columns.scratch(line)
        + [
            pltpu.SemaphoreType.DMA((n_cx,)),
            pltpu.SemaphoreType.DMA((n_cx,)),
            pltpu.SemaphoreType.DMA,
            pltpu.SemaphoreType.DMA((line,)),
            pltpu.SemaphoreType.DMA((line,)),
            pltpu.SemaphoreType.DMA,
        ],
        compiler_params=params(1),
        cost_estimate=cost(),
    )(kv, cols, wo_all)


class Collect:
    def __init__(self, partial, kept, near, half, far, sems):
        self.partial, self.kept, self.near, self.half, self.far = partial, kept, near, half, far
        self.sems = sems
        self.line = lax.axis_size("exp")
        self.order = list(range(1, self.line)) + [0]

    def start(self):
        core_send, core_recv, _, _, local = self.sems
        self.swaps, self.loads = {}, {}
        for k in self.order:
            self.swaps[k] = copy_to(
                self.partial.at[1, k],
                self.near.at[k],
                core_send.at[k],
                core_recv.at[k],
                moved(core=1),
            )
            self.loads[k] = pltpu.make_async_copy(
                self.partial.at[0, k], self.kept.at[k], local.at[k]
            )
            self.loads[k].start()

    def pair(self, k):
        self.loads[k].wait()
        self.swaps[k].wait_recv()
        return self.kept[k].astype(F32) + self.near[k].astype(F32)

    def reduce(self):
        _, _, send, recv, _ = self.sems
        copies = []
        for k in self.order[:-1]:
            self.half[k] = self.pair(k).astype(BF)
            copies.append(
                copy_to(
                    self.half.at[k], self.far.at[k], send.at[k], recv.at[k], moved(exp=k)
                )
            )
        total = self.pair(0)
        self.copies = copies
        for k, copy in sorted(zip(self.order, copies), key=lambda p: min(p[0], self.line - p[0])):
            copy.wait_recv()
            total = total + self.far[k].astype(F32)
        return total

    def finish(self):
        for k in self.order:
            self.swaps[k].wait_send()
        for copy in self.copies:
            copy.wait_send()

    @staticmethod
    def scratch(line, tok, width):
        buffer = pltpu.VMEM((line, tok, width), BF)
        return [buffer] * 4 + [pltpu.SemaphoreType.DMA((line,))] * 5


def ahead_body(
    partial_ref, x_ref, gain_ref, gu_ref, sd_ref, resid_ref, all_ref, wgu_ref, wsd_ref, *rest
):
    dp, cx, _, _ = places()
    greet(line_peers() + [moved(core=1)] + plane_peers())
    bufs, sems = rest[:4], rest[4:]
    normed_ref = sems[-1]
    collect = Collect(partial_ref, *bufs, sems[0:5])
    collect.start()
    local = sems[5]
    keep = [
        pltpu.make_async_copy(gu_ref, wgu_ref.at[dp, cx], local.at[0]),
        pltpu.make_async_copy(sd_ref, wsd_ref.at[dp, cx], local.at[1]),
    ]
    for copy in keep:
        copy.start()
    for copy in keep:
        copy.wait()
    gu = Plane(wgu_ref, sems[6:8])
    sd = Plane(wsd_ref, sems[8:10])
    gu.start()
    sd.start()
    total = collect.reduce()
    resid = x_ref[...].astype(F32) + total
    resid_ref[...] = resid
    normal, _ = rms_parts(resid)
    normed_ref[...] = (normal * gain_ref[...]).astype(BF)
    spread = Spread(normed_ref, all_ref, sems[10:14])
    spread.start()
    gu.forward()
    sd.forward()
    spread.forward()
    collect.finish()
    spread.finish()
    gu.finish()
    sd.finish()


def ahead(partial, x_own, gain, gu, sd):
    n_dp, n_cx, line = (lax.axis_size(axis) for axis in ("dp", "cx", "exp"))
    tok, width = x_own.shape
    return pl.pallas_call(
        ahead_body,
        out_shape=(
            jax.ShapeDtypeStruct((tok, width), F32),
            jax.ShapeDtypeStruct((CORES, line, tok, width), BF),
            jax.ShapeDtypeStruct((n_dp, n_cx) + gu.shape, BF),
            jax.ShapeDtypeStruct((n_dp, n_cx) + sd.shape, BF),
        ),
        in_specs=[ANY, VMEM, VMEM, ANY, ANY],
        out_specs=(VMEM, ANY, ANY, ANY),
        scratch_shapes=Collect.scratch(line, tok, width)
        + [pltpu.SemaphoreType.DMA((2,))]
        + Plane.scratch(n_dp, n_cx)
        + Plane.scratch(n_dp, n_cx)
        + Spread.scratch(line)
        + [pltpu.VMEM((tok, width), BF)],
        compiler_params=params(2),
        cost_estimate=cost(),
    )(partial, x_own, gain, gu, sd)


def back_body(
    partial_ref, extra_ref, resid_ref, gain_ref, cot_ref, dn_ref, dr_ref, all_ref, *rest
):
    greet(line_peers() + [moved(core=1)])
    bufs, sems = rest[:4], rest[4:]
    proj_ref = sems[-1]
    collect = Collect(partial_ref, *bufs, sems[0:5])
    collect.start()
    normal, inverse = rms_parts(resid_ref[...])
    d_normed = collect.reduce() + extra_ref[...]
    dn_ref[...] = d_normed
    d_hat = d_normed * gain_ref[...]
    d_resid = cot_ref[...].astype(F32) + inverse * (
        d_hat - normal * jnp.mean(d_hat * normal, 1, keepdims=True)
    )
    dr_ref[...] = d_resid
    proj_ref[...] = d_resid.astype(BF)
    spread = Spread(proj_ref, all_ref, sems[5:9])
    spread.start()
    spread.forward()
    collect.finish()
    spread.finish()


def back(partial, extra, resid, gain, cot):
    line = lax.axis_size("exp")
    tok, width = resid.shape
    return pl.pallas_call(
        back_body,
        out_shape=(
            jax.ShapeDtypeStruct((tok, width), F32),
            jax.ShapeDtypeStruct((tok, width), F32),
            jax.ShapeDtypeStruct((CORES, line, tok, width), BF),
        ),
        in_specs=[ANY, VMEM, VMEM, VMEM, VMEM],
        out_specs=(VMEM, VMEM, ANY),
        scratch_shapes=Collect.scratch(line, tok, width)
        + Spread.scratch(line)
        + [pltpu.VMEM((tok, width), BF)],
        compiler_params=params(3),
        cost_estimate=cost(),
    )(partial, extra, resid, gain, cot)


def last_body(partial_ref, out_ref, *rest):
    greet(line_peers() + [moved(core=1)])
    collect = Collect(partial_ref, *rest[:4], rest[4:])
    collect.start()
    out_ref[...] = collect.reduce()
    collect.finish()


def last(partial):
    line = lax.axis_size("exp")
    tok, width = partial.shape[2:]
    return pl.pallas_call(
        last_body,
        out_shape=jax.ShapeDtypeStruct((tok, width), F32),
        in_specs=[ANY],
        out_specs=VMEM,
        scratch_shapes=Collect.scratch(line, tok, width),
        compiler_params=params(4),
        cost_estimate=cost(),
    )(partial)


def on_device(
    tokens,
    cotangent,
    positions,
    lengths,
    routes,
    norm_attn,
    w_query,
    bias_query,
    w_key,
    bias_key,
    w_value,
    bias_value,
    w_output,
    norm_moe,
    w_router,
    w_shared_gate,
    w_shared_up,
    w_shared_down,
    w_shared_score,
    w_expert_gate,
    w_expert_up,
    w_expert_down,
):
    n_dp = lax.axis_size("dp")
    n_cx = lax.axis_size("cx")
    n_exp = lax.axis_size("exp")
    exp_at = lax.axis_index("exp")
    core_at = lax.axis_index("core")
    n_tp = CORES * n_exp
    n_data = n_dp * n_cx
    tok, width = tokens.shape[2:]
    shard = w_query.shape[0]
    block = CORES * n_exp * shard
    col = width // n_tp
    heads = col // HD
    n_experts = w_router.shape[1]
    sub = w_shared_down.shape[0]
    sub_width = n_data * sub
    every = tok * n_tp
    scale = HD ** (-0.5)
    top = routes.shape[3]
    ffe = w_expert_gate.shape[2]

    def by_core(first, second):
        return jnp.where(core_at == 0, first, second)

    x_own = tokens.reshape(tok, width)
    cot_own = cotangent.reshape(tok, width)

    small = jnp.concatenate(
        [
            norm_attn[None],
            norm_moe[None],
            w_shared_score[None],
            bias_query[None],
            bias_key[None],
            bias_value[None],
            w_router.T,
        ]
    ).astype(F32)
    n_small = small.shape[0]
    pack = jnp.concatenate(
        [
            positions.reshape(1, tok),
            routes.reshape(tok, top).T,
            jnp.pad(lengths.reshape(1, -1), ((0, 0), (0, tok - lengths.shape[2]))),
        ]
    ).astype(F32)
    pack = jnp.concatenate([pack, jnp.pad(small, ((0, 0), (0, tok - shard)))])
    pack = jnp.pad(pack, ((0, -pack.shape[0] % 8), (0, 0)))

    def exchange(value):
        return lax.all_to_all(value, ("core", "exp"), split_axis=0, concat_axis=0, tiled=True)

    def head_columns(value):
        parts = value.reshape(shard, n_exp, CORES, col)
        return jnp.transpose(parts, (2, 1, 0, 3))

    def hidden_columns(value):
        parts = value.reshape(shard, n_data, CORES, n_exp, sub)
        return jnp.transpose(parts, (2, 3, 0, 1, 4)).reshape(CORES, n_exp, shard, sub_width)

    qkv_cols = jnp.concatenate(
        [head_columns(w_query), head_columns(w_key), head_columns(w_value)], 3
    )
    x_all, w_qkv, wo_all, packs = load(x_own, qkv_cols, w_output, pack)
    w_egu = lax.all_gather(
        jnp.concatenate([w_expert_gate, w_expert_up], 2), ("dp", "cx", "core"), axis=1, tiled=True
    )
    w_edown = lax.all_gather(w_expert_down, ("dp", "cx", "core"), axis=1, tiled=True)
    w_egu = lax.dynamic_index_in_dim(w_egu, core_at, 0, keepdims=False)
    w_edown = lax.dynamic_index_in_dim(w_edown, core_at, 0, keepdims=False)
    w_qkv = w_qkv.reshape(width, 3 * col)
    gu_cols = jnp.concatenate(
        [hidden_columns(w_shared_gate), hidden_columns(w_shared_up)], 3
    )


    small = packs[:, :, :, :, 2 + top : 2 + top + n_small, :shard]
    small = jnp.moveaxis(small, 4, 0).reshape(n_small, width)
    gain_attn = small[0]
    gain_moe = small[1]
    score_vec = small[2]
    router_full = small[6:].T.astype(BF)
    rank = exp_at * CORES + core_at
    biases = lax.dynamic_slice_in_dim(small[3:6], rank * col, col, 1).reshape(3 * col)

    ints = lax.dynamic_index_in_dim(packs, lax.axis_index("dp"), 0, keepdims=False)
    ints = ints[:, :, :, : 2 + top]
    for dim, axis in enumerate(("cx", "core", "exp")):
        ints = roll_to_relative(ints, axis, dim)
    ints = ints.astype(jnp.int32)
    route_tok = jnp.swapaxes(ints[0, :, :, 1 : 1 + top], 2, 3).reshape(every, top)
    seq_lens = ints[0, 0, :, 1 + top, : lengths.shape[2]]
    seq_ends = jnp.cumsum(seq_lens, 1)
    pos_keys = jnp.moveaxis(ints[:, :, :, 0], 2, 0).reshape(n_exp, n_cx * CORES * tok)
    after_end = (pos_keys[:, :, None] >= seq_ends[:, None, :]).astype(jnp.int32)
    seg_keys = jnp.sum(after_end, 2)
    rel_keys = pos_keys - jnp.sum(after_end * seq_lens[:, None, :], 2)
    own_keys = CORES * tok
    allowed = (seg_keys[:, None, :] == seg_keys[:, :own_keys, None]) & (
        pos_keys[:, None, :] <= pos_keys[:, :own_keys, None]
    )
    freq = ROTARY_BASE ** (-(jnp.arange(HD // 2, dtype=F32) * 2.0 / HD))
    angle = rel_keys[:, :own_keys].astype(F32)[:, :, None] * freq
    cos_table = jnp.cos(angle)[:, :, None, :]
    sin_table = jnp.sin(angle)[:, :, None, :]

    x_all = x_all.reshape(every, width).astype(F32)
    normal_one, inverse_one = rms_parts(x_all)
    normed_one = (normal_one * gain_attn).astype(BF)
    qkv = project(normed_one, w_qkv) + biases

    def by_group(value):
        parts = value.reshape(CORES, n_exp, tok, -1)
        return jnp.swapaxes(parts, 0, 1).reshape(n_exp, CORES * tok, heads, HD)

    def by_token(value):
        parts = value.reshape(n_exp, CORES, tok, heads * HD)
        return jnp.swapaxes(parts, 0, 1).reshape(every, heads * HD)

    query = rotate(by_group(qkv[:, :col]), cos_table, sin_table, 1.0).astype(BF)
    key = rotate(by_group(qkv[:, col : 2 * col]), cos_table, sin_table, 1.0).astype(BF)
    value = by_group(qkv[:, 2 * col :]).astype(BF)
    key_value = jnp.stack([key, value]).reshape(2, n_exp, CORES * tok, col)
    key_value, gu_block, w_out = keys_call(key_value, gu_cols, wo_all)
    w_out = w_out.reshape(col, width)
    cot_own, key_value = lax.optimization_barrier((cot_own, key_value))
    cot_tok = spread(cot_own)
    key_value = jnp.moveaxis(key_value, 0, 2).reshape(
        2, n_exp, n_cx * CORES * tok, heads, HD
    )
    keys, values = key_value[0], key_value[1]
    scores = jnp.einsum("gqhd,gkhd->ghqk", query, keys, preferred_element_type=F32) * scale
    scores = jnp.where(allowed[:, None], scores, NEGATIVE)
    weights = jnp.exp(scores - jnp.max(scores, -1, keepdims=True))
    weights = weights / jnp.sum(weights, -1, keepdims=True)
    probs = weights.astype(BF)
    attn = jnp.einsum("ghqk,gkhd->gqhd", probs, values, preferred_element_type=F32)
    attn_low = by_token(attn.astype(BF))
    partial = project(attn_low, w_out).astype(BF)
    resid, normed_two, w_sgu, w_sdown = ahead(
        partial.reshape(CORES, n_exp, tok, width),
        x_own,
        gain_moe[None],
        gu_block,
        w_shared_down.reshape(2, sub // 2, width),
    )
    normed_two = normed_two.reshape(every, width)
    normed_two_own = normed_two[:tok]
    w_sgu = w_sgu.reshape(width, 2 * sub_width)
    w_sdown = w_sdown.reshape(sub_width, width)

    small_cols = jnp.concatenate([router_full, score_vec.astype(BF)[:, None]], 1)
    small_out = project(normed_two, small_cols)
    router_all = jax.nn.softmax(small_out[:, :n_experts], axis=-1)
    score_all = jax.nn.sigmoid(small_out[:, n_experts])
    chosen = jnp.any(route_tok == rank, axis=1)
    at_rank = (jnp.arange(n_experts) == rank).astype(F32)
    gate = jnp.where(chosen, jnp.sum(router_all * at_rank[None, :], 1), 0.0)
    cot_all = cot_tok.reshape(every, width).astype(F32)

    shared_pre = project(normed_two, w_sgu)
    s_gate = shared_pre[:, :sub_width]
    s_up = shared_pre[:, sub_width:]
    s_act, s_slope = silu_parts(s_gate)
    s_hidden = (s_act * s_up).astype(BF)
    shared = project(s_hidden, w_sdown)
    expert_pre = project(normed_two, w_egu)
    e_gate = expert_pre[:, :ffe]
    e_up = expert_pre[:, ffe:]
    e_act, e_slope = silu_parts(e_gate)
    e_hidden = (e_act * e_up).astype(BF)
    e_out = project(e_hidden, w_edown).astype(BF).astype(F32)
    mix = (score_all[:, None] * shared + gate[:, None] * e_out).astype(BF)
    dots = jnp.stack(
        [
            jnp.where(chosen, jnp.sum(cot_all * e_out, 1), 0.0),
            jnp.sum(cot_all * shared, 1),
        ]
    )

    d_shared = (score_all[:, None] * cot_all).astype(BF)
    d_sh = project_t(d_shared, w_sdown)
    d_sgu = jnp.concatenate(
        [(d_sh * s_up * s_slope).astype(BF), (d_sh * s_act).astype(BF)], 1
    )
    d_eout = (gate[:, None] * cot_all).astype(BF)
    d_eh = project_t(d_eout, w_edown)
    d_egu = jnp.concatenate(
        [(d_eh * e_up * e_slope).astype(BF), (d_eh * e_act).astype(BF)], 1
    )
    grad_egu = weight_grad(normed_two, d_egu).astype(BF)
    grad_edown = weight_grad(e_hidden, d_eout).astype(BF)
    partial_two = (project_t(d_sgu, w_sgu) + project_t(d_egu, w_egu)).astype(BF)
    grad_egu, grad_edown, partial_two = lax.optimization_barrier(
        (grad_egu, grad_edown, partial_two)
    )
    grad_egu = lax.psum_scatter(grad_egu, ("dp", "cx"), scatter_dimension=0, tiled=True)
    grad_edown = lax.psum_scatter(grad_edown, ("dp", "cx"), scatter_dimension=0, tiled=True)

    dots = dots.reshape(2, CORES, n_exp, tok)
    pair = jnp.stack([dots[:, 0], push(dots[:, 1], "core", 1)])
    d_router = jnp.zeros((tok, n_experts), F32)
    d_score = jnp.zeros((tok,), F32)
    for k in range(n_exp):
        came = pair[:, :, k] if k == 0 else push(pair[:, :, k], "exp", k)
        for c in range(CORES):
            source = lax.rem(exp_at - k + n_exp, n_exp) * CORES + lax.rem(core_at + c, CORES)
            spot = (jnp.arange(n_experts) == source).astype(F32)
            d_router = d_router + came[c, 0][:, None] * spot[None, :]
            d_score = d_score + came[c, 1]
    router_own = router_all[:tok]
    score_own = score_all[:tok]
    d_score = d_score * score_own * (1.0 - score_own)
    d_logits = (
        router_own * (d_router - jnp.sum(router_own * d_router, 1, keepdims=True))
    ).astype(BF)
    extra = project_t(d_logits, router_full) + d_score[:, None] * score_vec[None, :]
    d_normed_two, d_resid, d_proj = back(
        partial_two.reshape(CORES, n_exp, tok, width), extra, resid, gain_moe[None], cot_own
    )
    d_proj = d_proj.reshape(every, width)
    mix, d_proj, s_hidden, d_sgu = lax.optimization_barrier((mix, d_proj, s_hidden, d_sgu))
    mixed = (resid + collect(mix.reshape(CORES, n_exp, tok, width))).astype(BF)
    grad_router = weight_grad(d_logits, normed_two_own)
    grad_score = jnp.sum(d_score[:, None] * normed_two_own.astype(F32), 0)
    grad_gain_moe = jnp.sum(d_normed_two * rms_parts(resid)[0], 0)

    def to_both(value):
        rows = value.shape[0] // 2
        low = value[:rows].astype(F32)
        high = value[rows:].astype(F32)
        mine = by_core(low, high)
        theirs = push(by_core(high, low).astype(BF), "core", 1).astype(F32)
        return jnp.stack([by_core(mine, theirs), by_core(theirs, mine)])

    grad_egu = to_both(grad_egu)
    grad_edown = to_both(grad_edown)
    grad_sdown = sum_scatter(row_blocks(weight_grad(s_hidden, d_shared).astype(BF)), "cx")
    grad_sgu = sum_scatter(row_blocks(weight_grad(normed_two, d_sgu).astype(BF)), "dp")
    grad_sgu = exchange(grad_sgu.astype(BF).reshape(n_tp, shard, 2 * sub_width))

    def from_hidden(value):
        parts = value.reshape(CORES, n_exp, shard, n_data, sub)
        return jnp.transpose(parts, (2, 3, 0, 1, 4)).reshape(shard, -1).astype(F32)

    d_attn = by_group(project_t(d_proj, w_out).astype(BF))
    delta = jnp.sum(d_attn.astype(F32) * attn, -1)
    d_probs = jnp.einsum("gqhd,gkhd->ghqk", d_attn, values, preferred_element_type=F32)
    d_scores = (weights * (d_probs - jnp.swapaxes(delta, 1, 2)[..., None])).astype(BF)
    d_query = jnp.einsum("ghqk,gkhd->gqhd", d_scores, keys, preferred_element_type=F32) * scale
    d_key = jnp.einsum("ghqk,gqhd->gkhd", d_scores, query, preferred_element_type=F32) * scale
    d_value = jnp.einsum("ghqk,gqhd->gkhd", probs, d_attn, preferred_element_type=F32)
    d_kv = jnp.stack([d_key, d_value]).reshape(2, n_exp, n_cx, CORES * tok, heads, HD)
    d_kv_own = d_kv[:, :, 0]
    for k in range(1, n_cx):
        d_kv_own = d_kv_own + push(d_kv[:, :, k].astype(BF), "cx", k).astype(F32)
    d_qkv = jnp.concatenate(
        [
            by_token(rotate(d_query, cos_table, sin_table, -1.0).astype(BF)),
            by_token(rotate(d_kv_own[0], cos_table, sin_table, -1.0).astype(BF)),
            by_token(d_kv_own[1].astype(BF)),
        ],
        1,
    )
    partial_one = project_t(d_qkv, w_qkv)
    d_normed_one = last(partial_one.astype(BF).reshape(CORES, n_exp, tok, width))
    grad_gain_attn = jnp.sum(partial_one * normal_one, 0)
    d_hat_one = d_normed_one * gain_attn
    normal_own = normal_one[:tok]
    from_attn = inverse_one[:tok] * (
        d_hat_one - normal_own * jnp.mean(d_hat_one * normal_own, 1, keepdims=True)
    )
    grad_tokens = (d_resid + from_attn).astype(BF)
    grad_qkv = sum_scatter(row_blocks(weight_grad(normed_one, d_qkv).astype(BF)), "cx")
    grad_qkv = exchange(grad_qkv.astype(BF).reshape(n_tp, shard, 3 * col))

    def from_heads(value):
        parts = value.reshape(CORES, n_exp, shard, col)
        return jnp.transpose(parts, (2, 1, 0, 3)).reshape(shard, width).astype(F32)

    grad_out = lax.all_to_all(
        weight_grad(attn_low, d_proj).astype(BF).reshape(n_exp, shard, width),
        "exp",
        split_axis=0,
        concat_axis=0,
        tiled=True,
    ).reshape(n_data * shard, width)
    grad_out = sum_scatter(row_blocks(grad_out), "dp")

    grad_bias = jnp.sum(d_qkv.astype(F32), 0).reshape(3, col)
    grad_bias = lax.dynamic_update_slice_in_dim(
        jnp.zeros((3, width), F32), grad_bias, rank * col, 1
    )
    totals = jnp.concatenate(
        [
            grad_gain_attn[None],
            grad_gain_moe[None],
            grad_score[None],
            grad_bias,
            grad_router,
        ]
    )
    totals = sum_small(totals.reshape(-1, n_dp, n_cx, CORES, n_exp, shard))
    return (
        mixed.reshape(tokens.shape),
        grad_tokens.reshape(tokens.shape),
        totals[0],
        from_heads(grad_qkv[:, :, :col]),
        totals[3],
        from_heads(grad_qkv[:, :, col : 2 * col]),
        totals[4],
        from_heads(grad_qkv[:, :, 2 * col :]),
        totals[5],
        grad_out,
        totals[1],
        totals[6:].T,
        from_hidden(grad_sgu[:, :, :sub_width]),
        from_hidden(grad_sgu[:, :, sub_width:]),
        grad_sdown,
        totals[2],
        grad_egu[:, :, :ffe],
        grad_egu[:, :, ffe:],
        grad_edown,
    )


def solution(mesh):
    sizes = dict(mesh.shape)
    fine = Mesh(
        mesh.devices.reshape(sizes["dp"], sizes["ctx"] // CORES, CORES, sizes["exp"]),
        ("dp", "cx", "core", "exp"),
    )
    own = P("dp", "exp", ("cx", "core"), None)
    flat = P(("dp", "cx", "core", "exp"))
    rows = P(("dp", "cx", "core", "exp"), None)
    expert = P("exp", ("dp", "cx", "core"), None)
    placed = (
        own,
        own,
        P("dp", "exp", ("cx", "core")),
        P("dp", "exp", None),
        own,
        flat,
        rows,
        flat,
        rows,
        flat,
        rows,
        flat,
        rows,
        flat,
        rows,
        rows,
        rows,
        rows,
        flat,
        expert,
        expert,
        expert,
    )
    return jax.shard_map(
        on_device,
        mesh=fine,
        in_specs=placed,
        out_specs=(
            own,
            own,
            flat,
            rows,
            flat,
            rows,
            flat,
            rows,
            flat,
            rows,
            flat,
            rows,
            rows,
            rows,
            rows,
            flat,
            expert,
            expert,
            expert,
        ),
        check_vma=False,
    )
```

```python
import itertools

import jax
import jax.numpy as jnp
from jax import lax
from jax.experimental import pallas as pl
from jax.experimental.pallas import tpu as pltpu
from jax.sharding import Mesh
from jax.sharding import PartitionSpec as P

HD = 128
CORES = 2
EPSILON = 1e-06
ROTARY_BASE = 1000000.0
NEGATIVE = -1e30
BF = jnp.bfloat16
F32 = jnp.float32


def project(left, right):
    return jnp.dot(left, right, preferred_element_type=F32)


def project_t(left, right):
    return lax.dot_general(left, right, (((1,), (1,)), ((), ())), preferred_element_type=F32)


def weight_grad(left, right):
    return lax.dot_general(left, right, (((0,), (0,)), ((), ())), preferred_element_type=F32)


def rms_parts(value):
    inverse = lax.rsqrt(jnp.mean(value * value, axis=-1, keepdims=True) + EPSILON)
    return (value * inverse, inverse)


def silu_parts(value):
    sigmoid = jax.nn.sigmoid(value)
    return (value * sigmoid, sigmoid * (1.0 + value * (1.0 - sigmoid)))


def fetch(value, axis, step):
    size = lax.axis_size(axis)
    if step % size == 0:
        return value
    return lax.ppermute(value, axis, [((i + step) % size, i) for i in range(size)])


def push(value, axis, step):
    size = lax.axis_size(axis)
    return lax.ppermute(value, axis, [(i, (i + step) % size) for i in range(size)])


def roll_to_relative(value, axis, dim):
    size = lax.axis_size(axis)
    both = lax.concatenate([value, value], dim)
    return lax.dynamic_slice_in_dim(both, lax.axis_index(axis), size, dim)


def spread(value):
    line = [fetch(value, "exp", k) for k in range(lax.axis_size("exp"))]
    other = [fetch(piece, "core", 1) for piece in line]
    return jnp.stack(line + other).reshape((CORES, len(line)) + value.shape)


def collect(partial):
    line = lax.axis_size("exp")
    halves = [
        partial[0, k].astype(F32) + push(partial[1, k], "core", 1).astype(F32) for k in range(line)
    ]
    total = halves[0]
    for k in range(1, line):
        total = total + push(halves[k].astype(BF), "exp", k).astype(F32)
    return total


MESH = pl.DeviceIdType.MESH
ANY = pl.BlockSpec(memory_space=pl.ANY)
VMEM = pl.BlockSpec(memory_space=pltpu.VMEM)


def places():
    return tuple(lax.axis_index(axis) for axis in ("dp", "cx", "core", "exp"))


def moved(dp=0, cx=0, core=0, exp=0):
    steps = (dp, cx, core, exp)
    return tuple(
        at if step == 0 else lax.rem(at + step, lax.axis_size(axis))
        for at, step, axis in zip(places(), steps, ("dp", "cx", "core", "exp"))
    )


def copy_to(source, target, send_sem, recv_sem, device):
    copy = pltpu.make_async_remote_copy(
        src_ref=source,
        dst_ref=target,
        send_sem=send_sem,
        recv_sem=recv_sem,
        device_id=device,
        device_id_type=MESH,
    )
    copy.start()
    return copy


def greet(devices):
    barrier = pltpu.get_barrier_semaphore()
    for device in devices:
        pl.semaphore_signal(barrier, inc=1, device_id=device, device_id_type=MESH)
    pl.semaphore_wait(barrier, len(devices))


def line_peers():
    return [moved(exp=k) for k in range(1, lax.axis_size("exp"))]


def plane_peers():
    steps = [(j, k) for j in range(lax.axis_size("dp")) for k in range(lax.axis_size("cx"))]
    return [moved(dp=j, cx=k) for j, k in steps[1:]]


class Spread:
    def __init__(self, source, out, sems):
        self.source, self.out = source, out
        self.up, self.down, self.over, self.local = sems
        self.line = lax.axis_size("exp")
        self.at = lax.axis_index("exp")

    def hop(self, step, way):
        slot = (self.line - step) % self.line if way > 0 else step
        landing = self.line - step - 1 if way > 0 else step + 1
        sems = self.up if way > 0 else self.down
        return pltpu.make_async_remote_copy(
            src_ref=self.source if step == 0 else self.out.at[0, slot],
            dst_ref=self.out.at[0, landing],
            send_sem=sems.at[0, step],
            recv_sem=sems.at[1, step + 1],
            device_id=moved(exp=1 if way > 0 else self.line - 1),
            device_id_type=MESH,
        )

    def sends(self, step, way):
        if way > 0:
            return jnp.logical_and(self.at >= step, self.at < self.line - 1)
        return jnp.logical_and(self.at + step <= self.line - 1, self.at > 0)

    def gets(self, step, way):
        return self.at >= step if way > 0 else self.at + step <= self.line - 1

    def across(self, slot):
        return pltpu.make_async_remote_copy(
            src_ref=self.source if slot == 0 else self.out.at[0, slot],
            dst_ref=self.out.at[1, slot],
            send_sem=self.over.at[0, slot],
            recv_sem=self.over.at[1, slot],
            device_id=moved(core=1),
            device_id_type=MESH,
        )

    def start(self):
        self.keep = pltpu.make_async_copy(self.source, self.out.at[0, 0], self.local)
        self.keep.start()
        for way in (1, -1):
            pl.when(self.sends(0, way))(self.hop(0, way).start)
        self.across(0).start()

    def forward(self):
        for step in range(1, self.line):
            for way in (1, -1):
                slot = self.line - step if way > 0 else step

                @pl.when(self.gets(step, way))
                def _():
                    self.hop(step - 1, way).wait_recv()
                    self.across(slot).start()

                if step < self.line - 1:
                    pl.when(self.sends(step, way))(self.hop(step, way).start)

    def finish(self):
        self.keep.wait()
        for step in range(self.line - 1):
            for way in (1, -1):
                pl.when(self.sends(step, way))(self.hop(step, way).wait_send)
        for slot in range(self.line):
            self.across(slot).wait()

    @staticmethod
    def scratch(line):
        return [
            pltpu.SemaphoreType.DMA((2, line)),
            pltpu.SemaphoreType.DMA((2, line)),
            pltpu.SemaphoreType.DMA((2, line)),
            pltpu.SemaphoreType.DMA,
        ]


class Columns:
    def __init__(self, cols, out, sems):
        self.cols, self.out, self.sems = cols, out, sems

    def start(self):
        send, recv, local = self.sems
        line = lax.axis_size("exp")
        _, _, core, exp = places()
        self.local = pltpu.make_async_copy(
            self.cols.at[core, exp], self.out.at[core, exp], local
        )
        self.local.start()
        self.copies = []
        for c in range(CORES):
            for k in range(line):
                if c or k:
                    target = moved(core=c, exp=k)
                    self.copies.append(
                        copy_to(
                            self.cols.at[target[2], target[3]],
                            self.out.at[core, exp],
                            send.at[c, k],
                            recv.at[c, k],
                            target,
                        )
                    )

    def arrive(self):
        self.local.wait()
        for copy in self.copies:
            copy.wait_recv()

    def finish(self):
        for copy in self.copies:
            copy.wait_send()

    @staticmethod
    def scratch(line):
        return [
            pltpu.SemaphoreType.DMA((CORES, line)),
            pltpu.SemaphoreType.DMA((CORES, line)),
            pltpu.SemaphoreType.DMA,
        ]


class Plane:
    def __init__(self, out, sems):
        self.out, self.sems = out, sems
        self.n = (lax.axis_size("dp"), lax.axis_size("cx"))

    def send(self, half, j, k, dp, cx):
        send, recv = self.sems
        at = places()
        n_dp, n_cx = self.n
        from_dp = lax.rem(at[0] + n_dp - j, n_dp)
        from_cx = lax.rem(at[1] + n_cx - k, n_cx)
        block = self.out.at[from_dp, from_cx, half]
        a, b = j + dp, k + cx
        return copy_to(
            block, block, send.at[half, a, b], recv.at[half, a, b], moved(dp=dp, cx=cx)
        )

    def start(self):
        n_dp, n_cx = self.n
        self.along_cx = [[self.send(h, 0, 0, 0, k) for k in range(1, n_cx)] for h in range(2)]
        self.along_dp = [[self.send(h, 0, 0, j, 0) for j in range(1, n_dp)] for h in range(2)]

    def forward(self):
        n_dp, n_cx = self.n
        self.rest = []
        for k in range(1, n_cx):
            self.along_cx[0][k - 1].wait_recv()
            for j in range(1, n_dp):
                self.rest.append(self.send(0, 0, k, j, 0))
        for j in range(1, n_dp):
            self.along_dp[1][j - 1].wait_recv()
            for k in range(1, n_cx):
                self.rest.append(self.send(1, j, 0, 0, k))

    def finish(self):
        for copy in self.along_cx[1] + self.along_dp[0] + self.rest:
            copy.wait()
        for copy in self.along_cx[0] + self.along_dp[1]:
            copy.wait_send()

    @staticmethod
    def scratch(n_dp, n_cx):
        return [
            pltpu.SemaphoreType.DMA((2, n_dp, n_cx)),
            pltpu.SemaphoreType.DMA((2, n_dp, n_cx)),
        ]


def params(number):
    return pltpu.CompilerParams(
        collective_id=number, has_side_effects=True, vmem_limit_bytes=40 * 2**20
    )


def cost():
    return pl.CostEstimate(flops=1, bytes_accessed=1, transcendentals=0)


def tp_peers():
    line = lax.axis_size("exp")
    steps = [(c, k) for c in range(CORES) for k in range(line)]
    return [moved(core=c, exp=k) for c, k in steps[1:]]


def all_peers():
    sizes = [range(lax.axis_size(axis)) for axis in ("dp", "cx", "core", "exp")]
    return [moved(*steps) for steps in itertools.product(*sizes) if any(steps)]


def load_body(x_ref, cols_ref, wo_ref, pack_ref, xall_ref, wqkv_ref, woall_ref, packs_ref, *sems):
    dp, cx, core, exp = places()
    greet(all_peers())
    tokens = Spread(x_ref, xall_ref, sems[0:4])
    block = wqkv_ref.at[dp, cx]
    columns = Columns(cols_ref, block, sems[4:7])
    plane = Plane(wqkv_ref, sems[7:9])
    send, recv, local = sems[9:12]
    columns.start()
    own = [
        pltpu.make_async_copy(wo_ref, woall_ref.at[dp, cx], local.at[0]),
        pltpu.make_async_copy(pack_ref, packs_ref.at[dp, cx, core, exp], local.at[1]),
    ]
    for copy in own:
        copy.start()
    pack_send, pack_recv = sems[12:14]
    sizes = [range(lax.axis_size(axis)) for axis in ("dp", "cx", "core", "exp")]
    outs = [
        copy_to(
            pack_ref,
            packs_ref.at[dp, cx, core, exp],
            pack_send.at[steps],
            pack_recv.at[steps],
            moved(*steps),
        )
        for steps in itertools.product(*sizes)
        if any(steps)
    ]
    columns.arrive()
    tokens.start()
    plane.start()
    tokens.forward()
    plane.forward()
    for j in range(lax.axis_size("dp")):
        for k in range(lax.axis_size("cx")):
            if j or k:
                outs.append(
                    copy_to(
                        wo_ref,
                        woall_ref.at[dp, cx],
                        send.at[j, k],
                        recv.at[j, k],
                        moved(dp=j, cx=k),
                    )
                )
    columns.finish()
    tokens.finish()
    plane.finish()
    for copy in own + outs:
        copy.wait()


def load(x_own, cols, w_output, pack):
    n_dp, n_cx, line = (lax.axis_size(axis) for axis in ("dp", "cx", "exp"))
    return pl.pallas_call(
        load_body,
        out_shape=(
            jax.ShapeDtypeStruct((CORES, line) + x_own.shape, BF),
            jax.ShapeDtypeStruct((n_dp, n_cx) + cols.shape, BF),
            jax.ShapeDtypeStruct((n_dp, n_cx) + w_output.shape, BF),
            jax.ShapeDtypeStruct((n_dp, n_cx, CORES, line) + pack.shape, F32),
        ),
        in_specs=[ANY] * 4,
        out_specs=(ANY,) * 4,
        scratch_shapes=Spread.scratch(line)
        + Columns.scratch(line)
        + Plane.scratch(n_dp, n_cx)
        + [
            pltpu.SemaphoreType.DMA((n_dp, n_cx)),
            pltpu.SemaphoreType.DMA((n_dp, n_cx)),
            pltpu.SemaphoreType.DMA((2,)),
            pltpu.SemaphoreType.DMA((n_dp, n_cx, CORES, line)),
            pltpu.SemaphoreType.DMA((n_dp, n_cx, CORES, line)),
        ],
        compiler_params=params(0),
        cost_estimate=cost(),
    )(x_own, cols, w_output, pack)


def keys_body(kv_ref, cols_ref, wo_ref, kvall_ref, gu_ref, wout_ref, *sems):
    _, _, _, exp = places()
    n_cx = lax.axis_size("cx")
    line = lax.axis_size("exp")
    greet(tp_peers() + [moved(cx=k) for k in range(1, n_cx)])
    send, recv, local = sems[3:6]
    own = pltpu.make_async_copy(kv_ref, kvall_ref.at[0], local)
    own.start()
    keys = [
        copy_to(kv_ref, kvall_ref.at[n_cx - k], send.at[k], recv.at[k], moved(cx=k))
        for k in range(1, n_cx)
    ]
    columns = Columns(cols_ref, gu_ref, sems[0:3])
    columns.start()
    send, recv, local = sems[6:9]
    keep = pltpu.make_async_copy(wo_ref.at[exp // n_cx, exp % n_cx], wout_ref.at[exp], local)
    keep.start()
    outs = []
    for k in range(1, line):
        target = moved(exp=k)
        at = target[3]
        outs.append(
            copy_to(
                wo_ref.at[at // n_cx, at % n_cx],
                wout_ref.at[exp],
                send.at[k],
                recv.at[k],
                target,
            )
        )
    own.wait()
    keep.wait()
    columns.arrive()
    columns.finish()
    for copy in keys + outs:
        copy.wait()


def keys_call(kv, cols, wo_all):
    n_cx, line = lax.axis_size("cx"), lax.axis_size("exp")
    return pl.pallas_call(
        keys_body,
        out_shape=(
            jax.ShapeDtypeStruct((n_cx,) + kv.shape, BF),
            jax.ShapeDtypeStruct(cols.shape, BF),
            jax.ShapeDtypeStruct((line,) + wo_all.shape[2:], BF),
        ),
        in_specs=[ANY] * 3,
        out_specs=(ANY,) * 3,
        scratch_shapes=Columns.scratch(line)
        + [
            pltpu.SemaphoreType.DMA((n_cx,)),
            pltpu.SemaphoreType.DMA((n_cx,)),
            pltpu.SemaphoreType.DMA,
            pltpu.SemaphoreType.DMA((line,)),
            pltpu.SemaphoreType.DMA((line,)),
            pltpu.SemaphoreType.DMA,
        ],
        compiler_params=params(1),
        cost_estimate=cost(),
    )(kv, cols, wo_all)


class Collect:
    def __init__(self, partial, kept, near, half, far, sems):
        self.partial, self.kept, self.near, self.half, self.far = partial, kept, near, half, far
        self.sems = sems
        self.line = lax.axis_size("exp")
        self.order = list(range(1, self.line)) + [0]

    def start(self):
        core_send, core_recv, _, _, local = self.sems
        self.swaps, self.loads = {}, {}
        for k in self.order:
            self.swaps[k] = copy_to(
                self.partial.at[1, k],
                self.near.at[k],
                core_send.at[k],
                core_recv.at[k],
                moved(core=1),
            )
            self.loads[k] = pltpu.make_async_copy(
                self.partial.at[0, k], self.kept.at[k], local.at[k]
            )
            self.loads[k].start()

    def pair(self, k):
        self.loads[k].wait()
        self.swaps[k].wait_recv()
        return self.kept[k].astype(F32) + self.near[k].astype(F32)

    def reduce(self):
        self.send()
        return self.gather()

    def send(self):
        _, _, send, recv, _ = self.sems
        copies = []
        for k in self.order[:-1]:
            self.half[k] = self.pair(k).astype(BF)
            copies.append(
                copy_to(
                    self.half.at[k], self.far.at[k], send.at[k], recv.at[k], moved(exp=k)
                )
            )
        self.copies = copies

    def gather(self):
        total = self.pair(0)
        near = sorted(zip(self.order, self.copies), key=lambda p: min(p[0], self.line - p[0]))
        for k, copy in near:
            copy.wait_recv()
            total = total + self.far[k].astype(F32)
        return total

    def finish(self):
        for k in self.order:
            self.swaps[k].wait_send()
        for copy in self.copies:
            copy.wait_send()

    @staticmethod
    def scratch(line, tok, width):
        buffer = pltpu.VMEM((line, tok, width), BF)
        return [buffer] * 4 + [pltpu.SemaphoreType.DMA((line,))] * 5


def by_chunks(rows, work):
    chunk = 16 if rows % 16 == 0 else 8

    @pl.loop(0, rows // chunk)
    def _(step):
        work(pl.ds(pl.multiple_of(step * chunk, chunk), chunk))


def split_hidden(gate, up, n_exp, piece):
    shard, total = gate.shape
    blocks = total // (CORES * n_exp * piece)

    def body(gate_ref, up_ref, out_ref):
        sides = (gate_ref[...].astype(F32), up_ref[...].astype(F32))
        for c in range(CORES):
            for e in range(n_exp):
                parts = []
                for side in sides:
                    for b in range(blocks):
                        start = ((b * CORES + c) * n_exp + e) * piece
                        parts.append(side[:, start : start + piece])
                out_ref[c, e] = jnp.concatenate(parts, 1).astype(BF)

    return pl.pallas_call(
        body,
        out_shape=jax.ShapeDtypeStruct((CORES, n_exp, shard, 2 * blocks * piece), BF),
        in_specs=[VMEM, VMEM],
        out_specs=VMEM,
        compiler_params=local_params(),
        cost_estimate=cost(),
    )(gate, up)


def merge_hidden(value, piece):
    _, n_exp, shard, both = value.shape
    blocks = both // (2 * piece)
    total = blocks * CORES * n_exp * piece

    def body(in_ref, gate_ref, up_ref):
        for side, out_ref in enumerate((gate_ref, up_ref)):
            parts = []
            for b in range(blocks):
                start = (side * blocks + b) * piece
                for c in range(CORES):
                    for e in range(n_exp):
                        parts.append(in_ref[c, e].astype(F32)[:, start : start + piece])
            out_ref[...] = jnp.concatenate(parts, 1)

    shape = jax.ShapeDtypeStruct((shard, total), F32)
    return pl.pallas_call(
        body,
        out_shape=(shape, shape),
        in_specs=[VMEM],
        out_specs=(VMEM, VMEM),
        compiler_params=local_params(),
        cost_estimate=cost(),
    )(value)


class HalfSum:
    def __init__(self, blocks, half, bufs, sems):
        self.blocks, self.half = blocks, half
        self.own, self.came, self.sums, self.final = bufs
        self.sem = sems
        n_dp, n_cx = lax.axis_size("dp"), lax.axis_size("cx")
        self.cx_first = half == 0
        self.n_in, self.n_out = (n_cx, n_dp) if self.cx_first else (n_dp, n_cx)

    def block(self, inner, outer):
        dp, cx = (outer, inner) if self.cx_first else (inner, outer)
        at = moved(dp=dp, cx=cx)
        return self.blocks.at[at[0], at[1], self.half]

    def far(self, inner, outer):
        dp, cx = (outer, inner) if self.cx_first else (inner, outer)
        return moved(dp=dp, cx=cx)

    def start(self):
        first_send, first_recv, _, _, local = self.sem
        self.first, self.loads = {}, []
        for a in range(self.n_out):
            for b in range(1, self.n_in):
                self.first[b, a] = copy_to(
                    self.block(b, a),
                    self.came.at[b - 1, a],
                    first_send.at[b - 1, a],
                    first_recv.at[b - 1, a],
                    self.far(b, 0),
                )
            load = pltpu.make_async_copy(self.block(0, a), self.own.at[a], local.at[a])
            load.start()
            self.loads.append(load)

    def near(self, a, rows):
        total = self.own[a, rows].astype(F32)
        for b in range(1, self.n_in):
            total = total + self.came[b - 1, a, rows].astype(F32)
        return total

    def middle(self):
        _, _, send, recv, _ = self.sem
        for load in self.loads:
            load.wait()
        self.second = []
        for a in range(1, self.n_out):
            for b in range(1, self.n_in):
                self.first[b, a].wait_recv()

            def work(rows):
                self.sums[a - 1, rows] = self.near(a, rows).astype(BF)

            by_chunks(self.sums.shape[1], work)
            self.second.append(
                copy_to(
                    self.sums.at[a - 1],
                    self.final.at[a - 1],
                    send.at[a - 1],
                    recv.at[a - 1],
                    self.far(0, a),
                )
            )

    def end(self, out):
        for b in range(1, self.n_in):
            self.first[b, 0].wait_recv()
        for copy in self.second:
            copy.wait_recv()

        def work(rows):
            total = self.near(0, rows)
            for a in range(1, self.n_out):
                total = total + self.final[a - 1, rows].astype(F32)
            out[rows] = total.astype(out.dtype)

        by_chunks(self.sums.shape[1], work)
        for copy in self.first.values():
            copy.wait_send()
        for copy in self.second:
            copy.wait_send()

    @staticmethod
    def scratch(half, rows, width):
        n_dp, n_cx = lax.axis_size("dp"), lax.axis_size("cx")
        n_in, n_out = (n_cx, n_dp) if half == 0 else (n_dp, n_cx)
        dma = pltpu.SemaphoreType.DMA
        return (
            [
                pltpu.VMEM((n_out, rows, width), BF),
                pltpu.VMEM((n_in - 1, n_out, rows, width), BF),
                pltpu.VMEM((n_out - 1, rows, width), BF),
                pltpu.VMEM((n_out - 1, rows, width), BF),
            ],
            [
                dma((n_in - 1, n_out)),
                dma((n_in - 1, n_out)),
                dma((n_out - 1,)),
                dma((n_out - 1,)),
                dma((n_out,)),
            ],
        )


class PlaneSum:
    def __init__(self, blocks, out, scratch):
        self.out = out
        self.halves = [
            HalfSum(blocks, h, scratch[9 * h : 9 * h + 4], scratch[9 * h + 4 : 9 * h + 9])
            for h in range(2)
        ]

    def start(self):
        for half in self.halves:
            half.start()

    def middle(self):
        for half in self.halves:
            half.middle()

    def end(self):
        for h, half in enumerate(self.halves):
            half.end(self.out.at[h])

    @staticmethod
    def scratch(rows, width):
        both = [HalfSum.scratch(h, rows, width) for h in range(2)]
        return both[0][0] + both[0][1] + both[1][0] + both[1][1]


def full(shape):
    return pl.BlockSpec(shape, lambda g: (0,) * len(shape))


def turn(value, cos, sin):
    return value * cos + pltpu.roll(value, HD // 2, 1) * sin


def project_qkv_body(x_ref, w_ref, gain_ref, bias_ref, cos_ref, sin_ref, n_ref, q_ref, kv_ref):
    rows = x_ref.shape[0] * x_ref.shape[2]
    width = x_ref.shape[3]
    col = q_ref.shape[2]
    normal, _ = rms_parts(x_ref[...].reshape(rows, width).astype(F32))
    normed = (normal * gain_ref[...]).astype(BF)
    n_ref[...] = normed.reshape(n_ref.shape)
    lin = project(normed, w_ref[...]) + bias_ref[...]
    cos, sin = cos_ref[0], sin_ref[0]
    for h in range(col // HD):
        at = slice(h * HD, (h + 1) * HD)
        q_ref[0, :, at] = turn(lin[:, at], cos, sin).astype(BF)
        head = lin[:, col + h * HD : col + (h + 1) * HD]
        kv_ref[0, 0, :, at] = turn(head, cos, sin).astype(BF)
    kv_ref[1, 0] = lin[:, 2 * col :].astype(BF)


def project_qkv(x_all, w_qkv, gain, bias, cos, sin):
    cores, line, tok, width = x_all.shape
    col = w_qkv.shape[1] // 3
    rows = cores * tok
    tokens = pl.BlockSpec((cores, 1, tok, width), lambda g: (0, g, 0, 0))
    table = pl.BlockSpec((1, rows, HD), lambda g: (g, 0, 0))
    return pl.pallas_call(
        project_qkv_body,
        grid=(line,),
        out_shape=(
            jax.ShapeDtypeStruct(x_all.shape, BF),
            jax.ShapeDtypeStruct((line, rows, col), BF),
            jax.ShapeDtypeStruct((2, line, rows, col), BF),
        ),
        in_specs=[
            tokens,
            full(w_qkv.shape),
            full((1, width)),
            full((1, 3 * col)),
            table,
            table,
        ],
        out_specs=(
            tokens,
            pl.BlockSpec((1, rows, col), lambda g: (g, 0, 0)),
            pl.BlockSpec((2, 1, rows, col), lambda g: (0, g, 0, 0)),
        ),
        compiler_params=local_params(),
        cost_estimate=cost(),
    )(x_all, w_qkv, gain[None], bias[None], cos, sin)


def local_params():
    return pltpu.CompilerParams(vmem_limit_bytes=40 * 2**20)


def head_probs(query, keys, allowed):
    scores = project_t(query, keys) * (HD**-0.5)
    scores = jnp.where(allowed, scores, NEGATIVE)
    weights = jnp.exp(scores - jnp.max(scores, -1, keepdims=True))
    return weights / jnp.sum(weights, -1, keepdims=True)


def key_value(kv_ref, which):
    part = kv_ref[:, which, 0]
    return part.reshape(part.shape[0] * part.shape[1], part.shape[2])


def attend_body(q_ref, kv_ref, high_ref, low_ref, code_ref, w_ref, attn_ref, partial_ref):
    col = q_ref.shape[2]
    keys, values = key_value(kv_ref, 0), key_value(kv_ref, 1)
    allowed = (code_ref[0] <= high_ref[0]) & (code_ref[0] >= low_ref[0])
    outs = []
    for h in range(col // HD):
        at = slice(h * HD, (h + 1) * HD)
        probs = head_probs(q_ref[0, :, at], keys[:, at], allowed).astype(BF)
        outs.append(project(probs, values[:, at]).astype(BF))
    attn = jnp.concatenate(outs, 1) if len(outs) > 1 else outs[0]
    attn_ref[...] = attn.reshape(attn_ref.shape)
    partial_ref[...] = project(attn, w_ref[...]).astype(BF).reshape(partial_ref.shape)


def attention_specs(line, rows, col, n_cx):
    return [
        pl.BlockSpec((1, rows, col), lambda g: (g, 0, 0)),
        pl.BlockSpec((n_cx, 2, 1, rows, col), lambda g: (0, 0, g, 0, 0)),
        pl.BlockSpec((1, rows, 1), lambda g: (g, 0, 0)),
        pl.BlockSpec((1, rows, 1), lambda g: (g, 0, 0)),
        pl.BlockSpec((1, 1, n_cx * rows), lambda g: (g, 0, 0)),
    ]


def attend(query, kv, codes, w_out):
    line, rows, col = query.shape
    tok, width = rows // CORES, w_out.shape[1]
    return pl.pallas_call(
        attend_body,
        grid=(line,),
        out_shape=(
            jax.ShapeDtypeStruct((CORES, line, tok, col), BF),
            jax.ShapeDtypeStruct((CORES, line, tok, width), BF),
        ),
        in_specs=attention_specs(line, rows, col, kv.shape[0]) + [full(w_out.shape)],
        out_specs=(
            pl.BlockSpec((CORES, 1, tok, col), lambda g: (0, g, 0, 0)),
            pl.BlockSpec((CORES, 1, tok, width), lambda g: (0, g, 0, 0)),
        ),
        compiler_params=local_params(),
        cost_estimate=cost(),
    )(query, kv, *codes, w_out)


def attend_back_body(
    q_ref, kv_ref, high_ref, low_ref, code_ref, w_ref, dp_ref, cos_ref, sin_ref, dq_ref, dkv_ref
):
    col = q_ref.shape[2]
    rows = q_ref.shape[1]
    keys, values = key_value(kv_ref, 0), key_value(kv_ref, 1)
    allowed = (code_ref[0] <= high_ref[0]) & (code_ref[0] >= low_ref[0])
    d_proj = dp_ref[...].reshape(rows, dp_ref.shape[3])
    d_attn = project_t(d_proj, w_ref[...]).astype(BF)
    scale = HD**-0.5
    cos, sin = cos_ref[0], sin_ref[0]
    for h in range(col // HD):
        at = slice(h * HD, (h + 1) * HD)
        query = q_ref[0, :, at]
        weights = head_probs(query, keys[:, at], allowed)
        probs = weights.astype(BF)
        d_probs = project_t(d_attn[:, at], values[:, at])
        delta = jnp.sum(probs.astype(F32) * d_probs, -1, keepdims=True)
        d_scores = (weights * (d_probs - delta)).astype(BF)
        d_query = project(d_scores, keys[:, at]) * scale
        d_key = weight_grad(d_scores, query) * scale
        d_value = weight_grad(probs, d_attn[:, at])
        dq_ref[:, :, :, at] = (
            turn(d_query, cos, -sin).astype(BF).reshape(dq_ref.shape[:3] + (HD,))
        )
        shape = (dkv_ref.shape[0], rows, HD)
        dkv_ref[:, 0, 0, :, at] = d_key.astype(BF).reshape(shape)
        dkv_ref[:, 1, 0, :, at] = d_value.astype(BF).reshape(shape)


def attend_back(query, kv, codes, w_out, d_proj, cos, sin):
    line, rows, col = query.shape
    tok, width = rows // CORES, w_out.shape[1]
    table = pl.BlockSpec((1, rows, HD), lambda g: (g, 0, 0))
    specs = attention_specs(line, rows, col, kv.shape[0])
    return pl.pallas_call(
        attend_back_body,
        grid=(line,),
        out_shape=(
            jax.ShapeDtypeStruct((CORES, line, tok, col), BF),
            jax.ShapeDtypeStruct(kv.shape, BF),
        ),
        in_specs=specs
        + [
            full(w_out.shape),
            pl.BlockSpec((CORES, 1, tok, width), lambda g: (0, g, 0, 0)),
            table,
            table,
        ],
        out_specs=(pl.BlockSpec((CORES, 1, tok, col), lambda g: (0, g, 0, 0)), specs[1]),
        compiler_params=local_params(),
        cost_estimate=cost(),
    )(query, kv, *codes, w_out, d_proj, cos, sin)


def qkv_back_body(
    dq_ref, own_ref, came_ref, cos_ref, sin_ref, w_ref, x_ref, d_ref, partial_ref, gain_ref, bias_ref
):
    rows = own_ref.shape[2]
    col = own_ref.shape[3]
    cos, sin = cos_ref[0], sin_ref[0]
    d_key, d_value = own_ref[0, 0].astype(F32), own_ref[1, 0].astype(F32)
    for k in range(came_ref.shape[0]):
        d_key = d_key + came_ref[k, 0, 0].astype(F32)
        d_value = d_value + came_ref[k, 1, 0].astype(F32)
    keys = [
        turn(d_key[:, h * HD : (h + 1) * HD], cos, -sin).astype(BF) for h in range(col // HD)
    ]
    d_lin = jnp.concatenate([dq_ref[...].reshape(rows, col)] + keys + [d_value.astype(BF)], 1)
    d_ref[...] = d_lin.reshape(d_ref.shape)
    partial = project_t(d_lin, w_ref[...])
    partial_ref[...] = partial.astype(BF).reshape(partial_ref.shape)
    normal, _ = rms_parts(x_ref[...].reshape(rows, x_ref.shape[3]).astype(F32))
    gain = jnp.sum(partial * normal, 0, keepdims=True)
    bias = jnp.sum(d_lin.astype(F32), 0, keepdims=True)

    @pl.when(pl.program_id(0) == 0)
    def _():
        gain_ref[...] = jnp.zeros_like(gain_ref)
        bias_ref[...] = jnp.zeros_like(bias_ref)

    gain_ref[...] += gain
    bias_ref[...] += bias


def qkv_back(d_query, own, came, cos, sin, w_qkv, x_all):
    cores, line, tok, width = x_all.shape
    _, _, rows, col = own.shape
    tokens = pl.BlockSpec((cores, 1, tok, width), lambda g: (0, g, 0, 0))
    table = pl.BlockSpec((1, rows, HD), lambda g: (g, 0, 0))
    return pl.pallas_call(
        qkv_back_body,
        grid=(line,),
        out_shape=(
            jax.ShapeDtypeStruct((cores, line, tok, 3 * col), BF),
            jax.ShapeDtypeStruct(x_all.shape, BF),
            jax.ShapeDtypeStruct((1, width), F32),
            jax.ShapeDtypeStruct((1, 3 * col), F32),
        ),
        in_specs=[
            pl.BlockSpec((cores, 1, tok, col), lambda g: (0, g, 0, 0)),
            pl.BlockSpec((2, 1, rows, col), lambda g: (0, g, 0, 0)),
            pl.BlockSpec((came.shape[0], 2, 1, rows, col), lambda g: (0, 0, g, 0, 0)),
            table,
            table,
            full(w_qkv.shape),
            tokens,
        ],
        out_specs=(
            pl.BlockSpec((cores, 1, tok, 3 * col), lambda g: (0, g, 0, 0)),
            tokens,
            full((1, width)),
            full((1, 3 * col)),
        ),
        compiler_params=local_params(),
        cost_estimate=cost(),
    )(d_query, own, came, cos, sin, w_qkv, x_all)


def ahead_body(
    partial_ref, x_ref, gain_ref, gu_ref, sd_ref, resid_ref, all_ref, wgu_ref, wsd_ref, *rest
):
    dp, cx, _, _ = places()
    greet(line_peers() + [moved(core=1)] + plane_peers())
    bufs, sems = rest[:4], rest[4:]
    normed_ref = sems[-1]
    collect = Collect(partial_ref, *bufs, sems[0:5])
    collect.start()
    local = sems[5]
    keep = [
        pltpu.make_async_copy(gu_ref, wgu_ref.at[dp, cx], local.at[0]),
        pltpu.make_async_copy(sd_ref, wsd_ref.at[dp, cx], local.at[1]),
    ]
    for copy in keep:
        copy.start()
    for copy in keep:
        copy.wait()
    gu = Plane(wgu_ref, sems[6:8])
    sd = Plane(wsd_ref, sems[8:10])
    gu.start()
    sd.start()
    total = collect.reduce()
    resid = x_ref[...].astype(F32) + total
    resid_ref[...] = resid
    normal, _ = rms_parts(resid)
    normed_ref[...] = (normal * gain_ref[...]).astype(BF)
    spread = Spread(normed_ref, all_ref, sems[10:14])
    spread.start()
    gu.forward()
    sd.forward()
    spread.forward()
    collect.finish()
    spread.finish()
    gu.finish()
    sd.finish()


def ahead(partial, x_own, gain, gu, sd):
    n_dp, n_cx, line = (lax.axis_size(axis) for axis in ("dp", "cx", "exp"))
    tok, width = x_own.shape
    return pl.pallas_call(
        ahead_body,
        out_shape=(
            jax.ShapeDtypeStruct((tok, width), F32),
            jax.ShapeDtypeStruct((CORES, line, tok, width), BF),
            jax.ShapeDtypeStruct((n_dp, n_cx) + gu.shape, BF),
            jax.ShapeDtypeStruct((n_dp, n_cx) + sd.shape, BF),
        ),
        in_specs=[ANY, VMEM, VMEM, ANY, ANY],
        out_specs=(VMEM, ANY, ANY, ANY),
        scratch_shapes=Collect.scratch(line, tok, width)
        + [pltpu.SemaphoreType.DMA((2,))]
        + Plane.scratch(n_dp, n_cx)
        + Plane.scratch(n_dp, n_cx)
        + Spread.scratch(line)
        + [pltpu.VMEM((tok, width), BF)],
        compiler_params=params(2),
        cost_estimate=cost(),
    )(partial, x_own, gain, gu, sd)


def back_body(
    partial_ref,
    resid_ref,
    gain_ref,
    cot_ref,
    ggu_ref,
    gsd_ref,
    dots_ref,
    router_ref,
    score_ref,
    small_ref,
    dn_ref,
    dr_ref,
    all_ref,
    gu_ref,
    sd_ref,
    logits_ref,
    dscore_ref,
    *rest,
):
    greet(tp_peers() + plane_peers())
    bufs, sems = rest[:4], rest[4:]
    collect = Collect(partial_ref, *bufs, sems[0:5])
    collect.start()
    proj_ref = sems[9]
    gu = PlaneSum(ggu_ref, gu_ref, sems[10:28])
    sd = PlaneSum(gsd_ref, sd_ref, sems[28:46])
    dot_send, dot_recv, came_ref, keep_sem = sems[46:50]
    line = lax.axis_size("exp")
    keep = pltpu.make_async_copy(dots_ref.at[0, 0], came_ref.at[0, 0], keep_sem)
    keep.start()
    outs = [
        copy_to(
            dots_ref.at[c, k],
            came_ref.at[c, k],
            dot_send.at[c, k],
            dot_recv.at[c, k],
            moved(core=c, exp=k),
        )
        for c in range(CORES)
        for k in range(line)
        if c or k
    ]
    gu.start()
    sd.start()
    collect.send()
    keep.wait()
    for copy in outs:
        copy.wait()
    _, _, core, exp = places()
    n_experts = router_ref.shape[0]
    row = lax.broadcasted_iota(jnp.int32, router_ref.shape, 0)
    d_router = jnp.zeros(router_ref.shape, F32)
    d_score = jnp.zeros(score_ref.shape, F32)
    for c in range(CORES):
        for k in range(line):
            tile = came_ref[c, k]
            source = lax.rem(exp + line - k, line) * CORES + lax.rem(core + CORES - c, CORES)
            d_router = d_router + jnp.where(row == source, tile[0:1], 0.0)
            d_score = d_score + tile[1:2]
    score = score_ref[...]
    d_score = d_score * score * (1.0 - score)
    router = router_ref[...]
    d_logits = (router * (d_router - jnp.sum(router * d_router, 0, keepdims=True))).astype(BF)
    high = d_score.astype(BF)
    mid = (d_score - high.astype(F32)).astype(BF)
    tail = (d_score - high.astype(F32) - mid.astype(F32)).astype(BF)
    logits_ref[...] = d_logits
    dscore_ref[...] = jnp.concatenate([high, mid, tail], 0)
    extra = weight_grad(d_logits, small_ref[0:n_experts])
    for part in (high, mid, tail):
        extra = extra + weight_grad(part, small_ref[n_experts : n_experts + 1])
    normal, inverse = rms_parts(resid_ref[...])
    d_normed = collect.gather() + extra
    dn_ref[...] = d_normed
    d_hat = d_normed * gain_ref[...]
    d_resid = cot_ref[...].astype(F32) + inverse * (
        d_hat - normal * jnp.mean(d_hat * normal, 1, keepdims=True)
    )
    dr_ref[...] = d_resid
    proj_ref[...] = d_resid.astype(BF)
    spread = Spread(proj_ref, all_ref, sems[5:9])
    spread.start()
    spread.forward()
    gu.middle()
    sd.middle()
    collect.finish()
    gu.end()
    sd.end()
    spread.finish()


def back(partial, resid, gain, cot, grad_gu, grad_sd, dots, router, score, small):
    line = lax.axis_size("exp")
    tok, width = resid.shape
    dma = pltpu.SemaphoreType.DMA
    return pl.pallas_call(
        back_body,
        out_shape=(
            jax.ShapeDtypeStruct((tok, width), F32),
            jax.ShapeDtypeStruct((tok, width), F32),
            jax.ShapeDtypeStruct((CORES, line, tok, width), BF),
            jax.ShapeDtypeStruct(grad_gu.shape[2:], BF),
            jax.ShapeDtypeStruct(grad_sd.shape[2:], F32),
            jax.ShapeDtypeStruct(router.shape, BF),
            jax.ShapeDtypeStruct((3, tok), BF),
        ),
        in_specs=[ANY, VMEM, VMEM, VMEM, ANY, ANY, ANY, VMEM, VMEM, VMEM],
        out_specs=(VMEM, VMEM, ANY, VMEM, VMEM, VMEM, VMEM),
        scratch_shapes=Collect.scratch(line, tok, width)
        + Spread.scratch(line)
        + [pltpu.VMEM((tok, width), BF)]
        + PlaneSum.scratch(*grad_gu.shape[3:])
        + PlaneSum.scratch(*grad_sd.shape[3:])
        + [dma((CORES, line)), dma((CORES, line)), pltpu.VMEM(dots.shape, F32), dma],
        compiler_params=params(3),
        cost_estimate=cost(),
    )(partial, resid, gain, cot, grad_gu, grad_sd, dots, router, score, small)


class Rows:
    def __init__(self, block, line):
        self.block, self.rows = block, block.shape[1] // line

    @property
    def at(self):
        return self

    def __getitem__(self, spot):
        core, exp = spot
        start = pl.multiple_of(exp * self.rows, self.rows)
        return self.block.at[core, pl.ds(start, self.rows)]


def last_body(
    partial_ref,
    gq_ref,
    go_ref,
    tot_ref,
    egu_ref,
    ed_ref,
    out_ref,
    q_ref,
    k_ref,
    v_ref,
    wo_ref,
    sum_ref,
    eg_ref,
    eu_ref,
    edown_ref,
    *rest,
):
    dp, cx, core, exp = places()
    line = lax.axis_size("exp")
    greet(all_peers())
    collect = Collect(partial_ref, *rest[:4], rest[4:9])
    qkv_block, tots_ref, cols_ref = rest[9:12]
    qkv = PlaneSum(gq_ref, qkv_block, rest[12:30])
    wo = PlaneSum(go_ref, wo_ref, rest[30:48])
    tot_send, tot_recv, local = rest[48:51]
    columns = Columns(Rows(qkv_block, line), cols_ref, rest[51:54])
    gu_came, d_came, swap_send, swap_recv, store = rest[54:59]
    wide, tall = rest[59:61]
    collect.start()
    rows, down = gu_came.shape[0], d_came.shape[0]
    swaps = [
        copy_to(
            source.at[pl.ds((1 - core) * height, height)],
            target,
            swap_send.at[n],
            swap_recv.at[n],
            moved(core=1),
        )
        for n, (source, target, height) in enumerate(
            ((egu_ref, gu_came, rows), (ed_ref, d_came, down))
        )
    ]
    qkv.start()
    wo.start()
    collect.send()
    keep = pltpu.make_async_copy(
        tot_ref.at[dp, cx, core, exp], tots_ref.at[0, 0, 0, 0], local
    )
    keep.start()
    sizes = [range(lax.axis_size(axis)) for axis in ("dp", "cx", "core", "exp")]
    outs = []
    for steps in itertools.product(*sizes):
        if any(steps):
            target = moved(*steps)
            outs.append(
                copy_to(
                    tot_ref.at[target],
                    tots_ref.at[steps],
                    tot_send.at[steps],
                    tot_recv.at[steps],
                    target,
                )
            )
    qkv.middle()
    qkv.end()
    columns.start()
    wo.middle()
    for copy in swaps:
        copy.wait_recv()
    ffe = wide.shape[3]

    def mine(at):
        piece = egu_ref[pl.ds(pl.multiple_of(core * rows + at.start, 8), at.size)].astype(F32)
        wide[0, core, at] = piece[:, :ffe]
        wide[1, core, at] = piece[:, ffe:]
        piece = gu_came[at].astype(F32)
        wide[0, 1 - core, at] = piece[:, :ffe]
        wide[1, 1 - core, at] = piece[:, ffe:]

    by_chunks(rows, mine)

    def down_rows(at):
        piece = ed_ref[pl.ds(pl.multiple_of(core * down + at.start, 8), at.size)]
        tall[core, at] = piece.astype(F32)
        tall[1 - core, at] = d_came[at].astype(F32)

    by_chunks(down, down_rows)
    stores = [
        pltpu.make_async_copy(wide.at[0], eg_ref, store.at[0]),
        pltpu.make_async_copy(wide.at[1], eu_ref, store.at[1]),
        pltpu.make_async_copy(tall, edown_ref, store.at[2]),
    ]
    for copy in stores:
        copy.start()
    out_ref[...] = collect.gather()
    wo.end()
    keep.wait()
    for copy in outs:
        copy.wait()
    sum_ref[...] = jnp.sum(tots_ref[...].reshape((-1,) + tots_ref.shape[4:]), 0)
    columns.arrive()
    col = cols_ref.shape[3] // 3
    for n, target in enumerate((q_ref, k_ref, v_ref)):
        for c in range(CORES):
            for e in range(line):
                at = (e * CORES + c) * col
                target[:, at : at + col] = cols_ref[c, e, :, n * col : (n + 1) * col].astype(F32)
    columns.finish()
    collect.finish()
    for copy in swaps:
        copy.wait_send()
    for copy in stores:
        copy.wait()


def last(partial, grad_qkv, grad_out, totals, grad_egu, grad_edown):
    n_dp, n_cx, line = (lax.axis_size(axis) for axis in ("dp", "cx", "exp"))
    tok, width = partial.shape[2:]
    dma = pltpu.SemaphoreType.DMA
    shard = grad_qkv.shape[3] // line
    rows, both = grad_egu.shape
    down = grad_edown.shape[0]
    heads = jax.ShapeDtypeStruct((shard, width), F32)
    wide = (CORES, rows // 2, both // 2)
    tall = (CORES, down // 2, width)
    return pl.pallas_call(
        last_body,
        out_shape=(
            jax.ShapeDtypeStruct((tok, width), F32),
            heads,
            heads,
            heads,
            jax.ShapeDtypeStruct(grad_out.shape[2:], F32),
            jax.ShapeDtypeStruct(totals.shape[4:], F32),
            jax.ShapeDtypeStruct(wide, F32),
            jax.ShapeDtypeStruct(wide, F32),
            jax.ShapeDtypeStruct(tall, F32),
        ),
        in_specs=[ANY, ANY, ANY, ANY, VMEM, VMEM],
        out_specs=(VMEM,) * 6 + (ANY,) * 3,
        scratch_shapes=Collect.scratch(line, tok, width)
        + [
            pltpu.VMEM(grad_qkv.shape[2:], BF),
            pltpu.VMEM(totals.shape, F32),
            pltpu.VMEM((CORES, line, shard, grad_qkv.shape[4]), BF),
        ]
        + PlaneSum.scratch(*grad_qkv.shape[3:])
        + PlaneSum.scratch(*grad_out.shape[3:])
        + [dma((n_dp, n_cx, CORES, line)), dma((n_dp, n_cx, CORES, line)), dma]
        + Columns.scratch(line)
        + [
            pltpu.VMEM((rows // 2, both), BF),
            pltpu.VMEM((down // 2, width), BF),
            dma((2,)),
            dma((2,)),
            dma((3,)),
            pltpu.VMEM((2,) + wide, F32),
            pltpu.VMEM(tall, F32),
        ],
        compiler_params=params(4),
        cost_estimate=cost(),
    )(partial, grad_qkv, grad_out, totals, grad_egu, grad_edown)


def on_device(
    tokens,
    cotangent,
    positions,
    lengths,
    routes,
    norm_attn,
    w_query,
    bias_query,
    w_key,
    bias_key,
    w_value,
    bias_value,
    w_output,
    norm_moe,
    w_router,
    w_shared_gate,
    w_shared_up,
    w_shared_down,
    w_shared_score,
    w_expert_gate,
    w_expert_up,
    w_expert_down,
):
    n_dp = lax.axis_size("dp")
    n_cx = lax.axis_size("cx")
    n_exp = lax.axis_size("exp")
    exp_at = lax.axis_index("exp")
    core_at = lax.axis_index("core")
    n_tp = CORES * n_exp
    n_data = n_dp * n_cx
    tok, width = tokens.shape[2:]
    shard = w_query.shape[0]
    block = CORES * n_exp * shard
    col = width // n_tp
    heads = col // HD
    n_experts = w_router.shape[1]
    sub = w_shared_down.shape[0]
    sub_width = n_data * sub
    every = tok * n_tp
    scale = HD ** (-0.5)
    top = routes.shape[3]
    ffe = w_expert_gate.shape[2]

    def by_core(first, second):
        return jnp.where(core_at == 0, first, second)

    x_own = tokens.reshape(tok, width)
    cot_own = cotangent.reshape(tok, width)

    small = jnp.concatenate(
        [
            norm_attn[None],
            norm_moe[None],
            w_shared_score[None],
            bias_query[None],
            bias_key[None],
            bias_value[None],
            w_router.T,
        ]
    ).astype(F32)
    n_small = small.shape[0]
    pack = jnp.concatenate(
        [
            positions.reshape(1, tok),
            routes.reshape(tok, top).T,
            jnp.pad(lengths.reshape(1, -1), ((0, 0), (0, tok - lengths.shape[2]))),
        ]
    ).astype(F32)
    pack = jnp.concatenate([pack, jnp.pad(small, ((0, 0), (0, tok - shard)))])
    pack = jnp.pad(pack, ((0, -pack.shape[0] % 8), (0, 0)))

    def exchange(value):
        return lax.all_to_all(value, ("core", "exp"), split_axis=0, concat_axis=0, tiled=True)

    def head_columns(value):
        parts = value.reshape(shard, n_exp, CORES, col)
        return jnp.transpose(parts, (2, 1, 0, 3))

    qkv_cols = jnp.concatenate(
        [head_columns(w_query), head_columns(w_key), head_columns(w_value)], 3
    )
    x_all, w_qkv, wo_all, packs = load(x_own, qkv_cols, w_output, pack)
    w_egu = lax.all_gather(
        jnp.concatenate([w_expert_gate, w_expert_up], 2), ("dp", "cx", "core"), axis=1, tiled=True
    )
    w_edown = lax.all_gather(w_expert_down, ("dp", "cx", "core"), axis=1, tiled=True)
    w_egu = lax.dynamic_index_in_dim(w_egu, core_at, 0, keepdims=False)
    w_edown = lax.dynamic_index_in_dim(w_edown, core_at, 0, keepdims=False)
    w_qkv = w_qkv.reshape(width, 3 * col)
    gu_cols = split_hidden(w_shared_gate, w_shared_up, n_exp, sub)

    small = packs[:, :, :, :, 2 + top : 2 + top + n_small, :shard]
    small = jnp.moveaxis(small, 4, 0).reshape(n_small, width)
    gain_attn = small[0]
    gain_moe = small[1]
    score_vec = small[2]
    router_full = small[6:].T.astype(BF)
    rank = exp_at * CORES + core_at
    biases = lax.dynamic_slice_in_dim(small[3:6], rank * col, col, 1).reshape(3 * col)

    ints = lax.dynamic_index_in_dim(packs, lax.axis_index("dp"), 0, keepdims=False)
    ints = ints[:, :, :, : 2 + top]
    for dim, axis in enumerate(("cx", "core", "exp")):
        ints = roll_to_relative(ints, axis, dim)
    ints = ints.astype(jnp.int32)
    route_tok = jnp.swapaxes(ints[0, :, :, 1 : 1 + top], 2, 3).reshape(every, top)
    seq_lens = ints[0, 0, :, 1 + top, : lengths.shape[2]]
    seq_ends = jnp.cumsum(seq_lens, 1)
    pos_keys = jnp.moveaxis(ints[:, :, :, 0], 2, 0).reshape(n_exp, n_cx * CORES * tok)
    after_end = (pos_keys[:, :, None] >= seq_ends[:, None, :]).astype(jnp.int32)
    seg_keys = jnp.sum(after_end, 2)
    rel_keys = pos_keys - jnp.sum(after_end * seq_lens[:, None, :], 2)
    own_keys = CORES * tok
    code_keys = (seg_keys * 4096 + pos_keys)[:, None, :]
    low = (seg_keys[:, :own_keys] * 4096)[:, :, None]
    codes = (low + pos_keys[:, :own_keys, None], low, code_keys)
    freq = ROTARY_BASE ** (-(jnp.arange(HD // 2, dtype=F32) * 2.0 / HD))
    angle = rel_keys[:, :own_keys].astype(F32)[:, :, None] * freq
    cos_table = jnp.cos(angle)
    sin_table = jnp.sin(angle)
    cos_table = jnp.concatenate([cos_table, cos_table], 2)
    sin_table = jnp.concatenate([-sin_table, sin_table], 2)

    normed_one, query, kv = project_qkv(x_all, w_qkv, gain_attn, biases, cos_table, sin_table)
    normed_one = normed_one.reshape(every, width)
    kv_all, gu_block, w_out = keys_call(kv, gu_cols, wo_all)
    w_out = w_out.reshape(col, width)
    attn_low, partial = attend(query, kv_all, codes, w_out)
    resid, normed_two, w_sgu, w_sdown = ahead(
        partial,
        x_own,
        gain_moe[None],
        gu_block,
        w_shared_down.reshape(2, sub // 2, width),
    )
    cot_own, normed_two = lax.optimization_barrier((cot_own, normed_two))
    cot_tok = spread(cot_own)
    normed_two = normed_two.reshape(every, width)
    normed_two_own = normed_two[:tok]
    w_sgu = w_sgu.reshape(width, 2 * sub_width)
    w_sdown = w_sdown.reshape(sub_width, width)

    small_cols = jnp.concatenate([router_full, score_vec.astype(BF)[:, None]], 1)
    small_out = project(normed_two, small_cols)
    router_all = jax.nn.softmax(small_out[:, :n_experts], axis=-1)
    score_all = jax.nn.sigmoid(small_out[:, n_experts])
    chosen = jnp.any(route_tok == rank, axis=1)
    at_rank = (jnp.arange(n_experts) == rank).astype(F32)
    gate = jnp.where(chosen, jnp.sum(router_all * at_rank[None, :], 1), 0.0)

    shared_pre = project(normed_two, w_sgu)
    s_gate = shared_pre[:, :sub_width]
    s_up = shared_pre[:, sub_width:]
    s_act, s_slope = silu_parts(s_gate)
    s_hidden = (s_act * s_up).astype(BF)
    shared = project(s_hidden, w_sdown)
    normed_late, shared = lax.optimization_barrier((normed_two, shared))
    expert_pre = project(normed_late, w_egu)
    cot_tok, expert_pre = lax.optimization_barrier((cot_tok, expert_pre))
    cot_all = cot_tok.reshape(every, width).astype(F32)
    e_gate = expert_pre[:, :ffe]
    e_up = expert_pre[:, ffe:]
    e_act, e_slope = silu_parts(e_gate)
    e_hidden = (e_act * e_up).astype(BF)
    e_out = project(e_hidden, w_edown).astype(BF).astype(F32)
    mix = (score_all[:, None] * shared + gate[:, None] * e_out).astype(BF)
    dots = jnp.stack(
        [
            jnp.where(chosen, jnp.sum(cot_all * e_out, 1), 0.0),
            jnp.sum(cot_all * shared, 1),
        ]
    )

    mix, gate = lax.optimization_barrier((mix, gate))
    d_eout = (gate[:, None] * cot_all).astype(BF)
    d_eh = project_t(d_eout, w_edown)
    d_egu = jnp.concatenate(
        [(d_eh * e_up * e_slope).astype(BF), (d_eh * e_act).astype(BF)], 1
    )
    grad_egu = weight_grad(normed_two, d_egu).astype(BF)
    grad_edown = weight_grad(e_hidden, d_eout).astype(BF)
    score_back, grad_egu, grad_edown = lax.optimization_barrier((score_all, grad_egu, grad_edown))
    grad_egu = lax.psum_scatter(grad_egu, ("dp", "cx"), scatter_dimension=0, tiled=True)
    grad_edown = lax.psum_scatter(grad_edown, ("dp", "cx"), scatter_dimension=0, tiled=True)
    d_shared = (score_back[:, None] * cot_all).astype(BF)
    d_sh = project_t(d_shared, w_sdown)
    d_sgu = jnp.concatenate(
        [(d_sh * s_up * s_slope).astype(BF), (d_sh * s_act).astype(BF)], 1
    )
    partial_two = (project_t(d_sgu, w_sgu) + project_t(d_egu, w_egu)).astype(BF)
    grad_sdown = weight_grad(s_hidden, d_shared).astype(BF)
    grad_sgu = weight_grad(normed_two, d_sgu).astype(BF)
    mixed = (resid + collect(mix.reshape(CORES, n_exp, tok, width))).astype(BF)
    mixed, partial_two = lax.optimization_barrier((mixed, partial_two))

    dots = jnp.pad(dots.reshape(2, n_tp, tok).swapaxes(0, 1), ((0, 0), (0, 6), (0, 0)))
    d_normed_two, d_resid, d_proj, grad_sgu, grad_sdown, d_logits, d_score = back(
        partial_two.reshape(CORES, n_exp, tok, width),
        resid,
        gain_moe[None],
        cot_own,
        grad_sgu.reshape(n_dp, n_cx, 2, -1, 2 * sub_width),
        grad_sdown.reshape(n_dp, n_cx, 2, -1, width),
        dots.reshape(CORES, n_exp, 8, tok),
        router_all[:tok].T,
        score_all[None, :tok],
        jnp.concatenate([router_full.T, score_vec.astype(BF)[None]]),
    )
    grad_router = project(d_logits, normed_two_own)
    grad_score = project(d_score, normed_two_own).sum(0)
    grad_gain_moe = jnp.sum(d_normed_two * rms_parts(resid)[0], 0)

    grad_sdown = grad_sdown.reshape(sub, width)
    grad_sgu = exchange(grad_sgu.reshape(n_tp, shard, 2 * sub_width))
    grad_sgu = grad_sgu.reshape(CORES, n_exp, shard, 2 * sub_width)

    d_query, d_kv = attend_back(query, kv_all, codes, w_out, d_proj, cos_table, sin_table)
    came = jnp.stack([push(d_kv[k], "cx", k) for k in range(1, n_cx)])
    came, grad_sgu = lax.optimization_barrier((came, grad_sgu))
    d_qkv, partial_one, grad_gain_attn, grad_bias = qkv_back(
        d_query, d_kv[0], came, cos_table, sin_table, w_qkv, x_all
    )
    grad_qkv = weight_grad(normed_one, d_qkv.reshape(every, 3 * col)).astype(BF)
    grad_out = lax.all_to_all(
        weight_grad(attn_low.reshape(every, col), d_proj.reshape(every, width))
        .astype(BF)
        .reshape(n_exp, shard, width),
        "exp",
        split_axis=0,
        concat_axis=0,
        tiled=True,
    )
    grad_bias = lax.dynamic_update_slice_in_dim(
        jnp.zeros((3, width), F32), grad_bias.reshape(3, col), rank * col, 1
    )
    totals = jnp.concatenate(
        [
            grad_gain_attn,
            grad_gain_moe[None],
            grad_score[None],
            grad_bias,
            grad_router,
        ]
    )
    totals = jnp.moveaxis(totals.reshape(n_small, n_data * n_tp, shard), 0, 1)
    totals = totals.reshape(n_data * n_tp, -1)
    totals = jnp.pad(totals, ((0, 0), (0, -totals.shape[1] % 1024)))
    grad_sgate, grad_sup = merge_hidden(grad_sgu, sub)
    partial_one, grad_sgate, grad_sup = lax.optimization_barrier(
        (partial_one, grad_sgate, grad_sup)
    )
    (
        d_normed_one,
        grad_query,
        grad_key,
        grad_value,
        grad_out,
        totals,
        grad_egate,
        grad_eup,
        grad_edown,
    ) = last(
        partial_one,
        grad_qkv.reshape(n_dp, n_cx, 2, -1, 3 * col),
        grad_out.reshape(n_dp, n_cx, 2, shard // 2, width),
        totals.reshape(n_dp, n_cx, CORES, n_exp, -1, 128),
        grad_egu,
        grad_edown,
    )
    grad_out = grad_out.reshape(shard, width)
    totals = totals.reshape(-1)[: n_small * shard].reshape(n_small, shard)
    normal_own, inverse_own = rms_parts(x_own.astype(F32))
    d_hat_one = d_normed_one * gain_attn
    from_attn = inverse_own * (
        d_hat_one - normal_own * jnp.mean(d_hat_one * normal_own, 1, keepdims=True)
    )
    grad_tokens = (d_resid + from_attn).astype(BF)

    return (
        mixed.reshape(tokens.shape),
        grad_tokens.reshape(tokens.shape),
        totals[0],
        grad_query,
        totals[3],
        grad_key,
        totals[4],
        grad_value,
        totals[5],
        grad_out,
        totals[1],
        totals[6:].T,
        grad_sgate,
        grad_sup,
        grad_sdown,
        totals[2],
        grad_egate,
        grad_eup,
        grad_edown,
    )


def solution(mesh):
    sizes = dict(mesh.shape)
    fine = Mesh(
        mesh.devices.reshape(sizes["dp"], sizes["ctx"] // CORES, CORES, sizes["exp"]),
        ("dp", "cx", "core", "exp"),
    )
    own = P("dp", "exp", ("cx", "core"), None)
    flat = P(("dp", "cx", "core", "exp"))
    rows = P(("dp", "cx", "core", "exp"), None)
    expert = P("exp", ("dp", "cx", "core"), None)
    placed = (
        own,
        own,
        P("dp", "exp", ("cx", "core")),
        P("dp", "exp", None),
        own,
        flat,
        rows,
        flat,
        rows,
        flat,
        rows,
        flat,
        rows,
        flat,
        rows,
        rows,
        rows,
        rows,
        flat,
        expert,
        expert,
        expert,
    )
    return jax.shard_map(
        on_device,
        mesh=fine,
        in_specs=placed,
        out_specs=(
            own,
            own,
            flat,
            rows,
            flat,
            rows,
            flat,
            rows,
            flat,
            rows,
            flat,
            rows,
            rows,
            rows,
            rows,
            flat,
            expert,
            expert,
            expert,
        ),
        check_vma=False,
    )
```

```python
import itertools

import jax
import jax.numpy as jnp
from jax import lax
from jax.experimental import pallas as pl
from jax.experimental.pallas import tpu as pltpu
from jax.sharding import Mesh
from jax.sharding import PartitionSpec as P

HD = 128
CORES = 2
EPSILON = 1e-06
ROTARY_BASE = 1000000.0
NEGATIVE = -1e30
BF = jnp.bfloat16
F32 = jnp.float32


def project(left, right):
    return jnp.dot(left, right, preferred_element_type=F32)


def project_t(left, right):
    return lax.dot_general(left, right, (((1,), (1,)), ((), ())), preferred_element_type=F32)


def weight_grad(left, right):
    return lax.dot_general(left, right, (((0,), (0,)), ((), ())), preferred_element_type=F32)


def rms_parts(value):
    inverse = lax.rsqrt(jnp.mean(value * value, axis=-1, keepdims=True) + EPSILON)
    return (value * inverse, inverse)


def silu_parts(value):
    sigmoid = jax.nn.sigmoid(value)
    return (value * sigmoid, sigmoid * (1.0 + value * (1.0 - sigmoid)))


def fetch(value, axis, step):
    size = lax.axis_size(axis)
    if step % size == 0:
        return value
    return lax.ppermute(value, axis, [((i + step) % size, i) for i in range(size)])


def push(value, axis, step):
    size = lax.axis_size(axis)
    return lax.ppermute(value, axis, [(i, (i + step) % size) for i in range(size)])


def roll_to_relative(value, axis, dim):
    size = lax.axis_size(axis)
    both = lax.concatenate([value, value], dim)
    return lax.dynamic_slice_in_dim(both, lax.axis_index(axis), size, dim)


MESH = pl.DeviceIdType.MESH
ANY = pl.BlockSpec(memory_space=pltpu.HBM)
VMEM = pl.BlockSpec(memory_space=pltpu.VMEM)


def places():
    return tuple(lax.axis_index(axis) for axis in ("dp", "cx", "core", "exp"))


def moved(dp=0, cx=0, core=0, exp=0):
    steps = (dp, cx, core, exp)
    return tuple(
        at if step == 0 else lax.rem(at + step, lax.axis_size(axis))
        for at, step, axis in zip(places(), steps, ("dp", "cx", "core", "exp"))
    )


def copy_to(source, target, send_sem, recv_sem, device):
    copy = pltpu.make_async_remote_copy(
        src_ref=source,
        dst_ref=target,
        send_sem=send_sem,
        recv_sem=recv_sem,
        device_id=device,
        device_id_type=MESH,
    )
    copy.start()
    return copy


def greet(devices):
    barrier = pltpu.get_barrier_semaphore()
    for device in devices:
        pl.semaphore_signal(barrier, inc=1, device_id=device, device_id_type=MESH)
    pl.semaphore_wait(barrier, len(devices))


def line_peers():
    return [moved(exp=k) for k in range(1, lax.axis_size("exp"))]


def plane_peers():
    steps = [(j, k) for j in range(lax.axis_size("dp")) for k in range(lax.axis_size("cx"))]
    return [moved(dp=j, cx=k) for j, k in steps[1:]]


class Spread:
    def __init__(self, source, out, sems):
        self.source, self.out = source, out
        self.up, self.down, self.over, self.local = sems
        self.line = lax.axis_size("exp")
        self.at = lax.axis_index("exp")

    def hop(self, step, way):
        slot = (self.line - step) % self.line if way > 0 else step
        landing = self.line - step - 1 if way > 0 else step + 1
        sems = self.up if way > 0 else self.down
        return pltpu.make_async_remote_copy(
            src_ref=self.source if step == 0 else self.out.at[0, slot],
            dst_ref=self.out.at[0, landing],
            send_sem=sems.at[0, step],
            recv_sem=sems.at[1, step + 1],
            device_id=moved(exp=1 if way > 0 else self.line - 1),
            device_id_type=MESH,
        )

    def sends(self, step, way):
        if way > 0:
            return jnp.logical_and(self.at >= step, self.at < self.line - 1)
        return jnp.logical_and(self.at + step <= self.line - 1, self.at > 0)

    def gets(self, step, way):
        return self.at >= step if way > 0 else self.at + step <= self.line - 1

    def across(self, slot):
        return pltpu.make_async_remote_copy(
            src_ref=self.source if slot == 0 else self.out.at[0, slot],
            dst_ref=self.out.at[1, slot],
            send_sem=self.over.at[0, slot],
            recv_sem=self.over.at[1, slot],
            device_id=moved(core=1),
            device_id_type=MESH,
        )

    def start(self):
        self.keep = pltpu.make_async_copy(self.source, self.out.at[0, 0], self.local)
        self.keep.start()
        for way in (1, -1):
            pl.when(self.sends(0, way))(self.hop(0, way).start)
        self.across(0).start()

    def forward(self):
        for step in range(1, self.line):
            for way in (1, -1):
                slot = self.line - step if way > 0 else step

                @pl.when(self.gets(step, way))
                def _():
                    self.hop(step - 1, way).wait_recv()
                    self.across(slot).start()

                if step < self.line - 1:
                    pl.when(self.sends(step, way))(self.hop(step, way).start)

    def finish(self):
        self.keep.wait()
        for step in range(self.line - 1):
            for way in (1, -1):
                pl.when(self.sends(step, way))(self.hop(step, way).wait_send)
        for slot in range(self.line):
            self.across(slot).wait()

    @staticmethod
    def scratch(line):
        return [
            pltpu.SemaphoreType.DMA((2, line)),
            pltpu.SemaphoreType.DMA((2, line)),
            pltpu.SemaphoreType.DMA((2, line)),
            pltpu.SemaphoreType.DMA,
        ]


class Columns:
    def __init__(self, cols, out, sems):
        self.cols, self.out, self.sems = cols, out, sems

    def start(self):
        send, recv, local = self.sems
        line = lax.axis_size("exp")
        _, _, core, exp = places()
        self.local = pltpu.make_async_copy(
            self.cols.at[core, exp], self.out.at[core, exp], local
        )
        self.local.start()
        self.copies = []
        for c in range(CORES):
            for k in range(line):
                if c or k:
                    target = moved(core=c, exp=k)
                    self.copies.append(
                        copy_to(
                            self.cols.at[target[2], target[3]],
                            self.out.at[core, exp],
                            send.at[c, k],
                            recv.at[c, k],
                            target,
                        )
                    )

    def arrive(self):
        self.local.wait()
        for copy in self.copies:
            copy.wait_recv()

    def finish(self):
        for copy in self.copies:
            copy.wait_send()

    @staticmethod
    def scratch(line):
        return [
            pltpu.SemaphoreType.DMA((CORES, line)),
            pltpu.SemaphoreType.DMA((CORES, line)),
            pltpu.SemaphoreType.DMA,
        ]


class Plane:
    def __init__(self, out, sems):
        self.out, self.sems = out, sems
        self.n = (lax.axis_size("dp"), lax.axis_size("cx"))

    def send(self, half, j, k, dp, cx):
        send, recv = self.sems
        at = places()
        n_dp, n_cx = self.n
        from_dp = lax.rem(at[0] + n_dp - j, n_dp)
        from_cx = lax.rem(at[1] + n_cx - k, n_cx)
        block = self.out.at[from_dp, from_cx, half]
        a, b = j + dp, k + cx
        return copy_to(
            block, block, send.at[half, a, b], recv.at[half, a, b], moved(dp=dp, cx=cx)
        )

    def start(self):
        n_dp, n_cx = self.n
        self.along_cx = [[self.send(h, 0, 0, 0, k) for k in range(1, n_cx)] for h in range(2)]
        self.along_dp = [[self.send(h, 0, 0, j, 0) for j in range(1, n_dp)] for h in range(2)]

    def forward(self):
        n_dp, n_cx = self.n
        self.rest = []
        for k in range(1, n_cx):
            self.along_cx[0][k - 1].wait_recv()
            for j in range(1, n_dp):
                self.rest.append(self.send(0, 0, k, j, 0))
        for j in range(1, n_dp):
            self.along_dp[1][j - 1].wait_recv()
            for k in range(1, n_cx):
                self.rest.append(self.send(1, j, 0, 0, k))

    def finish(self):
        for copy in self.along_cx[1] + self.along_dp[0] + self.rest:
            copy.wait()
        for copy in self.along_cx[0] + self.along_dp[1]:
            copy.wait_send()

    @staticmethod
    def scratch(n_dp, n_cx):
        return [
            pltpu.SemaphoreType.DMA((2, n_dp, n_cx)),
            pltpu.SemaphoreType.DMA((2, n_dp, n_cx)),
        ]


def params(number):
    mebibytes = 24 + 4 * lax.axis_size("exp")
    return pltpu.CompilerParams(
        collective_id=number, has_side_effects=True, vmem_limit_bytes=mebibytes * 2**20
    )


def cost():
    return pl.CostEstimate(flops=1, bytes_accessed=1, transcendentals=0)


def tp_peers():
    line = lax.axis_size("exp")
    steps = [(c, k) for c in range(CORES) for k in range(line)]
    return [moved(core=c, exp=k) for c, k in steps[1:]]


def all_peers():
    sizes = [range(lax.axis_size(axis)) for axis in ("dp", "cx", "core", "exp")]
    return [moved(*steps) for steps in itertools.product(*sizes) if any(steps)]


def load_body(
    x_ref,
    cols_ref,
    wo_ref,
    pack_ref,
    cot_ref,
    xall_ref,
    wqkv_ref,
    woall_ref,
    packs_ref,
    cotall_ref,
    *sems,
):
    dp, cx, core, exp = places()
    greet(all_peers())
    tokens = Spread(x_ref, xall_ref, sems[0:4])
    block = wqkv_ref.at[dp, cx]
    columns = Columns(cols_ref, block, sems[4:7])
    plane = Plane(wqkv_ref, sems[7:9])
    send, recv, local = sems[9:12]
    columns.start()
    own = [
        pltpu.make_async_copy(wo_ref, woall_ref.at[dp, cx], local.at[0]),
        pltpu.make_async_copy(pack_ref, packs_ref.at[dp, cx, core, exp], local.at[1]),
    ]
    for copy in own:
        copy.start()
    pack_send, pack_recv = sems[12:14]
    sizes = [range(lax.axis_size(axis)) for axis in ("dp", "cx", "core", "exp")]
    outs = [
        copy_to(
            pack_ref,
            packs_ref.at[dp, cx, core, exp],
            pack_send.at[steps],
            pack_recv.at[steps],
            moved(*steps),
        )
        for steps in itertools.product(*sizes)
        if any(steps)
    ]
    cotangent = Spread(cot_ref, cotall_ref, sems[14:18])
    columns.arrive()
    tokens.start()
    plane.start()
    tokens.forward()
    cotangent.start()
    plane.forward()
    for j in range(lax.axis_size("dp")):
        for k in range(lax.axis_size("cx")):
            if j or k:
                outs.append(
                    copy_to(
                        wo_ref,
                        woall_ref.at[dp, cx],
                        send.at[j, k],
                        recv.at[j, k],
                        moved(dp=j, cx=k),
                    )
                )
    cotangent.forward()
    columns.finish()
    tokens.finish()
    plane.finish()
    cotangent.finish()
    for copy in own + outs:
        copy.wait()


def load(x_own, cols, w_output, pack, cot_own):
    n_dp, n_cx, line = (lax.axis_size(axis) for axis in ("dp", "cx", "exp"))
    return pl.pallas_call(
        load_body,
        out_shape=(
            jax.ShapeDtypeStruct((CORES, line) + x_own.shape, BF),
            jax.ShapeDtypeStruct((n_dp, n_cx) + cols.shape, BF),
            jax.ShapeDtypeStruct((n_dp, n_cx) + w_output.shape, BF),
            jax.ShapeDtypeStruct((n_dp, n_cx, CORES, line) + pack.shape, F32),
            jax.ShapeDtypeStruct((CORES, line) + cot_own.shape, BF),
        ),
        in_specs=[ANY] * 5,
        out_specs=(ANY,) * 5,
        scratch_shapes=Spread.scratch(line)
        + Columns.scratch(line)
        + Plane.scratch(n_dp, n_cx)
        + [
            pltpu.SemaphoreType.DMA((n_dp, n_cx)),
            pltpu.SemaphoreType.DMA((n_dp, n_cx)),
            pltpu.SemaphoreType.DMA((2,)),
            pltpu.SemaphoreType.DMA((n_dp, n_cx, CORES, line)),
            pltpu.SemaphoreType.DMA((n_dp, n_cx, CORES, line)),
        ]
        + Spread.scratch(line),
        compiler_params=params(0),
        cost_estimate=cost(),
    )(x_own, cols, w_output, pack, cot_own)


def keys_body(kv_ref, cols_ref, wo_ref, kvall_ref, gu_ref, wout_ref, *sems):
    _, _, _, exp = places()
    n_cx = lax.axis_size("cx")
    line = lax.axis_size("exp")
    greet(tp_peers() + [moved(cx=k) for k in range(1, n_cx)])
    send, recv, local = sems[3:6]
    own = pltpu.make_async_copy(kv_ref, kvall_ref.at[0], local)
    own.start()
    keys = [
        copy_to(kv_ref, kvall_ref.at[n_cx - k], send.at[k], recv.at[k], moved(cx=k))
        for k in range(1, n_cx)
    ]
    columns = Columns(cols_ref, gu_ref, sems[0:3])
    columns.start()
    send, recv, local = sems[6:9]
    keep = pltpu.make_async_copy(wo_ref.at[exp // n_cx, exp % n_cx], wout_ref.at[exp], local)
    keep.start()
    outs = []
    for k in range(1, line):
        target = moved(exp=k)
        at = target[3]
        outs.append(
            copy_to(
                wo_ref.at[at // n_cx, at % n_cx],
                wout_ref.at[exp],
                send.at[k],
                recv.at[k],
                target,
            )
        )
    own.wait()
    keep.wait()
    columns.arrive()
    columns.finish()
    for copy in keys + outs:
        copy.wait()


def keys_call(kv, cols, wo_all):
    n_cx, line = lax.axis_size("cx"), lax.axis_size("exp")
    return pl.pallas_call(
        keys_body,
        out_shape=(
            jax.ShapeDtypeStruct((n_cx,) + kv.shape, BF),
            jax.ShapeDtypeStruct(cols.shape, BF),
            jax.ShapeDtypeStruct((line,) + wo_all.shape[2:], BF),
        ),
        in_specs=[ANY] * 3,
        out_specs=(ANY,) * 3,
        scratch_shapes=Columns.scratch(line)
        + [
            pltpu.SemaphoreType.DMA((n_cx,)),
            pltpu.SemaphoreType.DMA((n_cx,)),
            pltpu.SemaphoreType.DMA,
            pltpu.SemaphoreType.DMA((line,)),
            pltpu.SemaphoreType.DMA((line,)),
            pltpu.SemaphoreType.DMA,
        ],
        compiler_params=params(1),
        cost_estimate=cost(),
    )(kv, cols, wo_all)


class Collect:
    def __init__(self, partial, kept, near, half, far, sems):
        self.partial, self.kept, self.near, self.half, self.far = partial, kept, near, half, far
        self.sems = sems
        self.line = lax.axis_size("exp")
        self.order = list(range(1, self.line)) + [0]

    def start(self):
        core_send, core_recv, _, _, local = self.sems
        self.swaps, self.loads = {}, {}
        for k in self.order:
            self.swaps[k] = copy_to(
                self.partial.at[1, k],
                self.near.at[k],
                core_send.at[k],
                core_recv.at[k],
                moved(core=1),
            )
            self.loads[k] = pltpu.make_async_copy(
                self.partial.at[0, k], self.kept.at[k], local.at[k]
            )
            self.loads[k].start()

    def pair(self, k):
        self.loads[k].wait()
        self.swaps[k].wait_recv()
        return self.kept[k].astype(F32) + self.near[k].astype(F32)

    def reduce(self):
        self.send()
        return self.gather()

    def send(self):
        _, _, send, recv, _ = self.sems
        copies = []
        for k in self.order[:-1]:
            self.half[k] = self.pair(k).astype(BF)
            copies.append(
                copy_to(
                    self.half.at[k], self.far.at[k], send.at[k], recv.at[k], moved(exp=k)
                )
            )
        self.copies = copies

    def gather(self):
        total = self.pair(0)
        near = sorted(zip(self.order, self.copies), key=lambda p: min(p[0], self.line - p[0]))
        for k, copy in near:
            copy.wait_recv()
            total = total + self.far[k].astype(F32)
        return total

    def finish(self):
        for k in self.order:
            self.swaps[k].wait_send()
        for copy in self.copies:
            copy.wait_send()

    @staticmethod
    def scratch(line, tok, width):
        buffer = pltpu.VMEM((line, tok, width), BF)
        return [buffer] * 4 + [pltpu.SemaphoreType.DMA((line,))] * 5


def by_chunks(rows, work):
    chunk = 16 if rows % 16 == 0 else 8

    @pl.loop(0, rows // chunk)
    def _(step):
        work(pl.ds(pl.multiple_of(step * chunk, chunk), chunk))


def split_hidden(gate, up, n_exp, piece):
    shard, total = gate.shape
    blocks = total // (CORES * n_exp * piece)

    def body(gate_ref, up_ref, out_ref):
        sides = (gate_ref[...].astype(F32), up_ref[...].astype(F32))
        for c in range(CORES):
            for e in range(n_exp):
                parts = []
                for side in sides:
                    for b in range(blocks):
                        start = ((b * CORES + c) * n_exp + e) * piece
                        parts.append(side[:, start : start + piece])
                out_ref[c, e] = jnp.concatenate(parts, 1).astype(BF)

    return pl.pallas_call(
        body,
        out_shape=jax.ShapeDtypeStruct((CORES, n_exp, shard, 2 * blocks * piece), BF),
        in_specs=[VMEM, VMEM],
        out_specs=VMEM,
        compiler_params=local_params(),
        cost_estimate=cost(),
    )(gate, up)


def merge_hidden(value, piece):
    _, n_exp, shard, both = value.shape
    blocks = both // (2 * piece)
    total = blocks * CORES * n_exp * piece

    def body(in_ref, gate_ref, up_ref):
        for side, out_ref in enumerate((gate_ref, up_ref)):
            parts = []
            for b in range(blocks):
                start = (side * blocks + b) * piece
                for c in range(CORES):
                    for e in range(n_exp):
                        parts.append(in_ref[c, e].astype(F32)[:, start : start + piece])
            out_ref[...] = jnp.concatenate(parts, 1)

    shape = jax.ShapeDtypeStruct((shard, total), F32)
    return pl.pallas_call(
        body,
        out_shape=(shape, shape),
        in_specs=[VMEM],
        out_specs=(VMEM, VMEM),
        compiler_params=local_params(),
        cost_estimate=cost(),
    )(value)


class HalfSum:
    def __init__(self, blocks, half, bufs, sems):
        self.blocks, self.half = blocks, half
        self.own, self.came, self.sums, self.final = bufs
        self.sem = sems
        n_dp, n_cx = lax.axis_size("dp"), lax.axis_size("cx")
        self.cx_first = half == 0
        self.n_in, self.n_out = (n_cx, n_dp) if self.cx_first else (n_dp, n_cx)

    def block(self, inner, outer):
        dp, cx = (outer, inner) if self.cx_first else (inner, outer)
        at = moved(dp=dp, cx=cx)
        return self.blocks.at[at[0], at[1], self.half]

    def far(self, inner, outer):
        dp, cx = (outer, inner) if self.cx_first else (inner, outer)
        return moved(dp=dp, cx=cx)

    def start(self):
        first_send, first_recv, _, _, local = self.sem
        self.first, self.loads = {}, []
        for a in range(self.n_out):
            for b in range(1, self.n_in):
                self.first[b, a] = copy_to(
                    self.block(b, a),
                    self.came.at[b - 1, a],
                    first_send.at[b - 1, a],
                    first_recv.at[b - 1, a],
                    self.far(b, 0),
                )
            load = pltpu.make_async_copy(self.block(0, a), self.own.at[a], local.at[a])
            load.start()
            self.loads.append(load)

    def near(self, a, rows):
        total = self.own[a, rows].astype(F32)
        for b in range(1, self.n_in):
            total = total + self.came[b - 1, a, rows].astype(F32)
        return total

    def middle(self):
        _, _, send, recv, _ = self.sem
        for load in self.loads:
            load.wait()
        self.second = []
        for a in range(1, self.n_out):
            for b in range(1, self.n_in):
                self.first[b, a].wait_recv()

            def work(rows):
                self.sums[a - 1, rows] = self.near(a, rows).astype(BF)

            by_chunks(self.sums.shape[1], work)
            self.second.append(
                copy_to(
                    self.sums.at[a - 1],
                    self.final.at[a - 1],
                    send.at[a - 1],
                    recv.at[a - 1],
                    self.far(0, a),
                )
            )

    def end(self, out):
        for b in range(1, self.n_in):
            self.first[b, 0].wait_recv()
        for copy in self.second:
            copy.wait_recv()

        def work(rows):
            total = self.near(0, rows)
            for a in range(1, self.n_out):
                total = total + self.final[a - 1, rows].astype(F32)
            out[rows] = total.astype(out.dtype)

        by_chunks(self.sums.shape[1], work)
        for copy in self.first.values():
            copy.wait_send()
        for copy in self.second:
            copy.wait_send()

    @staticmethod
    def scratch(half, rows, width):
        n_dp, n_cx = lax.axis_size("dp"), lax.axis_size("cx")
        n_in, n_out = (n_cx, n_dp) if half == 0 else (n_dp, n_cx)
        dma = pltpu.SemaphoreType.DMA
        return (
            [
                pltpu.VMEM((n_out, rows, width), BF),
                pltpu.VMEM((n_in - 1, n_out, rows, width), BF),
                pltpu.VMEM((n_out - 1, rows, width), BF),
                pltpu.VMEM((n_out - 1, rows, width), BF),
            ],
            [
                dma((n_in - 1, n_out)),
                dma((n_in - 1, n_out)),
                dma((n_out - 1,)),
                dma((n_out - 1,)),
                dma((n_out,)),
            ],
        )


class PlaneSum:
    def __init__(self, blocks, out, scratch):
        self.out = out
        self.halves = [
            HalfSum(blocks, h, scratch[9 * h : 9 * h + 4], scratch[9 * h + 4 : 9 * h + 9])
            for h in range(2)
        ]

    def start(self):
        for half in self.halves:
            half.start()

    def middle(self):
        for half in self.halves:
            half.middle()

    def end(self):
        for h, half in enumerate(self.halves):
            half.end(self.out.at[h])

    @staticmethod
    def scratch(rows, width):
        both = [HalfSum.scratch(h, rows, width) for h in range(2)]
        return both[0][0] + both[0][1] + both[1][0] + both[1][1]


def full(shape):
    return pl.BlockSpec(shape, lambda g: (0,) * len(shape))


def turn(value, cos, sin):
    return value * cos + pltpu.roll(value, HD // 2, 1) * sin


def project_qkv_body(x_ref, w_ref, gain_ref, bias_ref, cos_ref, sin_ref, n_ref, q_ref, kv_ref):
    rows = x_ref.shape[0] * x_ref.shape[2]
    width = x_ref.shape[3]
    col = q_ref.shape[2]
    normal, _ = rms_parts(x_ref[...].reshape(rows, width).astype(F32))
    normed = (normal * gain_ref[...]).astype(BF)
    n_ref[...] = normed.reshape(n_ref.shape)
    lin = project(normed, w_ref[...]) + bias_ref[...]
    cos, sin = cos_ref[0], sin_ref[0]
    for h in range(col // HD):
        at = slice(h * HD, (h + 1) * HD)
        q_ref[0, :, at] = turn(lin[:, at], cos, sin).astype(BF)
        head = lin[:, col + h * HD : col + (h + 1) * HD]
        kv_ref[0, 0, :, at] = turn(head, cos, sin).astype(BF)
    kv_ref[1, 0] = lin[:, 2 * col :].astype(BF)


def project_qkv(x_all, w_qkv, gain, bias, cos, sin):
    cores, line, tok, width = x_all.shape
    col = w_qkv.shape[1] // 3
    rows = cores * tok
    tokens = pl.BlockSpec((cores, 1, tok, width), lambda g: (0, g, 0, 0))
    table = pl.BlockSpec((1, rows, HD), lambda g: (g, 0, 0))
    return pl.pallas_call(
        project_qkv_body,
        grid=(line,),
        out_shape=(
            jax.ShapeDtypeStruct(x_all.shape, BF),
            jax.ShapeDtypeStruct((line, rows, col), BF),
            jax.ShapeDtypeStruct((2, line, rows, col), BF),
        ),
        in_specs=[
            tokens,
            full(w_qkv.shape),
            full((1, width)),
            full((1, 3 * col)),
            table,
            table,
        ],
        out_specs=(
            tokens,
            pl.BlockSpec((1, rows, col), lambda g: (g, 0, 0)),
            pl.BlockSpec((2, 1, rows, col), lambda g: (0, g, 0, 0)),
        ),
        compiler_params=local_params(),
        cost_estimate=cost(),
    )(x_all, w_qkv, gain[None], bias[None], cos, sin)


def local_params():
    return pltpu.CompilerParams(vmem_limit_bytes=40 * 2**20)


def head_probs(query, keys, allowed):
    scores = project_t(query, keys) * (HD**-0.5)
    scores = jnp.where(allowed, scores, NEGATIVE)
    weights = jnp.exp(scores - jnp.max(scores, -1, keepdims=True))
    return weights / jnp.sum(weights, -1, keepdims=True)


def key_value(kv_ref, which):
    part = kv_ref[:, which, 0]
    return part.reshape(part.shape[0] * part.shape[1], part.shape[2])


def attend_body(q_ref, kv_ref, high_ref, low_ref, code_ref, w_ref, attn_ref, partial_ref):
    col = q_ref.shape[2]
    keys, values = key_value(kv_ref, 0), key_value(kv_ref, 1)
    allowed = (code_ref[0] <= high_ref[0]) & (code_ref[0] >= low_ref[0])
    outs = []
    for h in range(col // HD):
        at = slice(h * HD, (h + 1) * HD)
        probs = head_probs(q_ref[0, :, at], keys[:, at], allowed).astype(BF)
        outs.append(project(probs, values[:, at]).astype(BF))
    attn = jnp.concatenate(outs, 1) if len(outs) > 1 else outs[0]
    attn_ref[...] = attn.reshape(attn_ref.shape)
    partial_ref[...] = project(attn, w_ref[...]).astype(BF).reshape(partial_ref.shape)


def attention_specs(line, rows, col, n_cx):
    return [
        pl.BlockSpec((1, rows, col), lambda g: (g, 0, 0)),
        pl.BlockSpec((n_cx, 2, 1, rows, col), lambda g: (0, 0, g, 0, 0)),
        pl.BlockSpec((1, rows, 1), lambda g: (g, 0, 0)),
        pl.BlockSpec((1, rows, 1), lambda g: (g, 0, 0)),
        pl.BlockSpec((1, 1, n_cx * rows), lambda g: (g, 0, 0)),
    ]


def attend(query, kv, codes, w_out):
    line, rows, col = query.shape
    tok, width = rows // CORES, w_out.shape[1]
    return pl.pallas_call(
        attend_body,
        grid=(line,),
        out_shape=(
            jax.ShapeDtypeStruct((CORES, line, tok, col), BF),
            jax.ShapeDtypeStruct((CORES, line, tok, width), BF),
        ),
        in_specs=attention_specs(line, rows, col, kv.shape[0]) + [full(w_out.shape)],
        out_specs=(
            pl.BlockSpec((CORES, 1, tok, col), lambda g: (0, g, 0, 0)),
            pl.BlockSpec((CORES, 1, tok, width), lambda g: (0, g, 0, 0)),
        ),
        compiler_params=local_params(),
        cost_estimate=cost(),
    )(query, kv, *codes, w_out)


def attend_back_body(
    q_ref, kv_ref, high_ref, low_ref, code_ref, w_ref, dp_ref, cos_ref, sin_ref, dq_ref, dkv_ref
):
    col = q_ref.shape[2]
    rows = q_ref.shape[1]
    keys, values = key_value(kv_ref, 0), key_value(kv_ref, 1)
    allowed = (code_ref[0] <= high_ref[0]) & (code_ref[0] >= low_ref[0])
    d_proj = dp_ref[...].reshape(rows, dp_ref.shape[3])
    d_attn = project_t(d_proj, w_ref[...]).astype(BF)
    scale = HD**-0.5
    cos, sin = cos_ref[0], sin_ref[0]
    for h in range(col // HD):
        at = slice(h * HD, (h + 1) * HD)
        query = q_ref[0, :, at]
        weights = head_probs(query, keys[:, at], allowed)
        probs = weights.astype(BF)
        d_probs = project_t(d_attn[:, at], values[:, at])
        delta = jnp.sum(probs.astype(F32) * d_probs, -1, keepdims=True)
        d_scores = (weights * (d_probs - delta)).astype(BF)
        d_query = project(d_scores, keys[:, at]) * scale
        d_key = weight_grad(d_scores, query) * scale
        d_value = weight_grad(probs, d_attn[:, at])
        dq_ref[:, :, :, at] = (
            turn(d_query, cos, -sin).astype(BF).reshape(dq_ref.shape[:3] + (HD,))
        )
        shape = (dkv_ref.shape[0], rows, HD)
        dkv_ref[:, 0, 0, :, at] = d_key.astype(BF).reshape(shape)
        dkv_ref[:, 1, 0, :, at] = d_value.astype(BF).reshape(shape)


def attend_back(query, kv, codes, w_out, d_proj, cos, sin):
    line, rows, col = query.shape
    tok, width = rows // CORES, w_out.shape[1]
    table = pl.BlockSpec((1, rows, HD), lambda g: (g, 0, 0))
    specs = attention_specs(line, rows, col, kv.shape[0])
    return pl.pallas_call(
        attend_back_body,
        grid=(line,),
        out_shape=(
            jax.ShapeDtypeStruct((CORES, line, tok, col), BF),
            jax.ShapeDtypeStruct(kv.shape, BF),
        ),
        in_specs=specs
        + [
            full(w_out.shape),
            pl.BlockSpec((CORES, 1, tok, width), lambda g: (0, g, 0, 0)),
            table,
            table,
        ],
        out_specs=(pl.BlockSpec((CORES, 1, tok, col), lambda g: (0, g, 0, 0)), specs[1]),
        compiler_params=local_params(),
        cost_estimate=cost(),
    )(query, kv, *codes, w_out, d_proj, cos, sin)


def qkv_back_body(
    dq_ref, own_ref, came_ref, cos_ref, sin_ref, w_ref, x_ref, d_ref, partial_ref, gain_ref, bias_ref
):
    rows = own_ref.shape[2]
    col = own_ref.shape[3]
    cos, sin = cos_ref[0], sin_ref[0]
    d_key, d_value = own_ref[0, 0].astype(F32), own_ref[1, 0].astype(F32)
    for k in range(came_ref.shape[0]):
        d_key = d_key + came_ref[k, 0, 0].astype(F32)
        d_value = d_value + came_ref[k, 1, 0].astype(F32)
    keys = [
        turn(d_key[:, h * HD : (h + 1) * HD], cos, -sin).astype(BF) for h in range(col // HD)
    ]
    d_lin = jnp.concatenate([dq_ref[...].reshape(rows, col)] + keys + [d_value.astype(BF)], 1)
    d_ref[...] = d_lin.reshape(d_ref.shape)
    partial = project_t(d_lin, w_ref[...])
    partial_ref[...] = partial.astype(BF).reshape(partial_ref.shape)
    normal, _ = rms_parts(x_ref[...].reshape(rows, x_ref.shape[3]).astype(F32))
    gain = jnp.sum(partial * normal, 0, keepdims=True)
    bias = jnp.sum(d_lin.astype(F32), 0, keepdims=True)

    @pl.when(pl.program_id(0) == 0)
    def _():
        gain_ref[...] = jnp.zeros_like(gain_ref)
        bias_ref[...] = jnp.zeros_like(bias_ref)

    gain_ref[...] += gain
    bias_ref[...] += bias


def qkv_back(d_query, own, came, cos, sin, w_qkv, x_all):
    cores, line, tok, width = x_all.shape
    _, _, rows, col = own.shape
    tokens = pl.BlockSpec((cores, 1, tok, width), lambda g: (0, g, 0, 0))
    table = pl.BlockSpec((1, rows, HD), lambda g: (g, 0, 0))
    return pl.pallas_call(
        qkv_back_body,
        grid=(line,),
        out_shape=(
            jax.ShapeDtypeStruct((cores, line, tok, 3 * col), BF),
            jax.ShapeDtypeStruct(x_all.shape, BF),
            jax.ShapeDtypeStruct((1, width), F32),
            jax.ShapeDtypeStruct((1, 3 * col), F32),
        ),
        in_specs=[
            pl.BlockSpec((cores, 1, tok, col), lambda g: (0, g, 0, 0)),
            pl.BlockSpec((2, 1, rows, col), lambda g: (0, g, 0, 0)),
            pl.BlockSpec((came.shape[0], 2, 1, rows, col), lambda g: (0, 0, g, 0, 0)),
            table,
            table,
            full(w_qkv.shape),
            tokens,
        ],
        out_specs=(
            pl.BlockSpec((cores, 1, tok, 3 * col), lambda g: (0, g, 0, 0)),
            tokens,
            full((1, width)),
            full((1, 3 * col)),
        ),
        compiler_params=local_params(),
        cost_estimate=cost(),
    )(d_query, own, came, cos, sin, w_qkv, x_all)


def ahead_body(
    partial_ref, x_ref, gain_ref, gu_ref, sd_ref, resid_ref, all_ref, wgu_ref, wsd_ref, *rest
):
    dp, cx, _, _ = places()
    greet(line_peers() + [moved(core=1)] + plane_peers())
    bufs, sems = rest[:4], rest[4:]
    normed_ref = sems[-1]
    collect = Collect(partial_ref, *bufs, sems[0:5])
    collect.start()
    local = sems[5]
    keep = [
        pltpu.make_async_copy(gu_ref, wgu_ref.at[dp, cx], local.at[0]),
        pltpu.make_async_copy(sd_ref, wsd_ref.at[dp, cx], local.at[1]),
    ]
    for copy in keep:
        copy.start()
    for copy in keep:
        copy.wait()
    gu = Plane(wgu_ref, sems[6:8])
    sd = Plane(wsd_ref, sems[8:10])
    gu.start()
    sd.start()
    total = collect.reduce()
    resid = x_ref[...].astype(F32) + total
    resid_ref[...] = resid
    normal, _ = rms_parts(resid)
    normed_ref[...] = (normal * gain_ref[...]).astype(BF)
    spread = Spread(normed_ref, all_ref, sems[10:14])
    spread.start()
    gu.forward()
    sd.forward()
    spread.forward()
    collect.finish()
    spread.finish()
    gu.finish()
    sd.finish()


def ahead(partial, x_own, gain, gu, sd):
    n_dp, n_cx, line = (lax.axis_size(axis) for axis in ("dp", "cx", "exp"))
    tok, width = x_own.shape
    return pl.pallas_call(
        ahead_body,
        out_shape=(
            jax.ShapeDtypeStruct((tok, width), F32),
            jax.ShapeDtypeStruct((CORES, line, tok, width), BF),
            jax.ShapeDtypeStruct((n_dp, n_cx) + gu.shape, BF),
            jax.ShapeDtypeStruct((n_dp, n_cx) + sd.shape, BF),
        ),
        in_specs=[ANY, VMEM, VMEM, ANY, ANY],
        out_specs=(VMEM, ANY, ANY, ANY),
        scratch_shapes=Collect.scratch(line, tok, width)
        + [pltpu.SemaphoreType.DMA((2,))]
        + Plane.scratch(n_dp, n_cx)
        + Plane.scratch(n_dp, n_cx)
        + Spread.scratch(line)
        + [pltpu.VMEM((tok, width), BF)],
        compiler_params=params(2),
        cost_estimate=cost(),
    )(partial, x_own, gain, gu, sd)


def back_body(
    partial_ref,
    resid_ref,
    gain_ref,
    cot_ref,
    ggu_ref,
    gsd_ref,
    dots_ref,
    router_ref,
    score_ref,
    small_ref,
    mix_ref,
    dn_ref,
    dr_ref,
    all_ref,
    gu_ref,
    sd_ref,
    logits_ref,
    dscore_ref,
    mixed_ref,
    *rest,
):
    greet(tp_peers() + plane_peers())
    bufs, sems = rest[:4], rest[4:]
    collect = Collect(partial_ref, *bufs, sems[0:5])
    collect.start()
    mix = Collect(mix_ref, *sems[50:54], sems[54:59])
    proj_ref = sems[9]
    gu = PlaneSum(ggu_ref, gu_ref, sems[10:28])
    sd = PlaneSum(gsd_ref, sd_ref, sems[28:46])
    dot_send, dot_recv, came_ref, keep_sem = sems[46:50]
    line = lax.axis_size("exp")
    keep = pltpu.make_async_copy(dots_ref.at[0, 0], came_ref.at[0, 0], keep_sem)
    keep.start()
    outs = [
        copy_to(
            dots_ref.at[c, k],
            came_ref.at[c, k],
            dot_send.at[c, k],
            dot_recv.at[c, k],
            moved(core=c, exp=k),
        )
        for c in range(CORES)
        for k in range(line)
        if c or k
    ]
    gu.start()
    sd.start()
    collect.send()
    mix.start()
    keep.wait()
    for copy in outs:
        copy.wait()
    _, _, core, exp = places()
    n_experts = router_ref.shape[0]
    row = lax.broadcasted_iota(jnp.int32, router_ref.shape, 0)
    d_router = jnp.zeros(router_ref.shape, F32)
    d_score = jnp.zeros(score_ref.shape, F32)
    for c in range(CORES):
        for k in range(line):
            tile = came_ref[c, k]
            source = lax.rem(exp + line - k, line) * CORES + lax.rem(core + CORES - c, CORES)
            d_router = d_router + jnp.where(row == source, tile[0:1], 0.0)
            d_score = d_score + tile[1:2]
    score = score_ref[...]
    d_score = d_score * score * (1.0 - score)
    router = router_ref[...]
    d_logits = (router * (d_router - jnp.sum(router * d_router, 0, keepdims=True))).astype(BF)
    high = d_score.astype(BF)
    mid = (d_score - high.astype(F32)).astype(BF)
    tail = (d_score - high.astype(F32) - mid.astype(F32)).astype(BF)
    logits_ref[...] = d_logits
    dscore_ref[...] = jnp.concatenate([high, mid, tail], 0)
    extra = weight_grad(d_logits, small_ref[0:n_experts])
    for part in (high, mid, tail):
        extra = extra + weight_grad(part, small_ref[n_experts : n_experts + 1])
    normal, inverse = rms_parts(resid_ref[...])
    d_normed = collect.gather() + extra
    dn_ref[...] = d_normed
    d_hat = d_normed * gain_ref[...]
    d_resid = cot_ref[...].astype(F32) + inverse * (
        d_hat - normal * jnp.mean(d_hat * normal, 1, keepdims=True)
    )
    dr_ref[...] = d_resid
    proj_ref[...] = d_resid.astype(BF)
    spread = Spread(proj_ref, all_ref, sems[5:9])
    spread.start()
    spread.forward()
    mix.send()
    gu.middle()
    sd.middle()
    collect.finish()
    gu.end()
    sd.end()
    spread.finish()
    mixed_ref[...] = (resid_ref[...] + mix.gather()).astype(BF)
    mix.finish()


def back(partial, resid, gain, cot, grad_gu, grad_sd, dots, router, score, small, mix):
    line = lax.axis_size("exp")
    tok, width = resid.shape
    dma = pltpu.SemaphoreType.DMA
    return pl.pallas_call(
        back_body,
        out_shape=(
            jax.ShapeDtypeStruct((tok, width), F32),
            jax.ShapeDtypeStruct((tok, width), F32),
            jax.ShapeDtypeStruct((CORES, line, tok, width), BF),
            jax.ShapeDtypeStruct(grad_gu.shape[2:], BF),
            jax.ShapeDtypeStruct(grad_sd.shape[2:], F32),
            jax.ShapeDtypeStruct(router.shape, BF),
            jax.ShapeDtypeStruct((3, tok), BF),
            jax.ShapeDtypeStruct((tok, width), BF),
        ),
        in_specs=[ANY, VMEM, VMEM, VMEM, ANY, ANY, ANY, VMEM, VMEM, VMEM, ANY],
        out_specs=(VMEM, VMEM, ANY, VMEM, VMEM, VMEM, VMEM, VMEM),
        scratch_shapes=Collect.scratch(line, tok, width)
        + Spread.scratch(line)
        + [pltpu.VMEM((tok, width), BF)]
        + PlaneSum.scratch(*grad_gu.shape[3:])
        + PlaneSum.scratch(*grad_sd.shape[3:])
        + [dma((CORES, line)), dma((CORES, line)), pltpu.VMEM(dots.shape, F32), dma]
        + Collect.scratch(line, tok, width),
        compiler_params=params(3),
        cost_estimate=cost(),
    )(partial, resid, gain, cot, grad_gu, grad_sd, dots, router, score, small, mix)


class Rows:
    def __init__(self, block, line):
        self.block, self.rows = block, block.shape[1] // line

    @property
    def at(self):
        return self

    def __getitem__(self, spot):
        core, exp = spot
        start = pl.multiple_of(exp * self.rows, self.rows)
        return self.block.at[core, pl.ds(start, self.rows)]


def last_body(
    partial_ref,
    gq_ref,
    go_ref,
    tot_ref,
    egu_ref,
    ed_ref,
    out_ref,
    q_ref,
    k_ref,
    v_ref,
    wo_ref,
    sum_ref,
    eg_ref,
    eu_ref,
    edown_ref,
    *rest,
):
    dp, cx, core, exp = places()
    line = lax.axis_size("exp")
    greet(all_peers())
    collect = Collect(partial_ref, *rest[:4], rest[4:9])
    qkv_block, tots_ref, cols_ref = rest[9:12]
    qkv = PlaneSum(gq_ref, qkv_block, rest[12:30])
    wo = PlaneSum(go_ref, wo_ref, rest[30:48])
    tot_send, tot_recv, local = rest[48:51]
    columns = Columns(Rows(qkv_block, line), cols_ref, rest[51:54])
    gu_came, d_came, swap_send, swap_recv, store = rest[54:59]
    wide, tall = rest[59:61]
    collect.start()
    rows, down = gu_came.shape[0], d_came.shape[0]
    swaps = [
        copy_to(
            source.at[pl.ds((1 - core) * height, height)],
            target,
            swap_send.at[n],
            swap_recv.at[n],
            moved(core=1),
        )
        for n, (source, target, height) in enumerate(
            ((egu_ref, gu_came, rows), (ed_ref, d_came, down))
        )
    ]
    qkv.start()
    wo.start()
    collect.send()
    keep = pltpu.make_async_copy(
        tot_ref.at[dp, cx, core, exp], tots_ref.at[0, 0, 0, 0], local
    )
    keep.start()
    sizes = [range(lax.axis_size(axis)) for axis in ("dp", "cx", "core", "exp")]
    outs = []
    for steps in itertools.product(*sizes):
        if any(steps):
            target = moved(*steps)
            outs.append(
                copy_to(
                    tot_ref.at[target],
                    tots_ref.at[steps],
                    tot_send.at[steps],
                    tot_recv.at[steps],
                    target,
                )
            )
    qkv.middle()
    qkv.end()
    columns.start()
    wo.middle()
    for copy in swaps:
        copy.wait_recv()
    ffe = wide.shape[3]

    def mine(at):
        piece = egu_ref[pl.ds(pl.multiple_of(core * rows + at.start, 8), at.size)].astype(F32)
        wide[0, core, at] = piece[:, :ffe]
        wide[1, core, at] = piece[:, ffe:]
        piece = gu_came[at].astype(F32)
        wide[0, 1 - core, at] = piece[:, :ffe]
        wide[1, 1 - core, at] = piece[:, ffe:]

    by_chunks(rows, mine)

    def down_rows(at):
        piece = ed_ref[pl.ds(pl.multiple_of(core * down + at.start, 8), at.size)]
        tall[core, at] = piece.astype(F32)
        tall[1 - core, at] = d_came[at].astype(F32)

    by_chunks(down, down_rows)
    stores = [
        pltpu.make_async_copy(wide.at[0], eg_ref, store.at[0]),
        pltpu.make_async_copy(wide.at[1], eu_ref, store.at[1]),
        pltpu.make_async_copy(tall, edown_ref, store.at[2]),
    ]
    for copy in stores:
        copy.start()
    out_ref[...] = collect.gather()
    wo.end()
    keep.wait()
    for copy in outs:
        copy.wait()
    sum_ref[...] = jnp.sum(tots_ref[...].reshape((-1,) + tots_ref.shape[4:]), 0)
    columns.arrive()
    col = cols_ref.shape[3] // 3
    for n, target in enumerate((q_ref, k_ref, v_ref)):
        for c in range(CORES):
            for e in range(line):
                at = (e * CORES + c) * col
                target[:, at : at + col] = cols_ref[c, e, :, n * col : (n + 1) * col].astype(F32)
    columns.finish()
    collect.finish()
    for copy in swaps:
        copy.wait_send()
    for copy in stores:
        copy.wait()


def last(partial, grad_qkv, grad_out, totals, grad_egu, grad_edown):
    n_dp, n_cx, line = (lax.axis_size(axis) for axis in ("dp", "cx", "exp"))
    tok, width = partial.shape[2:]
    dma = pltpu.SemaphoreType.DMA
    shard = grad_qkv.shape[3] // line
    rows, both = grad_egu.shape
    down = grad_edown.shape[0]
    heads = jax.ShapeDtypeStruct((shard, width), F32)
    wide = (CORES, rows // 2, both // 2)
    tall = (CORES, down // 2, width)
    return pl.pallas_call(
        last_body,
        out_shape=(
            jax.ShapeDtypeStruct((tok, width), F32),
            heads,
            heads,
            heads,
            jax.ShapeDtypeStruct(grad_out.shape[2:], F32),
            jax.ShapeDtypeStruct(totals.shape[4:], F32),
            jax.ShapeDtypeStruct(wide, F32),
            jax.ShapeDtypeStruct(wide, F32),
            jax.ShapeDtypeStruct(tall, F32),
        ),
        in_specs=[ANY, ANY, ANY, ANY, VMEM, VMEM],
        out_specs=(VMEM,) * 6 + (ANY,) * 3,
        scratch_shapes=Collect.scratch(line, tok, width)
        + [
            pltpu.VMEM(grad_qkv.shape[2:], BF),
            pltpu.VMEM(totals.shape, F32),
            pltpu.VMEM((CORES, line, shard, grad_qkv.shape[4]), BF),
        ]
        + PlaneSum.scratch(*grad_qkv.shape[3:])
        + PlaneSum.scratch(*grad_out.shape[3:])
        + [dma((n_dp, n_cx, CORES, line)), dma((n_dp, n_cx, CORES, line)), dma]
        + Columns.scratch(line)
        + [
            pltpu.VMEM((rows // 2, both), BF),
            pltpu.VMEM((down // 2, width), BF),
            dma((2,)),
            dma((2,)),
            dma((3,)),
            pltpu.VMEM((2,) + wide, F32),
            pltpu.VMEM(tall, F32),
        ],
        compiler_params=params(4),
        cost_estimate=cost(),
    )(partial, grad_qkv, grad_out, totals, grad_egu, grad_edown)


def on_device(
    tokens,
    cotangent,
    positions,
    lengths,
    routes,
    norm_attn,
    w_query,
    bias_query,
    w_key,
    bias_key,
    w_value,
    bias_value,
    w_output,
    norm_moe,
    w_router,
    w_shared_gate,
    w_shared_up,
    w_shared_down,
    w_shared_score,
    w_expert_gate,
    w_expert_up,
    w_expert_down,
):
    n_dp = lax.axis_size("dp")
    n_cx = lax.axis_size("cx")
    n_exp = lax.axis_size("exp")
    exp_at = lax.axis_index("exp")
    core_at = lax.axis_index("core")
    n_tp = CORES * n_exp
    n_data = n_dp * n_cx
    tok, width = tokens.shape[2:]
    shard = w_query.shape[0]
    block = CORES * n_exp * shard
    col = width // n_tp
    heads = col // HD
    n_experts = w_router.shape[1]
    sub = w_shared_down.shape[0]
    sub_width = n_data * sub
    every = tok * n_tp
    scale = HD ** (-0.5)
    top = routes.shape[3]
    ffe = w_expert_gate.shape[2]

    def by_core(first, second):
        return jnp.where(core_at == 0, first, second)

    x_own = tokens.reshape(tok, width)
    cot_own = cotangent.reshape(tok, width)

    small = jnp.concatenate(
        [
            norm_attn[None],
            norm_moe[None],
            w_shared_score[None],
            bias_query[None],
            bias_key[None],
            bias_value[None],
            w_router.T,
        ]
    ).astype(F32)
    n_small = small.shape[0]
    pack = jnp.concatenate(
        [
            positions.reshape(1, tok),
            routes.reshape(tok, top).T,
            jnp.pad(lengths.reshape(1, -1), ((0, 0), (0, tok - lengths.shape[2]))),
        ]
    ).astype(F32)
    pack = jnp.concatenate([pack, jnp.pad(small, ((0, 0), (0, tok - shard)))])
    pack = jnp.pad(pack, ((0, -pack.shape[0] % 8), (0, 0)))

    def exchange(value):
        return lax.all_to_all(value, ("core", "exp"), split_axis=0, concat_axis=0, tiled=True)

    def head_columns(value):
        parts = value.reshape(shard, n_exp, CORES, col)
        return jnp.transpose(parts, (2, 1, 0, 3))

    qkv_cols = jnp.concatenate(
        [head_columns(w_query), head_columns(w_key), head_columns(w_value)], 3
    )
    x_all, w_qkv, wo_all, packs, cot_tok = load(x_own, qkv_cols, w_output, pack, cot_own)
    w_egu = lax.all_gather(
        jnp.concatenate([w_expert_gate, w_expert_up], 2), ("dp", "cx", "core"), axis=1, tiled=True
    )
    w_edown = lax.all_gather(w_expert_down, ("dp", "cx", "core"), axis=1, tiled=True)
    w_egu = lax.dynamic_index_in_dim(w_egu, core_at, 0, keepdims=False)
    w_edown = lax.dynamic_index_in_dim(w_edown, core_at, 0, keepdims=False)
    w_qkv = w_qkv.reshape(width, 3 * col)
    gu_cols = split_hidden(w_shared_gate, w_shared_up, n_exp, sub)

    small = packs[:, :, :, :, 2 + top : 2 + top + n_small, :shard]
    small = jnp.moveaxis(small, 4, 0).reshape(n_small, width)
    gain_attn = small[0]
    gain_moe = small[1]
    score_vec = small[2]
    router_full = small[6:].T.astype(BF)
    rank = exp_at * CORES + core_at
    biases = lax.dynamic_slice_in_dim(small[3:6], rank * col, col, 1).reshape(3 * col)

    ints = lax.dynamic_index_in_dim(packs, lax.axis_index("dp"), 0, keepdims=False)
    ints = ints[:, :, :, : 2 + top]
    for dim, axis in enumerate(("cx", "core", "exp")):
        ints = roll_to_relative(ints, axis, dim)
    ints = ints.astype(jnp.int32)
    route_tok = jnp.swapaxes(ints[0, :, :, 1 : 1 + top], 2, 3).reshape(every, top)
    seq_lens = ints[0, 0, :, 1 + top, : lengths.shape[2]]
    seq_ends = jnp.cumsum(seq_lens, 1)
    pos_keys = jnp.moveaxis(ints[:, :, :, 0], 2, 0).reshape(n_exp, n_cx * CORES * tok)
    after_end = (pos_keys[:, :, None] >= seq_ends[:, None, :]).astype(jnp.int32)
    seg_keys = jnp.sum(after_end, 2)
    rel_keys = pos_keys - jnp.sum(after_end * seq_lens[:, None, :], 2)
    own_keys = CORES * tok
    code_keys = (seg_keys * 4096 + pos_keys)[:, None, :]
    low = (seg_keys[:, :own_keys] * 4096)[:, :, None]
    codes = (low + pos_keys[:, :own_keys, None], low, code_keys)
    freq = ROTARY_BASE ** (-(jnp.arange(HD // 2, dtype=F32) * 2.0 / HD))
    angle = rel_keys[:, :own_keys].astype(F32)[:, :, None] * freq
    cos_table = jnp.cos(angle)
    sin_table = jnp.sin(angle)
    cos_table = jnp.concatenate([cos_table, cos_table], 2)
    sin_table = jnp.concatenate([-sin_table, sin_table], 2)

    normed_one, query, kv = project_qkv(x_all, w_qkv, gain_attn, biases, cos_table, sin_table)
    normed_one = normed_one.reshape(every, width)
    kv_all, gu_block, w_out = keys_call(kv, gu_cols, wo_all)
    w_out = w_out.reshape(col, width)
    attn_low, partial = attend(query, kv_all, codes, w_out)
    resid, normed_two, w_sgu, w_sdown = ahead(
        partial,
        x_own,
        gain_moe[None],
        gu_block,
        w_shared_down.reshape(2, sub // 2, width),
    )
    normed_two = normed_two.reshape(every, width)
    normed_two_own = normed_two[:tok]
    w_sgu = w_sgu.reshape(width, 2 * sub_width)
    w_sdown = w_sdown.reshape(sub_width, width)

    small_cols = jnp.concatenate([router_full, score_vec.astype(BF)[:, None]], 1)
    small_out = project(normed_two, small_cols)
    router_all = jax.nn.softmax(small_out[:, :n_experts], axis=-1)
    score_all = jax.nn.sigmoid(small_out[:, n_experts])
    chosen = jnp.any(route_tok == rank, axis=1)
    at_rank = (jnp.arange(n_experts) == rank).astype(F32)
    gate = jnp.where(chosen, jnp.sum(router_all * at_rank[None, :], 1), 0.0)

    shared_pre = project(normed_two, w_sgu)
    s_gate = shared_pre[:, :sub_width]
    s_up = shared_pre[:, sub_width:]
    s_act, s_slope = silu_parts(s_gate)
    s_hidden = (s_act * s_up).astype(BF)
    shared = project(s_hidden, w_sdown)
    normed_late, shared = lax.optimization_barrier((normed_two, shared))
    expert_pre = project(normed_late, w_egu)
    cot_all = cot_tok.reshape(every, width).astype(F32)
    e_gate = expert_pre[:, :ffe]
    e_up = expert_pre[:, ffe:]
    e_act, e_slope = silu_parts(e_gate)
    e_hidden = (e_act * e_up).astype(BF)
    e_out = project(e_hidden, w_edown).astype(BF).astype(F32)
    mix = (score_all[:, None] * shared + gate[:, None] * e_out).astype(BF)
    dots = jnp.stack(
        [
            jnp.where(chosen, jnp.sum(cot_all * e_out, 1), 0.0),
            jnp.sum(cot_all * shared, 1),
        ]
    )

    mix, gate = lax.optimization_barrier((mix, gate))
    d_eout = (gate[:, None] * cot_all).astype(BF)
    d_eh = project_t(d_eout, w_edown)
    d_egu = jnp.concatenate(
        [(d_eh * e_up * e_slope).astype(BF), (d_eh * e_act).astype(BF)], 1
    )
    grad_egu = weight_grad(normed_two, d_egu).astype(BF)
    grad_edown = weight_grad(e_hidden, d_eout).astype(BF)
    score_back, grad_egu, grad_edown = lax.optimization_barrier((score_all, grad_egu, grad_edown))
    grad_egu = lax.psum_scatter(grad_egu, ("dp", "cx"), scatter_dimension=0, tiled=True)
    grad_edown = lax.psum_scatter(grad_edown, ("dp", "cx"), scatter_dimension=0, tiled=True)
    d_shared = (score_back[:, None] * cot_all).astype(BF)
    d_sh = project_t(d_shared, w_sdown)
    d_sgu = jnp.concatenate(
        [(d_sh * s_up * s_slope).astype(BF), (d_sh * s_act).astype(BF)], 1
    )
    partial_two = (project_t(d_sgu, w_sgu) + project_t(d_egu, w_egu)).astype(BF)
    grad_sdown = weight_grad(s_hidden, d_shared).astype(BF)
    grad_sgu = weight_grad(normed_two, d_sgu).astype(BF)

    dots = jnp.pad(dots.reshape(2, n_tp, tok).swapaxes(0, 1), ((0, 0), (0, 6), (0, 0)))
    d_normed_two, d_resid, d_proj, grad_sgu, grad_sdown, d_logits, d_score, mixed = back(
        partial_two.reshape(CORES, n_exp, tok, width),
        resid,
        gain_moe[None],
        cot_own,
        grad_sgu.reshape(n_dp, n_cx, 2, -1, 2 * sub_width),
        grad_sdown.reshape(n_dp, n_cx, 2, -1, width),
        dots.reshape(CORES, n_exp, 8, tok),
        router_all[:tok].T,
        score_all[None, :tok],
        jnp.concatenate([router_full.T, score_vec.astype(BF)[None]]),
        mix.reshape(CORES, n_exp, tok, width),
    )
    grad_router = project(d_logits, normed_two_own)
    grad_score = project(d_score, normed_two_own).sum(0)
    grad_gain_moe = jnp.sum(d_normed_two * rms_parts(resid)[0], 0)

    grad_sdown = grad_sdown.reshape(sub, width)
    grad_sgu = exchange(grad_sgu.reshape(n_tp, shard, 2 * sub_width))
    grad_sgu = grad_sgu.reshape(CORES, n_exp, shard, 2 * sub_width)

    d_query, d_kv = attend_back(query, kv_all, codes, w_out, d_proj, cos_table, sin_table)
    came = jnp.stack([push(d_kv[k], "cx", k) for k in range(1, n_cx)])
    came, grad_sgu = lax.optimization_barrier((came, grad_sgu))
    d_qkv, partial_one, grad_gain_attn, grad_bias = qkv_back(
        d_query, d_kv[0], came, cos_table, sin_table, w_qkv, x_all
    )
    grad_qkv = weight_grad(normed_one, d_qkv.reshape(every, 3 * col)).astype(BF)
    grad_out = lax.all_to_all(
        weight_grad(attn_low.reshape(every, col), d_proj.reshape(every, width))
        .astype(BF)
        .reshape(n_exp, shard, width),
        "exp",
        split_axis=0,
        concat_axis=0,
        tiled=True,
    )
    grad_bias = lax.dynamic_update_slice_in_dim(
        jnp.zeros((3, width), F32), grad_bias.reshape(3, col), rank * col, 1
    )
    totals = jnp.concatenate(
        [
            grad_gain_attn,
            grad_gain_moe[None],
            grad_score[None],
            grad_bias,
            grad_router,
        ]
    )
    totals = jnp.moveaxis(totals.reshape(n_small, n_data * n_tp, shard), 0, 1)
    totals = totals.reshape(n_data * n_tp, -1)
    totals = jnp.pad(totals, ((0, 0), (0, -totals.shape[1] % 1024)))
    grad_sgate, grad_sup = merge_hidden(grad_sgu, sub)
    partial_one, grad_sgate, grad_sup = lax.optimization_barrier(
        (partial_one, grad_sgate, grad_sup)
    )
    (
        d_normed_one,
        grad_query,
        grad_key,
        grad_value,
        grad_out,
        totals,
        grad_egate,
        grad_eup,
        grad_edown,
    ) = last(
        partial_one,
        grad_qkv.reshape(n_dp, n_cx, 2, -1, 3 * col),
        grad_out.reshape(n_dp, n_cx, 2, shard // 2, width),
        totals.reshape(n_dp, n_cx, CORES, n_exp, -1, 128),
        grad_egu,
        grad_edown,
    )
    grad_out = grad_out.reshape(shard, width)
    totals = totals.reshape(-1)[: n_small * shard].reshape(n_small, shard)
    normal_own, inverse_own = rms_parts(x_own.astype(F32))
    d_hat_one = d_normed_one * gain_attn
    from_attn = inverse_own * (
        d_hat_one - normal_own * jnp.mean(d_hat_one * normal_own, 1, keepdims=True)
    )
    grad_tokens = (d_resid + from_attn).astype(BF)

    return (
        mixed.reshape(tokens.shape),
        grad_tokens.reshape(tokens.shape),
        totals[0],
        grad_query,
        totals[3],
        grad_key,
        totals[4],
        grad_value,
        totals[5],
        grad_out,
        totals[1],
        totals[6:].T,
        grad_sgate,
        grad_sup,
        grad_sdown,
        totals[2],
        grad_egate,
        grad_eup,
        grad_edown,
    )


def solution(mesh):
    sizes = dict(mesh.shape)
    fine = Mesh(
        mesh.devices.reshape(sizes["dp"], sizes["ctx"] // CORES, CORES, sizes["exp"]),
        ("dp", "cx", "core", "exp"),
    )
    own = P("dp", "exp", ("cx", "core"), None)
    flat = P(("dp", "cx", "core", "exp"))
    rows = P(("dp", "cx", "core", "exp"), None)
    expert = P("exp", ("dp", "cx", "core"), None)
    placed = (
        own,
        own,
        P("dp", "exp", ("cx", "core")),
        P("dp", "exp", None),
        own,
        flat,
        rows,
        flat,
        rows,
        flat,
        rows,
        flat,
        rows,
        flat,
        rows,
        rows,
        rows,
        rows,
        flat,
        expert,
        expert,
        expert,
    )
    return jax.shard_map(
        on_device,
        mesh=fine,
        in_specs=placed,
        out_specs=(
            own,
            own,
            flat,
            rows,
            flat,
            rows,
            flat,
            rows,
            flat,
            rows,
            flat,
            rows,
            rows,
            rows,
            rows,
            flat,
            expert,
            expert,
            expert,
        ),
        check_vma=False,
    )
```

```python
import itertools

import jax
import jax.numpy as jnp
from jax import lax
from jax.experimental import pallas as pl
from jax.experimental.pallas import tpu as pltpu
from jax.sharding import Mesh
from jax.sharding import PartitionSpec as P

HD = 128
CORES = 2
EPSILON = 1e-06
ROTARY_BASE = 1000000.0
NEGATIVE = -1e30
BF = jnp.bfloat16
F32 = jnp.float32


def project(left, right):
    return jnp.dot(left, right, preferred_element_type=F32)


def project_t(left, right):
    return lax.dot_general(left, right, (((1,), (1,)), ((), ())), preferred_element_type=F32)


def weight_grad(left, right):
    return lax.dot_general(left, right, (((0,), (0,)), ((), ())), preferred_element_type=F32)


def rms_parts(value):
    inverse = lax.rsqrt(jnp.mean(value * value, axis=-1, keepdims=True) + EPSILON)
    return (value * inverse, inverse)


def silu_parts(value):
    sigmoid = jax.nn.sigmoid(value)
    return (value * sigmoid, sigmoid * (1.0 + value * (1.0 - sigmoid)))


def fetch(value, axis, step):
    size = lax.axis_size(axis)
    if step % size == 0:
        return value
    return lax.ppermute(value, axis, [((i + step) % size, i) for i in range(size)])


def push(value, axis, step):
    size = lax.axis_size(axis)
    return lax.ppermute(value, axis, [(i, (i + step) % size) for i in range(size)])


def roll_to_relative(value, axis, dim):
    size = lax.axis_size(axis)
    both = lax.concatenate([value, value], dim)
    return lax.dynamic_slice_in_dim(both, lax.axis_index(axis), size, dim)


MESH = pl.DeviceIdType.MESH
ANY = pl.BlockSpec(memory_space=pltpu.HBM)
VMEM = pl.BlockSpec(memory_space=pltpu.VMEM)


def places():
    return tuple(lax.axis_index(axis) for axis in ("dp", "cx", "core", "exp"))


def moved(dp=0, cx=0, core=0, exp=0):
    steps = (dp, cx, core, exp)
    return tuple(
        at if step == 0 else lax.rem(at + step, lax.axis_size(axis))
        for at, step, axis in zip(places(), steps, ("dp", "cx", "core", "exp"))
    )


def copy_to(source, target, send_sem, recv_sem, device):
    copy = pltpu.make_async_remote_copy(
        src_ref=source,
        dst_ref=target,
        send_sem=send_sem,
        recv_sem=recv_sem,
        device_id=device,
        device_id_type=MESH,
    )
    copy.start()
    return copy


def greet(devices):
    barrier = pltpu.get_barrier_semaphore()
    for device in devices:
        pl.semaphore_signal(barrier, inc=1, device_id=device, device_id_type=MESH)
    pl.semaphore_wait(barrier, len(devices))


def line_peers():
    return [moved(exp=k) for k in range(1, lax.axis_size("exp"))]


def plane_peers():
    steps = [(j, k) for j in range(lax.axis_size("dp")) for k in range(lax.axis_size("cx"))]
    return [moved(dp=j, cx=k) for j, k in steps[1:]]


class Spread:
    def __init__(self, source, out, sems):
        self.source, self.out = source, out
        self.up, self.down, self.over, self.local = sems
        self.line = lax.axis_size("exp")
        self.at = lax.axis_index("exp")

    def hop(self, step, way):
        slot = (self.line - step) % self.line if way > 0 else step
        landing = self.line - step - 1 if way > 0 else step + 1
        sems = self.up if way > 0 else self.down
        return pltpu.make_async_remote_copy(
            src_ref=self.source if step == 0 else self.out.at[0, slot],
            dst_ref=self.out.at[0, landing],
            send_sem=sems.at[0, step],
            recv_sem=sems.at[1, step + 1],
            device_id=moved(exp=1 if way > 0 else self.line - 1),
            device_id_type=MESH,
        )

    def sends(self, step, way):
        if way > 0:
            return jnp.logical_and(self.at >= step, self.at < self.line - 1)
        return jnp.logical_and(self.at + step <= self.line - 1, self.at > 0)

    def gets(self, step, way):
        return self.at >= step if way > 0 else self.at + step <= self.line - 1

    def across(self, slot):
        return pltpu.make_async_remote_copy(
            src_ref=self.source if slot == 0 else self.out.at[0, slot],
            dst_ref=self.out.at[1, slot],
            send_sem=self.over.at[0, slot],
            recv_sem=self.over.at[1, slot],
            device_id=moved(core=1),
            device_id_type=MESH,
        )

    def start(self):
        self.keep = pltpu.make_async_copy(self.source, self.out.at[0, 0], self.local)
        self.keep.start()
        for way in (1, -1):
            pl.when(self.sends(0, way))(self.hop(0, way).start)
        self.across(0).start()

    def forward(self):
        for step in range(1, self.line):
            self.forward_step(step)

    def forward_step(self, step):
        for way in (1, -1):
            slot = self.line - step if way > 0 else step

            @pl.when(self.gets(step, way))
            def _():
                self.hop(step - 1, way).wait_recv()
                self.across(slot).start()

            if step < self.line - 1:
                pl.when(self.sends(step, way))(self.hop(step, way).start)

    def finish(self):
        self.keep.wait()
        for step in range(self.line - 1):
            for way in (1, -1):
                pl.when(self.sends(step, way))(self.hop(step, way).wait_send)
        for slot in range(self.line):
            self.across(slot).wait()

    @staticmethod
    def scratch(line):
        return [
            pltpu.SemaphoreType.DMA((2, line)),
            pltpu.SemaphoreType.DMA((2, line)),
            pltpu.SemaphoreType.DMA((2, line)),
            pltpu.SemaphoreType.DMA,
        ]


class Columns:
    def __init__(self, cols, out, sems):
        self.cols, self.out, self.sems = cols, out, sems

    def start(self):
        send, recv, local = self.sems
        line = lax.axis_size("exp")
        _, _, core, exp = places()
        self.local = pltpu.make_async_copy(
            self.cols.at[core, exp], self.out.at[core, exp], local
        )
        self.local.start()
        self.copies = []
        for c in range(CORES):
            for k in range(line):
                if c or k:
                    target = moved(core=c, exp=k)
                    self.copies.append(
                        copy_to(
                            self.cols.at[target[2], target[3]],
                            self.out.at[core, exp],
                            send.at[c, k],
                            recv.at[c, k],
                            target,
                        )
                    )

    def arrive(self):
        self.local.wait()
        for copy in self.copies:
            copy.wait_recv()

    def finish(self):
        for copy in self.copies:
            copy.wait_send()

    @staticmethod
    def scratch(line):
        return [
            pltpu.SemaphoreType.DMA((CORES, line)),
            pltpu.SemaphoreType.DMA((CORES, line)),
            pltpu.SemaphoreType.DMA,
        ]


class Plane:
    def __init__(self, out, sems, source=None):
        self.out, self.sems, self.source = out, sems, source
        self.n = (lax.axis_size("dp"), lax.axis_size("cx"))

    def send(self, half, j, k, dp, cx):
        send, recv = self.sems
        at = places()
        n_dp, n_cx = self.n
        from_dp = lax.rem(at[0] + n_dp - j, n_dp)
        from_cx = lax.rem(at[1] + n_cx - k, n_cx)
        block = self.out.at[from_dp, from_cx, half]
        a, b = j + dp, k + cx
        first = self.source is not None and j == 0 and k == 0
        origin = self.source.at[half] if first else block
        return copy_to(
            origin, block, send.at[half, a, b], recv.at[half, a, b], moved(dp=dp, cx=cx)
        )

    def start(self):
        n_dp, n_cx = self.n
        self.along_cx = [[self.send(h, 0, 0, 0, k) for k in range(1, n_cx)] for h in range(2)]
        self.along_dp = [[self.send(h, 0, 0, j, 0) for j in range(1, n_dp)] for h in range(2)]

    def forward(self):
        n_dp, n_cx = self.n
        self.rest = []
        for k in range(1, n_cx):
            self.along_cx[0][k - 1].wait_recv()
            for j in range(1, n_dp):
                self.rest.append(self.send(0, 0, k, j, 0))
        for j in range(1, n_dp):
            self.along_dp[1][j - 1].wait_recv()
            for k in range(1, n_cx):
                self.rest.append(self.send(1, j, 0, 0, k))

    def finish(self):
        for copy in self.along_cx[1] + self.along_dp[0] + self.rest:
            copy.wait()
        for copy in self.along_cx[0] + self.along_dp[1]:
            copy.wait_send()

    @staticmethod
    def scratch(n_dp, n_cx):
        return [
            pltpu.SemaphoreType.DMA((2, n_dp, n_cx)),
            pltpu.SemaphoreType.DMA((2, n_dp, n_cx)),
        ]


def params(number, mebibytes):
    return pltpu.CompilerParams(
        collective_id=number, has_side_effects=True, vmem_limit_bytes=mebibytes * 2**20
    )


def cost():
    return pl.CostEstimate(flops=1, bytes_accessed=1, transcendentals=0)


def tp_peers():
    line = lax.axis_size("exp")
    steps = [(c, k) for c in range(CORES) for k in range(line)]
    return [moved(core=c, exp=k) for c, k in steps[1:]]


def all_peers():
    sizes = [range(lax.axis_size(axis)) for axis in ("dp", "cx", "core", "exp")]
    return [moved(*steps) for steps in itertools.product(*sizes) if any(steps)]


def load_body(
    x_ref,
    cols_ref,
    wo_ref,
    pack_ref,
    cot_ref,
    xall_ref,
    wqkv_ref,
    woall_ref,
    packs_ref,
    cotall_ref,
    *sems,
):
    dp, cx, core, exp = places()
    greet(all_peers())
    tokens = Spread(x_ref, xall_ref, sems[0:4])
    block = wqkv_ref.at[dp, cx]
    columns = Columns(cols_ref, block, sems[4:7])
    plane = Plane(wqkv_ref, sems[7:9])
    send, recv, local = sems[9:12]
    columns.start()
    own = [
        pltpu.make_async_copy(wo_ref, woall_ref.at[dp, cx], local.at[0]),
        pltpu.make_async_copy(pack_ref, packs_ref.at[dp, cx, core, exp], local.at[1]),
    ]
    for copy in own:
        copy.start()
    pack_send, pack_recv = sems[12:14]
    sizes = [range(lax.axis_size(axis)) for axis in ("dp", "cx", "core", "exp")]
    outs = [
        copy_to(
            pack_ref,
            packs_ref.at[dp, cx, core, exp],
            pack_send.at[steps],
            pack_recv.at[steps],
            moved(*steps),
        )
        for steps in itertools.product(*sizes)
        if any(steps)
    ]
    cotangent = Spread(cot_ref, cotall_ref, sems[14:18])
    columns.arrive()
    tokens.start()
    plane.start()
    tokens.forward()
    cotangent.start()
    plane.forward()
    for j in range(lax.axis_size("dp")):
        for k in range(lax.axis_size("cx")):
            if j or k:
                outs.append(
                    copy_to(
                        wo_ref,
                        woall_ref.at[dp, cx],
                        send.at[j, k],
                        recv.at[j, k],
                        moved(dp=j, cx=k),
                    )
                )
    cotangent.forward()
    columns.finish()
    tokens.finish()
    plane.finish()
    cotangent.finish()
    for copy in own + outs:
        copy.wait()


def load(x_own, cols, w_output, pack, cot_own):
    n_dp, n_cx, line = (lax.axis_size(axis) for axis in ("dp", "cx", "exp"))
    return pl.pallas_call(
        load_body,
        out_shape=(
            jax.ShapeDtypeStruct((CORES, line) + x_own.shape, BF),
            jax.ShapeDtypeStruct((n_dp, n_cx) + cols.shape, BF),
            jax.ShapeDtypeStruct((n_dp, n_cx) + w_output.shape, BF),
            jax.ShapeDtypeStruct((n_dp, n_cx, CORES, line) + pack.shape, F32),
            jax.ShapeDtypeStruct((CORES, line) + cot_own.shape, BF),
        ),
        in_specs=[ANY] * 5,
        out_specs=(ANY,) * 5,
        scratch_shapes=Spread.scratch(line)
        + Columns.scratch(line)
        + Plane.scratch(n_dp, n_cx)
        + [
            pltpu.SemaphoreType.DMA((n_dp, n_cx)),
            pltpu.SemaphoreType.DMA((n_dp, n_cx)),
            pltpu.SemaphoreType.DMA((2,)),
            pltpu.SemaphoreType.DMA((n_dp, n_cx, CORES, line)),
            pltpu.SemaphoreType.DMA((n_dp, n_cx, CORES, line)),
        ]
        + Spread.scratch(line),
        compiler_params=params(0, 58),
        cost_estimate=cost(),
    )(x_own, cols, w_output, pack, cot_own)


def keys_body(kv_ref, cols_ref, wo_ref, kvall_ref, gu_ref, wout_ref, *sems):
    _, _, _, exp = places()
    n_cx = lax.axis_size("cx")
    line = lax.axis_size("exp")
    greet(tp_peers() + [moved(cx=k) for k in range(1, n_cx)])
    send, recv, local = sems[3:6]
    own = pltpu.make_async_copy(kv_ref, kvall_ref.at[0], local)
    own.start()
    keys = [
        copy_to(kv_ref, kvall_ref.at[n_cx - k], send.at[k], recv.at[k], moved(cx=k))
        for k in range(1, n_cx)
    ]
    columns = Columns(cols_ref, gu_ref, sems[0:3])
    columns.start()
    send, recv, local = sems[6:9]
    keep = pltpu.make_async_copy(wo_ref.at[exp // n_cx, exp % n_cx], wout_ref.at[exp], local)
    keep.start()
    outs = []
    for k in range(1, line):
        target = moved(exp=k)
        at = target[3]
        outs.append(
            copy_to(
                wo_ref.at[at // n_cx, at % n_cx],
                wout_ref.at[exp],
                send.at[k],
                recv.at[k],
                target,
            )
        )
    own.wait()
    keep.wait()
    columns.arrive()
    columns.finish()
    for copy in keys + outs:
        copy.wait()


def keys_call(kv, cols, wo_all):
    n_cx, line = lax.axis_size("cx"), lax.axis_size("exp")
    return pl.pallas_call(
        keys_body,
        out_shape=(
            jax.ShapeDtypeStruct((n_cx,) + kv.shape, BF),
            jax.ShapeDtypeStruct(cols.shape, BF),
            jax.ShapeDtypeStruct((line,) + wo_all.shape[2:], BF),
        ),
        in_specs=[ANY] * 3,
        out_specs=(ANY,) * 3,
        scratch_shapes=Columns.scratch(line)
        + [
            pltpu.SemaphoreType.DMA((n_cx,)),
            pltpu.SemaphoreType.DMA((n_cx,)),
            pltpu.SemaphoreType.DMA,
            pltpu.SemaphoreType.DMA((line,)),
            pltpu.SemaphoreType.DMA((line,)),
            pltpu.SemaphoreType.DMA,
        ],
        compiler_params=params(1, 58),
        cost_estimate=cost(),
    )(kv, cols, wo_all)


def by_chunks(rows, work):
    chunk = 16 if rows % 16 == 0 else 8

    @pl.loop(0, rows // chunk)
    def _(step):
        work(pl.ds(pl.multiple_of(step * chunk, chunk), chunk))


class Collect:
    def __init__(self, partial, kept, near, far, sems):
        self.partial, self.kept, self.near, self.far = partial, kept, near, far
        self.core_send, self.core_recv, self.hop_send, self.hop_recv, self.local = sems
        self.line = lax.axis_size("exp")
        self.at = lax.axis_index("exp")

    def start(self):
        self.swaps, self.loads = [], []
        for k in range(self.line):
            self.swaps.append(
                copy_to(
                    self.partial.at[1, k],
                    self.near.at[k],
                    self.core_send.at[k],
                    self.core_recv.at[k],
                    moved(core=1),
                )
            )
            load = pltpu.make_async_copy(self.partial.at[0, k], self.kept.at[k], self.local.at[k])
            load.start()
            self.loads.append(load)

    def hop(self, way, step):
        slot = step if way == 0 else self.line - step
        return pltpu.make_async_remote_copy(
            src_ref=self.kept.at[slot],
            dst_ref=self.far.at[way, step - 1],
            send_sem=self.hop_send.at[way, step],
            recv_sem=self.hop_recv.at[way, step - 1],
            device_id=moved(exp=1 if way == 0 else self.line - 1),
            device_id_type=MESH,
        )

    def reaches(self, way, step):
        return self.at + step <= self.line - 1 if way == 0 else self.at >= step

    def fed(self, way):
        return self.at >= 1 if way == 0 else self.at <= self.line - 2

    def ready(self):
        for load in self.loads:
            load.wait()
        for swap in self.swaps:
            swap.wait_recv()

    def pair(self, k, rows):
        return self.kept[k, rows].astype(F32) + self.near[k, rows].astype(F32)

    def send_step(self, step):
        tok = self.kept.shape[1]
        for way in range(2):
            slot = step if way == 0 else self.line - step

            @pl.when(self.reaches(way, step))
            def _():
                @pl.when(self.fed(way))
                def _():
                    self.hop(way, step + 1).wait_recv()

                    def work(rows):
                        total = self.pair(slot, rows) + self.far[way, step, rows].astype(F32)
                        self.kept[slot, rows] = total.astype(BF)

                    by_chunks(tok, work)

                @pl.when(jnp.logical_not(self.fed(way)))
                def _():
                    def work(rows):
                        self.kept[slot, rows] = self.pair(slot, rows).astype(BF)

                    by_chunks(tok, work)

                self.hop(way, step).start()

    def send(self):
        self.ready()
        for step in range(self.line - 1, 0, -1):
            self.send_step(step)

    def gather(self):
        for way in range(2):

            @pl.when(self.fed(way))
            def _():
                self.hop(way, 1).wait_recv()

            @pl.when(jnp.logical_not(self.fed(way)))
            def _():
                self.far[way, 0] = jnp.zeros(self.far.shape[2:], BF)

        return (
            self.kept[0].astype(F32)
            + self.near[0].astype(F32)
            + (self.far[0, 0].astype(F32) + self.far[1, 0].astype(F32))
        )

    def reduce(self):
        self.send()
        return self.gather()

    def finish(self):
        for swap in self.swaps:
            swap.wait_send()
        for step in range(1, self.line):
            for way in range(2):
                pl.when(self.reaches(way, step))(self.hop(way, step).wait_send)

    @staticmethod
    def scratch(line, tok, width):
        dma = pltpu.SemaphoreType.DMA
        return [
            pltpu.VMEM((line, tok, width), BF),
            pltpu.VMEM((line, tok, width), BF),
            pltpu.VMEM((2, line, tok, width), BF),
            dma((line,)),
            dma((line,)),
            dma((2, line + 1)),
            dma((2, line + 1)),
            dma((line,)),
        ]


def split_hidden(gate, up, n_exp, piece):
    shard, total = gate.shape
    blocks = total // (CORES * n_exp * piece)

    def body(gate_ref, up_ref, out_ref):
        sides = (gate_ref[...].astype(F32), up_ref[...].astype(F32))
        for c in range(CORES):
            for e in range(n_exp):
                parts = []
                for side in sides:
                    for b in range(blocks):
                        start = ((b * CORES + c) * n_exp + e) * piece
                        parts.append(side[:, start : start + piece])
                out_ref[c, e] = jnp.concatenate(parts, 1).astype(BF)

    return pl.pallas_call(
        body,
        out_shape=jax.ShapeDtypeStruct((CORES, n_exp, shard, 2 * blocks * piece), BF),
        in_specs=[VMEM, VMEM],
        out_specs=VMEM,
        compiler_params=local_params(56),
        cost_estimate=cost(),
    )(gate, up)


def merge_hidden(value, piece):
    _, n_exp, shard, both = value.shape
    blocks = both // (2 * piece)
    total = blocks * CORES * n_exp * piece

    def body(in_ref, gate_ref, up_ref):
        for side, out_ref in enumerate((gate_ref, up_ref)):
            parts = []
            for b in range(blocks):
                start = (side * blocks + b) * piece
                for c in range(CORES):
                    for e in range(n_exp):
                        parts.append(in_ref[c, e].astype(F32)[:, start : start + piece])
            out_ref[...] = jnp.concatenate(parts, 1)

    shape = jax.ShapeDtypeStruct((shard, total), F32)
    return pl.pallas_call(
        body,
        out_shape=(shape, shape),
        in_specs=[VMEM],
        out_specs=(VMEM, VMEM),
        compiler_params=local_params(56),
        cost_estimate=cost(),
    )(value)


class HalfSum:
    def __init__(self, blocks, half, bufs, sems):
        self.blocks, self.half = blocks, half
        self.own, self.came, self.sums, self.final = bufs
        self.sem = sems
        n_dp, n_cx = lax.axis_size("dp"), lax.axis_size("cx")
        self.cx_first = half == 0
        self.n_in, self.n_out = (n_cx, n_dp) if self.cx_first else (n_dp, n_cx)

    def block(self, inner, outer):
        dp, cx = (outer, inner) if self.cx_first else (inner, outer)
        at = moved(dp=dp, cx=cx)
        return self.blocks.at[at[0], at[1], self.half]

    def far(self, inner, outer):
        dp, cx = (outer, inner) if self.cx_first else (inner, outer)
        return moved(dp=dp, cx=cx)

    def start(self):
        first_send, first_recv, _, _, local = self.sem
        self.first, self.loads = {}, []
        for a in range(self.n_out):
            for b in range(1, self.n_in):
                self.first[b, a] = copy_to(
                    self.block(b, a),
                    self.came.at[b - 1, a],
                    first_send.at[b - 1, a],
                    first_recv.at[b - 1, a],
                    self.far(b, 0),
                )
            load = pltpu.make_async_copy(self.block(0, a), self.own.at[a], local.at[a])
            load.start()
            self.loads.append(load)

    def near(self, a, rows):
        total = self.own[a, rows].astype(F32)
        for b in range(1, self.n_in):
            total = total + self.came[b - 1, a, rows].astype(F32)
        return total

    def middle(self):
        _, _, send, recv, _ = self.sem
        for load in self.loads:
            load.wait()
        self.second = []
        for a in range(1, self.n_out):
            for b in range(1, self.n_in):
                self.first[b, a].wait_recv()

            def work(rows):
                self.sums[a - 1, rows] = self.near(a, rows).astype(BF)

            by_chunks(self.sums.shape[1], work)
            self.second.append(
                copy_to(
                    self.sums.at[a - 1],
                    self.final.at[a - 1],
                    send.at[a - 1],
                    recv.at[a - 1],
                    self.far(0, a),
                )
            )

    def end(self, out):
        for b in range(1, self.n_in):
            self.first[b, 0].wait_recv()
        for copy in self.second:
            copy.wait_recv()

        def work(rows):
            total = self.near(0, rows)
            for a in range(1, self.n_out):
                total = total + self.final[a - 1, rows].astype(F32)
            out[rows] = total.astype(out.dtype)

        by_chunks(self.sums.shape[1], work)
        for copy in self.first.values():
            copy.wait_send()
        for copy in self.second:
            copy.wait_send()

    @staticmethod
    def scratch(half, rows, width):
        n_dp, n_cx = lax.axis_size("dp"), lax.axis_size("cx")
        n_in, n_out = (n_cx, n_dp) if half == 0 else (n_dp, n_cx)
        dma = pltpu.SemaphoreType.DMA
        return (
            [
                pltpu.VMEM((n_out, rows, width), BF),
                pltpu.VMEM((n_in - 1, n_out, rows, width), BF),
                pltpu.VMEM((n_out - 1, rows, width), BF),
                pltpu.VMEM((n_out - 1, rows, width), BF),
            ],
            [
                dma((n_in - 1, n_out)),
                dma((n_in - 1, n_out)),
                dma((n_out - 1,)),
                dma((n_out - 1,)),
                dma((n_out,)),
            ],
        )


class PlaneSum:
    def __init__(self, blocks, out, scratch):
        self.out = out
        self.halves = [
            HalfSum(blocks, h, scratch[9 * h : 9 * h + 4], scratch[9 * h + 4 : 9 * h + 9])
            for h in range(2)
        ]

    def start(self):
        for half in self.halves:
            half.start()

    def middle(self):
        for half in self.halves:
            half.middle()

    def end(self):
        for h, half in enumerate(self.halves):
            half.end(self.out.at[h])

    @staticmethod
    def scratch(rows, width):
        both = [HalfSum.scratch(h, rows, width) for h in range(2)]
        return both[0][0] + both[0][1] + both[1][0] + both[1][1]


def full(shape):
    return pl.BlockSpec(shape, lambda g: (0,) * len(shape))


def turn(value, cos, sin):
    return value * cos + pltpu.roll(value, HD // 2, 1) * sin


def project_qkv_body(x_ref, w_ref, gain_ref, bias_ref, cos_ref, sin_ref, n_ref, q_ref, kv_ref):
    rows = x_ref.shape[0] * x_ref.shape[2]
    width = x_ref.shape[3]
    col = q_ref.shape[2]
    normal, _ = rms_parts(x_ref[...].reshape(rows, width).astype(F32))
    normed = (normal * gain_ref[...]).astype(BF)
    n_ref[...] = normed.reshape(n_ref.shape)
    lin = project(normed, w_ref[...]) + bias_ref[...]
    cos, sin = cos_ref[0], sin_ref[0]
    for h in range(col // HD):
        at = slice(h * HD, (h + 1) * HD)
        q_ref[0, :, at] = turn(lin[:, at], cos, sin).astype(BF)
        head = lin[:, col + h * HD : col + (h + 1) * HD]
        kv_ref[0, 0, :, at] = turn(head, cos, sin).astype(BF)
    kv_ref[1, 0] = lin[:, 2 * col :].astype(BF)


def project_qkv(x_all, w_qkv, gain, bias, cos, sin):
    cores, line, tok, width = x_all.shape
    col = w_qkv.shape[1] // 3
    rows = cores * tok
    tokens = pl.BlockSpec((cores, 1, tok, width), lambda g: (0, g, 0, 0))
    table = pl.BlockSpec((1, rows, HD), lambda g: (g, 0, 0))
    return pl.pallas_call(
        project_qkv_body,
        grid=(line,),
        out_shape=(
            jax.ShapeDtypeStruct(x_all.shape, BF),
            jax.ShapeDtypeStruct((line, rows, col), BF),
            jax.ShapeDtypeStruct((2, line, rows, col), BF),
        ),
        in_specs=[
            tokens,
            full(w_qkv.shape),
            full((1, width)),
            full((1, 3 * col)),
            table,
            table,
        ],
        out_specs=(
            tokens,
            pl.BlockSpec((1, rows, col), lambda g: (g, 0, 0)),
            pl.BlockSpec((2, 1, rows, col), lambda g: (0, g, 0, 0)),
        ),
        compiler_params=local_params(56),
        cost_estimate=cost(),
    )(x_all, w_qkv, gain[None], bias[None], cos, sin)


def local_params(mebibytes):
    return pltpu.CompilerParams(vmem_limit_bytes=mebibytes * 2**20)


def head_probs(query, keys, allowed):
    scores = project_t(query, keys) * (HD**-0.5)
    scores = jnp.where(allowed, scores, NEGATIVE)
    weights = jnp.exp(scores - jnp.max(scores, -1, keepdims=True))
    return weights / jnp.sum(weights, -1, keepdims=True)


def key_value(kv_ref, which):
    part = kv_ref[:, which, 0]
    return part.reshape(part.shape[0] * part.shape[1], part.shape[2])


def attend_body(q_ref, kv_ref, high_ref, low_ref, code_ref, w_ref, attn_ref, partial_ref):
    col = q_ref.shape[2]
    keys, values = key_value(kv_ref, 0), key_value(kv_ref, 1)
    allowed = (code_ref[0] <= high_ref[0]) & (code_ref[0] >= low_ref[0])
    outs = []
    for h in range(col // HD):
        at = slice(h * HD, (h + 1) * HD)
        probs = head_probs(q_ref[0, :, at], keys[:, at], allowed).astype(BF)
        outs.append(project(probs, values[:, at]).astype(BF))
    attn = jnp.concatenate(outs, 1) if len(outs) > 1 else outs[0]
    attn_ref[...] = attn.reshape(attn_ref.shape)
    partial_ref[...] = project(attn, w_ref[...]).astype(BF).reshape(partial_ref.shape)


def attention_specs(line, rows, col, n_cx):
    return [
        pl.BlockSpec((1, rows, col), lambda g: (g, 0, 0)),
        pl.BlockSpec((n_cx, 2, 1, rows, col), lambda g: (0, 0, g, 0, 0)),
        pl.BlockSpec((1, rows, 1), lambda g: (g, 0, 0)),
        pl.BlockSpec((1, rows, 1), lambda g: (g, 0, 0)),
        pl.BlockSpec((1, 1, n_cx * rows), lambda g: (g, 0, 0)),
    ]


def attend(query, kv, codes, w_out):
    line, rows, col = query.shape
    tok, width = rows // CORES, w_out.shape[1]
    return pl.pallas_call(
        attend_body,
        grid=(line,),
        out_shape=(
            jax.ShapeDtypeStruct((CORES, line, tok, col), BF),
            jax.ShapeDtypeStruct((CORES, line, tok, width), BF),
        ),
        in_specs=attention_specs(line, rows, col, kv.shape[0]) + [full(w_out.shape)],
        out_specs=(
            pl.BlockSpec((CORES, 1, tok, col), lambda g: (0, g, 0, 0)),
            pl.BlockSpec((CORES, 1, tok, width), lambda g: (0, g, 0, 0)),
        ),
        compiler_params=local_params(56),
        cost_estimate=cost(),
    )(query, kv, *codes, w_out)


def attend_back_body(
    q_ref, kv_ref, high_ref, low_ref, code_ref, w_ref, dp_ref, cos_ref, sin_ref, dq_ref, dkv_ref
):
    col = q_ref.shape[2]
    rows = q_ref.shape[1]
    keys, values = key_value(kv_ref, 0), key_value(kv_ref, 1)
    allowed = (code_ref[0] <= high_ref[0]) & (code_ref[0] >= low_ref[0])
    d_proj = dp_ref[...].reshape(rows, dp_ref.shape[3])
    d_attn = project_t(d_proj, w_ref[...]).astype(BF)
    scale = HD**-0.5
    cos, sin = cos_ref[0], sin_ref[0]
    for h in range(col // HD):
        at = slice(h * HD, (h + 1) * HD)
        query = q_ref[0, :, at]
        weights = head_probs(query, keys[:, at], allowed)
        probs = weights.astype(BF)
        d_probs = project_t(d_attn[:, at], values[:, at])
        delta = jnp.sum(probs.astype(F32) * d_probs, -1, keepdims=True)
        d_scores = (weights * (d_probs - delta)).astype(BF)
        d_query = project(d_scores, keys[:, at]) * scale
        d_key = weight_grad(d_scores, query) * scale
        d_value = weight_grad(probs, d_attn[:, at])
        dq_ref[:, :, :, at] = (
            turn(d_query, cos, -sin).astype(BF).reshape(dq_ref.shape[:3] + (HD,))
        )
        shape = (dkv_ref.shape[0], rows, HD)
        dkv_ref[:, 0, 0, :, at] = d_key.astype(BF).reshape(shape)
        dkv_ref[:, 1, 0, :, at] = d_value.astype(BF).reshape(shape)


def attend_back(query, kv, codes, w_out, d_proj, cos, sin):
    line, rows, col = query.shape
    tok, width = rows // CORES, w_out.shape[1]
    table = pl.BlockSpec((1, rows, HD), lambda g: (g, 0, 0))
    specs = attention_specs(line, rows, col, kv.shape[0])
    return pl.pallas_call(
        attend_back_body,
        grid=(line,),
        out_shape=(
            jax.ShapeDtypeStruct((CORES, line, tok, col), BF),
            jax.ShapeDtypeStruct(kv.shape, BF),
        ),
        in_specs=specs
        + [
            full(w_out.shape),
            pl.BlockSpec((CORES, 1, tok, width), lambda g: (0, g, 0, 0)),
            table,
            table,
        ],
        out_specs=(pl.BlockSpec((CORES, 1, tok, col), lambda g: (0, g, 0, 0)), specs[1]),
        compiler_params=local_params(56),
        cost_estimate=cost(),
    )(query, kv, *codes, w_out, d_proj, cos, sin)


def qkv_back_body(
    dq_ref, own_ref, came_ref, cos_ref, sin_ref, w_ref, x_ref, d_ref, partial_ref, gain_ref, bias_ref
):
    rows = own_ref.shape[2]
    col = own_ref.shape[3]
    cos, sin = cos_ref[0], sin_ref[0]
    d_key, d_value = own_ref[0, 0].astype(F32), own_ref[1, 0].astype(F32)
    for k in range(came_ref.shape[0]):
        d_key = d_key + came_ref[k, 0, 0].astype(F32)
        d_value = d_value + came_ref[k, 1, 0].astype(F32)
    keys = [
        turn(d_key[:, h * HD : (h + 1) * HD], cos, -sin).astype(BF) for h in range(col // HD)
    ]
    d_lin = jnp.concatenate([dq_ref[...].reshape(rows, col)] + keys + [d_value.astype(BF)], 1)
    d_ref[...] = d_lin.reshape(d_ref.shape)
    partial = project_t(d_lin, w_ref[...])
    partial_ref[...] = partial.astype(BF).reshape(partial_ref.shape)
    normal, _ = rms_parts(x_ref[...].reshape(rows, x_ref.shape[3]).astype(F32))
    gain = jnp.sum(partial * normal, 0, keepdims=True)
    bias = jnp.sum(d_lin.astype(F32), 0, keepdims=True)

    @pl.when(pl.program_id(0) == 0)
    def _():
        gain_ref[...] = jnp.zeros_like(gain_ref)
        bias_ref[...] = jnp.zeros_like(bias_ref)

    gain_ref[...] += gain
    bias_ref[...] += bias


def qkv_back(d_query, own, came, cos, sin, w_qkv, x_all):
    cores, line, tok, width = x_all.shape
    _, _, rows, col = own.shape
    tokens = pl.BlockSpec((cores, 1, tok, width), lambda g: (0, g, 0, 0))
    table = pl.BlockSpec((1, rows, HD), lambda g: (g, 0, 0))
    return pl.pallas_call(
        qkv_back_body,
        grid=(line,),
        out_shape=(
            jax.ShapeDtypeStruct((cores, line, tok, 3 * col), BF),
            jax.ShapeDtypeStruct(x_all.shape, BF),
            jax.ShapeDtypeStruct((1, width), F32),
            jax.ShapeDtypeStruct((1, 3 * col), F32),
        ),
        in_specs=[
            pl.BlockSpec((cores, 1, tok, col), lambda g: (0, g, 0, 0)),
            pl.BlockSpec((2, 1, rows, col), lambda g: (0, g, 0, 0)),
            pl.BlockSpec((came.shape[0], 2, 1, rows, col), lambda g: (0, 0, g, 0, 0)),
            table,
            table,
            full(w_qkv.shape),
            tokens,
        ],
        out_specs=(
            pl.BlockSpec((cores, 1, tok, 3 * col), lambda g: (0, g, 0, 0)),
            tokens,
            full((1, width)),
            full((1, 3 * col)),
        ),
        compiler_params=local_params(56),
        cost_estimate=cost(),
    )(d_query, own, came, cos, sin, w_qkv, x_all)


def ahead_body(
    partial_ref, x_ref, gain_ref, gu_ref, sd_ref, resid_ref, all_ref, wgu_ref, wsd_ref, *rest
):
    dp, cx, _, _ = places()
    greet(line_peers() + [moved(core=1)] + plane_peers())
    bufs, sems = rest[:3], rest[3:]
    normed_ref = sems[-1]
    collect = Collect(partial_ref, *bufs, sems[0:5])
    collect.start()
    local = sems[5]
    keep = [
        pltpu.make_async_copy(gu_ref, wgu_ref.at[dp, cx], local.at[0]),
        pltpu.make_async_copy(sd_ref, wsd_ref.at[dp, cx], local.at[1]),
    ]
    for copy in keep:
        copy.start()
    gu = Plane(wgu_ref, sems[6:8], gu_ref)
    sd = Plane(wsd_ref, sems[8:10], sd_ref)
    gu.start()
    sd.start()
    total = collect.reduce()
    resid = x_ref[...].astype(F32) + total
    resid_ref[...] = resid
    normal, _ = rms_parts(resid)
    normed_ref[...] = (normal * gain_ref[...]).astype(BF)
    spread = Spread(normed_ref, all_ref, sems[10:14])
    spread.start()
    spread.forward_step(1)
    gu.forward()
    for step in range(2, lax.axis_size("exp")):
        spread.forward_step(step)
        if step == 2:
            sd.forward()
    collect.finish()
    spread.finish()
    gu.finish()
    sd.finish()
    for copy in keep:
        copy.wait()


def ahead(partial, x_own, gain, gu, sd):
    n_dp, n_cx, line = (lax.axis_size(axis) for axis in ("dp", "cx", "exp"))
    tok, width = x_own.shape
    return pl.pallas_call(
        ahead_body,
        out_shape=(
            jax.ShapeDtypeStruct((tok, width), F32),
            jax.ShapeDtypeStruct((CORES, line, tok, width), BF),
            jax.ShapeDtypeStruct((n_dp, n_cx) + gu.shape, BF),
            jax.ShapeDtypeStruct((n_dp, n_cx) + sd.shape, BF),
        ),
        in_specs=[ANY, VMEM, VMEM, ANY, ANY],
        out_specs=(VMEM, ANY, ANY, ANY),
        scratch_shapes=Collect.scratch(line, tok, width)
        + [pltpu.SemaphoreType.DMA((2,))]
        + Plane.scratch(n_dp, n_cx)
        + Plane.scratch(n_dp, n_cx)
        + Spread.scratch(line)
        + [pltpu.VMEM((tok, width), BF)],
        compiler_params=params(2, 54),
        cost_estimate=cost(),
    )(partial, x_own, gain, gu, sd)


def back_body(
    partial_ref,
    resid_ref,
    gain_ref,
    cot_ref,
    ggu_ref,
    dots_ref,
    router_ref,
    score_ref,
    small_ref,
    mix_ref,
    dn_ref,
    dr_ref,
    all_ref,
    gu_ref,
    logits_ref,
    dscore_ref,
    mixed_ref,
    *rest,
):
    greet(tp_peers() + plane_peers())
    bufs, sems = rest[:3], rest[3:]
    collect = Collect(partial_ref, *bufs, sems[0:5])
    collect.start()
    mix = Collect(mix_ref, *sems[32:35], sems[35:40])
    proj_ref = sems[9]
    gu = PlaneSum(ggu_ref, gu_ref, sems[10:28])
    dot_send, dot_recv, came_ref, keep_sem = sems[28:32]
    line = lax.axis_size("exp")
    keep = pltpu.make_async_copy(dots_ref.at[0, 0], came_ref.at[0, 0], keep_sem)
    keep.start()
    outs = [
        copy_to(
            dots_ref.at[c, k],
            came_ref.at[c, k],
            dot_send.at[c, k],
            dot_recv.at[c, k],
            moved(core=c, exp=k),
        )
        for c in range(CORES)
        for k in range(line)
        if c or k
    ]
    gu.start()
    mix.start()
    collect.send()
    mix.ready()
    keep.wait()
    for copy in outs:
        copy.wait()
    _, _, core, exp = places()
    n_experts = router_ref.shape[0]
    row = lax.broadcasted_iota(jnp.int32, router_ref.shape, 0)
    d_router = jnp.zeros(router_ref.shape, F32)
    d_score = jnp.zeros(score_ref.shape, F32)
    for c in range(CORES):
        for k in range(line):
            tile = came_ref[c, k]
            source = lax.rem(exp + line - k, line) * CORES + lax.rem(core + CORES - c, CORES)
            d_router = d_router + jnp.where(row == source, tile[0:1], 0.0)
            d_score = d_score + tile[1:2]
    score = score_ref[...]
    d_score = d_score * score * (1.0 - score)
    router = router_ref[...]
    d_logits = (router * (d_router - jnp.sum(router * d_router, 0, keepdims=True))).astype(BF)
    high = d_score.astype(BF)
    mid = (d_score - high.astype(F32)).astype(BF)
    tail = (d_score - high.astype(F32) - mid.astype(F32)).astype(BF)
    logits_ref[...] = d_logits
    dscore_ref[...] = jnp.concatenate([high, mid, tail], 0)
    extra = weight_grad(d_logits, small_ref[0:n_experts])
    for part in (high, mid, tail):
        extra = extra + weight_grad(part, small_ref[n_experts : n_experts + 1])
    normal, inverse = rms_parts(resid_ref[...])
    d_normed = collect.gather() + extra
    dn_ref[...] = d_normed
    d_hat = d_normed * gain_ref[...]
    d_resid = cot_ref[...].astype(F32) + inverse * (
        d_hat - normal * jnp.mean(d_hat * normal, 1, keepdims=True)
    )
    dr_ref[...] = d_resid
    proj_ref[...] = d_resid.astype(BF)
    spread = Spread(proj_ref, all_ref, sems[5:9])
    spread.start()
    for step in range(1, line):
        spread.forward_step(step)
        mix.send_step(line - step)
    gu.middle()
    collect.finish()
    gu.end()
    spread.finish()
    mixed_ref[...] = (resid_ref[...] + mix.gather()).astype(BF)
    mix.finish()


def back(partial, resid, gain, cot, grad_gu, dots, router, score, small, mix):
    line = lax.axis_size("exp")
    tok, width = resid.shape
    dma = pltpu.SemaphoreType.DMA
    return pl.pallas_call(
        back_body,
        out_shape=(
            jax.ShapeDtypeStruct((tok, width), F32),
            jax.ShapeDtypeStruct((tok, width), F32),
            jax.ShapeDtypeStruct((CORES, line, tok, width), BF),
            jax.ShapeDtypeStruct(grad_gu.shape[2:], BF),
            jax.ShapeDtypeStruct(router.shape, BF),
            jax.ShapeDtypeStruct((3, tok), BF),
            jax.ShapeDtypeStruct((tok, width), BF),
        ),
        in_specs=[ANY, VMEM, VMEM, VMEM, ANY, ANY, VMEM, VMEM, VMEM, ANY],
        out_specs=(VMEM, VMEM, ANY, VMEM, VMEM, VMEM, VMEM),
        scratch_shapes=Collect.scratch(line, tok, width)
        + Spread.scratch(line)
        + [pltpu.VMEM((tok, width), BF)]
        + PlaneSum.scratch(*grad_gu.shape[3:])
        + [dma((CORES, line)), dma((CORES, line)), pltpu.VMEM(dots.shape, F32), dma]
        + Collect.scratch(line, tok, width),
        compiler_params=params(3, 52 + line // 2),
        cost_estimate=cost(),
    )(partial, resid, gain, cot, grad_gu, dots, router, score, small, mix)


class Rows:
    def __init__(self, block, line):
        self.block, self.rows = block, block.shape[1] // line

    @property
    def at(self):
        return self

    def __getitem__(self, spot):
        core, exp = spot
        start = pl.multiple_of(exp * self.rows, self.rows)
        return self.block.at[core, pl.ds(start, self.rows)]


def last_body(
    partial_ref,
    gq_ref,
    go_ref,
    tot_ref,
    egu_ref,
    ed_ref,
    gsd_ref,
    out_ref,
    q_ref,
    k_ref,
    v_ref,
    wo_ref,
    sum_ref,
    eg_ref,
    eu_ref,
    edown_ref,
    sd_ref,
    *rest,
):
    dp, cx, core, exp = places()
    line = lax.axis_size("exp")
    greet(all_peers())
    collect = Collect(partial_ref, *rest[:3], rest[3:8])
    qkv_block, tots_ref, cols_ref = rest[8:11]
    qkv = PlaneSum(gq_ref, qkv_block, rest[11:29])
    wo = PlaneSum(go_ref, wo_ref, rest[29:47])
    tot_send, tot_recv, local = rest[47:50]
    columns = Columns(Rows(qkv_block, line), cols_ref, rest[50:53])
    gu_came, d_came, swap_send, swap_recv, store = rest[53:58]
    wide, tall = rest[58:60]
    sd = PlaneSum(gsd_ref, sd_ref, rest[60:78])
    collect.start()
    rows, down = gu_came.shape[0], d_came.shape[0]
    swaps = [
        copy_to(
            source.at[pl.ds((1 - core) * height, height)],
            target,
            swap_send.at[n],
            swap_recv.at[n],
            moved(core=1),
        )
        for n, (source, target, height) in enumerate(
            ((egu_ref, gu_came, rows), (ed_ref, d_came, down))
        )
    ]
    qkv.start()
    collect.ready()
    steps_left = list(range(line - 1, 0, -1))
    while len(steps_left) > 2:
        collect.send_step(steps_left.pop(0))
    keep = pltpu.make_async_copy(
        tot_ref.at[dp, cx, core, exp], tots_ref.at[0, 0, 0, 0], local
    )
    keep.start()
    sizes = [range(lax.axis_size(axis)) for axis in ("dp", "cx", "core", "exp")]
    outs = []
    for steps in itertools.product(*sizes):
        if any(steps):
            target = moved(*steps)
            outs.append(
                copy_to(
                    tot_ref.at[target],
                    tots_ref.at[steps],
                    tot_send.at[steps],
                    tot_recv.at[steps],
                    target,
                )
            )
    qkv.middle()
    wo.start()
    sd.start()
    collect.send_step(steps_left.pop(0))
    qkv.end()
    columns.start()
    collect.send_step(steps_left.pop(0))
    wo.middle()
    sd.middle()
    for copy in swaps:
        copy.wait_recv()
    ffe = wide.shape[3]

    def mine(at):
        piece = egu_ref[pl.ds(pl.multiple_of(core * rows + at.start, 8), at.size)].astype(F32)
        wide[0, core, at] = piece[:, :ffe]
        wide[1, core, at] = piece[:, ffe:]
        piece = gu_came[at].astype(F32)
        wide[0, 1 - core, at] = piece[:, :ffe]
        wide[1, 1 - core, at] = piece[:, ffe:]

    by_chunks(rows, mine)

    def down_rows(at):
        piece = ed_ref[pl.ds(pl.multiple_of(core * down + at.start, 8), at.size)]
        tall[core, at] = piece.astype(F32)
        tall[1 - core, at] = d_came[at].astype(F32)

    by_chunks(down, down_rows)
    stores = [
        pltpu.make_async_copy(wide.at[0], eg_ref, store.at[0]),
        pltpu.make_async_copy(wide.at[1], eu_ref, store.at[1]),
        pltpu.make_async_copy(tall, edown_ref, store.at[2]),
    ]
    for copy in stores:
        copy.start()
    out_ref[...] = collect.gather()
    wo.end()
    sd.end()
    keep.wait()
    for copy in outs:
        copy.wait()
    sum_ref[...] = jnp.sum(tots_ref[...].reshape((-1,) + tots_ref.shape[4:]), 0)
    columns.arrive()
    col = cols_ref.shape[3] // 3
    for n, target in enumerate((q_ref, k_ref, v_ref)):
        for c in range(CORES):
            for e in range(line):
                at = (e * CORES + c) * col
                target[:, at : at + col] = cols_ref[c, e, :, n * col : (n + 1) * col].astype(F32)
    columns.finish()
    collect.finish()
    for copy in swaps:
        copy.wait_send()
    for copy in stores:
        copy.wait()


def last(partial, grad_qkv, grad_out, totals, grad_egu, grad_edown, grad_sd):
    n_dp, n_cx, line = (lax.axis_size(axis) for axis in ("dp", "cx", "exp"))
    tok, width = partial.shape[2:]
    dma = pltpu.SemaphoreType.DMA
    shard = grad_qkv.shape[3] // line
    rows, both = grad_egu.shape
    down = grad_edown.shape[0]
    heads = jax.ShapeDtypeStruct((shard, width), F32)
    wide = (CORES, rows // 2, both // 2)
    tall = (CORES, down // 2, width)
    return pl.pallas_call(
        last_body,
        out_shape=(
            jax.ShapeDtypeStruct((tok, width), F32),
            heads,
            heads,
            heads,
            jax.ShapeDtypeStruct(grad_out.shape[2:], F32),
            jax.ShapeDtypeStruct(totals.shape[4:], F32),
            jax.ShapeDtypeStruct(wide, F32),
            jax.ShapeDtypeStruct(wide, F32),
            jax.ShapeDtypeStruct(tall, F32),
            jax.ShapeDtypeStruct(grad_sd.shape[2:], F32),
        ),
        in_specs=[ANY, ANY, ANY, ANY, VMEM, VMEM, ANY],
        out_specs=(VMEM,) * 6 + (ANY,) * 3 + (VMEM,),
        scratch_shapes=Collect.scratch(line, tok, width)
        + [
            pltpu.VMEM(grad_qkv.shape[2:], BF),
            pltpu.VMEM(totals.shape, F32),
            pltpu.VMEM((CORES, line, shard, grad_qkv.shape[4]), BF),
        ]
        + PlaneSum.scratch(*grad_qkv.shape[3:])
        + PlaneSum.scratch(*grad_out.shape[3:])
        + [dma((n_dp, n_cx, CORES, line)), dma((n_dp, n_cx, CORES, line)), dma]
        + Columns.scratch(line)
        + [
            pltpu.VMEM((rows // 2, both), BF),
            pltpu.VMEM((down // 2, width), BF),
            dma((2,)),
            dma((2,)),
            dma((3,)),
            pltpu.VMEM((2,) + wide, F32),
            pltpu.VMEM(tall, F32),
        ]
        + PlaneSum.scratch(*grad_sd.shape[3:]),
        compiler_params=params(4, 50 + line // 2),
        cost_estimate=cost(),
    )(partial, grad_qkv, grad_out, totals, grad_egu, grad_edown, grad_sd)


def on_device(
    tokens,
    cotangent,
    positions,
    lengths,
    routes,
    norm_attn,
    w_query,
    bias_query,
    w_key,
    bias_key,
    w_value,
    bias_value,
    w_output,
    norm_moe,
    w_router,
    w_shared_gate,
    w_shared_up,
    w_shared_down,
    w_shared_score,
    w_expert_gate,
    w_expert_up,
    w_expert_down,
):
    n_dp = lax.axis_size("dp")
    n_cx = lax.axis_size("cx")
    n_exp = lax.axis_size("exp")
    exp_at = lax.axis_index("exp")
    core_at = lax.axis_index("core")
    n_tp = CORES * n_exp
    n_data = n_dp * n_cx
    tok, width = tokens.shape[2:]
    shard = w_query.shape[0]
    block = CORES * n_exp * shard
    col = width // n_tp
    heads = col // HD
    n_experts = w_router.shape[1]
    sub = w_shared_down.shape[0]
    sub_width = n_data * sub
    every = tok * n_tp
    scale = HD ** (-0.5)
    top = routes.shape[3]
    ffe = w_expert_gate.shape[2]

    def by_core(first, second):
        return jnp.where(core_at == 0, first, second)

    x_own = tokens.reshape(tok, width)
    cot_own = cotangent.reshape(tok, width)

    small = jnp.concatenate(
        [
            norm_attn[None],
            norm_moe[None],
            w_shared_score[None],
            bias_query[None],
            bias_key[None],
            bias_value[None],
            w_router.T,
        ]
    ).astype(F32)
    n_small = small.shape[0]
    pack = jnp.concatenate(
        [
            positions.reshape(1, tok),
            routes.reshape(tok, top).T,
            jnp.pad(lengths.reshape(1, -1), ((0, 0), (0, tok - lengths.shape[2]))),
        ]
    ).astype(F32)
    pack = jnp.concatenate([pack, jnp.pad(small, ((0, 0), (0, tok - shard)))])
    pack = jnp.pad(pack, ((0, -pack.shape[0] % 8), (0, 0)))

    def exchange(value):
        return lax.all_to_all(value, ("core", "exp"), split_axis=0, concat_axis=0, tiled=True)

    def head_columns(value):
        parts = value.reshape(shard, n_exp, CORES, col)
        return jnp.transpose(parts, (2, 1, 0, 3))

    qkv_cols = jnp.concatenate(
        [head_columns(w_query), head_columns(w_key), head_columns(w_value)], 3
    )
    x_all, w_qkv, wo_all, packs, cot_tok = load(x_own, qkv_cols, w_output, pack, cot_own)
    w_egu = lax.all_gather(
        jnp.concatenate([w_expert_gate, w_expert_up], 2), ("dp", "cx", "core"), axis=1, tiled=True
    )
    w_edown = lax.all_gather(w_expert_down, ("dp", "cx", "core"), axis=1, tiled=True)
    w_egu = lax.dynamic_index_in_dim(w_egu, core_at, 0, keepdims=False)
    w_edown = lax.dynamic_index_in_dim(w_edown, core_at, 0, keepdims=False)
    w_qkv = w_qkv.reshape(width, 3 * col)
    gu_cols = split_hidden(w_shared_gate, w_shared_up, n_exp, sub)

    small = packs[:, :, :, :, 2 + top : 2 + top + n_small, :shard]
    small = jnp.moveaxis(small, 4, 0).reshape(n_small, width)
    gain_attn = small[0]
    gain_moe = small[1]
    score_vec = small[2]
    router_full = small[6:].T.astype(BF)
    rank = exp_at * CORES + core_at
    biases = lax.dynamic_slice_in_dim(small[3:6], rank * col, col, 1).reshape(3 * col)

    ints = lax.dynamic_index_in_dim(packs, lax.axis_index("dp"), 0, keepdims=False)
    ints = ints[:, :, :, : 2 + top]
    for dim, axis in enumerate(("cx", "core", "exp")):
        ints = roll_to_relative(ints, axis, dim)
    ints = ints.astype(jnp.int32)
    route_tok = jnp.swapaxes(ints[0, :, :, 1 : 1 + top], 2, 3).reshape(every, top)
    seq_lens = ints[0, 0, :, 1 + top, : lengths.shape[2]]
    seq_ends = jnp.cumsum(seq_lens, 1)
    pos_keys = jnp.moveaxis(ints[:, :, :, 0], 2, 0).reshape(n_exp, n_cx * CORES * tok)
    after_end = (pos_keys[:, :, None] >= seq_ends[:, None, :]).astype(jnp.int32)
    seg_keys = jnp.sum(after_end, 2)
    rel_keys = pos_keys - jnp.sum(after_end * seq_lens[:, None, :], 2)
    own_keys = CORES * tok
    code_keys = (seg_keys * 4096 + pos_keys)[:, None, :]
    low = (seg_keys[:, :own_keys] * 4096)[:, :, None]
    codes = (low + pos_keys[:, :own_keys, None], low, code_keys)
    freq = ROTARY_BASE ** (-(jnp.arange(HD // 2, dtype=F32) * 2.0 / HD))
    angle = rel_keys[:, :own_keys].astype(F32)[:, :, None] * freq
    cos_table = jnp.cos(angle)
    sin_table = jnp.sin(angle)
    cos_table = jnp.concatenate([cos_table, cos_table], 2)
    sin_table = jnp.concatenate([-sin_table, sin_table], 2)

    normed_one, query, kv = project_qkv(x_all, w_qkv, gain_attn, biases, cos_table, sin_table)
    normed_one = normed_one.reshape(every, width)
    kv_all, gu_block, w_out = keys_call(kv, gu_cols, wo_all)
    w_out = w_out.reshape(col, width)
    attn_low, partial = attend(query, kv_all, codes, w_out)
    resid, normed_two, w_sgu, w_sdown = ahead(
        partial,
        x_own,
        gain_moe[None],
        gu_block,
        w_shared_down.reshape(2, sub // 2, width),
    )
    normed_two = normed_two.reshape(every, width)
    normed_two_own = normed_two[:tok]
    w_sgu = w_sgu.reshape(width, 2 * sub_width)
    w_sdown = w_sdown.reshape(sub_width, width)

    small_cols = jnp.concatenate([router_full, score_vec.astype(BF)[:, None]], 1)
    small_out = project(normed_two, small_cols)
    router_all = jax.nn.softmax(small_out[:, :n_experts], axis=-1)
    score_all = jax.nn.sigmoid(small_out[:, n_experts])
    chosen = jnp.any(route_tok == rank, axis=1)
    at_rank = (jnp.arange(n_experts) == rank).astype(F32)
    gate = jnp.where(chosen, jnp.sum(router_all * at_rank[None, :], 1), 0.0)

    shared_pre = project(normed_two, w_sgu)
    s_gate = shared_pre[:, :sub_width]
    s_up = shared_pre[:, sub_width:]
    s_act, s_slope = silu_parts(s_gate)
    s_hidden = (s_act * s_up).astype(BF)
    shared = project(s_hidden, w_sdown)
    normed_late, shared = lax.optimization_barrier((normed_two, shared))
    expert_pre = project(normed_late, w_egu)
    cot_all = cot_tok.reshape(every, width).astype(F32)
    e_gate = expert_pre[:, :ffe]
    e_up = expert_pre[:, ffe:]
    e_act, e_slope = silu_parts(e_gate)
    e_hidden = (e_act * e_up).astype(BF)
    e_out = project(e_hidden, w_edown).astype(BF).astype(F32)
    mix = (score_all[:, None] * shared + gate[:, None] * e_out).astype(BF)
    dots = jnp.stack(
        [
            jnp.where(chosen, jnp.sum(cot_all * e_out, 1), 0.0),
            jnp.sum(cot_all * shared, 1),
        ]
    )

    mix, gate = lax.optimization_barrier((mix, gate))
    d_eout = (gate[:, None] * cot_all).astype(BF)
    d_eh = project_t(d_eout, w_edown)
    d_egu = jnp.concatenate(
        [(d_eh * e_up * e_slope).astype(BF), (d_eh * e_act).astype(BF)], 1
    )
    grad_egu = weight_grad(normed_two, d_egu).astype(BF)
    grad_edown = weight_grad(e_hidden, d_eout).astype(BF)
    score_back, grad_egu, grad_edown = lax.optimization_barrier((score_all, grad_egu, grad_edown))
    grad_egu = lax.psum_scatter(grad_egu, ("dp", "cx"), scatter_dimension=0, tiled=True)
    grad_edown = lax.psum_scatter(grad_edown, ("dp", "cx"), scatter_dimension=0, tiled=True)
    d_shared = (score_back[:, None] * cot_all).astype(BF)
    d_sh = project_t(d_shared, w_sdown)
    d_sgu = jnp.concatenate(
        [(d_sh * s_up * s_slope).astype(BF), (d_sh * s_act).astype(BF)], 1
    )
    partial_two = (project_t(d_sgu, w_sgu) + project_t(d_egu, w_egu)).astype(BF)
    grad_sdown = weight_grad(s_hidden, d_shared).astype(BF)
    grad_sgu = weight_grad(normed_two, d_sgu).astype(BF)

    dots = jnp.pad(dots.reshape(2, n_tp, tok).swapaxes(0, 1), ((0, 0), (0, 6), (0, 0)))
    d_normed_two, d_resid, d_proj, grad_sgu, d_logits, d_score, mixed = back(
        partial_two.reshape(CORES, n_exp, tok, width),
        resid,
        gain_moe[None],
        cot_own,
        grad_sgu.reshape(n_dp, n_cx, 2, -1, 2 * sub_width),
        dots.reshape(CORES, n_exp, 8, tok),
        router_all[:tok].T,
        score_all[None, :tok],
        jnp.concatenate([router_full.T, score_vec.astype(BF)[None]]),
        mix.reshape(CORES, n_exp, tok, width),
    )
    grad_router = project(d_logits, normed_two_own)
    grad_score = project(d_score, normed_two_own).sum(0)
    grad_gain_moe = jnp.sum(d_normed_two * rms_parts(resid)[0], 0)

    grad_sgu = exchange(grad_sgu.reshape(n_tp, shard, 2 * sub_width))
    grad_sgu = grad_sgu.reshape(CORES, n_exp, shard, 2 * sub_width)

    d_query, d_kv = attend_back(query, kv_all, codes, w_out, d_proj, cos_table, sin_table)
    came = jnp.stack([push(d_kv[k], "cx", k) for k in range(1, n_cx)])
    came, grad_sgu = lax.optimization_barrier((came, grad_sgu))
    d_qkv, partial_one, grad_gain_attn, grad_bias = qkv_back(
        d_query, d_kv[0], came, cos_table, sin_table, w_qkv, x_all
    )
    grad_qkv = weight_grad(normed_one, d_qkv.reshape(every, 3 * col)).astype(BF)
    grad_out = lax.all_to_all(
        weight_grad(attn_low.reshape(every, col), d_proj.reshape(every, width))
        .astype(BF)
        .reshape(n_exp, shard, width),
        "exp",
        split_axis=0,
        concat_axis=0,
        tiled=True,
    )
    grad_bias = lax.dynamic_update_slice_in_dim(
        jnp.zeros((3, width), F32), grad_bias.reshape(3, col), rank * col, 1
    )
    totals = jnp.concatenate(
        [
            grad_gain_attn,
            grad_gain_moe[None],
            grad_score[None],
            grad_bias,
            grad_router,
        ]
    )
    totals = jnp.moveaxis(totals.reshape(n_small, n_data * n_tp, shard), 0, 1)
    totals = totals.reshape(n_data * n_tp, -1)
    totals = jnp.pad(totals, ((0, 0), (0, -totals.shape[1] % 1024)))
    grad_sgate, grad_sup = merge_hidden(grad_sgu, sub)
    partial_one, grad_sgate, grad_sup = lax.optimization_barrier(
        (partial_one, grad_sgate, grad_sup)
    )
    (
        d_normed_one,
        grad_query,
        grad_key,
        grad_value,
        grad_out,
        totals,
        grad_egate,
        grad_eup,
        grad_edown,
        grad_sdown,
    ) = last(
        partial_one,
        grad_qkv.reshape(n_dp, n_cx, 2, -1, 3 * col),
        grad_out.reshape(n_dp, n_cx, 2, shard // 2, width),
        totals.reshape(n_dp, n_cx, CORES, n_exp, -1, 128),
        grad_egu,
        grad_edown,
        grad_sdown.reshape(n_dp, n_cx, 2, -1, width),
    )
    grad_sdown = grad_sdown.reshape(sub, width)
    grad_out = grad_out.reshape(shard, width)
    totals = totals.reshape(-1)[: n_small * shard].reshape(n_small, shard)
    normal_own, inverse_own = rms_parts(x_own.astype(F32))
    d_hat_one = d_normed_one * gain_attn
    from_attn = inverse_own * (
        d_hat_one - normal_own * jnp.mean(d_hat_one * normal_own, 1, keepdims=True)
    )
    grad_tokens = (d_resid + from_attn).astype(BF)

    return (
        mixed.reshape(tokens.shape),
        grad_tokens.reshape(tokens.shape),
        totals[0],
        grad_query,
        totals[3],
        grad_key,
        totals[4],
        grad_value,
        totals[5],
        grad_out,
        totals[1],
        totals[6:].T,
        grad_sgate,
        grad_sup,
        grad_sdown,
        totals[2],
        grad_egate,
        grad_eup,
        grad_edown,
    )


def solution(mesh):
    sizes = dict(mesh.shape)
    fine = Mesh(
        mesh.devices.reshape(sizes["dp"], sizes["ctx"] // CORES, CORES, sizes["exp"]),
        ("dp", "cx", "core", "exp"),
    )
    own = P("dp", "exp", ("cx", "core"), None)
    flat = P(("dp", "cx", "core", "exp"))
    rows = P(("dp", "cx", "core", "exp"), None)
    expert = P("exp", ("dp", "cx", "core"), None)
    placed = (
        own,
        own,
        P("dp", "exp", ("cx", "core")),
        P("dp", "exp", None),
        own,
        flat,
        rows,
        flat,
        rows,
        flat,
        rows,
        flat,
        rows,
        flat,
        rows,
        rows,
        rows,
        rows,
        flat,
        expert,
        expert,
        expert,
    )
    return jax.shard_map(
        on_device,
        mesh=fine,
        in_specs=placed,
        out_specs=(
            own,
            own,
            flat,
            rows,
            flat,
            rows,
            flat,
            rows,
            flat,
            rows,
            flat,
            rows,
            rows,
            rows,
            rows,
            flat,
            expert,
            expert,
            expert,
        ),
        check_vma=False,
    )
```

```python
import itertools

import jax
import jax.numpy as jnp
from jax import lax
from jax.experimental import pallas as pl
from jax.experimental.pallas import tpu as pltpu
from jax.sharding import Mesh
from jax.sharding import PartitionSpec as P

HD = 128
CORES = 2
EPSILON = 1e-06
ROTARY_BASE = 1000000.0
NEGATIVE = -1e30
BF = jnp.bfloat16
F32 = jnp.float32


def project(left, right):
    return jnp.dot(left, right, preferred_element_type=F32)


def project_t(left, right):
    return lax.dot_general(left, right, (((1,), (1,)), ((), ())), preferred_element_type=F32)


def weight_grad(left, right):
    return lax.dot_general(left, right, (((0,), (0,)), ((), ())), preferred_element_type=F32)


def held(value):
    return lax.optimization_barrier(value.astype(BF)).astype(F32)


def rms_parts(value):
    inverse = lax.rsqrt(jnp.mean(value * value, axis=-1, keepdims=True) + EPSILON)
    return (value * inverse, inverse)


def silu_parts(value):
    sigmoid = jax.nn.sigmoid(value)
    return (value * sigmoid, sigmoid * (1.0 + value * (1.0 - sigmoid)))


def fetch(value, axis, step):
    size = lax.axis_size(axis)
    if step % size == 0:
        return value
    return lax.ppermute(value, axis, [((i + step) % size, i) for i in range(size)])


def push(value, axis, step):
    size = lax.axis_size(axis)
    return lax.ppermute(value, axis, [(i, (i + step) % size) for i in range(size)])


def roll_to_relative(value, axis, dim):
    size = lax.axis_size(axis)
    both = lax.concatenate([value, value], dim)
    return lax.dynamic_slice_in_dim(both, lax.axis_index(axis), size, dim)


MESH = pl.DeviceIdType.MESH
ANY = pl.BlockSpec(memory_space=pltpu.HBM)
VMEM = pl.BlockSpec(memory_space=pltpu.VMEM)


def places():
    return tuple(lax.axis_index(axis) for axis in ("dp", "cx", "core", "exp"))


def moved(dp=0, cx=0, core=0, exp=0):
    steps = (dp, cx, core, exp)
    return tuple(
        at if step == 0 else lax.rem(at + step, lax.axis_size(axis))
        for at, step, axis in zip(places(), steps, ("dp", "cx", "core", "exp"))
    )


def copy_to(source, target, send_sem, recv_sem, device):
    copy = pltpu.make_async_remote_copy(
        src_ref=source,
        dst_ref=target,
        send_sem=send_sem,
        recv_sem=recv_sem,
        device_id=device,
        device_id_type=MESH,
    )
    copy.start()
    return copy


def greet(devices):
    barrier = pltpu.get_barrier_semaphore()
    for device in devices:
        pl.semaphore_signal(barrier, inc=1, device_id=device, device_id_type=MESH)
    pl.semaphore_wait(barrier, len(devices))


def line_peers():
    return [moved(exp=k) for k in range(1, lax.axis_size("exp"))]


def plane_peers():
    steps = [(j, k) for j in range(lax.axis_size("dp")) for k in range(lax.axis_size("cx"))]
    return [moved(dp=j, cx=k) for j, k in steps[1:]]


class Spread:
    def __init__(self, source, out, sems):
        self.source, self.out = source, out
        self.up, self.down, self.over, self.local = sems
        self.line = lax.axis_size("exp")
        self.at = lax.axis_index("exp")

    def hop(self, step, way):
        slot = (self.line - step) % self.line if way > 0 else step
        landing = self.line - step - 1 if way > 0 else step + 1
        sems = self.up if way > 0 else self.down
        return pltpu.make_async_remote_copy(
            src_ref=self.source if step == 0 else self.out.at[0, slot],
            dst_ref=self.out.at[0, landing],
            send_sem=sems.at[0, step],
            recv_sem=sems.at[1, step + 1],
            device_id=moved(exp=1 if way > 0 else self.line - 1),
            device_id_type=MESH,
        )

    def sends(self, step, way):
        if way > 0:
            return jnp.logical_and(self.at >= step, self.at < self.line - 1)
        return jnp.logical_and(self.at + step <= self.line - 1, self.at > 0)

    def gets(self, step, way):
        return self.at >= step if way > 0 else self.at + step <= self.line - 1

    def across(self, slot):
        return pltpu.make_async_remote_copy(
            src_ref=self.source if slot == 0 else self.out.at[0, slot],
            dst_ref=self.out.at[1, slot],
            send_sem=self.over.at[0, slot],
            recv_sem=self.over.at[1, slot],
            device_id=moved(core=1),
            device_id_type=MESH,
        )

    def start(self):
        self.keep = pltpu.make_async_copy(self.source, self.out.at[0, 0], self.local)
        self.keep.start()
        for way in (1, -1):
            pl.when(self.sends(0, way))(self.hop(0, way).start)
        self.across(0).start()

    def forward(self):
        for step in range(1, self.line):
            self.forward_step(step)

    def forward_step(self, step):
        for way in (1, -1):
            slot = self.line - step if way > 0 else step

            @pl.when(self.gets(step, way))
            def _():
                self.hop(step - 1, way).wait_recv()
                self.across(slot).start()

            if step < self.line - 1:
                pl.when(self.sends(step, way))(self.hop(step, way).start)

    def finish(self):
        self.keep.wait()
        for step in range(self.line - 1):
            for way in (1, -1):
                pl.when(self.sends(step, way))(self.hop(step, way).wait_send)
        for slot in range(self.line):
            self.across(slot).wait()

    @staticmethod
    def scratch(line):
        return [
            pltpu.SemaphoreType.DMA((2, line)),
            pltpu.SemaphoreType.DMA((2, line)),
            pltpu.SemaphoreType.DMA((2, line)),
            pltpu.SemaphoreType.DMA,
        ]


class Columns:
    def __init__(self, cols, out, sems):
        self.cols, self.out, self.sems = cols, out, sems

    def start(self):
        send, recv, local = self.sems
        line = lax.axis_size("exp")
        _, _, core, exp = places()
        self.local = pltpu.make_async_copy(
            self.cols.at[core, exp], self.out.at[core, exp], local
        )
        self.local.start()
        self.copies = []
        for c in range(CORES):
            for k in range(line):
                if c or k:
                    target = moved(core=c, exp=k)
                    self.copies.append(
                        copy_to(
                            self.cols.at[target[2], target[3]],
                            self.out.at[core, exp],
                            send.at[c, k],
                            recv.at[c, k],
                            target,
                        )
                    )

    def arrive(self):
        self.local.wait()
        for copy in self.copies:
            copy.wait_recv()

    def finish(self):
        for copy in self.copies:
            copy.wait_send()

    @staticmethod
    def scratch(line):
        return [
            pltpu.SemaphoreType.DMA((CORES, line)),
            pltpu.SemaphoreType.DMA((CORES, line)),
            pltpu.SemaphoreType.DMA,
        ]


class Plane:
    def __init__(self, out, sems, source=None):
        self.out, self.sems, self.source = out, sems, source
        self.n = (lax.axis_size("dp"), lax.axis_size("cx"))

    def send(self, half, j, k, dp, cx):
        send, recv = self.sems
        at = places()
        n_dp, n_cx = self.n
        from_dp = lax.rem(at[0] + n_dp - j, n_dp)
        from_cx = lax.rem(at[1] + n_cx - k, n_cx)
        block = self.out.at[from_dp, from_cx, half]
        a, b = j + dp, k + cx
        first = self.source is not None and j == 0 and k == 0
        origin = self.source.at[half] if first else block
        return copy_to(
            origin, block, send.at[half, a, b], recv.at[half, a, b], moved(dp=dp, cx=cx)
        )

    def start(self):
        n_dp, n_cx = self.n
        self.along_cx = [[self.send(h, 0, 0, 0, k) for k in range(1, n_cx)] for h in range(2)]
        self.along_dp = [[self.send(h, 0, 0, j, 0) for j in range(1, n_dp)] for h in range(2)]

    def forward(self):
        n_dp, n_cx = self.n
        self.rest = []
        for k in range(1, n_cx):
            self.along_cx[0][k - 1].wait_recv()
            for j in range(1, n_dp):
                self.rest.append(self.send(0, 0, k, j, 0))
        for j in range(1, n_dp):
            self.along_dp[1][j - 1].wait_recv()
            for k in range(1, n_cx):
                self.rest.append(self.send(1, j, 0, 0, k))

    def finish(self):
        for copy in self.along_cx[1] + self.along_dp[0] + self.rest:
            copy.wait()
        for copy in self.along_cx[0] + self.along_dp[1]:
            copy.wait_send()

    @staticmethod
    def scratch(n_dp, n_cx):
        return [
            pltpu.SemaphoreType.DMA((2, n_dp, n_cx)),
            pltpu.SemaphoreType.DMA((2, n_dp, n_cx)),
        ]


def params(number, mebibytes):
    return pltpu.CompilerParams(
        collective_id=number, has_side_effects=True, vmem_limit_bytes=mebibytes * 2**20
    )


def cost():
    return pl.CostEstimate(flops=1, bytes_accessed=1, transcendentals=0)


def tp_peers():
    line = lax.axis_size("exp")
    steps = [(c, k) for c in range(CORES) for k in range(line)]
    return [moved(core=c, exp=k) for c, k in steps[1:]]


def all_peers():
    sizes = [range(lax.axis_size(axis)) for axis in ("dp", "cx", "core", "exp")]
    return [moved(*steps) for steps in itertools.product(*sizes) if any(steps)]


def load_body(
    x_ref,
    cols_ref,
    wo_ref,
    pack_ref,
    cot_ref,
    xall_ref,
    wqkv_ref,
    woall_ref,
    packs_ref,
    cotall_ref,
    *sems,
):
    dp, cx, core, exp = places()
    greet(all_peers())
    tokens = Spread(x_ref, xall_ref, sems[0:4])
    block = wqkv_ref.at[dp, cx]
    columns = Columns(cols_ref, block, sems[4:7])
    plane = Plane(wqkv_ref, sems[7:9])
    send, recv, local = sems[9:12]
    columns.start()
    own = [
        pltpu.make_async_copy(wo_ref, woall_ref.at[dp, cx], local.at[0]),
        pltpu.make_async_copy(pack_ref, packs_ref.at[dp, cx, core, exp], local.at[1]),
    ]
    for copy in own:
        copy.start()
    pack_send, pack_recv = sems[12:14]
    sizes = [range(lax.axis_size(axis)) for axis in ("dp", "cx", "core", "exp")]
    outs = [
        copy_to(
            pack_ref,
            packs_ref.at[dp, cx, core, exp],
            pack_send.at[steps],
            pack_recv.at[steps],
            moved(*steps),
        )
        for steps in itertools.product(*sizes)
        if any(steps)
    ]
    cotangent = Spread(cot_ref, cotall_ref, sems[14:18])
    columns.arrive()
    tokens.start()
    plane.start()
    tokens.forward()
    cotangent.start()
    plane.forward()
    for j in range(lax.axis_size("dp")):
        for k in range(lax.axis_size("cx")):
            if j or k:
                outs.append(
                    copy_to(
                        wo_ref,
                        woall_ref.at[dp, cx],
                        send.at[j, k],
                        recv.at[j, k],
                        moved(dp=j, cx=k),
                    )
                )
    cotangent.forward()
    columns.finish()
    tokens.finish()
    plane.finish()
    cotangent.finish()
    for copy in own + outs:
        copy.wait()


def load(x_own, cols, w_output, pack, cot_own):
    n_dp, n_cx, line = (lax.axis_size(axis) for axis in ("dp", "cx", "exp"))
    return pl.pallas_call(
        load_body,
        out_shape=(
            jax.ShapeDtypeStruct((CORES, line) + x_own.shape, BF),
            jax.ShapeDtypeStruct((n_dp, n_cx) + cols.shape, BF),
            jax.ShapeDtypeStruct((n_dp, n_cx) + w_output.shape, BF),
            jax.ShapeDtypeStruct((n_dp, n_cx, CORES, line) + pack.shape, F32),
            jax.ShapeDtypeStruct((CORES, line) + cot_own.shape, BF),
        ),
        in_specs=[ANY] * 5,
        out_specs=(ANY,) * 5,
        scratch_shapes=Spread.scratch(line)
        + Columns.scratch(line)
        + Plane.scratch(n_dp, n_cx)
        + [
            pltpu.SemaphoreType.DMA((n_dp, n_cx)),
            pltpu.SemaphoreType.DMA((n_dp, n_cx)),
            pltpu.SemaphoreType.DMA((2,)),
            pltpu.SemaphoreType.DMA((n_dp, n_cx, CORES, line)),
            pltpu.SemaphoreType.DMA((n_dp, n_cx, CORES, line)),
        ]
        + Spread.scratch(line),
        compiler_params=params(0, 58),
        cost_estimate=cost(),
    )(x_own, cols, w_output, pack, cot_own)


def keys_body(kv_ref, cols_ref, wo_ref, kvall_ref, gu_ref, wout_ref, *sems):
    _, _, _, exp = places()
    n_cx = lax.axis_size("cx")
    line = lax.axis_size("exp")
    greet(tp_peers() + [moved(cx=k) for k in range(1, n_cx)])
    send, recv, local = sems[3:6]
    own = pltpu.make_async_copy(kv_ref, kvall_ref.at[0], local)
    own.start()
    keys = [
        copy_to(kv_ref, kvall_ref.at[n_cx - k], send.at[k], recv.at[k], moved(cx=k))
        for k in range(1, n_cx)
    ]
    columns = Columns(cols_ref, gu_ref, sems[0:3])
    columns.start()
    send, recv, local = sems[6:9]
    keep = pltpu.make_async_copy(wo_ref.at[exp // n_cx, exp % n_cx], wout_ref.at[exp], local)
    keep.start()
    outs = []
    for k in range(1, line):
        target = moved(exp=k)
        at = target[3]
        outs.append(
            copy_to(
                wo_ref.at[at // n_cx, at % n_cx],
                wout_ref.at[exp],
                send.at[k],
                recv.at[k],
                target,
            )
        )
    own.wait()
    keep.wait()
    columns.arrive()
    columns.finish()
    for copy in keys + outs:
        copy.wait()


def keys_call(kv, cols, wo_all):
    n_cx, line = lax.axis_size("cx"), lax.axis_size("exp")
    return pl.pallas_call(
        keys_body,
        out_shape=(
            jax.ShapeDtypeStruct((n_cx,) + kv.shape, BF),
            jax.ShapeDtypeStruct(cols.shape, BF),
            jax.ShapeDtypeStruct((line,) + wo_all.shape[2:], BF),
        ),
        in_specs=[ANY] * 3,
        out_specs=(ANY,) * 3,
        scratch_shapes=Columns.scratch(line)
        + [
            pltpu.SemaphoreType.DMA((n_cx,)),
            pltpu.SemaphoreType.DMA((n_cx,)),
            pltpu.SemaphoreType.DMA,
            pltpu.SemaphoreType.DMA((line,)),
            pltpu.SemaphoreType.DMA((line,)),
            pltpu.SemaphoreType.DMA,
        ],
        compiler_params=params(1, 58),
        cost_estimate=cost(),
    )(kv, cols, wo_all)


def by_chunks(rows, work):
    chunk = 16 if rows % 16 == 0 else 8

    @pl.loop(0, rows // chunk)
    def _(step):
        work(pl.ds(pl.multiple_of(step * chunk, chunk), chunk))


class Collect:
    def __init__(self, partial, kept, near, far, sems):
        self.partial, self.kept, self.near, self.far = partial, kept, near, far
        self.core_send, self.core_recv, self.hop_send, self.hop_recv, self.local = sems
        self.line = lax.axis_size("exp")
        self.at = lax.axis_index("exp")

    def start(self):
        self.swaps, self.loads = [], []
        for k in range(self.line):
            self.swaps.append(
                copy_to(
                    self.partial.at[1, k],
                    self.near.at[k],
                    self.core_send.at[k],
                    self.core_recv.at[k],
                    moved(core=1),
                )
            )
            load = pltpu.make_async_copy(self.partial.at[0, k], self.kept.at[k], self.local.at[k])
            load.start()
            self.loads.append(load)

    def hop(self, way, step):
        slot = step if way == 0 else self.line - step
        return pltpu.make_async_remote_copy(
            src_ref=self.kept.at[slot],
            dst_ref=self.far.at[way, step - 1],
            send_sem=self.hop_send.at[way, step],
            recv_sem=self.hop_recv.at[way, step - 1],
            device_id=moved(exp=1 if way == 0 else self.line - 1),
            device_id_type=MESH,
        )

    def reaches(self, way, step):
        return self.at + step <= self.line - 1 if way == 0 else self.at >= step

    def fed(self, way):
        return self.at >= 1 if way == 0 else self.at <= self.line - 2

    def ready(self):
        for load in self.loads:
            load.wait()
        for swap in self.swaps:
            swap.wait_recv()

    def pair(self, k, rows):
        return self.kept[k, rows].astype(F32) + self.near[k, rows].astype(F32)

    def send_step(self, step):
        tok = self.kept.shape[1]
        for way in range(2):
            slot = step if way == 0 else self.line - step

            @pl.when(self.reaches(way, step))
            def _():
                @pl.when(self.fed(way))
                def _():
                    self.hop(way, step + 1).wait_recv()

                    def work(rows):
                        total = self.pair(slot, rows) + self.far[way, step, rows].astype(F32)
                        self.kept[slot, rows] = total.astype(BF)

                    by_chunks(tok, work)

                @pl.when(jnp.logical_not(self.fed(way)))
                def _():
                    def work(rows):
                        self.kept[slot, rows] = self.pair(slot, rows).astype(BF)

                    by_chunks(tok, work)

                self.hop(way, step).start()

    def send(self):
        self.ready()
        for step in range(self.line - 1, 0, -1):
            self.send_step(step)

    def gather(self):
        for way in range(2):

            @pl.when(self.fed(way))
            def _():
                self.hop(way, 1).wait_recv()

            @pl.when(jnp.logical_not(self.fed(way)))
            def _():
                self.far[way, 0] = jnp.zeros(self.far.shape[2:], BF)

        return (
            self.kept[0].astype(F32)
            + self.near[0].astype(F32)
            + (self.far[0, 0].astype(F32) + self.far[1, 0].astype(F32))
        )

    def reduce(self):
        self.send()
        return self.gather()

    def finish(self):
        for swap in self.swaps:
            swap.wait_send()
        for step in range(1, self.line):
            for way in range(2):
                pl.when(self.reaches(way, step))(self.hop(way, step).wait_send)

    @staticmethod
    def scratch(line, tok, width):
        dma = pltpu.SemaphoreType.DMA
        return [
            pltpu.VMEM((line, tok, width), BF),
            pltpu.VMEM((line, tok, width), BF),
            pltpu.VMEM((2, line, tok, width), BF),
            dma((line,)),
            dma((line,)),
            dma((2, line + 1)),
            dma((2, line + 1)),
            dma((line,)),
        ]


def split_hidden(gate, up, n_exp, piece):
    shard, total = gate.shape
    blocks = total // (CORES * n_exp * piece)

    def body(gate_ref, up_ref, out_ref):
        sides = (gate_ref[...].astype(F32), up_ref[...].astype(F32))
        for c in range(CORES):
            for e in range(n_exp):
                parts = []
                for side in sides:
                    for b in range(blocks):
                        start = ((b * CORES + c) * n_exp + e) * piece
                        parts.append(side[:, start : start + piece])
                out_ref[c, e] = jnp.concatenate(parts, 1).astype(BF)

    return pl.pallas_call(
        body,
        out_shape=jax.ShapeDtypeStruct((CORES, n_exp, shard, 2 * blocks * piece), BF),
        in_specs=[VMEM, VMEM],
        out_specs=VMEM,
        compiler_params=local_params(56),
        cost_estimate=cost(),
    )(gate, up)


def merge_hidden(value, piece):
    _, n_exp, shard, both = value.shape
    blocks = both // (2 * piece)
    total = blocks * CORES * n_exp * piece

    def body(in_ref, gate_ref, up_ref):
        for side, out_ref in enumerate((gate_ref, up_ref)):
            parts = []
            for b in range(blocks):
                start = (side * blocks + b) * piece
                for c in range(CORES):
                    for e in range(n_exp):
                        parts.append(in_ref[c, e].astype(F32)[:, start : start + piece])
            out_ref[...] = jnp.concatenate(parts, 1)

    shape = jax.ShapeDtypeStruct((shard, total), F32)
    return pl.pallas_call(
        body,
        out_shape=(shape, shape),
        in_specs=[VMEM],
        out_specs=(VMEM, VMEM),
        compiler_params=local_params(56),
        cost_estimate=cost(),
    )(value)


class HalfSum:
    def __init__(self, blocks, half, bufs, sems):
        self.blocks, self.half = blocks, half
        self.own, self.came, self.sums, self.final = bufs
        self.sem = sems
        n_dp, n_cx = lax.axis_size("dp"), lax.axis_size("cx")
        self.cx_first = half == 0
        self.n_in, self.n_out = (n_cx, n_dp) if self.cx_first else (n_dp, n_cx)

    def block(self, inner, outer):
        dp, cx = (outer, inner) if self.cx_first else (inner, outer)
        at = moved(dp=dp, cx=cx)
        return self.blocks.at[at[0], at[1], self.half]

    def far(self, inner, outer):
        dp, cx = (outer, inner) if self.cx_first else (inner, outer)
        return moved(dp=dp, cx=cx)

    def start(self):
        first_send, first_recv, _, _, local = self.sem
        self.first, self.loads = {}, []
        for a in range(self.n_out):
            for b in range(1, self.n_in):
                self.first[b, a] = copy_to(
                    self.block(b, a),
                    self.came.at[b - 1, a],
                    first_send.at[b - 1, a],
                    first_recv.at[b - 1, a],
                    self.far(b, 0),
                )
            load = pltpu.make_async_copy(self.block(0, a), self.own.at[a], local.at[a])
            load.start()
            self.loads.append(load)

    def near(self, a, rows):
        total = self.own[a, rows].astype(F32)
        for b in range(1, self.n_in):
            total = total + self.came[b - 1, a, rows].astype(F32)
        return total

    def middle(self):
        _, _, send, recv, _ = self.sem
        for load in self.loads:
            load.wait()
        self.second = []
        for a in range(1, self.n_out):
            for b in range(1, self.n_in):
                self.first[b, a].wait_recv()

            def work(rows):
                self.sums[a - 1, rows] = self.near(a, rows).astype(BF)

            by_chunks(self.sums.shape[1], work)
            self.second.append(
                copy_to(
                    self.sums.at[a - 1],
                    self.final.at[a - 1],
                    send.at[a - 1],
                    recv.at[a - 1],
                    self.far(0, a),
                )
            )

    def end(self, out):
        for b in range(1, self.n_in):
            self.first[b, 0].wait_recv()
        for copy in self.second:
            copy.wait_recv()

        def work(rows):
            total = self.near(0, rows)
            for a in range(1, self.n_out):
                total = total + self.final[a - 1, rows].astype(F32)
            out[rows] = total.astype(out.dtype)

        by_chunks(self.sums.shape[1], work)
        for copy in self.first.values():
            copy.wait_send()
        for copy in self.second:
            copy.wait_send()

    @staticmethod
    def scratch(half, rows, width):
        n_dp, n_cx = lax.axis_size("dp"), lax.axis_size("cx")
        n_in, n_out = (n_cx, n_dp) if half == 0 else (n_dp, n_cx)
        dma = pltpu.SemaphoreType.DMA
        return (
            [
                pltpu.VMEM((n_out, rows, width), BF),
                pltpu.VMEM((n_in - 1, n_out, rows, width), BF),
                pltpu.VMEM((n_out - 1, rows, width), BF),
                pltpu.VMEM((n_out - 1, rows, width), BF),
            ],
            [
                dma((n_in - 1, n_out)),
                dma((n_in - 1, n_out)),
                dma((n_out - 1,)),
                dma((n_out - 1,)),
                dma((n_out,)),
            ],
        )


class PlaneSum:
    def __init__(self, blocks, out, scratch):
        self.out = out
        self.halves = [
            HalfSum(blocks, h, scratch[9 * h : 9 * h + 4], scratch[9 * h + 4 : 9 * h + 9])
            for h in range(2)
        ]

    def start(self):
        for half in self.halves:
            half.start()

    def middle(self):
        for half in self.halves:
            half.middle()

    def end(self):
        for h, half in enumerate(self.halves):
            half.end(self.out.at[h])

    @staticmethod
    def scratch(rows, width):
        both = [HalfSum.scratch(h, rows, width) for h in range(2)]
        return both[0][0] + both[0][1] + both[1][0] + both[1][1]


def full(shape):
    return pl.BlockSpec(shape, lambda g: (0,) * len(shape))


def turn(value, cos, sin):
    return value * cos + pltpu.roll(value, HD // 2, 1) * sin


def project_qkv_body(x_ref, w_ref, gain_ref, bias_ref, cos_ref, sin_ref, n_ref, q_ref, kv_ref):
    rows = x_ref.shape[0] * x_ref.shape[2]
    width = x_ref.shape[3]
    col = q_ref.shape[2]
    normal, _ = rms_parts(x_ref[...].reshape(rows, width).astype(F32))
    normed = (normal * gain_ref[...]).astype(BF)
    n_ref[...] = normed.reshape(n_ref.shape)
    lin = project(normed, w_ref[...]) + bias_ref[...]
    cos, sin = cos_ref[0], sin_ref[0]
    for h in range(col // HD):
        at = slice(h * HD, (h + 1) * HD)
        q_ref[0, :, at] = turn(lin[:, at], cos, sin).astype(BF)
        head = lin[:, col + h * HD : col + (h + 1) * HD]
        kv_ref[0, 0, :, at] = turn(head, cos, sin).astype(BF)
    kv_ref[1, 0] = lin[:, 2 * col :].astype(BF)


def project_qkv(x_all, w_qkv, gain, bias, cos, sin):
    cores, line, tok, width = x_all.shape
    col = w_qkv.shape[1] // 3
    rows = cores * tok
    tokens = pl.BlockSpec((cores, 1, tok, width), lambda g: (0, g, 0, 0))
    table = pl.BlockSpec((1, rows, HD), lambda g: (g, 0, 0))
    return pl.pallas_call(
        project_qkv_body,
        grid=(line,),
        out_shape=(
            jax.ShapeDtypeStruct(x_all.shape, BF),
            jax.ShapeDtypeStruct((line, rows, col), BF),
            jax.ShapeDtypeStruct((2, line, rows, col), BF),
        ),
        in_specs=[
            tokens,
            full(w_qkv.shape),
            full((1, width)),
            full((1, 3 * col)),
            table,
            table,
        ],
        out_specs=(
            tokens,
            pl.BlockSpec((1, rows, col), lambda g: (g, 0, 0)),
            pl.BlockSpec((2, 1, rows, col), lambda g: (0, g, 0, 0)),
        ),
        compiler_params=local_params(56),
        cost_estimate=cost(),
    )(x_all, w_qkv, gain[None], bias[None], cos, sin)


def local_params(mebibytes):
    return pltpu.CompilerParams(vmem_limit_bytes=mebibytes * 2**20)


def head_probs(query, keys, allowed):
    scores = project_t(query, keys) * (HD**-0.5)
    scores = jnp.where(allowed, scores, NEGATIVE)
    weights = jnp.exp(scores - jnp.max(scores, -1, keepdims=True))
    return weights / jnp.sum(weights, -1, keepdims=True)


def key_value(kv_ref, which):
    part = kv_ref[:, which, 0]
    return part.reshape(part.shape[0] * part.shape[1], part.shape[2])


def attend_body(q_ref, kv_ref, high_ref, low_ref, code_ref, w_ref, attn_ref, partial_ref):
    col = q_ref.shape[2]
    keys, values = key_value(kv_ref, 0), key_value(kv_ref, 1)
    allowed = (code_ref[0] <= high_ref[0]) & (code_ref[0] >= low_ref[0])
    outs = []
    for h in range(col // HD):
        at = slice(h * HD, (h + 1) * HD)
        probs = head_probs(q_ref[0, :, at], keys[:, at], allowed).astype(BF)
        outs.append(project(probs, values[:, at]).astype(BF))
    attn = jnp.concatenate(outs, 1) if len(outs) > 1 else outs[0]
    attn_ref[...] = attn.reshape(attn_ref.shape)
    partial_ref[...] = project(attn, w_ref[...]).astype(BF).reshape(partial_ref.shape)


def attention_specs(line, rows, col, n_cx):
    return [
        pl.BlockSpec((1, rows, col), lambda g: (g, 0, 0)),
        pl.BlockSpec((n_cx, 2, 1, rows, col), lambda g: (0, 0, g, 0, 0)),
        pl.BlockSpec((1, rows, 1), lambda g: (g, 0, 0)),
        pl.BlockSpec((1, rows, 1), lambda g: (g, 0, 0)),
        pl.BlockSpec((1, 1, n_cx * rows), lambda g: (g, 0, 0)),
    ]


def attend(query, kv, codes, w_out):
    line, rows, col = query.shape
    tok, width = rows // CORES, w_out.shape[1]
    return pl.pallas_call(
        attend_body,
        grid=(line,),
        out_shape=(
            jax.ShapeDtypeStruct((CORES, line, tok, col), BF),
            jax.ShapeDtypeStruct((CORES, line, tok, width), BF),
        ),
        in_specs=attention_specs(line, rows, col, kv.shape[0]) + [full(w_out.shape)],
        out_specs=(
            pl.BlockSpec((CORES, 1, tok, col), lambda g: (0, g, 0, 0)),
            pl.BlockSpec((CORES, 1, tok, width), lambda g: (0, g, 0, 0)),
        ),
        compiler_params=local_params(56),
        cost_estimate=cost(),
    )(query, kv, *codes, w_out)


def attend_back_body(
    q_ref,
    kv_ref,
    high_ref,
    low_ref,
    code_ref,
    w_ref,
    dp_ref,
    cos_ref,
    sin_ref,
    dq_ref,
    own_ref,
    far_ref,
):
    col = q_ref.shape[2]
    rows = q_ref.shape[1]
    keys, values = key_value(kv_ref, 0), key_value(kv_ref, 1)
    allowed = (code_ref[0] <= high_ref[0]) & (code_ref[0] >= low_ref[0])
    d_proj = dp_ref[...].reshape(rows, dp_ref.shape[3])
    d_attn = project_t(d_proj, w_ref[...]).astype(BF)
    scale = HD**-0.5
    cos, sin = cos_ref[0], sin_ref[0]
    for h in range(col // HD):
        at = slice(h * HD, (h + 1) * HD)
        query = q_ref[0, :, at]
        weights = head_probs(query, keys[:, at], allowed)
        probs = weights.astype(BF)
        d_probs = project_t(d_attn[:, at], values[:, at])
        delta = jnp.sum(probs.astype(F32) * d_probs, -1, keepdims=True)
        d_scores = (weights * (d_probs - delta)).astype(BF)
        d_query = project(d_scores, keys[:, at]) * scale
        d_key = weight_grad(d_scores, query) * scale
        d_value = weight_grad(probs, d_attn[:, at])
        dq_ref[:, :, :, at] = (
            turn(d_query, cos, -sin).astype(BF).reshape(dq_ref.shape[:3] + (HD,))
        )
        for which, value in enumerate((d_key, d_value)):
            own_ref[which, 0, :, at] = value[:rows].astype(BF)
            far_ref[:, which, 0, :, at] = (
                value[rows:].astype(BF).reshape((far_ref.shape[0], rows, HD))
            )


def attend_back(query, kv, codes, w_out, d_proj, cos, sin):
    line, rows, col = query.shape
    tok, width = rows // CORES, w_out.shape[1]
    table = pl.BlockSpec((1, rows, HD), lambda g: (g, 0, 0))
    specs = attention_specs(line, rows, col, kv.shape[0])
    return pl.pallas_call(
        attend_back_body,
        grid=(line,),
        out_shape=(
            jax.ShapeDtypeStruct((CORES, line, tok, col), BF),
            jax.ShapeDtypeStruct(kv.shape[1:], BF),
            jax.ShapeDtypeStruct((kv.shape[0] - 1,) + kv.shape[1:], BF),
        ),
        in_specs=specs
        + [
            full(w_out.shape),
            pl.BlockSpec((CORES, 1, tok, width), lambda g: (0, g, 0, 0)),
            table,
            table,
        ],
        out_specs=(
            pl.BlockSpec((CORES, 1, tok, col), lambda g: (0, g, 0, 0)),
            pl.BlockSpec((2, 1, rows, col), lambda g: (0, g, 0, 0)),
            pl.BlockSpec((kv.shape[0] - 1, 2, 1, rows, col), lambda g: (0, 0, g, 0, 0)),
        ),
        compiler_params=local_params(56),
        cost_estimate=cost(),
    )(query, kv, *codes, w_out, d_proj, cos, sin)


def qkv_back_body(
    dq_ref, own_ref, came_ref, cos_ref, sin_ref, w_ref, x_ref, d_ref, partial_ref, gain_ref, bias_ref
):
    rows = own_ref.shape[2]
    col = own_ref.shape[3]
    cos, sin = cos_ref[0], sin_ref[0]
    d_key, d_value = own_ref[0, 0].astype(F32), own_ref[1, 0].astype(F32)
    for k in range(came_ref.shape[0]):
        d_key = d_key + came_ref[k, 0, 0].astype(F32)
        d_value = d_value + came_ref[k, 1, 0].astype(F32)
    keys = [
        turn(d_key[:, h * HD : (h + 1) * HD], cos, -sin).astype(BF) for h in range(col // HD)
    ]
    d_lin = jnp.concatenate([dq_ref[...].reshape(rows, col)] + keys + [d_value.astype(BF)], 1)
    d_ref[...] = d_lin.reshape(d_ref.shape)
    partial = project_t(d_lin, w_ref[...])
    partial_ref[...] = partial.astype(BF).reshape(partial_ref.shape)
    normal, _ = rms_parts(x_ref[...].reshape(rows, x_ref.shape[3]).astype(F32))
    gain = jnp.sum(partial * normal, 0, keepdims=True)
    bias = jnp.sum(d_lin.astype(F32), 0, keepdims=True)

    @pl.when(pl.program_id(0) == 0)
    def _():
        gain_ref[...] = jnp.zeros_like(gain_ref)
        bias_ref[...] = jnp.zeros_like(bias_ref)

    gain_ref[...] += gain
    bias_ref[...] += bias


def qkv_back(d_query, own, came, cos, sin, w_qkv, x_all):
    cores, line, tok, width = x_all.shape
    _, _, rows, col = own.shape
    tokens = pl.BlockSpec((cores, 1, tok, width), lambda g: (0, g, 0, 0))
    table = pl.BlockSpec((1, rows, HD), lambda g: (g, 0, 0))
    return pl.pallas_call(
        qkv_back_body,
        grid=(line,),
        out_shape=(
            jax.ShapeDtypeStruct((cores, line, tok, 3 * col), BF),
            jax.ShapeDtypeStruct(x_all.shape, BF),
            jax.ShapeDtypeStruct((1, width), F32),
            jax.ShapeDtypeStruct((1, 3 * col), F32),
        ),
        in_specs=[
            pl.BlockSpec((cores, 1, tok, col), lambda g: (0, g, 0, 0)),
            pl.BlockSpec((2, 1, rows, col), lambda g: (0, g, 0, 0)),
            pl.BlockSpec((came.shape[0], 2, 1, rows, col), lambda g: (0, 0, g, 0, 0)),
            table,
            table,
            full(w_qkv.shape),
            tokens,
        ],
        out_specs=(
            pl.BlockSpec((cores, 1, tok, 3 * col), lambda g: (0, g, 0, 0)),
            tokens,
            full((1, width)),
            full((1, 3 * col)),
        ),
        compiler_params=local_params(56),
        cost_estimate=cost(),
    )(d_query, own, came, cos, sin, w_qkv, x_all)


def ahead_body(
    partial_ref, x_ref, gain_ref, gu_ref, sd_ref, resid_ref, all_ref, wgu_ref, wsd_ref, *rest
):
    dp, cx, _, _ = places()
    greet(line_peers() + [moved(core=1)] + plane_peers())
    bufs, sems = rest[:3], rest[3:]
    normed_ref = sems[-1]
    collect = Collect(partial_ref, *bufs, sems[0:5])
    collect.start()
    local = sems[5]
    keep = [
        pltpu.make_async_copy(gu_ref, wgu_ref.at[dp, cx], local.at[0]),
        pltpu.make_async_copy(sd_ref, wsd_ref.at[dp, cx], local.at[1]),
    ]
    for copy in keep:
        copy.start()
    gu = Plane(wgu_ref, sems[6:8], gu_ref)
    sd = Plane(wsd_ref, sems[8:10], sd_ref)
    gu.start()
    sd.start()
    total = collect.reduce()
    resid = x_ref[...].astype(F32) + total
    resid_ref[...] = resid
    normal, _ = rms_parts(resid)
    normed_ref[...] = (normal * gain_ref[...]).astype(BF)
    spread = Spread(normed_ref, all_ref, sems[10:14])
    spread.start()
    spread.forward_step(1)
    gu.forward()
    for step in range(2, lax.axis_size("exp")):
        spread.forward_step(step)
        if step == 2:
            sd.forward()
    collect.finish()
    spread.finish()
    gu.finish()
    sd.finish()
    for copy in keep:
        copy.wait()


def ahead(partial, x_own, gain, gu, sd):
    n_dp, n_cx, line = (lax.axis_size(axis) for axis in ("dp", "cx", "exp"))
    tok, width = x_own.shape
    return pl.pallas_call(
        ahead_body,
        out_shape=(
            jax.ShapeDtypeStruct((tok, width), F32),
            jax.ShapeDtypeStruct((CORES, line, tok, width), BF),
            jax.ShapeDtypeStruct((n_dp, n_cx) + gu.shape, BF),
            jax.ShapeDtypeStruct((n_dp, n_cx) + sd.shape, BF),
        ),
        in_specs=[ANY, VMEM, VMEM, ANY, ANY],
        out_specs=(VMEM, ANY, ANY, ANY),
        scratch_shapes=Collect.scratch(line, tok, width)
        + [pltpu.SemaphoreType.DMA((2,))]
        + Plane.scratch(n_dp, n_cx)
        + Plane.scratch(n_dp, n_cx)
        + Spread.scratch(line)
        + [pltpu.VMEM((tok, width), BF)],
        compiler_params=params(2, 54),
        cost_estimate=cost(),
    )(partial, x_own, gain, gu, sd)


def back_body(
    partial_ref,
    resid_ref,
    gain_ref,
    cot_ref,
    dots_ref,
    router_ref,
    score_ref,
    small_ref,
    mix_ref,
    dn_ref,
    dr_ref,
    all_ref,
    logits_ref,
    dscore_ref,
    mixed_ref,
    *rest,
):
    greet(tp_peers())
    bufs, sems = rest[:3], rest[3:]
    collect = Collect(partial_ref, *bufs, sems[0:5])
    collect.start()
    mix = Collect(mix_ref, *sems[14:17], sems[17:22])
    proj_ref = sems[9]
    dot_send, dot_recv, came_ref, keep_sem = sems[10:14]
    line = lax.axis_size("exp")
    keep = pltpu.make_async_copy(dots_ref.at[0, 0], came_ref.at[0, 0], keep_sem)
    keep.start()
    outs = [
        copy_to(
            dots_ref.at[c, k],
            came_ref.at[c, k],
            dot_send.at[c, k],
            dot_recv.at[c, k],
            moved(core=c, exp=k),
        )
        for c in range(CORES)
        for k in range(line)
        if c or k
    ]
    mix.start()
    collect.send()
    mix.ready()
    keep.wait()
    for copy in outs:
        copy.wait()
    _, _, core, exp = places()
    n_experts = router_ref.shape[0]
    row = lax.broadcasted_iota(jnp.int32, router_ref.shape, 0)
    d_router = jnp.zeros(router_ref.shape, F32)
    d_score = jnp.zeros(score_ref.shape, F32)
    for c in range(CORES):
        for k in range(line):
            tile = came_ref[c, k]
            source = lax.rem(exp + line - k, line) * CORES + lax.rem(core + CORES - c, CORES)
            d_router = d_router + jnp.where(row == source, tile[0:1], 0.0)
            d_score = d_score + tile[1:2]
    score = score_ref[...]
    d_score = d_score * score * (1.0 - score)
    router = router_ref[...]
    d_logits = (router * (d_router - jnp.sum(router * d_router, 0, keepdims=True))).astype(BF)
    high = d_score.astype(BF)
    mid = (d_score - high.astype(F32)).astype(BF)
    tail = (d_score - high.astype(F32) - mid.astype(F32)).astype(BF)
    logits_ref[...] = d_logits
    dscore_ref[...] = jnp.concatenate([high, mid, tail], 0)
    extra = weight_grad(d_logits, small_ref[0:n_experts])
    for part in (high, mid, tail):
        extra = extra + weight_grad(part, small_ref[n_experts : n_experts + 1])
    normal, inverse = rms_parts(resid_ref[...])
    d_normed = collect.gather() + extra
    dn_ref[...] = d_normed
    d_hat = d_normed * gain_ref[...]
    d_resid = cot_ref[...].astype(F32) + inverse * (
        d_hat - normal * jnp.mean(d_hat * normal, 1, keepdims=True)
    )
    dr_ref[...] = d_resid
    proj_ref[...] = d_resid.astype(BF)
    spread = Spread(proj_ref, all_ref, sems[5:9])
    spread.start()
    for step in range(1, line):
        spread.forward_step(step)
        mix.send_step(line - step)
    collect.finish()
    spread.finish()
    mixed_ref[...] = (resid_ref[...] + mix.gather()).astype(BF)
    mix.finish()


def back(partial, resid, gain, cot, dots, router, score, small, mix):
    line = lax.axis_size("exp")
    tok, width = resid.shape
    dma = pltpu.SemaphoreType.DMA
    return pl.pallas_call(
        back_body,
        out_shape=(
            jax.ShapeDtypeStruct((tok, width), F32),
            jax.ShapeDtypeStruct((tok, width), F32),
            jax.ShapeDtypeStruct((CORES, line, tok, width), BF),
            jax.ShapeDtypeStruct(router.shape, BF),
            jax.ShapeDtypeStruct((3, tok), BF),
            jax.ShapeDtypeStruct((tok, width), BF),
        ),
        in_specs=[ANY, VMEM, VMEM, VMEM, ANY, VMEM, VMEM, VMEM, ANY],
        out_specs=(VMEM, VMEM, ANY, VMEM, VMEM, VMEM),
        scratch_shapes=Collect.scratch(line, tok, width)
        + Spread.scratch(line)
        + [pltpu.VMEM((tok, width), BF)]
        + [dma((CORES, line)), dma((CORES, line)), pltpu.VMEM(dots.shape, F32), dma]
        + Collect.scratch(line, tok, width),
        compiler_params=params(3, 52 + line // 2),
        cost_estimate=cost(),
    )(partial, resid, gain, cot, dots, router, score, small, mix)


class Rows:
    def __init__(self, block, line):
        self.block, self.rows = block, block.shape[1] // line

    @property
    def at(self):
        return self

    def __getitem__(self, spot):
        core, exp = spot
        start = pl.multiple_of(exp * self.rows, self.rows)
        return self.block.at[core, pl.ds(start, self.rows)]


def last_body(
    partial_ref,
    gq_ref,
    go_ref,
    tot_ref,
    egu_ref,
    ed_ref,
    gsd_ref,
    x_ref,
    gain_ref,
    dres_ref,
    out_ref,
    q_ref,
    k_ref,
    v_ref,
    wo_ref,
    sum_ref,
    eg_ref,
    eu_ref,
    edown_ref,
    sd_ref,
    *rest,
):
    dp, cx, core, exp = places()
    line = lax.axis_size("exp")
    greet(all_peers())
    collect = Collect(partial_ref, *rest[:3], rest[3:8])
    qkv_block, tots_ref, cols_ref = rest[8:11]
    qkv = PlaneSum(gq_ref, qkv_block, rest[11:29])
    wo = PlaneSum(go_ref, wo_ref, rest[29:47])
    tot_send, tot_recv, local = rest[47:50]
    columns = Columns(Rows(qkv_block, line), cols_ref, rest[50:53])
    gu_came, d_came, swap_send, swap_recv, store = rest[53:58]
    wide, tall = rest[58:60]
    sd = PlaneSum(gsd_ref, sd_ref, rest[60:78])
    collect.start()
    rows, down = gu_came.shape[0], d_came.shape[0]
    swaps = [
        copy_to(
            source.at[pl.ds((1 - core) * height, height)],
            target,
            swap_send.at[n],
            swap_recv.at[n],
            moved(core=1),
        )
        for n, (source, target, height) in enumerate(
            ((egu_ref, gu_came, rows), (ed_ref, d_came, down))
        )
    ]
    qkv.start()
    collect.ready()
    steps_left = list(range(line - 1, 0, -1))
    while len(steps_left) > 2:
        collect.send_step(steps_left.pop(0))
    keep = pltpu.make_async_copy(
        tot_ref.at[dp, cx, core, exp], tots_ref.at[0, 0, 0, 0], local
    )
    keep.start()
    sizes = [range(lax.axis_size(axis)) for axis in ("dp", "cx", "core", "exp")]
    outs = []
    for steps in itertools.product(*sizes):
        if any(steps):
            target = moved(*steps)
            outs.append(
                copy_to(
                    tot_ref.at[target],
                    tots_ref.at[steps],
                    tot_send.at[steps],
                    tot_recv.at[steps],
                    target,
                )
            )
    qkv.middle()
    wo.start()
    sd.start()
    collect.send_step(steps_left.pop(0))
    qkv.end()
    columns.start()
    collect.send_step(steps_left.pop(0))
    wo.middle()
    sd.middle()
    for copy in swaps:
        copy.wait_recv()
    ffe = wide.shape[3]

    def mine(at):
        piece = egu_ref[pl.ds(pl.multiple_of(core * rows + at.start, 8), at.size)].astype(F32)
        wide[0, core, at] = piece[:, :ffe]
        wide[1, core, at] = piece[:, ffe:]
        piece = gu_came[at].astype(F32)
        wide[0, 1 - core, at] = piece[:, :ffe]
        wide[1, 1 - core, at] = piece[:, ffe:]

    by_chunks(rows, mine)

    def down_rows(at):
        piece = ed_ref[pl.ds(pl.multiple_of(core * down + at.start, 8), at.size)]
        tall[core, at] = piece.astype(F32)
        tall[1 - core, at] = d_came[at].astype(F32)

    by_chunks(down, down_rows)
    stores = [
        pltpu.make_async_copy(wide.at[0], eg_ref, store.at[0]),
        pltpu.make_async_copy(wide.at[1], eu_ref, store.at[1]),
        pltpu.make_async_copy(tall, edown_ref, store.at[2]),
    ]
    for copy in stores:
        copy.start()
    normal, inverse = rms_parts(x_ref[...].astype(F32))
    d_hat = collect.gather() * gain_ref[...]
    out_ref[...] = (
        dres_ref[...]
        + inverse * (d_hat - normal * jnp.mean(d_hat * normal, 1, keepdims=True))
    ).astype(BF)
    wo.end()
    sd.end()
    keep.wait()
    for copy in outs:
        copy.wait()
    sum_ref[...] = jnp.sum(tots_ref[...].reshape((-1,) + tots_ref.shape[4:]), 0)
    columns.arrive()
    col = cols_ref.shape[3] // 3
    for n, target in enumerate((q_ref, k_ref, v_ref)):
        for c in range(CORES):
            for e in range(line):
                at = (e * CORES + c) * col
                target[:, at : at + col] = cols_ref[c, e, :, n * col : (n + 1) * col].astype(F32)
    columns.finish()
    collect.finish()
    for copy in swaps:
        copy.wait_send()
    for copy in stores:
        copy.wait()


def last(
    partial, grad_qkv, grad_out, totals, grad_egu, grad_edown, grad_sd, x_own, gain, d_resid
):
    n_dp, n_cx, line = (lax.axis_size(axis) for axis in ("dp", "cx", "exp"))
    tok, width = partial.shape[2:]
    dma = pltpu.SemaphoreType.DMA
    shard = grad_qkv.shape[3] // line
    rows, both = grad_egu.shape
    down = grad_edown.shape[0]
    heads = jax.ShapeDtypeStruct((shard, width), F32)
    wide = (CORES, rows // 2, both // 2)
    tall = (CORES, down // 2, width)
    return pl.pallas_call(
        last_body,
        out_shape=(
            jax.ShapeDtypeStruct((tok, width), BF),
            heads,
            heads,
            heads,
            jax.ShapeDtypeStruct(grad_out.shape[2:], F32),
            jax.ShapeDtypeStruct(totals.shape[4:], F32),
            jax.ShapeDtypeStruct(wide, F32),
            jax.ShapeDtypeStruct(wide, F32),
            jax.ShapeDtypeStruct(tall, F32),
            jax.ShapeDtypeStruct(grad_sd.shape[2:], F32),
        ),
        in_specs=[ANY, ANY, ANY, ANY, VMEM, VMEM, ANY, VMEM, VMEM, VMEM],
        out_specs=(VMEM,) * 6 + (ANY,) * 3 + (VMEM,),
        scratch_shapes=Collect.scratch(line, tok, width)
        + [
            pltpu.VMEM(grad_qkv.shape[2:], BF),
            pltpu.VMEM(totals.shape, F32),
            pltpu.VMEM((CORES, line, shard, grad_qkv.shape[4]), BF),
        ]
        + PlaneSum.scratch(*grad_qkv.shape[3:])
        + PlaneSum.scratch(*grad_out.shape[3:])
        + [dma((n_dp, n_cx, CORES, line)), dma((n_dp, n_cx, CORES, line)), dma]
        + Columns.scratch(line)
        + [
            pltpu.VMEM((rows // 2, both), BF),
            pltpu.VMEM((down // 2, width), BF),
            dma((2,)),
            dma((2,)),
            dma((3,)),
            pltpu.VMEM((2,) + wide, F32),
            pltpu.VMEM(tall, F32),
        ]
        + PlaneSum.scratch(*grad_sd.shape[3:]),
        compiler_params=params(4, 50 + line // 2),
        cost_estimate=cost(),
    )(
        partial,
        grad_qkv,
        grad_out,
        totals,
        grad_egu,
        grad_edown,
        grad_sd,
        x_own,
        gain,
        d_resid,
    )


def on_device(
    tokens,
    cotangent,
    positions,
    lengths,
    routes,
    norm_attn,
    w_query,
    bias_query,
    w_key,
    bias_key,
    w_value,
    bias_value,
    w_output,
    norm_moe,
    w_router,
    w_shared_gate,
    w_shared_up,
    w_shared_down,
    w_shared_score,
    w_expert_gate,
    w_expert_up,
    w_expert_down,
):
    n_dp = lax.axis_size("dp")
    n_cx = lax.axis_size("cx")
    n_exp = lax.axis_size("exp")
    exp_at = lax.axis_index("exp")
    core_at = lax.axis_index("core")
    n_tp = CORES * n_exp
    n_data = n_dp * n_cx
    tok, width = tokens.shape[2:]
    shard = w_query.shape[0]
    block = CORES * n_exp * shard
    col = width // n_tp
    heads = col // HD
    n_experts = w_router.shape[1]
    sub = w_shared_down.shape[0]
    sub_width = n_data * sub
    every = tok * n_tp
    scale = HD ** (-0.5)
    top = routes.shape[3]
    ffe = w_expert_gate.shape[2]

    def by_core(first, second):
        return jnp.where(core_at == 0, first, second)

    x_own = tokens.reshape(tok, width)
    cot_own = cotangent.reshape(tok, width)

    small = jnp.concatenate(
        [
            norm_attn[None],
            norm_moe[None],
            w_shared_score[None],
            bias_query[None],
            bias_key[None],
            bias_value[None],
            w_router.T,
        ]
    ).astype(F32)
    n_small = small.shape[0]
    pack = jnp.concatenate(
        [
            positions.reshape(1, tok),
            routes.reshape(tok, top).T,
            jnp.pad(lengths.reshape(1, -1), ((0, 0), (0, tok - lengths.shape[2]))),
        ]
    ).astype(F32)
    pack = jnp.concatenate([pack, jnp.pad(small, ((0, 0), (0, tok - shard)))])
    pack = jnp.pad(pack, ((0, -pack.shape[0] % 8), (0, 0)))

    def exchange(value):
        return lax.all_to_all(value, ("core", "exp"), split_axis=0, concat_axis=0, tiled=True)

    def head_columns(value):
        parts = value.reshape(shard, n_exp, CORES, col)
        return jnp.transpose(parts, (2, 1, 0, 3))

    qkv_cols = jnp.concatenate(
        [head_columns(w_query), head_columns(w_key), head_columns(w_value)], 3
    )
    x_all, w_qkv, wo_all, packs, cot_tok = load(x_own, qkv_cols, w_output, pack, cot_own)
    w_egu = lax.all_gather(
        jnp.concatenate([w_expert_gate, w_expert_up], 2), ("dp", "cx", "core"), axis=1, tiled=True
    )
    w_edown = lax.all_gather(w_expert_down, ("dp", "cx", "core"), axis=1, tiled=True)
    w_egu = lax.dynamic_index_in_dim(w_egu, core_at, 0, keepdims=False)
    w_edown = lax.dynamic_index_in_dim(w_edown, core_at, 0, keepdims=False)
    w_qkv = w_qkv.reshape(width, 3 * col)
    gu_cols = split_hidden(w_shared_gate, w_shared_up, n_exp, sub)

    small = packs[:, :, :, :, 2 + top : 2 + top + n_small, :shard]
    small = jnp.moveaxis(small, 4, 0).reshape(n_small, width)
    gain_attn = small[0]
    gain_moe = small[1]
    score_vec = small[2]
    router_full = small[6:].T.astype(BF)
    rank = exp_at * CORES + core_at
    biases = lax.dynamic_slice_in_dim(small[3:6], rank * col, col, 1).reshape(3 * col)

    ints = lax.dynamic_index_in_dim(packs, lax.axis_index("dp"), 0, keepdims=False)
    ints = ints[:, :, :, : 2 + top]
    for dim, axis in enumerate(("cx", "core", "exp")):
        ints = roll_to_relative(ints, axis, dim)
    ints = ints.astype(jnp.int32)
    route_tok = jnp.swapaxes(ints[0, :, :, 1 : 1 + top], 2, 3).reshape(every, top)
    seq_lens = ints[0, 0, :, 1 + top, : lengths.shape[2]]
    seq_ends = jnp.cumsum(seq_lens, 1)
    pos_keys = jnp.moveaxis(ints[:, :, :, 0], 2, 0).reshape(n_exp, n_cx * CORES * tok)
    after_end = (pos_keys[:, :, None] >= seq_ends[:, None, :]).astype(jnp.int32)
    seg_keys = jnp.sum(after_end, 2)
    rel_keys = pos_keys - jnp.sum(after_end * seq_lens[:, None, :], 2)
    own_keys = CORES * tok
    code_keys = (seg_keys * 4096 + pos_keys)[:, None, :]
    low = (seg_keys[:, :own_keys] * 4096)[:, :, None]
    codes = (low + pos_keys[:, :own_keys, None], low, code_keys)
    freq = ROTARY_BASE ** (-(jnp.arange(HD // 2, dtype=F32) * 2.0 / HD))
    angle = rel_keys[:, :own_keys].astype(F32)[:, :, None] * freq
    cos_table = jnp.cos(angle)
    sin_table = jnp.sin(angle)
    cos_table = jnp.concatenate([cos_table, cos_table], 2)
    sin_table = jnp.concatenate([-sin_table, sin_table], 2)

    normed_one, query, kv = project_qkv(x_all, w_qkv, gain_attn, biases, cos_table, sin_table)
    normed_one = normed_one.reshape(every, width)
    kv_all, gu_block, w_out = keys_call(kv, gu_cols, wo_all)
    w_out = w_out.reshape(col, width)
    attn_low, partial = attend(query, kv_all, codes, w_out)
    resid, normed_two, w_sgu, w_sdown = ahead(
        partial,
        x_own,
        gain_moe[None],
        gu_block,
        w_shared_down.reshape(2, sub // 2, width),
    )
    normed_two = normed_two.reshape(every, width)
    normed_two_own = normed_two[:tok]
    w_sgu = w_sgu.reshape(width, 2 * sub_width)
    w_sdown = w_sdown.reshape(sub_width, width)

    small_cols = jnp.concatenate([router_full, score_vec.astype(BF)[:, None]], 1)
    small_out = project(normed_two, small_cols)
    router_all = jax.nn.softmax(small_out[:, :n_experts], axis=-1)
    score_all = jax.nn.sigmoid(small_out[:, n_experts])
    chosen = jnp.any(route_tok == rank, axis=1)
    at_rank = (jnp.arange(n_experts) == rank).astype(F32)
    gate = jnp.where(chosen, jnp.sum(router_all * at_rank[None, :], 1), 0.0)

    cot_all = cot_tok.reshape(every, width).astype(F32)
    shared_pre = held(project(normed_two, w_sgu))
    s_gate = shared_pre[:, :sub_width]
    s_up = shared_pre[:, sub_width:]
    s_act, s_slope = silu_parts(s_gate)
    s_hidden = (s_act * s_up).astype(BF)
    shared = held(project(s_hidden, w_sdown))
    d_shared = (score_all[:, None] * cot_all).astype(BF)
    d_sh = project_t(d_shared, w_sdown)
    d_sgu = jnp.concatenate(
        [(d_sh * s_up * s_slope).astype(BF), (d_sh * s_act).astype(BF)], 1
    )
    grad_sgu = weight_grad(normed_two, d_sgu).astype(BF)
    normed_late, grad_sgu = lax.optimization_barrier((normed_two, grad_sgu))
    grad_sgu = lax.psum_scatter(grad_sgu, ("dp", "cx"), scatter_dimension=0, tiled=True)
    expert_pre = held(project(normed_late, w_egu))
    e_gate = expert_pre[:, :ffe]
    e_up = expert_pre[:, ffe:]
    e_act, e_slope = silu_parts(e_gate)
    e_hidden = (e_act * e_up).astype(BF)
    e_out = project(e_hidden, w_edown).astype(BF).astype(F32)
    mix = (score_all[:, None] * shared + gate[:, None] * e_out).astype(BF)
    dots = jnp.stack(
        [
            jnp.where(chosen, jnp.sum(cot_all * e_out, 1), 0.0),
            jnp.sum(cot_all * shared, 1),
        ]
    )

    d_eout = (gate[:, None] * cot_all).astype(BF)
    d_eh = project_t(d_eout, w_edown)
    d_egu = jnp.concatenate(
        [(d_eh * e_up * e_slope).astype(BF), (d_eh * e_act).astype(BF)], 1
    )
    grad_egu = weight_grad(normed_late, d_egu).astype(BF)
    grad_edown = weight_grad(e_hidden, d_eout).astype(BF)
    d_egu, grad_egu, grad_edown = lax.optimization_barrier((d_egu, grad_egu, grad_edown))
    grad_egu = lax.psum_scatter(grad_egu, ("dp", "cx"), scatter_dimension=0, tiled=True)
    grad_edown = lax.psum_scatter(grad_edown, ("dp", "cx"), scatter_dimension=0, tiled=True)
    grad_sdown = weight_grad(s_hidden, d_shared).astype(BF)
    partial_two = (project_t(d_sgu, w_sgu) + held(project_t(d_egu, w_egu))).astype(BF)

    dots = jnp.pad(dots.reshape(2, n_tp, tok).swapaxes(0, 1), ((0, 0), (0, 6), (0, 0)))
    d_normed_two, d_resid, d_proj, d_logits, d_score, mixed = back(
        partial_two.reshape(CORES, n_exp, tok, width),
        resid,
        gain_moe[None],
        cot_own,
        dots.reshape(CORES, n_exp, 8, tok),
        router_all[:tok].T,
        score_all[None, :tok],
        jnp.concatenate([router_full.T, score_vec.astype(BF)[None]]),
        mix.reshape(CORES, n_exp, tok, width),
    )
    grad_router = project(d_logits, normed_two_own)
    grad_score = project(d_score, normed_two_own).sum(0)
    grad_gain_moe = jnp.sum(d_normed_two * rms_parts(resid)[0], 0)

    grad_sgu, d_proj = lax.optimization_barrier((grad_sgu, d_proj))
    grad_sgu = exchange(grad_sgu.reshape(n_tp, shard, 2 * sub_width))
    grad_sgu = grad_sgu.reshape(CORES, n_exp, shard, 2 * sub_width)

    d_query, d_kv_own, d_kv_far = attend_back(query, kv_all, codes, w_out, d_proj, cos_table, sin_table)
    came = jnp.stack([push(d_kv_far[k - 1], "cx", k) for k in range(1, n_cx)])
    came, grad_sgu = lax.optimization_barrier((came, grad_sgu))
    d_qkv, partial_one, grad_gain_attn, grad_bias = qkv_back(
        d_query, d_kv_own, came, cos_table, sin_table, w_qkv, x_all
    )
    grad_qkv = weight_grad(normed_one, d_qkv.reshape(every, 3 * col)).astype(BF)
    grad_out = lax.all_to_all(
        weight_grad(attn_low.reshape(every, col), d_proj.reshape(every, width))
        .astype(BF)
        .reshape(n_exp, shard, width),
        "exp",
        split_axis=0,
        concat_axis=0,
        tiled=True,
    )
    grad_bias = lax.dynamic_update_slice_in_dim(
        jnp.zeros((3, width), F32), grad_bias.reshape(3, col), rank * col, 1
    )
    totals = jnp.concatenate(
        [
            grad_gain_attn,
            grad_gain_moe[None],
            grad_score[None],
            grad_bias,
            grad_router,
        ]
    )
    totals = jnp.moveaxis(totals.reshape(n_small, n_data * n_tp, shard), 0, 1)
    totals = totals.reshape(n_data * n_tp, -1)
    totals = jnp.pad(totals, ((0, 0), (0, -totals.shape[1] % 1024)))
    grad_sgate, grad_sup = merge_hidden(grad_sgu, sub)
    partial_one, grad_sgate, grad_sup = lax.optimization_barrier(
        (partial_one, grad_sgate, grad_sup)
    )
    (
        grad_tokens,
        grad_query,
        grad_key,
        grad_value,
        grad_out,
        totals,
        grad_egate,
        grad_eup,
        grad_edown,
        grad_sdown,
    ) = last(
        partial_one,
        grad_qkv.reshape(n_dp, n_cx, 2, -1, 3 * col),
        grad_out.reshape(n_dp, n_cx, 2, shard // 2, width),
        totals.reshape(n_dp, n_cx, CORES, n_exp, -1, 128),
        grad_egu,
        grad_edown,
        grad_sdown.reshape(n_dp, n_cx, 2, -1, width),
        x_own,
        gain_attn[None],
        d_resid,
    )
    grad_sdown = grad_sdown.reshape(sub, width)
    grad_out = grad_out.reshape(shard, width)
    totals = totals.reshape(-1)[: n_small * shard].reshape(n_small, shard)
    return (
        mixed.reshape(tokens.shape),
        grad_tokens.reshape(tokens.shape),
        totals[0],
        grad_query,
        totals[3],
        grad_key,
        totals[4],
        grad_value,
        totals[5],
        grad_out,
        totals[1],
        totals[6:].T,
        grad_sgate,
        grad_sup,
        grad_sdown,
        totals[2],
        grad_egate,
        grad_eup,
        grad_edown,
    )


def solution(mesh):
    sizes = dict(mesh.shape)
    fine = Mesh(
        mesh.devices.reshape(sizes["dp"], sizes["ctx"] // CORES, CORES, sizes["exp"]),
        ("dp", "cx", "core", "exp"),
    )
    own = P("dp", "exp", ("cx", "core"), None)
    flat = P(("dp", "cx", "core", "exp"))
    rows = P(("dp", "cx", "core", "exp"), None)
    expert = P("exp", ("dp", "cx", "core"), None)
    placed = (
        own,
        own,
        P("dp", "exp", ("cx", "core")),
        P("dp", "exp", None),
        own,
        flat,
        rows,
        flat,
        rows,
        flat,
        rows,
        flat,
        rows,
        flat,
        rows,
        rows,
        rows,
        rows,
        flat,
        expert,
        expert,
        expert,
    )
    return jax.shard_map(
        on_device,
        mesh=fine,
        in_specs=placed,
        out_specs=(
            own,
            own,
            flat,
            rows,
            flat,
            rows,
            flat,
            rows,
            flat,
            rows,
            flat,
            rows,
            rows,
            rows,
            rows,
            flat,
            expert,
            expert,
            expert,
        ),
        check_vma=False,
    )
```

```python
import itertools

import jax
import jax.numpy as jnp
from jax import lax
from jax.experimental import pallas as pl
from jax.experimental.pallas import tpu as pltpu
from jax.sharding import Mesh
from jax.sharding import PartitionSpec as P

HD = 128
CORES = 2
EPSILON = 1e-06
ROTARY_BASE = 1000000.0
NEGATIVE = -1e30
BF = jnp.bfloat16
F32 = jnp.float32


def project(left, right):
    return jnp.dot(left, right, preferred_element_type=F32)


def project_t(left, right):
    return lax.dot_general(left, right, (((1,), (1,)), ((), ())), preferred_element_type=F32)


def weight_grad(left, right):
    return lax.dot_general(left, right, (((0,), (0,)), ((), ())), preferred_element_type=F32)


def held(value):
    return lax.optimization_barrier(value.astype(BF))


def rms_parts(value):
    inverse = lax.rsqrt(jnp.mean(value * value, axis=-1, keepdims=True) + EPSILON)
    return (value * inverse, inverse)


def silu_parts(value):
    sigmoid = jax.nn.sigmoid(value)
    return (value * sigmoid, sigmoid * (1.0 + value * (1.0 - sigmoid)))


def fetch(value, axis, step):
    size = lax.axis_size(axis)
    if step % size == 0:
        return value
    return lax.ppermute(value, axis, [((i + step) % size, i) for i in range(size)])


def push(value, axis, step):
    size = lax.axis_size(axis)
    return lax.ppermute(value, axis, [(i, (i + step) % size) for i in range(size)])


def roll_to_relative(value, axis, dim):
    size = lax.axis_size(axis)
    both = lax.concatenate([value, value], dim)
    return lax.dynamic_slice_in_dim(both, lax.axis_index(axis), size, dim)


MESH = pl.DeviceIdType.MESH
ANY = pl.BlockSpec(memory_space=pltpu.HBM)
VMEM = pl.BlockSpec(memory_space=pltpu.VMEM)


def places():
    return tuple(lax.axis_index(axis) for axis in ("dp", "cx", "core", "exp"))


def moved(dp=0, cx=0, core=0, exp=0):
    steps = (dp, cx, core, exp)
    return tuple(
        at if step == 0 else lax.rem(at + step, lax.axis_size(axis))
        for at, step, axis in zip(places(), steps, ("dp", "cx", "core", "exp"))
    )


def copy_to(source, target, send_sem, recv_sem, device):
    copy = pltpu.make_async_remote_copy(
        src_ref=source,
        dst_ref=target,
        send_sem=send_sem,
        recv_sem=recv_sem,
        device_id=device,
        device_id_type=MESH,
    )
    copy.start()
    return copy


def greet(devices):
    barrier = pltpu.get_barrier_semaphore()
    for device in devices:
        pl.semaphore_signal(barrier, inc=1, device_id=device, device_id_type=MESH)
    pl.semaphore_wait(barrier, len(devices))


def line_peers():
    return [moved(exp=k) for k in range(1, lax.axis_size("exp"))]


def plane_peers():
    steps = [(j, k) for j in range(lax.axis_size("dp")) for k in range(lax.axis_size("cx"))]
    return [moved(dp=j, cx=k) for j, k in steps[1:]]


class Spread:
    def __init__(self, source, out, sems):
        self.source, self.out = source, out
        self.up, self.down, self.over, self.local = sems
        self.line = lax.axis_size("exp")
        self.at = lax.axis_index("exp")

    def hop(self, step, way):
        slot = (self.line - step) % self.line if way > 0 else step
        landing = self.line - step - 1 if way > 0 else step + 1
        sems = self.up if way > 0 else self.down
        return pltpu.make_async_remote_copy(
            src_ref=self.source if step == 0 else self.out.at[0, slot],
            dst_ref=self.out.at[0, landing],
            send_sem=sems.at[0, step],
            recv_sem=sems.at[1, step + 1],
            device_id=moved(exp=1 if way > 0 else self.line - 1),
            device_id_type=MESH,
        )

    def sends(self, step, way):
        if way > 0:
            return jnp.logical_and(self.at >= step, self.at < self.line - 1)
        return jnp.logical_and(self.at + step <= self.line - 1, self.at > 0)

    def gets(self, step, way):
        return self.at >= step if way > 0 else self.at + step <= self.line - 1

    def across(self, slot):
        return pltpu.make_async_remote_copy(
            src_ref=self.source if slot == 0 else self.out.at[0, slot],
            dst_ref=self.out.at[1, slot],
            send_sem=self.over.at[0, slot],
            recv_sem=self.over.at[1, slot],
            device_id=moved(core=1),
            device_id_type=MESH,
        )

    def start(self):
        self.keep = pltpu.make_async_copy(self.source, self.out.at[0, 0], self.local)
        self.keep.start()
        for way in (1, -1):
            pl.when(self.sends(0, way))(self.hop(0, way).start)
        self.across(0).start()

    def forward(self):
        for step in range(1, self.line):
            self.forward_step(step)

    def forward_step(self, step):
        for way in (1, -1):
            slot = self.line - step if way > 0 else step

            @pl.when(self.gets(step, way))
            def _():
                self.hop(step - 1, way).wait_recv()
                self.across(slot).start()

            if step < self.line - 1:
                pl.when(self.sends(step, way))(self.hop(step, way).start)

    def finish(self):
        self.keep.wait()
        for step in range(self.line - 1):
            for way in (1, -1):
                pl.when(self.sends(step, way))(self.hop(step, way).wait_send)
        for slot in range(self.line):
            self.across(slot).wait()

    @staticmethod
    def scratch(line):
        return [
            pltpu.SemaphoreType.DMA((2, line)),
            pltpu.SemaphoreType.DMA((2, line)),
            pltpu.SemaphoreType.DMA((2, line)),
            pltpu.SemaphoreType.DMA,
        ]


class Columns:
    def __init__(self, cols, out, sems):
        self.cols, self.out, self.sems = cols, out, sems

    def start(self):
        send, recv, local = self.sems
        line = lax.axis_size("exp")
        _, _, core, exp = places()
        self.local = pltpu.make_async_copy(
            self.cols.at[core, exp], self.out.at[core, exp], local
        )
        self.local.start()
        self.copies = []
        for c in range(CORES):
            for k in range(line):
                if c or k:
                    target = moved(core=c, exp=k)
                    self.copies.append(
                        copy_to(
                            self.cols.at[target[2], target[3]],
                            self.out.at[core, exp],
                            send.at[c, k],
                            recv.at[c, k],
                            target,
                        )
                    )

    def arrive(self):
        self.local.wait()
        for copy in self.copies:
            copy.wait_recv()

    def finish(self):
        for copy in self.copies:
            copy.wait_send()

    @staticmethod
    def scratch(line):
        return [
            pltpu.SemaphoreType.DMA((CORES, line)),
            pltpu.SemaphoreType.DMA((CORES, line)),
            pltpu.SemaphoreType.DMA,
        ]


class Plane:
    def __init__(self, out, sems, source=None):
        self.out, self.sems, self.source = out, sems, source
        self.n = (lax.axis_size("dp"), lax.axis_size("cx"))

    def send(self, half, j, k, dp, cx):
        send, recv = self.sems
        at = places()
        n_dp, n_cx = self.n
        from_dp = lax.rem(at[0] + n_dp - j, n_dp)
        from_cx = lax.rem(at[1] + n_cx - k, n_cx)
        block = self.out.at[from_dp, from_cx, half]
        a, b = j + dp, k + cx
        first = self.source is not None and j == 0 and k == 0
        origin = self.source.at[half] if first else block
        return copy_to(
            origin, block, send.at[half, a, b], recv.at[half, a, b], moved(dp=dp, cx=cx)
        )

    def start(self):
        n_dp, n_cx = self.n
        self.along_cx = [[self.send(h, 0, 0, 0, k) for k in range(1, n_cx)] for h in range(2)]
        self.along_dp = [[self.send(h, 0, 0, j, 0) for j in range(1, n_dp)] for h in range(2)]

    def forward(self):
        n_dp, n_cx = self.n
        self.rest = []
        for k in range(1, n_cx):
            self.along_cx[0][k - 1].wait_recv()
            for j in range(1, n_dp):
                self.rest.append(self.send(0, 0, k, j, 0))
        for j in range(1, n_dp):
            self.along_dp[1][j - 1].wait_recv()
            for k in range(1, n_cx):
                self.rest.append(self.send(1, j, 0, 0, k))

    def finish(self):
        for copy in self.along_cx[1] + self.along_dp[0] + self.rest:
            copy.wait()
        for copy in self.along_cx[0] + self.along_dp[1]:
            copy.wait_send()

    @staticmethod
    def scratch(n_dp, n_cx):
        return [
            pltpu.SemaphoreType.DMA((2, n_dp, n_cx)),
            pltpu.SemaphoreType.DMA((2, n_dp, n_cx)),
        ]


def params(number, mebibytes):
    return pltpu.CompilerParams(
        collective_id=number, has_side_effects=True, vmem_limit_bytes=mebibytes * 2**20
    )


def cost():
    return pl.CostEstimate(flops=1, bytes_accessed=1, transcendentals=0)


def tp_peers():
    line = lax.axis_size("exp")
    steps = [(c, k) for c in range(CORES) for k in range(line)]
    return [moved(core=c, exp=k) for c, k in steps[1:]]


def all_peers():
    sizes = [range(lax.axis_size(axis)) for axis in ("dp", "cx", "core", "exp")]
    return [moved(*steps) for steps in itertools.product(*sizes) if any(steps)]


def load_body(
    x_ref,
    cols_ref,
    wo_ref,
    pack_ref,
    cot_ref,
    xall_ref,
    wqkv_ref,
    woall_ref,
    packs_ref,
    cotall_ref,
    *sems,
):
    dp, cx, core, exp = places()
    greet(all_peers())
    tokens = Spread(x_ref, xall_ref, sems[0:4])
    block = wqkv_ref.at[dp, cx]
    columns = Columns(cols_ref, block, sems[4:7])
    plane = Plane(wqkv_ref, sems[7:9])
    send, recv, local = sems[9:12]
    columns.start()
    own = [
        pltpu.make_async_copy(wo_ref, woall_ref.at[dp, cx], local.at[0]),
        pltpu.make_async_copy(pack_ref, packs_ref.at[dp, cx, core, exp], local.at[1]),
    ]
    for copy in own:
        copy.start()
    pack_send, pack_recv = sems[12:14]
    sizes = [range(lax.axis_size(axis)) for axis in ("dp", "cx", "core", "exp")]
    outs = [
        copy_to(
            pack_ref,
            packs_ref.at[dp, cx, core, exp],
            pack_send.at[steps],
            pack_recv.at[steps],
            moved(*steps),
        )
        for steps in itertools.product(*sizes)
        if any(steps)
    ]
    cotangent = Spread(cot_ref, cotall_ref, sems[14:18])
    columns.arrive()
    tokens.start()
    plane.start()
    tokens.forward()
    cotangent.start()
    plane.forward()
    for j in range(lax.axis_size("dp")):
        for k in range(lax.axis_size("cx")):
            if j or k:
                outs.append(
                    copy_to(
                        wo_ref,
                        woall_ref.at[dp, cx],
                        send.at[j, k],
                        recv.at[j, k],
                        moved(dp=j, cx=k),
                    )
                )
    cotangent.forward()
    columns.finish()
    tokens.finish()
    plane.finish()
    cotangent.finish()
    for copy in own + outs:
        copy.wait()


def load(x_own, cols, w_output, pack, cot_own):
    n_dp, n_cx, line = (lax.axis_size(axis) for axis in ("dp", "cx", "exp"))
    return pl.pallas_call(
        load_body,
        out_shape=(
            jax.ShapeDtypeStruct((CORES, line) + x_own.shape, BF),
            jax.ShapeDtypeStruct((n_dp, n_cx) + cols.shape, BF),
            jax.ShapeDtypeStruct((n_dp, n_cx) + w_output.shape, BF),
            jax.ShapeDtypeStruct((n_dp, n_cx, CORES, line) + pack.shape, F32),
            jax.ShapeDtypeStruct((CORES, line) + cot_own.shape, BF),
        ),
        in_specs=[ANY] * 5,
        out_specs=(ANY,) * 5,
        scratch_shapes=Spread.scratch(line)
        + Columns.scratch(line)
        + Plane.scratch(n_dp, n_cx)
        + [
            pltpu.SemaphoreType.DMA((n_dp, n_cx)),
            pltpu.SemaphoreType.DMA((n_dp, n_cx)),
            pltpu.SemaphoreType.DMA((2,)),
            pltpu.SemaphoreType.DMA((n_dp, n_cx, CORES, line)),
            pltpu.SemaphoreType.DMA((n_dp, n_cx, CORES, line)),
        ]
        + Spread.scratch(line),
        compiler_params=params(0, 58),
        cost_estimate=cost(),
    )(x_own, cols, w_output, pack, cot_own)


def keys_body(kv_ref, cols_ref, wo_ref, kvall_ref, gu_ref, wout_ref, *sems):
    _, _, _, exp = places()
    n_cx = lax.axis_size("cx")
    line = lax.axis_size("exp")
    greet(tp_peers() + [moved(cx=k) for k in range(1, n_cx)])
    send, recv, local = sems[3:6]
    own = pltpu.make_async_copy(kv_ref, kvall_ref.at[0], local)
    own.start()
    keys = [
        copy_to(kv_ref, kvall_ref.at[n_cx - k], send.at[k], recv.at[k], moved(cx=k))
        for k in range(1, n_cx)
    ]
    columns = Columns(cols_ref, gu_ref, sems[0:3])
    columns.start()
    send, recv, local = sems[6:9]
    keep = pltpu.make_async_copy(wo_ref.at[exp // n_cx, exp % n_cx], wout_ref.at[exp], local)
    keep.start()
    outs = []
    for k in range(1, line):
        target = moved(exp=k)
        at = target[3]
        outs.append(
            copy_to(
                wo_ref.at[at // n_cx, at % n_cx],
                wout_ref.at[exp],
                send.at[k],
                recv.at[k],
                target,
            )
        )
    own.wait()
    keep.wait()
    columns.arrive()
    columns.finish()
    for copy in keys + outs:
        copy.wait()


def keys_call(kv, cols, wo_all):
    n_cx, line = lax.axis_size("cx"), lax.axis_size("exp")
    return pl.pallas_call(
        keys_body,
        out_shape=(
            jax.ShapeDtypeStruct((n_cx,) + kv.shape, BF),
            jax.ShapeDtypeStruct(cols.shape, BF),
            jax.ShapeDtypeStruct((line,) + wo_all.shape[2:], BF),
        ),
        in_specs=[ANY] * 3,
        out_specs=(ANY,) * 3,
        scratch_shapes=Columns.scratch(line)
        + [
            pltpu.SemaphoreType.DMA((n_cx,)),
            pltpu.SemaphoreType.DMA((n_cx,)),
            pltpu.SemaphoreType.DMA,
            pltpu.SemaphoreType.DMA((line,)),
            pltpu.SemaphoreType.DMA((line,)),
            pltpu.SemaphoreType.DMA,
        ],
        compiler_params=params(1, 58),
        cost_estimate=cost(),
    )(kv, cols, wo_all)


def by_chunks(rows, work):
    chunk = 16 if rows % 16 == 0 else 8

    @pl.loop(0, rows // chunk)
    def _(step):
        work(pl.ds(pl.multiple_of(step * chunk, chunk), chunk))


class Collect:
    def __init__(self, partial, kept, near, far, sems):
        self.partial, self.kept, self.near, self.far = partial, kept, near, far
        self.core_send, self.core_recv, self.hop_send, self.hop_recv, self.local = sems
        self.line = lax.axis_size("exp")
        self.at = lax.axis_index("exp")

    def start(self):
        self.swaps, self.loads = [], []
        for k in range(self.line):
            self.swaps.append(
                copy_to(
                    self.partial.at[1, k],
                    self.near.at[k],
                    self.core_send.at[k],
                    self.core_recv.at[k],
                    moved(core=1),
                )
            )
            load = pltpu.make_async_copy(self.partial.at[0, k], self.kept.at[k], self.local.at[k])
            load.start()
            self.loads.append(load)

    def hop(self, way, step):
        slot = step if way == 0 else self.line - step
        return pltpu.make_async_remote_copy(
            src_ref=self.kept.at[slot],
            dst_ref=self.far.at[way, step - 1],
            send_sem=self.hop_send.at[way, step],
            recv_sem=self.hop_recv.at[way, step - 1],
            device_id=moved(exp=1 if way == 0 else self.line - 1),
            device_id_type=MESH,
        )

    def reaches(self, way, step):
        return self.at + step <= self.line - 1 if way == 0 else self.at >= step

    def fed(self, way):
        return self.at >= 1 if way == 0 else self.at <= self.line - 2

    def ready(self):
        for load in self.loads:
            load.wait()
        for swap in self.swaps:
            swap.wait_recv()

    def pair(self, k, rows):
        return self.kept[k, rows].astype(F32) + self.near[k, rows].astype(F32)

    def send_step(self, step):
        tok = self.kept.shape[1]
        for way in range(2):
            slot = step if way == 0 else self.line - step

            @pl.when(self.reaches(way, step))
            def _():
                @pl.when(self.fed(way))
                def _():
                    self.hop(way, step + 1).wait_recv()

                    def work(rows):
                        total = self.pair(slot, rows) + self.far[way, step, rows].astype(F32)
                        self.kept[slot, rows] = total.astype(BF)

                    by_chunks(tok, work)

                @pl.when(jnp.logical_not(self.fed(way)))
                def _():
                    def work(rows):
                        self.kept[slot, rows] = self.pair(slot, rows).astype(BF)

                    by_chunks(tok, work)

                self.hop(way, step).start()

    def send(self):
        self.ready()
        for step in range(self.line - 1, 0, -1):
            self.send_step(step)

    def gather(self):
        for way in range(2):

            @pl.when(self.fed(way))
            def _():
                self.hop(way, 1).wait_recv()

            @pl.when(jnp.logical_not(self.fed(way)))
            def _():
                self.far[way, 0] = jnp.zeros(self.far.shape[2:], BF)

        return (
            self.kept[0].astype(F32)
            + self.near[0].astype(F32)
            + (self.far[0, 0].astype(F32) + self.far[1, 0].astype(F32))
        )

    def reduce(self):
        self.send()
        return self.gather()

    def finish(self):
        for swap in self.swaps:
            swap.wait_send()
        for step in range(1, self.line):
            for way in range(2):
                pl.when(self.reaches(way, step))(self.hop(way, step).wait_send)

    @staticmethod
    def scratch(line, tok, width):
        dma = pltpu.SemaphoreType.DMA
        return [
            pltpu.VMEM((line, tok, width), BF),
            pltpu.VMEM((line, tok, width), BF),
            pltpu.VMEM((2, line, tok, width), BF),
            dma((line,)),
            dma((line,)),
            dma((2, line + 1)),
            dma((2, line + 1)),
            dma((line,)),
        ]


def split_hidden(gate, up, n_exp, piece):
    shard, total = gate.shape
    blocks = total // (CORES * n_exp * piece)

    def body(gate_ref, up_ref, out_ref):
        sides = (gate_ref[...].astype(F32), up_ref[...].astype(F32))
        for c in range(CORES):
            for e in range(n_exp):
                parts = []
                for side in sides:
                    for b in range(blocks):
                        start = ((b * CORES + c) * n_exp + e) * piece
                        parts.append(side[:, start : start + piece])
                out_ref[c, e] = jnp.concatenate(parts, 1).astype(BF)

    return pl.pallas_call(
        body,
        out_shape=jax.ShapeDtypeStruct((CORES, n_exp, shard, 2 * blocks * piece), BF),
        in_specs=[VMEM, VMEM],
        out_specs=VMEM,
        compiler_params=local_params(56),
        cost_estimate=cost(),
    )(gate, up)


def merge_hidden(value, piece):
    _, n_exp, shard, both = value.shape
    blocks = both // (2 * piece)
    total = blocks * CORES * n_exp * piece

    def body(in_ref, gate_ref, up_ref):
        for side, out_ref in enumerate((gate_ref, up_ref)):
            parts = []
            for b in range(blocks):
                start = (side * blocks + b) * piece
                for c in range(CORES):
                    for e in range(n_exp):
                        parts.append(in_ref[c, e].astype(F32)[:, start : start + piece])
            out_ref[...] = jnp.concatenate(parts, 1)

    shape = jax.ShapeDtypeStruct((shard, total), F32)
    return pl.pallas_call(
        body,
        out_shape=(shape, shape),
        in_specs=[VMEM],
        out_specs=(VMEM, VMEM),
        compiler_params=local_params(56),
        cost_estimate=cost(),
    )(value)


class HalfSum:
    def __init__(self, blocks, half, bufs, sems):
        self.blocks, self.half = blocks, half
        self.own, self.came, self.sums, self.final = bufs
        self.sem = sems
        n_dp, n_cx = lax.axis_size("dp"), lax.axis_size("cx")
        self.cx_first = half == 0
        self.n_in, self.n_out = (n_cx, n_dp) if self.cx_first else (n_dp, n_cx)

    def block(self, inner, outer):
        dp, cx = (outer, inner) if self.cx_first else (inner, outer)
        at = moved(dp=dp, cx=cx)
        return self.blocks.at[at[0], at[1], self.half]

    def far(self, inner, outer):
        dp, cx = (outer, inner) if self.cx_first else (inner, outer)
        return moved(dp=dp, cx=cx)

    def start(self):
        first_send, first_recv, _, _, local = self.sem
        self.first, self.loads = {}, []
        for a in range(self.n_out):
            for b in range(1, self.n_in):
                self.first[b, a] = copy_to(
                    self.block(b, a),
                    self.came.at[b - 1, a],
                    first_send.at[b - 1, a],
                    first_recv.at[b - 1, a],
                    self.far(b, 0),
                )
            load = pltpu.make_async_copy(self.block(0, a), self.own.at[a], local.at[a])
            load.start()
            self.loads.append(load)

    def near(self, a, rows):
        total = self.own[a, rows].astype(F32)
        for b in range(1, self.n_in):
            total = total + self.came[b - 1, a, rows].astype(F32)
        return total

    def middle(self):
        _, _, send, recv, _ = self.sem
        for load in self.loads:
            load.wait()
        self.second = []
        for a in range(1, self.n_out):
            for b in range(1, self.n_in):
                self.first[b, a].wait_recv()

            def work(rows):
                self.sums[a - 1, rows] = self.near(a, rows).astype(BF)

            by_chunks(self.sums.shape[1], work)
            self.second.append(
                copy_to(
                    self.sums.at[a - 1],
                    self.final.at[a - 1],
                    send.at[a - 1],
                    recv.at[a - 1],
                    self.far(0, a),
                )
            )

    def end(self, out):
        for b in range(1, self.n_in):
            self.first[b, 0].wait_recv()
        for copy in self.second:
            copy.wait_recv()

        def work(rows):
            total = self.near(0, rows)
            for a in range(1, self.n_out):
                total = total + self.final[a - 1, rows].astype(F32)
            out[rows] = total.astype(out.dtype)

        by_chunks(self.sums.shape[1], work)
        for copy in self.first.values():
            copy.wait_send()
        for copy in self.second:
            copy.wait_send()

    @staticmethod
    def scratch(half, rows, width):
        n_dp, n_cx = lax.axis_size("dp"), lax.axis_size("cx")
        n_in, n_out = (n_cx, n_dp) if half == 0 else (n_dp, n_cx)
        dma = pltpu.SemaphoreType.DMA
        return (
            [
                pltpu.VMEM((n_out, rows, width), BF),
                pltpu.VMEM((n_in - 1, n_out, rows, width), BF),
                pltpu.VMEM((n_out - 1, rows, width), BF),
                pltpu.VMEM((n_out - 1, rows, width), BF),
            ],
            [
                dma((n_in - 1, n_out)),
                dma((n_in - 1, n_out)),
                dma((n_out - 1,)),
                dma((n_out - 1,)),
                dma((n_out,)),
            ],
        )


class PlaneSum:
    def __init__(self, blocks, out, scratch):
        self.out = out
        self.halves = [
            HalfSum(blocks, h, scratch[9 * h : 9 * h + 4], scratch[9 * h + 4 : 9 * h + 9])
            for h in range(2)
        ]

    def start(self):
        for half in self.halves:
            half.start()

    def middle(self):
        for half in self.halves:
            half.middle()

    def end(self):
        for h, half in enumerate(self.halves):
            half.end(self.out.at[h])

    @staticmethod
    def scratch(rows, width):
        both = [HalfSum.scratch(h, rows, width) for h in range(2)]
        return both[0][0] + both[0][1] + both[1][0] + both[1][1]


def full(shape):
    return pl.BlockSpec(shape, lambda g: (0,) * len(shape))


def turn(value, cos, sin):
    return value * cos + pltpu.roll(value, HD // 2, 1) * sin


def project_qkv_body(x_ref, w_ref, gain_ref, bias_ref, cos_ref, sin_ref, n_ref, q_ref, kv_ref):
    rows = x_ref.shape[0] * x_ref.shape[2]
    width = x_ref.shape[3]
    col = q_ref.shape[2]
    normal, _ = rms_parts(x_ref[...].reshape(rows, width).astype(F32))
    normed = (normal * gain_ref[...]).astype(BF)
    n_ref[...] = normed.reshape(n_ref.shape)
    lin = project(normed, w_ref[...]) + bias_ref[...]
    cos, sin = cos_ref[0], sin_ref[0]
    for h in range(col // HD):
        at = slice(h * HD, (h + 1) * HD)
        q_ref[0, :, at] = turn(lin[:, at], cos, sin).astype(BF)
        head = lin[:, col + h * HD : col + (h + 1) * HD]
        kv_ref[0, 0, :, at] = turn(head, cos, sin).astype(BF)
    kv_ref[1, 0] = lin[:, 2 * col :].astype(BF)


def project_qkv(x_all, w_qkv, gain, bias, cos, sin):
    cores, line, tok, width = x_all.shape
    col = w_qkv.shape[1] // 3
    rows = cores * tok
    tokens = pl.BlockSpec((cores, 1, tok, width), lambda g: (0, g, 0, 0))
    table = pl.BlockSpec((1, rows, HD), lambda g: (g, 0, 0))
    return pl.pallas_call(
        project_qkv_body,
        grid=(line,),
        out_shape=(
            jax.ShapeDtypeStruct(x_all.shape, BF),
            jax.ShapeDtypeStruct((line, rows, col), BF),
            jax.ShapeDtypeStruct((2, line, rows, col), BF),
        ),
        in_specs=[
            tokens,
            full(w_qkv.shape),
            full((1, width)),
            full((1, 3 * col)),
            table,
            table,
        ],
        out_specs=(
            tokens,
            pl.BlockSpec((1, rows, col), lambda g: (g, 0, 0)),
            pl.BlockSpec((2, 1, rows, col), lambda g: (0, g, 0, 0)),
        ),
        compiler_params=local_params(56),
        cost_estimate=cost(),
    )(x_all, w_qkv, gain[None], bias[None], cos, sin)


def local_params(mebibytes):
    return pltpu.CompilerParams(vmem_limit_bytes=mebibytes * 2**20)


def head_probs(query, keys, allowed):
    scores = project_t(query, keys) * (HD**-0.5)
    scores = jnp.where(allowed, scores, NEGATIVE)
    weights = jnp.exp(scores - jnp.max(scores, -1, keepdims=True))
    return weights / jnp.sum(weights, -1, keepdims=True)


def key_value(kv_ref, which):
    part = kv_ref[:, which, 0]
    return part.reshape(part.shape[0] * part.shape[1], part.shape[2])


def attend_body(q_ref, kv_ref, high_ref, low_ref, code_ref, w_ref, attn_ref, partial_ref):
    col = q_ref.shape[2]
    keys, values = key_value(kv_ref, 0), key_value(kv_ref, 1)
    allowed = (code_ref[0] <= high_ref[0]) & (code_ref[0] >= low_ref[0])
    outs = []
    for h in range(col // HD):
        at = slice(h * HD, (h + 1) * HD)
        probs = head_probs(q_ref[0, :, at], keys[:, at], allowed).astype(BF)
        outs.append(project(probs, values[:, at]).astype(BF))
    attn = jnp.concatenate(outs, 1) if len(outs) > 1 else outs[0]
    attn_ref[...] = attn.reshape(attn_ref.shape)
    partial_ref[...] = project(attn, w_ref[...]).astype(BF).reshape(partial_ref.shape)


def attention_specs(line, rows, col, n_cx):
    return [
        pl.BlockSpec((1, rows, col), lambda g: (g, 0, 0)),
        pl.BlockSpec((n_cx, 2, 1, rows, col), lambda g: (0, 0, g, 0, 0)),
        pl.BlockSpec((1, rows, 1), lambda g: (g, 0, 0)),
        pl.BlockSpec((1, rows, 1), lambda g: (g, 0, 0)),
        pl.BlockSpec((1, 1, n_cx * rows), lambda g: (g, 0, 0)),
    ]


def attend(query, kv, codes, w_out):
    line, rows, col = query.shape
    tok, width = rows // CORES, w_out.shape[1]
    return pl.pallas_call(
        attend_body,
        grid=(line,),
        out_shape=(
            jax.ShapeDtypeStruct((CORES, line, tok, col), BF),
            jax.ShapeDtypeStruct((CORES, line, tok, width), BF),
        ),
        in_specs=attention_specs(line, rows, col, kv.shape[0]) + [full(w_out.shape)],
        out_specs=(
            pl.BlockSpec((CORES, 1, tok, col), lambda g: (0, g, 0, 0)),
            pl.BlockSpec((CORES, 1, tok, width), lambda g: (0, g, 0, 0)),
        ),
        compiler_params=local_params(56),
        cost_estimate=cost(),
    )(query, kv, *codes, w_out)


def attend_back_body(
    q_ref,
    kv_ref,
    high_ref,
    low_ref,
    code_ref,
    w_ref,
    dp_ref,
    cos_ref,
    sin_ref,
    dq_ref,
    own_ref,
    far_ref,
):
    col = q_ref.shape[2]
    rows = q_ref.shape[1]
    keys, values = key_value(kv_ref, 0), key_value(kv_ref, 1)
    allowed = (code_ref[0] <= high_ref[0]) & (code_ref[0] >= low_ref[0])
    d_proj = dp_ref[...].reshape(rows, dp_ref.shape[3])
    d_attn = project_t(d_proj, w_ref[...]).astype(BF)
    scale = HD**-0.5
    cos, sin = cos_ref[0], sin_ref[0]
    for h in range(col // HD):
        at = slice(h * HD, (h + 1) * HD)
        query = q_ref[0, :, at]
        weights = head_probs(query, keys[:, at], allowed)
        probs = weights.astype(BF)
        d_probs = project_t(d_attn[:, at], values[:, at])
        delta = jnp.sum(probs.astype(F32) * d_probs, -1, keepdims=True)
        d_scores = (weights * (d_probs - delta)).astype(BF)
        d_query = project(d_scores, keys[:, at]) * scale
        d_key = weight_grad(d_scores, query) * scale
        d_value = weight_grad(probs, d_attn[:, at])
        dq_ref[:, :, :, at] = (
            turn(d_query, cos, -sin).astype(BF).reshape(dq_ref.shape[:3] + (HD,))
        )
        for which, value in enumerate((d_key, d_value)):
            own_ref[which, 0, :, at] = value[:rows].astype(BF)
            far_ref[:, which, 0, :, at] = (
                value[rows:].astype(BF).reshape((far_ref.shape[0], rows, HD))
            )


def attend_back(query, kv, codes, w_out, d_proj, cos, sin):
    line, rows, col = query.shape
    tok, width = rows // CORES, w_out.shape[1]
    table = pl.BlockSpec((1, rows, HD), lambda g: (g, 0, 0))
    specs = attention_specs(line, rows, col, kv.shape[0])
    return pl.pallas_call(
        attend_back_body,
        grid=(line,),
        out_shape=(
            jax.ShapeDtypeStruct((CORES, line, tok, col), BF),
            jax.ShapeDtypeStruct(kv.shape[1:], BF),
            jax.ShapeDtypeStruct((kv.shape[0] - 1,) + kv.shape[1:], BF),
        ),
        in_specs=specs
        + [
            full(w_out.shape),
            pl.BlockSpec((CORES, 1, tok, width), lambda g: (0, g, 0, 0)),
            table,
            table,
        ],
        out_specs=(
            pl.BlockSpec((CORES, 1, tok, col), lambda g: (0, g, 0, 0)),
            pl.BlockSpec((2, 1, rows, col), lambda g: (0, g, 0, 0)),
            pl.BlockSpec((kv.shape[0] - 1, 2, 1, rows, col), lambda g: (0, 0, g, 0, 0)),
        ),
        compiler_params=local_params(56),
        cost_estimate=cost(),
    )(query, kv, *codes, w_out, d_proj, cos, sin)


def qkv_back_body(
    dq_ref, own_ref, came_ref, cos_ref, sin_ref, w_ref, x_ref, d_ref, partial_ref, gain_ref, bias_ref
):
    rows = own_ref.shape[2]
    col = own_ref.shape[3]
    cos, sin = cos_ref[0], sin_ref[0]
    d_key, d_value = own_ref[0, 0].astype(F32), own_ref[1, 0].astype(F32)
    for k in range(came_ref.shape[0]):
        d_key = d_key + came_ref[k, 0, 0].astype(F32)
        d_value = d_value + came_ref[k, 1, 0].astype(F32)
    keys = [
        turn(d_key[:, h * HD : (h + 1) * HD], cos, -sin).astype(BF) for h in range(col // HD)
    ]
    d_lin = jnp.concatenate([dq_ref[...].reshape(rows, col)] + keys + [d_value.astype(BF)], 1)
    d_ref[...] = d_lin.reshape(d_ref.shape)
    partial = project_t(d_lin, w_ref[...])
    partial_ref[...] = partial.astype(BF).reshape(partial_ref.shape)
    normal, _ = rms_parts(x_ref[...].reshape(rows, x_ref.shape[3]).astype(F32))
    gain = jnp.sum(partial * normal, 0, keepdims=True)
    bias = jnp.sum(d_lin.astype(F32), 0, keepdims=True)

    @pl.when(pl.program_id(0) == 0)
    def _():
        gain_ref[...] = jnp.zeros_like(gain_ref)
        bias_ref[...] = jnp.zeros_like(bias_ref)

    gain_ref[...] += gain
    bias_ref[...] += bias


def qkv_back(d_query, own, came, cos, sin, w_qkv, x_all):
    cores, line, tok, width = x_all.shape
    _, _, rows, col = own.shape
    tokens = pl.BlockSpec((cores, 1, tok, width), lambda g: (0, g, 0, 0))
    table = pl.BlockSpec((1, rows, HD), lambda g: (g, 0, 0))
    return pl.pallas_call(
        qkv_back_body,
        grid=(line,),
        out_shape=(
            jax.ShapeDtypeStruct((cores, line, tok, 3 * col), BF),
            jax.ShapeDtypeStruct(x_all.shape, BF),
            jax.ShapeDtypeStruct((1, width), F32),
            jax.ShapeDtypeStruct((1, 3 * col), F32),
        ),
        in_specs=[
            pl.BlockSpec((cores, 1, tok, col), lambda g: (0, g, 0, 0)),
            pl.BlockSpec((2, 1, rows, col), lambda g: (0, g, 0, 0)),
            pl.BlockSpec((came.shape[0], 2, 1, rows, col), lambda g: (0, 0, g, 0, 0)),
            table,
            table,
            full(w_qkv.shape),
            tokens,
        ],
        out_specs=(
            pl.BlockSpec((cores, 1, tok, 3 * col), lambda g: (0, g, 0, 0)),
            tokens,
            full((1, width)),
            full((1, 3 * col)),
        ),
        compiler_params=local_params(56),
        cost_estimate=cost(),
    )(d_query, own, came, cos, sin, w_qkv, x_all)


def ahead_body(
    partial_ref, x_ref, gain_ref, gu_ref, sd_ref, resid_ref, all_ref, wgu_ref, wsd_ref, *rest
):
    dp, cx, _, _ = places()
    greet(line_peers() + [moved(core=1)] + plane_peers())
    bufs, sems = rest[:3], rest[3:]
    normed_ref = sems[-1]
    collect = Collect(partial_ref, *bufs, sems[0:5])
    collect.start()
    local = sems[5]
    keep = [
        pltpu.make_async_copy(gu_ref, wgu_ref.at[dp, cx], local.at[0]),
        pltpu.make_async_copy(sd_ref, wsd_ref.at[dp, cx], local.at[1]),
    ]
    for copy in keep:
        copy.start()
    gu = Plane(wgu_ref, sems[6:8], gu_ref)
    sd = Plane(wsd_ref, sems[8:10], sd_ref)
    gu.start()
    sd.start()
    total = collect.reduce()
    resid = x_ref[...].astype(F32) + total
    resid_ref[...] = resid
    normal, _ = rms_parts(resid)
    normed_ref[...] = (normal * gain_ref[...]).astype(BF)
    spread = Spread(normed_ref, all_ref, sems[10:14])
    spread.start()
    spread.forward_step(1)
    gu.forward()
    for step in range(2, lax.axis_size("exp")):
        spread.forward_step(step)
        if step == 2:
            sd.forward()
    collect.finish()
    spread.finish()
    gu.finish()
    sd.finish()
    for copy in keep:
        copy.wait()


def ahead(partial, x_own, gain, gu, sd):
    n_dp, n_cx, line = (lax.axis_size(axis) for axis in ("dp", "cx", "exp"))
    tok, width = x_own.shape
    return pl.pallas_call(
        ahead_body,
        out_shape=(
            jax.ShapeDtypeStruct((tok, width), F32),
            jax.ShapeDtypeStruct((CORES, line, tok, width), BF),
            jax.ShapeDtypeStruct((n_dp, n_cx) + gu.shape, BF),
            jax.ShapeDtypeStruct((n_dp, n_cx) + sd.shape, BF),
        ),
        in_specs=[ANY, VMEM, VMEM, ANY, ANY],
        out_specs=(VMEM, ANY, ANY, ANY),
        scratch_shapes=Collect.scratch(line, tok, width)
        + [pltpu.SemaphoreType.DMA((2,))]
        + Plane.scratch(n_dp, n_cx)
        + Plane.scratch(n_dp, n_cx)
        + Spread.scratch(line)
        + [pltpu.VMEM((tok, width), BF)],
        compiler_params=params(2, 54),
        cost_estimate=cost(),
    )(partial, x_own, gain, gu, sd)


def back_body(
    partial_ref,
    resid_ref,
    gain_ref,
    cot_ref,
    dots_ref,
    router_ref,
    score_ref,
    small_ref,
    mix_ref,
    dn_ref,
    dr_ref,
    all_ref,
    logits_ref,
    dscore_ref,
    mixed_ref,
    *rest,
):
    greet(tp_peers())
    bufs, sems = rest[:3], rest[3:]
    collect = Collect(partial_ref, *bufs, sems[0:5])
    collect.start()
    mix = Collect(mix_ref, *sems[14:17], sems[17:22])
    proj_ref = sems[9]
    dot_send, dot_recv, came_ref, keep_sem = sems[10:14]
    line = lax.axis_size("exp")
    keep = pltpu.make_async_copy(dots_ref.at[0, 0], came_ref.at[0, 0], keep_sem)
    keep.start()
    outs = [
        copy_to(
            dots_ref.at[c, k],
            came_ref.at[c, k],
            dot_send.at[c, k],
            dot_recv.at[c, k],
            moved(core=c, exp=k),
        )
        for c in range(CORES)
        for k in range(line)
        if c or k
    ]
    mix.start()
    collect.send()
    mix.ready()
    keep.wait()
    for copy in outs:
        copy.wait()
    _, _, core, exp = places()
    n_experts = router_ref.shape[0]
    row = lax.broadcasted_iota(jnp.int32, router_ref.shape, 0)
    d_router = jnp.zeros(router_ref.shape, F32)
    d_score = jnp.zeros(score_ref.shape, F32)
    for c in range(CORES):
        for k in range(line):
            tile = came_ref[c, k]
            source = lax.rem(exp + line - k, line) * CORES + lax.rem(core + CORES - c, CORES)
            d_router = d_router + jnp.where(row == source, tile[0:1], 0.0)
            d_score = d_score + tile[1:2]
    score = score_ref[...]
    d_score = d_score * score * (1.0 - score)
    router = router_ref[...]
    d_logits = (router * (d_router - jnp.sum(router * d_router, 0, keepdims=True))).astype(BF)
    high = d_score.astype(BF)
    mid = (d_score - high.astype(F32)).astype(BF)
    tail = (d_score - high.astype(F32) - mid.astype(F32)).astype(BF)
    logits_ref[...] = d_logits
    dscore_ref[...] = jnp.concatenate([high, mid, tail], 0)
    extra = weight_grad(d_logits, small_ref[0:n_experts])
    for part in (high, mid, tail):
        extra = extra + weight_grad(part, small_ref[n_experts : n_experts + 1])
    normal, inverse = rms_parts(resid_ref[...])
    d_normed = collect.gather() + extra
    dn_ref[...] = d_normed
    d_hat = d_normed * gain_ref[...]
    d_resid = cot_ref[...].astype(F32) + inverse * (
        d_hat - normal * jnp.mean(d_hat * normal, 1, keepdims=True)
    )
    dr_ref[...] = d_resid
    proj_ref[...] = d_resid.astype(BF)
    spread = Spread(proj_ref, all_ref, sems[5:9])
    spread.start()
    for step in range(1, line):
        spread.forward_step(step)
        mix.send_step(line - step)
    collect.finish()
    spread.finish()
    mixed_ref[...] = (resid_ref[...] + mix.gather()).astype(BF)
    mix.finish()


def back(partial, resid, gain, cot, dots, router, score, small, mix):
    line = lax.axis_size("exp")
    tok, width = resid.shape
    dma = pltpu.SemaphoreType.DMA
    return pl.pallas_call(
        back_body,
        out_shape=(
            jax.ShapeDtypeStruct((tok, width), F32),
            jax.ShapeDtypeStruct((tok, width), F32),
            jax.ShapeDtypeStruct((CORES, line, tok, width), BF),
            jax.ShapeDtypeStruct(router.shape, BF),
            jax.ShapeDtypeStruct((3, tok), BF),
            jax.ShapeDtypeStruct((tok, width), BF),
        ),
        in_specs=[ANY, VMEM, VMEM, VMEM, ANY, VMEM, VMEM, VMEM, ANY],
        out_specs=(VMEM, VMEM, ANY, VMEM, VMEM, VMEM),
        scratch_shapes=Collect.scratch(line, tok, width)
        + Spread.scratch(line)
        + [pltpu.VMEM((tok, width), BF)]
        + [dma((CORES, line)), dma((CORES, line)), pltpu.VMEM(dots.shape, F32), dma]
        + Collect.scratch(line, tok, width),
        compiler_params=params(3, 52 + line // 2),
        cost_estimate=cost(),
    )(partial, resid, gain, cot, dots, router, score, small, mix)


class Rows:
    def __init__(self, block, line):
        self.block, self.rows = block, block.shape[1] // line

    @property
    def at(self):
        return self

    def __getitem__(self, spot):
        core, exp = spot
        start = pl.multiple_of(exp * self.rows, self.rows)
        return self.block.at[core, pl.ds(start, self.rows)]


def last_body(
    partial_ref,
    gq_ref,
    go_ref,
    tot_ref,
    egu_ref,
    ed_ref,
    gsd_ref,
    x_ref,
    gain_ref,
    dres_ref,
    out_ref,
    q_ref,
    k_ref,
    v_ref,
    wo_ref,
    sum_ref,
    eg_ref,
    eu_ref,
    edown_ref,
    sd_ref,
    *rest,
):
    dp, cx, core, exp = places()
    line = lax.axis_size("exp")
    greet(all_peers())
    collect = Collect(partial_ref, *rest[:3], rest[3:8])
    qkv_block, tots_ref, cols_ref = rest[8:11]
    qkv = PlaneSum(gq_ref, qkv_block, rest[11:29])
    wo = PlaneSum(go_ref, wo_ref, rest[29:47])
    tot_send, tot_recv, local = rest[47:50]
    columns = Columns(Rows(qkv_block, line), cols_ref, rest[50:53])
    gu_came, d_came, swap_send, swap_recv, store = rest[53:58]
    wide, tall = rest[58:60]
    sd = PlaneSum(gsd_ref, sd_ref, rest[60:78])
    collect.start()
    rows, down = gu_came.shape[0], d_came.shape[0]
    swaps = [
        copy_to(
            source.at[pl.ds((1 - core) * height, height)],
            target,
            swap_send.at[n],
            swap_recv.at[n],
            moved(core=1),
        )
        for n, (source, target, height) in enumerate(
            ((egu_ref, gu_came, rows), (ed_ref, d_came, down))
        )
    ]
    qkv.start()
    collect.ready()
    steps_left = list(range(line - 1, 0, -1))
    while len(steps_left) > 2:
        collect.send_step(steps_left.pop(0))
    keep = pltpu.make_async_copy(
        tot_ref.at[dp, cx, core, exp], tots_ref.at[0, 0, 0, 0], local
    )
    keep.start()
    sizes = [range(lax.axis_size(axis)) for axis in ("dp", "cx", "core", "exp")]
    outs = []
    for steps in itertools.product(*sizes):
        if any(steps):
            target = moved(*steps)
            outs.append(
                copy_to(
                    tot_ref.at[target],
                    tots_ref.at[steps],
                    tot_send.at[steps],
                    tot_recv.at[steps],
                    target,
                )
            )
    qkv.middle()
    wo.start()
    sd.start()
    collect.send_step(steps_left.pop(0))
    qkv.end()
    columns.start()
    collect.send_step(steps_left.pop(0))
    wo.middle()
    sd.middle()
    for copy in swaps:
        copy.wait_recv()
    ffe = wide.shape[3]

    def mine(at):
        piece = egu_ref[pl.ds(pl.multiple_of(core * rows + at.start, 8), at.size)].astype(F32)
        wide[0, core, at] = piece[:, :ffe]
        wide[1, core, at] = piece[:, ffe:]
        piece = gu_came[at].astype(F32)
        wide[0, 1 - core, at] = piece[:, :ffe]
        wide[1, 1 - core, at] = piece[:, ffe:]

    by_chunks(rows, mine)

    def down_rows(at):
        piece = ed_ref[pl.ds(pl.multiple_of(core * down + at.start, 8), at.size)]
        tall[core, at] = piece.astype(F32)
        tall[1 - core, at] = d_came[at].astype(F32)

    by_chunks(down, down_rows)
    stores = [
        pltpu.make_async_copy(wide.at[0], eg_ref, store.at[0]),
        pltpu.make_async_copy(wide.at[1], eu_ref, store.at[1]),
        pltpu.make_async_copy(tall, edown_ref, store.at[2]),
    ]
    for copy in stores:
        copy.start()
    normal, inverse = rms_parts(x_ref[...].astype(F32))
    d_hat = collect.gather() * gain_ref[...]
    out_ref[...] = (
        dres_ref[...]
        + inverse * (d_hat - normal * jnp.mean(d_hat * normal, 1, keepdims=True))
    ).astype(BF)
    wo.end()
    sd.end()
    keep.wait()
    for copy in outs:
        copy.wait()
    sum_ref[...] = jnp.sum(tots_ref[...].reshape((-1,) + tots_ref.shape[4:]), 0)
    columns.arrive()
    col = cols_ref.shape[3] // 3
    for n, target in enumerate((q_ref, k_ref, v_ref)):
        for c in range(CORES):
            for e in range(line):
                at = (e * CORES + c) * col
                target[:, at : at + col] = cols_ref[c, e, :, n * col : (n + 1) * col].astype(F32)
    columns.finish()
    collect.finish()
    for copy in swaps:
        copy.wait_send()
    for copy in stores:
        copy.wait()


def last(
    partial, grad_qkv, grad_out, totals, grad_egu, grad_edown, grad_sd, x_own, gain, d_resid
):
    n_dp, n_cx, line = (lax.axis_size(axis) for axis in ("dp", "cx", "exp"))
    tok, width = partial.shape[2:]
    dma = pltpu.SemaphoreType.DMA
    shard = grad_qkv.shape[3] // line
    rows, both = grad_egu.shape
    down = grad_edown.shape[0]
    heads = jax.ShapeDtypeStruct((shard, width), F32)
    wide = (CORES, rows // 2, both // 2)
    tall = (CORES, down // 2, width)
    return pl.pallas_call(
        last_body,
        out_shape=(
            jax.ShapeDtypeStruct((tok, width), BF),
            heads,
            heads,
            heads,
            jax.ShapeDtypeStruct(grad_out.shape[2:], F32),
            jax.ShapeDtypeStruct(totals.shape[4:], F32),
            jax.ShapeDtypeStruct(wide, F32),
            jax.ShapeDtypeStruct(wide, F32),
            jax.ShapeDtypeStruct(tall, F32),
            jax.ShapeDtypeStruct(grad_sd.shape[2:], F32),
        ),
        in_specs=[ANY, ANY, ANY, ANY, VMEM, VMEM, ANY, VMEM, VMEM, VMEM],
        out_specs=(VMEM,) * 6 + (ANY,) * 3 + (VMEM,),
        scratch_shapes=Collect.scratch(line, tok, width)
        + [
            pltpu.VMEM(grad_qkv.shape[2:], BF),
            pltpu.VMEM(totals.shape, F32),
            pltpu.VMEM((CORES, line, shard, grad_qkv.shape[4]), BF),
        ]
        + PlaneSum.scratch(*grad_qkv.shape[3:])
        + PlaneSum.scratch(*grad_out.shape[3:])
        + [dma((n_dp, n_cx, CORES, line)), dma((n_dp, n_cx, CORES, line)), dma]
        + Columns.scratch(line)
        + [
            pltpu.VMEM((rows // 2, both), BF),
            pltpu.VMEM((down // 2, width), BF),
            dma((2,)),
            dma((2,)),
            dma((3,)),
            pltpu.VMEM((2,) + wide, F32),
            pltpu.VMEM(tall, F32),
        ]
        + PlaneSum.scratch(*grad_sd.shape[3:]),
        compiler_params=params(4, 50 + line // 2),
        cost_estimate=cost(),
    )(
        partial,
        grad_qkv,
        grad_out,
        totals,
        grad_egu,
        grad_edown,
        grad_sd,
        x_own,
        gain,
        d_resid,
    )


def on_device(
    tokens,
    cotangent,
    positions,
    lengths,
    routes,
    norm_attn,
    w_query,
    bias_query,
    w_key,
    bias_key,
    w_value,
    bias_value,
    w_output,
    norm_moe,
    w_router,
    w_shared_gate,
    w_shared_up,
    w_shared_down,
    w_shared_score,
    w_expert_gate,
    w_expert_up,
    w_expert_down,
):
    n_dp = lax.axis_size("dp")
    n_cx = lax.axis_size("cx")
    n_exp = lax.axis_size("exp")
    exp_at = lax.axis_index("exp")
    core_at = lax.axis_index("core")
    n_tp = CORES * n_exp
    n_data = n_dp * n_cx
    tok, width = tokens.shape[2:]
    shard = w_query.shape[0]
    block = CORES * n_exp * shard
    col = width // n_tp
    heads = col // HD
    n_experts = w_router.shape[1]
    sub = w_shared_down.shape[0]
    sub_width = n_data * sub
    every = tok * n_tp
    scale = HD ** (-0.5)
    top = routes.shape[3]
    ffe = w_expert_gate.shape[2]

    def by_core(first, second):
        return jnp.where(core_at == 0, first, second)

    x_own = tokens.reshape(tok, width)
    cot_own = cotangent.reshape(tok, width)

    small = jnp.concatenate(
        [
            norm_attn[None],
            norm_moe[None],
            w_shared_score[None],
            bias_query[None],
            bias_key[None],
            bias_value[None],
            w_router.T,
        ]
    ).astype(F32)
    n_small = small.shape[0]
    pack = jnp.concatenate(
        [
            positions.reshape(1, tok),
            routes.reshape(tok, top).T,
            jnp.pad(lengths.reshape(1, -1), ((0, 0), (0, tok - lengths.shape[2]))),
        ]
    ).astype(F32)
    pack = jnp.concatenate([pack, jnp.pad(small, ((0, 0), (0, tok - shard)))])
    pack = jnp.pad(pack, ((0, -pack.shape[0] % 8), (0, 0)))

    def exchange(value):
        return lax.all_to_all(value, ("core", "exp"), split_axis=0, concat_axis=0, tiled=True)

    def head_columns(value):
        parts = value.reshape(shard, n_exp, CORES, col)
        return jnp.transpose(parts, (2, 1, 0, 3))

    qkv_cols = jnp.concatenate(
        [head_columns(w_query), head_columns(w_key), head_columns(w_value)], 3
    )
    x_all, w_qkv, wo_all, packs, cot_tok = load(x_own, qkv_cols, w_output, pack, cot_own)
    w_egu = lax.all_gather(
        jnp.concatenate([w_expert_gate, w_expert_up], 2), ("dp", "cx", "core"), axis=1, tiled=True
    )
    w_edown = lax.all_gather(w_expert_down, ("dp", "cx", "core"), axis=1, tiled=True)
    w_egu = lax.dynamic_index_in_dim(w_egu, core_at, 0, keepdims=False)
    w_edown = lax.dynamic_index_in_dim(w_edown, core_at, 0, keepdims=False)
    w_qkv = w_qkv.reshape(width, 3 * col)
    gu_cols = split_hidden(w_shared_gate, w_shared_up, n_exp, sub)

    small = packs[:, :, :, :, 2 + top : 2 + top + n_small, :shard]
    small = jnp.moveaxis(small, 4, 0).reshape(n_small, width)
    gain_attn = small[0]
    gain_moe = small[1]
    score_vec = small[2]
    router_full = small[6:].T.astype(BF)
    rank = exp_at * CORES + core_at
    biases = lax.dynamic_slice_in_dim(small[3:6], rank * col, col, 1).reshape(3 * col)

    ints = lax.dynamic_index_in_dim(packs, lax.axis_index("dp"), 0, keepdims=False)
    ints = ints[:, :, :, : 2 + top]
    for dim, axis in enumerate(("cx", "core", "exp")):
        ints = roll_to_relative(ints, axis, dim)
    ints = ints.astype(jnp.int32)
    route_tok = jnp.swapaxes(ints[0, :, :, 1 : 1 + top], 2, 3).reshape(every, top)
    seq_lens = ints[0, 0, :, 1 + top, : lengths.shape[2]]
    seq_ends = jnp.cumsum(seq_lens, 1)
    pos_keys = jnp.moveaxis(ints[:, :, :, 0], 2, 0).reshape(n_exp, n_cx * CORES * tok)
    after_end = (pos_keys[:, :, None] >= seq_ends[:, None, :]).astype(jnp.int32)
    seg_keys = jnp.sum(after_end, 2)
    rel_keys = pos_keys - jnp.sum(after_end * seq_lens[:, None, :], 2)
    own_keys = CORES * tok
    code_keys = (seg_keys * 4096 + pos_keys)[:, None, :]
    low = (seg_keys[:, :own_keys] * 4096)[:, :, None]
    codes = (low + pos_keys[:, :own_keys, None], low, code_keys)
    freq = ROTARY_BASE ** (-(jnp.arange(HD // 2, dtype=F32) * 2.0 / HD))
    angle = rel_keys[:, :own_keys].astype(F32)[:, :, None] * freq
    cos_table = jnp.cos(angle)
    sin_table = jnp.sin(angle)
    cos_table = jnp.concatenate([cos_table, cos_table], 2)
    sin_table = jnp.concatenate([-sin_table, sin_table], 2)

    normed_one, query, kv = project_qkv(x_all, w_qkv, gain_attn, biases, cos_table, sin_table)
    normed_one = normed_one.reshape(every, width)
    kv_all, gu_block, w_out = keys_call(kv, gu_cols, wo_all)
    w_out = w_out.reshape(col, width)
    attn_low, partial = attend(query, kv_all, codes, w_out)
    resid, normed_two, w_sgu, w_sdown = ahead(
        partial,
        x_own,
        gain_moe[None],
        gu_block,
        w_shared_down.reshape(2, sub // 2, width),
    )
    normed_two = normed_two.reshape(every, width)
    normed_two_own = normed_two[:tok]
    w_sgu = w_sgu.reshape(width, 2 * sub_width)
    w_sdown = w_sdown.reshape(sub_width, width)

    small_cols = jnp.concatenate([router_full, score_vec.astype(BF)[:, None]], 1)
    small_out = project(normed_two, small_cols)
    router_all = jax.nn.softmax(small_out[:, :n_experts], axis=-1)
    score_all = jax.nn.sigmoid(small_out[:, n_experts])
    chosen = jnp.any(route_tok == rank, axis=1)
    at_rank = (jnp.arange(n_experts) == rank).astype(F32)
    gate = jnp.where(chosen, jnp.sum(router_all * at_rank[None, :], 1), 0.0)

    cot_all = cot_tok.reshape(every, width).astype(F32)
    shared_pre = held(project(normed_two, w_sgu))
    s_gate = shared_pre[:, :sub_width].astype(F32)
    s_up = shared_pre[:, sub_width:].astype(F32)
    s_act, s_slope = silu_parts(s_gate)
    s_hidden = (s_act * s_up).astype(BF)
    shared = held(project(s_hidden, w_sdown)).astype(F32)
    d_shared = (score_all[:, None] * cot_all).astype(BF)
    d_sh = project_t(d_shared, w_sdown)
    d_sgu = jnp.concatenate(
        [(d_sh * s_up * s_slope).astype(BF), (d_sh * s_act).astype(BF)], 1
    )
    grad_sgu = weight_grad(normed_two, d_sgu).astype(BF)
    normed_late, grad_sgu = lax.optimization_barrier((normed_two, grad_sgu))
    grad_sgu = lax.psum_scatter(grad_sgu, ("dp", "cx"), scatter_dimension=0, tiled=True)
    expert_pre = held(project(normed_late, w_egu))
    e_gate = expert_pre[:, :ffe].astype(F32)
    e_up = expert_pre[:, ffe:].astype(F32)
    e_act, e_slope = silu_parts(e_gate)
    e_hidden = (e_act * e_up).astype(BF)
    e_out = project(e_hidden, w_edown).astype(BF).astype(F32)
    mix = (score_all[:, None] * shared + gate[:, None] * e_out).astype(BF)
    dots = jnp.stack(
        [
            jnp.where(chosen, jnp.sum(cot_all * e_out, 1), 0.0),
            jnp.sum(cot_all * shared, 1),
        ]
    )

    d_eout = (gate[:, None] * cot_all).astype(BF)
    d_eh = project_t(d_eout, w_edown)
    d_egu = jnp.concatenate(
        [(d_eh * e_up * e_slope).astype(BF), (d_eh * e_act).astype(BF)], 1
    )
    grad_egu = weight_grad(normed_late, d_egu).astype(BF)
    grad_edown = weight_grad(e_hidden, d_eout).astype(BF)
    d_egu, grad_egu, grad_edown = lax.optimization_barrier((d_egu, grad_egu, grad_edown))
    grad_egu = lax.psum_scatter(grad_egu, ("dp", "cx"), scatter_dimension=0, tiled=True)
    grad_edown = lax.psum_scatter(grad_edown, ("dp", "cx"), scatter_dimension=0, tiled=True)
    grad_sdown = weight_grad(s_hidden, d_shared).astype(BF)
    partial_two = (project_t(d_sgu, w_sgu) + held(project_t(d_egu, w_egu)).astype(F32)).astype(BF)

    dots = jnp.pad(dots.reshape(2, n_tp, tok).swapaxes(0, 1), ((0, 0), (0, 6), (0, 0)))
    d_normed_two, d_resid, d_proj, d_logits, d_score, mixed = back(
        partial_two.reshape(CORES, n_exp, tok, width),
        resid,
        gain_moe[None],
        cot_own,
        dots.reshape(CORES, n_exp, 8, tok),
        router_all[:tok].T,
        score_all[None, :tok],
        jnp.concatenate([router_full.T, score_vec.astype(BF)[None]]),
        mix.reshape(CORES, n_exp, tok, width),
    )
    grad_router = project(d_logits, normed_two_own)
    grad_score = project(d_score, normed_two_own).sum(0)
    grad_gain_moe = jnp.sum(d_normed_two * rms_parts(resid)[0], 0)

    grad_sgu, d_proj = lax.optimization_barrier((grad_sgu, d_proj))
    grad_sgu = exchange(grad_sgu.reshape(n_tp, shard, 2 * sub_width))
    grad_sgu = grad_sgu.reshape(CORES, n_exp, shard, 2 * sub_width)

    d_query, d_kv_own, d_kv_far = attend_back(query, kv_all, codes, w_out, d_proj, cos_table, sin_table)
    came = jnp.stack([push(d_kv_far[k - 1], "cx", k) for k in range(1, n_cx)])
    came, grad_sgu = lax.optimization_barrier((came, grad_sgu))
    d_qkv, partial_one, grad_gain_attn, grad_bias = qkv_back(
        d_query, d_kv_own, came, cos_table, sin_table, w_qkv, x_all
    )
    grad_qkv = weight_grad(normed_one, d_qkv.reshape(every, 3 * col)).astype(BF)
    grad_out = lax.all_to_all(
        weight_grad(attn_low.reshape(every, col), d_proj.reshape(every, width))
        .astype(BF)
        .reshape(n_exp, shard, width),
        "exp",
        split_axis=0,
        concat_axis=0,
        tiled=True,
    )
    grad_bias = lax.dynamic_update_slice_in_dim(
        jnp.zeros((3, width), F32), grad_bias.reshape(3, col), rank * col, 1
    )
    totals = jnp.concatenate(
        [
            grad_gain_attn,
            grad_gain_moe[None],
            grad_score[None],
            grad_bias,
            grad_router,
        ]
    )
    totals = jnp.moveaxis(totals.reshape(n_small, n_data * n_tp, shard), 0, 1)
    totals = totals.reshape(n_data * n_tp, -1)
    totals = jnp.pad(totals, ((0, 0), (0, -totals.shape[1] % 1024)))
    grad_sgate, grad_sup = merge_hidden(grad_sgu, sub)
    partial_one, grad_sgate, grad_sup = lax.optimization_barrier(
        (partial_one, grad_sgate, grad_sup)
    )
    (
        grad_tokens,
        grad_query,
        grad_key,
        grad_value,
        grad_out,
        totals,
        grad_egate,
        grad_eup,
        grad_edown,
        grad_sdown,
    ) = last(
        partial_one,
        grad_qkv.reshape(n_dp, n_cx, 2, -1, 3 * col),
        grad_out.reshape(n_dp, n_cx, 2, shard // 2, width),
        totals.reshape(n_dp, n_cx, CORES, n_exp, -1, 128),
        grad_egu,
        grad_edown,
        grad_sdown.reshape(n_dp, n_cx, 2, -1, width),
        x_own,
        gain_attn[None],
        d_resid,
    )
    grad_sdown = grad_sdown.reshape(sub, width)
    grad_out = grad_out.reshape(shard, width)
    totals = totals.reshape(-1)[: n_small * shard].reshape(n_small, shard)
    return (
        mixed.reshape(tokens.shape),
        grad_tokens.reshape(tokens.shape),
        totals[0],
        grad_query,
        totals[3],
        grad_key,
        totals[4],
        grad_value,
        totals[5],
        grad_out,
        totals[1],
        totals[6:].T,
        grad_sgate,
        grad_sup,
        grad_sdown,
        totals[2],
        grad_egate,
        grad_eup,
        grad_edown,
    )


def solution(mesh):
    sizes = dict(mesh.shape)
    fine = Mesh(
        mesh.devices.reshape(sizes["dp"], sizes["ctx"] // CORES, CORES, sizes["exp"]),
        ("dp", "cx", "core", "exp"),
    )
    own = P("dp", "exp", ("cx", "core"), None)
    flat = P(("dp", "cx", "core", "exp"))
    rows = P(("dp", "cx", "core", "exp"), None)
    expert = P("exp", ("dp", "cx", "core"), None)
    placed = (
        own,
        own,
        P("dp", "exp", ("cx", "core")),
        P("dp", "exp", None),
        own,
        flat,
        rows,
        flat,
        rows,
        flat,
        rows,
        flat,
        rows,
        flat,
        rows,
        rows,
        rows,
        rows,
        flat,
        expert,
        expert,
        expert,
    )
    return jax.shard_map(
        on_device,
        mesh=fine,
        in_specs=placed,
        out_specs=(
            own,
            own,
            flat,
            rows,
            flat,
            rows,
            flat,
            rows,
            flat,
            rows,
            flat,
            rows,
            rows,
            rows,
            rows,
            flat,
            expert,
            expert,
            expert,
        ),
        check_vma=False,
    )
```
